32 devices in a mesh: narrow: 8 (over z, x), wide: 4 (over y, core).
Axes of the slice: x: 2, y: 2, z: 4, core: 2. Of those that a mesh axis runs over, the one named last changes fastest.
Arguments:
- video: bfloat16 [8, 8, 256, 768], P('narrow', 'wide'), may hold values from -6 to 6
- text_states: bfloat16 [8, 120, 768], P('narrow'), may hold values from -6 to 6
- text_length: int32 [8], P('narrow'), may hold values from 16 to 120
- timestep: int32 [8], P('narrow'), may hold values from 0 to 999
- motion_free: int32 [8], P('narrow'), may hold values 0 or 1
- ada_weight: bfloat16 [768, 4608], replicated, may hold values from -0.625 to 0.625
- spatial_qkv_weight: bfloat16 [768, 2304], replicated, may hold values from -0.21875 to 0.21875
- spatial_out_weight: bfloat16 [768, 768], replicated, may hold values from -0.875 to 0.875
- temporal_qkv_weight: bfloat16 [768, 2304], replicated, may hold values from -0.21875 to 0.21875
- temporal_out_weight: bfloat16 [768, 768], replicated, may hold values from -0.4375 to 0.4375
- cross_query_weight: bfloat16 [768, 768], replicated, may hold values from -0.21875 to 0.21875
- cross_kv_weight: bfloat16 [768, 1536], replicated, may hold values from -0.21875 to 0.21875
- cross_out_weight: bfloat16 [768, 768], replicated, may hold values from -0.625 to 0.625
- mlp_in_weight: bfloat16 [768, 3072], replicated, may hold values from -0.21875 to 0.21875
- mlp_out_weight: bfloat16 [3072, 768], replicated, may hold values from -0.109375 to 0.109375
- cotangent: bfloat16 [8, 8, 256, 768], P('narrow', 'wide'), may hold values from -6 to 6
Outputs:
- result: bfloat16 [8, 8, 256, 768], P('narrow', 'wide')
- video_grad: float32 [8, 8, 256, 768], P('narrow', 'wide')
- ada_grad: float32 [3538944], P(('narrow', 'wide'))
- spatial_qkv_grad: float32 [1769472], P(('narrow', 'wide'))
- spatial_out_grad: float32 [589824], P(('narrow', 'wide'))
- temporal_qkv_grad: float32 [1769472], P(('narrow', 'wide'))
- temporal_out_grad: float32 [589824], P(('narrow', 'wide'))
- cross_query_grad: float32 [589824], P(('narrow', 'wide'))
- cross_kv_grad: float32 [1179648], P(('narrow', 'wide'))
- cross_out_grad: float32 [589824], P(('narrow', 'wide'))
- mlp_in_grad: float32 [2359296], P(('narrow', 'wide'))
- mlp_out_grad: float32 [2359296], P(('narrow', 'wide'))
The draws below stay inside these ranges and needn't reach their ends.
Inputs may be any that keep to these rules, and one draw needn't show every extreme that they name: Clip c attends to its first text_length[c] text tokens. A clip with motion_free 1 keeps no temporal branch.
All inputs are finite; a program needn't handle non-finite values. No bound on the sum of `motion_free` on one device may be relied on, other than what follows from the above.
Results may differ from the reference program's by a relative error of at most 0.03.
Values may be sent and summed in bfloat16 or wider, within the bound.
A program may use at most 256 MiB of HBM per device.

```python
import math
import jax
import jax.numpy as jnp
from jax import lax

D = 768
HEADS = 12
HEAD_DIM = 64
MLP = 3072
TXT = 120
PATCH = 256
FRAMES = 8
CLIPS = 8


def with_ends(values, key, least, top_value):
    longest = values.shape.index(max(values.shape))
    spots = []
    for shift in (0, 1):
        where = [jax.random.randint(jax.random.fold_in(key, axis), (), 0, length) for axis, length in enumerate(values.shape)]
        where[longest] = (where[longest] + shift) % values.shape[longest]
        spots.append(tuple(where))
    return values.at[spots[0]].set(least).at[spots[1]].set(top_value)


def steps_of(stream_key, dims, split, smallest, largest):
    factor_of = 1.0
    for axis_at, shards_of in split:
        heights = jax.random.uniform(jax.random.fold_in(jax.random.fold_in(stream_key, 6), axis_at), (shards_of,), jnp.float32, smallest / len(split), largest / len(split))
        factor_of = factor_of * jnp.repeat(jnp.exp(heights), dims[axis_at] // shards_of).reshape((-1,) + (1,) * (len(dims) - 1 - axis_at))
    return factor_of


def noise(rng, extent, scale, bound, shards=(), kind=jnp.bfloat16):
    values = jax.random.normal(rng, extent, jnp.float32) * scale
    if len(shards) > 0:
        values = steps_of(rng, extent, shards, -0.22, 0.18) * values
    return jnp.clip(values, min=-bound, max=bound).astype(kind)


def setup_inputs(seed: int = 0) -> dict:
    key_list = jax.random.split(jax.random.key(seed), 17)
    return {
        "video": noise(key_list[0], (CLIPS, FRAMES, PATCH, D), 1.0, 6.0, ((0, 8), (1, 4))),
        "text_states": noise(key_list[1], (CLIPS, TXT, D), 1.0, 6.0, ((0, 8),)),
        "text_length": with_ends(jax.random.randint(key_list[2], (CLIPS,), TXT // 8 + 1, TXT + 1), jax.random.fold_in(key_list[2], 1), TXT // 8 + 1, TXT).astype(jnp.int32),
        "timestep": with_ends(jax.random.randint(key_list[3], (CLIPS,), 0, 1000), jax.random.fold_in(key_list[3], 1), 0, 999).astype(jnp.int32),
        "motion_free": with_ends((jax.random.randint(key_list[4], (CLIPS,), 0, 4) < 1).astype(jnp.int32), jax.random.fold_in(key_list[4], 1), 0, 1),
        "ada_weight": noise(key_list[5], (D, 6 * D), (D // 8) ** -0.5, 0.625),
        "spatial_qkv_weight": noise(key_list[6], (D, 3 * D), D ** -0.5, 0.21875),
        "spatial_out_weight": noise(key_list[7], (D, D), (D // 16) ** -0.5, 0.875),
        "temporal_qkv_weight": noise(key_list[8], (D, 3 * D), D ** -0.5, 0.21875),
        "temporal_out_weight": noise(key_list[9], (D, D), (D // 4) ** -0.5, 0.4375),
        "cross_query_weight": noise(key_list[10], (D, D), D ** -0.5, 0.21875),
        "cross_kv_weight": noise(key_list[11], (D, 2 * D), D ** -0.5, 0.21875),
        "cross_out_weight": noise(key_list[12], (D, D), (D // 8) ** -0.5, 0.625),
        "mlp_in_weight": noise(key_list[13], (D, MLP), D ** -0.5, 0.21875),
        "mlp_out_weight": noise(key_list[14], (MLP, D), MLP ** -0.5, 0.109375),
        "cotangent": noise(key_list[15], (CLIPS, FRAMES, PATCH, D), 1.0, 6.0, ((0, 8), (1, 4))),
    }


EPSILON = 1e-06
NEG_LARGE = -1e+30
HIGH = lax.Precision.HIGHEST

@jax.custom_vjp
def low(v):
    return lax.optimization_barrier(v.astype(jnp.bfloat16)).astype(jnp.float32)

@jax.custom_vjp
def low_back(v):
    return v

def low_keep(v):
    return (low(v), None)

def low_pass(kept, grad):
    return (grad,)

def back_keep(v):
    return (v, None)

def back_low(kept, grad):
    return (low(grad),)
low.defvjp(low_keep, low_pass)
low_back.defvjp(back_keep, back_low)

def time_features(time_value):
    half = D // 2
    freqs = jnp.exp(-math.log(10000.0) * jnp.arange(half, dtype=jnp.float32) / half)
    angles = time_value.astype(jnp.float32)[..., None] * freqs
    return jnp.concatenate([jnp.cos(angles), jnp.sin(angles)], axis=-1)

def silu_of(values):
    return values / (1.0 + jnp.exp(-values))

def gelu_of(values):
    return 0.5 * values * (1.0 + jnp.tanh(0.7978845608 * (values + 0.044715 * values * values * values)))

def layer_norm(values):
    mean = lax.optimization_barrier(jnp.mean(values, -1, keepdims=True))
    centred = values - mean
    variance = lax.optimization_barrier(jnp.mean(centred * centred, -1, keepdims=True))
    return centred * lax.rsqrt(variance + EPSILON)

def high_dot(left, right):
    return jnp.dot(left, right, precision=HIGH)

def softmax_rows(scores):
    peak = lax.optimization_barrier(jnp.max(scores, -1, keepdims=True))
    expd = jnp.exp(scores - peak)
    return expd / lax.optimization_barrier(jnp.sum(expd, -1, keepdims=True))

def split_heads(values):
    return values.reshape(values.shape[:-1] + (HEADS, HEAD_DIM))

def clip_forward(values, text, length, time_value, keep_value, ada_w, sqkv_w, sout_w, tqkv_w, tout_w, cq_w, ckv_w, cout_w, fin_w, fout_w):
    width = values.shape[-1]
    scale = HEAD_DIM ** (-0.5)
    silu_time = low(silu_of(time_features(time_value)))
    modulation = high_dot(silu_time, ada_w)
    shift_one = modulation[:width]
    scale_one = modulation[width:2 * width]
    gate_one = modulation[2 * width:3 * width]
    shift_two = modulation[3 * width:4 * width]
    scale_two = modulation[4 * width:5 * width]
    gate_two = modulation[5 * width:]
    spatial_in = low(layer_norm(values) * (1.0 + scale_one) + shift_one)
    sproj = low(low_back(high_dot(spatial_in, sqkv_w)))
    spatial_query = split_heads(sproj[..., :width])
    spatial_key = split_heads(sproj[..., width:2 * width])
    spatial_value = split_heads(sproj[..., 2 * width:])
    sscores = low_back(jnp.einsum('fphd,fqhd->fhpq', spatial_query, spatial_key, precision=HIGH) * scale)
    sprobs = softmax_rows(sscores)
    smix = jnp.einsum('fhpq,fqhd->fphd', low(sprobs), spatial_value, precision=HIGH)
    smix = low(low_back(smix.reshape(values.shape)))
    sbranch = low_back(high_dot(smix, sout_w))
    first = values + gate_one * sbranch
    temporal_in = low(layer_norm(first))
    proj = low(low_back(high_dot(temporal_in, tqkv_w)))
    queries = split_heads(proj[..., :width])
    keys_rows = split_heads(proj[..., width:2 * width])
    value_rows = split_heads(proj[..., 2 * width:])
    scores = low_back(jnp.einsum('fphd,gphd->phfg', queries, keys_rows, precision=HIGH) * scale)
    probs = softmax_rows(scores)
    mixed = jnp.einsum('phfg,gphd->fphd', low(probs), value_rows, precision=HIGH)
    mixed = low(low_back(mixed.reshape(values.shape)))
    branch = low_back(high_dot(mixed, tout_w))
    mid = first + keep_value * branch
    cross_in = low(layer_norm(mid))
    cross_queries = low(low_back(high_dot(cross_in, cq_w))).reshape(-1, HEADS, HEAD_DIM)
    text_proj = low(low_back(high_dot(text, ckv_w)))
    text_keys = split_heads(text_proj[:, :width])
    text_values = split_heads(text_proj[:, width:])
    cross_scores = jnp.einsum('thd,jhd->htj', cross_queries, text_keys, precision=HIGH) * scale
    valid = jnp.arange(text.shape[0]) < length
    cross_scores = low_back(jnp.where(valid[None, None, :], cross_scores, NEG_LARGE))
    cross_probs = softmax_rows(cross_scores)
    cross_mix = jnp.einsum('htj,jhd->thd', low(cross_probs), text_values, precision=HIGH)
    cross_mix = low(low_back(cross_mix.reshape(-1, width)))
    cross_branch = low_back(high_dot(cross_mix, cout_w)).reshape(values.shape)
    third = mid + cross_branch
    mlp_in = low(layer_norm(third) * (1.0 + scale_two) + shift_two)
    pre = low_back(high_dot(mlp_in, fin_w))
    hidden = low(gelu_of(pre))
    mlp_branch = low_back(high_dot(hidden, fout_w))
    return third + gate_two * mlp_branch

def reference(video, text_states, text_length, timestep, motion_free, ada_weight, spatial_qkv_weight, spatial_out_weight, temporal_qkv_weight, temporal_out_weight, cross_query_weight, cross_kv_weight, cross_out_weight, mlp_in_weight, mlp_out_weight, cotangent):
    weights = tuple((w.astype(jnp.float32) for w in (ada_weight, spatial_qkv_weight, spatial_out_weight, temporal_qkv_weight, temporal_out_weight, cross_query_weight, cross_kv_weight, cross_out_weight, mlp_in_weight, mlp_out_weight)))

    def clip_step(totals, item):
        clip_video, clip_text, clip_length, clip_time, clip_free, clip_grad = item
        keep_value = (1 - clip_free).astype(jnp.float32)
        text_wide = clip_text.astype(jnp.float32)

        def forward(values, *params):
            return clip_forward(values, text_wide, clip_length, clip_time, keep_value, *params)
        outcome, pull = jax.vjp(forward, clip_video.astype(jnp.float32), *weights)
        grads = pull(clip_grad.astype(jnp.float32))
        totals = tuple((a + b for a, b in zip(totals, grads[1:])))
        return (totals, (outcome.astype(jnp.bfloat16), grads[0]))
    zeros = tuple((jnp.zeros(w.shape, jnp.float32) for w in weights))
    totals, (result, video_grad) = lax.scan(clip_step, zeros, (video, text_states, text_length, timestep, motion_free, cotangent))
    flat = [t.reshape(-1) for t in totals]
    return (result, video_grad, flat[0], flat[1], flat[2], flat[3], flat[4], flat[5], flat[6], flat[7], flat[8], flat[9])
```

```python
import functools
import math

import jax
import jax.numpy as jnp
from jax import lax
from jax.experimental import pallas as pl
from jax.experimental.pallas import tpu as pltpu
from jax.sharding import PartitionSpec as P

HEAD_DIM = 64
SLAB = 2 * HEAD_DIM
SCALE = HEAD_DIM ** (-0.5)
EPSILON = 1e-06
NEG_LARGE = -1e30
BF = jnp.bfloat16
F32 = jnp.float32
AXES = ("narrow", "wide")
ROWS = 256
VMEM_LIMIT = 60 * 1024 * 1024


def time_features(time_value, width):
    half = width // 2
    freqs = jnp.exp(-math.log(10000.0) * jnp.arange(half, dtype=F32) / half)
    angles = time_value[..., None] * freqs
    return jnp.concatenate([jnp.cos(angles), jnp.sin(angles)], axis=-1)


def silu_of(values):
    return values / (1.0 + jnp.exp(-values))


def normalize(values):
    mean = jnp.mean(values, -1, keepdims=True)
    centred = values - mean
    variance = jnp.mean(centred * centred, -1, keepdims=True)
    inv_std = lax.rsqrt(variance + EPSILON)
    return centred * inv_std, inv_std


def norm_back(grad_norm, normed, inv_std):
    return inv_std * (
        grad_norm
        - jnp.mean(grad_norm, -1, keepdims=True)
        - normed * jnp.mean(grad_norm * normed, -1, keepdims=True)
    )


def mm(left, right):
    return jnp.dot(left, right, preferred_element_type=F32)


def mm_nt(left, right):
    return lax.dot_general(left, right, (((1,), (1,)), ((), ())), preferred_element_type=F32)


def mm_tn(left, right):
    return lax.dot_general(left, right, (((0,), (0,)), ((), ())), preferred_element_type=F32)


def head_masks():
    lane = lax.broadcasted_iota(jnp.int32, (1, SLAB), 1)
    low = (lane < HEAD_DIM).astype(F32)
    return low.astype(BF), (1.0 - low).astype(BF)


def softmax_rows(scores):
    peak = jnp.max(scores, -1, keepdims=True)
    expd = jnp.exp(scores - peak)
    return expd * (1.0 / jnp.sum(expd, -1, keepdims=True))


def attend_slab(query, key, value, bias):
    mixed = None
    for mask in head_masks():
        scores = mm_nt(query * mask, key) * SCALE
        if bias is not None:
            scores = jnp.where(bias, scores, NEG_LARGE)
        probs = softmax_rows(scores).astype(BF)
        part = mm(probs, value * mask)
        mixed = part if mixed is None else mixed + part
    return mixed


def attend_slab_back(query, key, value, grad, bias):
    grad_query = grad_key = grad_value = 0.0
    for mask in head_masks():
        query_part = query * mask
        grad_part = grad * mask
        scores = mm_nt(query_part, key) * SCALE
        if bias is not None:
            scores = jnp.where(bias, scores, NEG_LARGE)
        probs = softmax_rows(scores)
        grad_probs = mm_nt(grad_part, value)
        inner = jnp.sum(grad_probs * probs, -1, keepdims=True)
        grad_scores = (probs * (grad_probs - inner)).astype(BF)
        grad_value = grad_value + mm_tn(probs.astype(BF), grad_part)
        grad_query = grad_query + mm(grad_scores, key * mask)
        grad_key = grad_key + mm_tn(grad_scores, query_part)
    return grad_query * SCALE, grad_key * SCALE, grad_value


def slab_at(index, offset=0):
    return pl.ds(pl.multiple_of(index * SLAB + offset, SLAB), SLAB)


def frame_mask(rows, per_chunk):
    row = lax.broadcasted_iota(jnp.int32, (rows, rows), 0)
    col = lax.broadcasted_iota(jnp.int32, (rows, rows), 1)
    return lax.rem(row, per_chunk) == lax.rem(col, per_chunk)


def part_of(mod, index, width):
    return mod[:, index * width : (index + 1) * width]


def cost(flops, bytes_accessed, transcendentals=0):
    return pl.CostEstimate(
        flops=int(flops), bytes_accessed=int(bytes_accessed), transcendentals=int(transcendentals)
    )


def params(**extra):
    return pltpu.CompilerParams(vmem_limit_bytes=VMEM_LIMIT, **extra)


def fixed(shape):
    rank = len(shape)
    return pl.BlockSpec(shape, lambda *_: (0,) * rank, pipeline_mode=pl.Buffered(1))


def spatial_forward(where_ref, *refs, groups, width):
    del where_ref
    videos, refs = refs[:groups], refs[groups:]
    mod_ref, qkv_ref, out_ref, refs = refs[0], refs[1], refs[2], refs[3:]
    in_ref, proj_ref, mix_ref, branch_ref, firsts = refs[0], refs[1], refs[2], refs[3], refs[4:]
    mod = mod_ref[...]
    video = jnp.concatenate([v[...].reshape(-1, width) for v in videos], 0).astype(F32)
    normed, _ = normalize(video)
    entry = (normed * (1.0 + part_of(mod, 1, width)) + part_of(mod, 0, width)).astype(BF)
    in_ref[...] = entry
    proj_ref[...] = mm(entry, qkv_ref[...]).astype(BF)

    def pair(index, carry):
        mixed = attend_slab(
            proj_ref[:, slab_at(index)],
            proj_ref[:, slab_at(index, width)],
            proj_ref[:, slab_at(index, 2 * width)],
            None,
        )
        mix_ref[:, slab_at(index)] = mixed.astype(BF)
        return carry

    lax.fori_loop(0, width // SLAB, pair, 0)
    branch = mm(mix_ref[...], out_ref[...])
    branch_ref[...] = branch.astype(BF)
    first = (video + part_of(mod, 2, width) * branch).astype(BF)
    share = first.shape[0] // groups
    for j, ref in enumerate(firsts):
        ref[...] = first[j * share : (j + 1) * share].reshape(ref.shape)


def middle_forward(length_ref, keep_ref, *refs, groups, width, per_chunk):
    pieces, refs = refs[:groups], refs[groups:]
    mod_ref, qkv_ref, tout_ref, cq_ref, text_ref, cout_ref = refs[:6]
    tin_ref, tproj_ref, tmix_ref, cin_ref, cq_out, cmix_ref, mlp_ref, mid_ref, third_ref = refs[6:]
    mod = mod_ref[...]
    first = jnp.concatenate([p[...].reshape(-1, width) for p in pieces], 0).astype(F32)
    rows = first.shape[0]
    normed, _ = normalize(first)
    entry = normed.astype(BF)
    tin_ref[...] = entry
    tproj_ref[...] = mm(entry, qkv_ref[...]).astype(BF)
    same = frame_mask(rows, per_chunk)

    def pair(index, carry):
        mixed = attend_slab(
            tproj_ref[:, slab_at(index)],
            tproj_ref[:, slab_at(index, width)],
            tproj_ref[:, slab_at(index, 2 * width)],
            same,
        )
        tmix_ref[:, slab_at(index)] = mixed.astype(BF)
        return carry

    lax.fori_loop(0, width // SLAB, pair, 0)
    keep = (1 - keep_ref[0]).astype(F32)
    mid = first + keep * mm(tmix_ref[...], tout_ref[...])
    mid_ref[...] = mid
    normed, _ = normalize(mid)
    entry = normed.astype(BF)
    cin_ref[...] = entry
    cq_out[...] = mm(entry, cq_ref[...]).astype(BF)
    keys = text_ref.shape[0]
    valid = lax.broadcasted_iota(jnp.int32, (rows, keys), 1) < length_ref[0]

    def cross_pair(index, carry):
        mixed = attend_slab(
            cq_out[:, slab_at(index)],
            text_ref[:, slab_at(index)],
            text_ref[:, slab_at(index, width)],
            valid,
        )
        cmix_ref[:, slab_at(index)] = mixed.astype(BF)
        return carry

    lax.fori_loop(0, width // SLAB, cross_pair, 0)
    third = mid + mm(cmix_ref[...], cout_ref[...])
    third_ref[...] = third
    normed, _ = normalize(third)
    mlp_ref[...] = (normed * (1.0 + part_of(mod, 4, width)) + part_of(mod, 3, width)).astype(BF)


def mlp_both(core_ref, *refs, groups, width, steps):
    cots, refs = refs[:groups], refs[groups:]
    mlp_ref, third_ref, mod_ref, win_ref, wout_ref = refs[:5]
    send_in, keep_in, send_out, keep_out, dmlp_ref, dgate_ref = refs[5:11]
    results, scratch = refs[11 : 11 + groups], refs[11 + groups :]
    mlp_t, dbranch, branch = scratch
    step = pl.program_id(0)
    mod = mod_ref[...]
    gate = part_of(mod, 5, width)
    tokens = mlp_ref.shape[0]
    chunks = tokens // ROWS
    share = ROWS // groups

    @pl.when(step == 0)
    def _():
        mlp_t[...] = mlp_ref[...].T
        for k in range(chunks):
            for j in range(groups):
                rows = pl.ds(k * ROWS + j * share, share)
                cot = cots[j][:, k].reshape(share, width).astype(F32)
                dbranch[rows, :] = (gate * cot).astype(BF)
        branch[...] = jnp.zeros_like(branch)
        dmlp_ref[...] = jnp.zeros_like(dmlp_ref)

    pre = mm(mlp_ref[...], win_ref[...])
    d_hidden = mm_nt(dbranch[...], wout_ref[...])
    square = pre * pre
    bend = jnp.tanh(0.7978845608 * pre * (1.0 + 0.044715 * square))
    half = 0.5 * (1.0 + bend)
    hidden = (pre * half).astype(BF)
    slope = half + 0.5 * pre * (1.0 - bend * bend) * (
        0.7978845608 * (1.0 + (3.0 * 0.044715) * square)
    )
    d_pre = (d_hidden * slope).astype(BF)
    branch[...] += mm(hidden, wout_ref[...])
    dmlp_ref[...] += mm_nt(d_pre, win_ref[...])
    grad_in = mm(mlp_t[...], d_pre).astype(BF)

    @pl.when(step < steps // 2)
    def _():
        send_in[...] = grad_in

    @pl.when(step >= steps // 2)
    def _():
        keep_in[...] = grad_in

    hidden_t = hidden.T
    core = core_ref[0]
    side = width // 2
    send_out[...] = mm(
        hidden_t, dbranch[:, pl.ds(pl.multiple_of((1 - core) * side, 128), side)]
    ).astype(BF)
    keep_out[...] = mm(
        hidden_t, dbranch[:, pl.ds(pl.multiple_of(core * side, 128), side)]
    ).astype(BF)

    @pl.when(step == steps - 1)
    def _():
        total = jnp.zeros((1, width), F32)
        for k in range(chunks):
            for j in range(groups):
                rows = pl.ds(k * ROWS + j * share, share)
                cot = cots[j][:, k].reshape(share, width).astype(F32)
                piece = branch[rows, :]
                total = total + jnp.sum(cot * piece, 0, keepdims=True)
                out = (third_ref[rows, :] + gate * piece).astype(BF)
                results[j][:, k] = out.reshape(results[j][:, k].shape)
        dgate_ref[...] = total


def middle_backward(length_ref, keep_ref, *refs, groups, width, per_chunk):
    cots, refs = refs[:groups], refs[groups:]
    dmlp_ref, third_ref, mid_ref, mod_ref = refs[:4]
    tin_ref, tproj_ref, cq_in, text_ref = refs[4:8]
    cout_ref, cq_ref, tout_ref, tqkv_ref = refs[8:12]
    first_refs, refs = refs[12 : 12 + groups], refs[12 + groups :]
    dcb_ref, dcq_ref, dtext_ref, dtb_ref, dtp_ref, dmod_ref = refs[:6]
    dfirsts = refs[6 : 6 + groups]
    text_acc, work = refs[6 + groups :]
    chunk = pl.program_id(0)
    mod = mod_ref[...]

    @pl.when(chunk == 0)
    def _():
        text_acc[...] = jnp.zeros_like(text_acc)
        dmod_ref[...] = jnp.zeros_like(dmod_ref)

    cot = jnp.concatenate([p[...].reshape(-1, width) for p in cots], 0).astype(F32)
    rows = cot.shape[0]
    d_mlp = dmlp_ref[...]
    normed, inv_std = normalize(third_ref[...])
    dmod_ref[0:1, :] += jnp.sum(d_mlp, 0, keepdims=True)
    dmod_ref[1:2, :] += jnp.sum(d_mlp * normed, 0, keepdims=True)
    d_third = cot + norm_back(d_mlp * (1.0 + part_of(mod, 4, width)), normed, inv_std)
    d_branch = d_third.astype(BF)
    dcb_ref[...] = d_branch
    work[...] = mm_nt(d_branch, cout_ref[...]).astype(BF)
    keys = text_ref.shape[0]
    valid = lax.broadcasted_iota(jnp.int32, (rows, keys), 1) < length_ref[0]

    def cross_pair(index, carry):
        at, after = slab_at(index), slab_at(index, width)
        grad_q, grad_k, grad_v = attend_slab_back(
            cq_in[:, at], text_ref[:, at], text_ref[:, after], work[:, at], valid
        )
        dcq_ref[:, at] = grad_q.astype(BF)
        text_acc[:, at] += grad_k
        text_acc[:, after] += grad_v
        return carry

    lax.fori_loop(0, width // SLAB, cross_pair, 0)
    dtext_ref[...] = text_acc[...].astype(BF)
    normed, inv_std = normalize(mid_ref[...])
    d_mid = d_third + norm_back(mm_nt(dcq_ref[...], cq_ref[...]), normed, inv_std)
    keep = (1 - keep_ref[0]).astype(F32)
    d_branch = (keep * d_mid).astype(BF)
    dtb_ref[...] = d_branch
    work[...] = mm_nt(d_branch, tout_ref[...]).astype(BF)
    same = frame_mask(rows, per_chunk)

    def pair(index, carry):
        at, after, last = slab_at(index), slab_at(index, width), slab_at(index, 2 * width)
        grad_q, grad_k, grad_v = attend_slab_back(
            tproj_ref[:, at], tproj_ref[:, after], tproj_ref[:, last], work[:, at], same
        )
        dtp_ref[:, at] = grad_q.astype(BF)
        dtp_ref[:, after] = grad_k.astype(BF)
        dtp_ref[:, last] = grad_v.astype(BF)
        return carry

    lax.fori_loop(0, width // SLAB, pair, 0)
    first = jnp.concatenate([p[...].reshape(-1, width) for p in first_refs], 0).astype(F32)
    normed, inv_std = normalize(first)
    d_first = d_mid + norm_back(mm_nt(dtp_ref[...], tqkv_ref[...]), normed, inv_std)
    d_first = d_first.astype(BF)
    share = rows // groups
    for j, ref in enumerate(dfirsts):
        ref[...] = d_first[j * share : (j + 1) * share].reshape(ref.shape)


def spatial_backward(*refs, groups, width):
    dfirsts, refs = refs[:groups], refs[groups:]
    mod_ref, branch_ref, proj_ref, out_ref = refs[:4]
    dsb_ref, dproj_ref, dgate_ref, work = refs[4:]
    frame = pl.program_id(0)
    mod = mod_ref[...]

    @pl.when(frame == 0)
    def _():
        dgate_ref[...] = jnp.zeros_like(dgate_ref)

    d_first = jnp.concatenate([p[...].reshape(-1, width) for p in dfirsts], 0).astype(F32)
    dgate_ref[...] += jnp.sum(d_first * branch_ref[...].astype(F32), 0, keepdims=True)
    d_branch = (part_of(mod, 2, width) * d_first).astype(BF)
    dsb_ref[...] = d_branch
    work[...] = mm_nt(d_branch, out_ref[...]).astype(BF)

    def pair(index, carry):
        at, after, last = slab_at(index), slab_at(index, width), slab_at(index, 2 * width)
        grad_q, grad_k, grad_v = attend_slab_back(
            proj_ref[:, at], proj_ref[:, after], proj_ref[:, last], work[:, at], None
        )
        dproj_ref[:, at] = grad_q.astype(BF)
        dproj_ref[:, after] = grad_k.astype(BF)
        dproj_ref[:, last] = grad_v.astype(BF)
        return carry

    lax.fori_loop(0, width // SLAB, pair, 0)


def video_backward(where_ref, *refs, groups, width):
    videos, refs = refs[:groups], refs[groups:]
    dfirsts, refs = refs[:groups], refs[groups:]
    results, refs = refs[:groups], refs[groups:]
    mod_ref, dproj_ref, qkv_ref, grad_ref, result_ref, dmod_ref = refs
    frame = pl.program_id(0)
    place = where_ref[0]
    mod = mod_ref[...]

    @pl.when(frame == 0)
    def _():
        dmod_ref[...] = jnp.zeros_like(dmod_ref)

    video = jnp.concatenate([v[...].reshape(-1, width) for v in videos], 0).astype(F32)
    d_first = jnp.concatenate([p[...].reshape(-1, width) for p in dfirsts], 0).astype(F32)
    normed, inv_std = normalize(video)
    d_in = mm_nt(dproj_ref[...], qkv_ref[...])
    dmod_ref[0:1, :] += jnp.sum(d_in, 0, keepdims=True)
    dmod_ref[1:2, :] += jnp.sum(d_in * normed, 0, keepdims=True)
    grad = d_first + norm_back(d_in * (1.0 + part_of(mod, 1, width)), normed, inv_std)
    share = grad.shape[0] // groups
    for j in range(groups):
        slot = jnp.bitwise_xor(place, j)
        grad_ref[0, slot] = grad[j * share : (j + 1) * share]
        result_ref[0, slot] = results[j][...].reshape(share, width)


def weight_grads(core_ref, *refs, count):
    pairs, outs = refs[: 2 * count], refs[2 * count :]
    core = core_ref[0]
    for sign, out in enumerate(outs):
        side = 1 - core if sign == 0 else core
        start = 0
        for k in range(count):
            left, right = pairs[2 * k], pairs[2 * k + 1]
            part = right.shape[1] // 2
            cols = pl.ds(pl.multiple_of(side * part, 128), part)
            out[:, start : start + part] = mm_tn(left[...], right[:, cols]).astype(BF)
            start += part


def weight_grads_call(core, pairs):
    depth = pairs[0][0].shape[1]
    total = sum(right.shape[1] for _, right in pairs)
    tile = 256
    specs = []
    for left, right in pairs:
        specs.append(pl.BlockSpec((left.shape[0], tile), lambda m, _: (0, m)))
        specs.append(fixed(right.shape))
    shape = jax.ShapeDtypeStruct((depth, total // 2), BF)
    flops = sum(2 * left.shape[0] * depth * right.shape[1] for left, right in pairs)
    return pl.pallas_call(
        functools.partial(weight_grads, count=len(pairs)),
        grid_spec=pltpu.PrefetchScalarGridSpec(
            num_scalar_prefetch=1,
            grid=(depth // tile,),
            in_specs=specs,
            out_specs=[pl.BlockSpec((tile, total // 2), lambda m, _: (m, 0))] * 2,
        ),
        out_shape=[shape, shape],
        compiler_params=params(),
        cost_estimate=cost(flops, 8e6),
        name="weight_grads",
    )(core, *[a for pair in pairs for a in pair])


def shards(
    video,
    text_states,
    text_length,
    timestep,
    motion_free,
    ada_weight,
    spatial_qkv_weight,
    spatial_out_weight,
    temporal_qkv_weight,
    temporal_out_weight,
    cross_query_weight,
    cross_kv_weight,
    cross_out_weight,
    mlp_in_weight,
    mlp_out_weight,
    cotangent,
    *,
    mesh_shape,
):
    clips, frames, patches, width = video.shape
    if clips != 1 or patches != ROWS:
        raise ValueError("unsupported shard")
    wide, narrow = mesh_shape["wide"], mesh_shape["narrow"]
    devices = wide * narrow
    groups = wide
    here = patches // groups
    tokens = frames * patches
    chunks = tokens // ROWS
    per_chunk = here // chunks
    hidden = mlp_in_weight.shape[1]
    text_rows = text_states.shape[1]
    text_pad = -(-text_rows // 128) * 128

    wide_at = lax.axis_index("wide")
    narrow_at = lax.axis_index("narrow")
    index = narrow_at * wide + wide_at
    core = jnp.bitwise_and(wide_at, 1)
    place = wide_at.reshape(1).astype(jnp.int32)
    core_arr = core.reshape(1).astype(jnp.int32)
    wide_bits = wide.bit_length() - 1
    bits = devices.bit_length() - 1

    def flip(value, mask):
        return lax.ppermute(value, AXES, [(i, i ^ mask) for i in range(devices)])

    def bit_of(b):
        return jnp.bitwise_and(lax.shift_right_logical(index, b), 1)

    def gather_narrow(row):
        for b in range(wide_bits, bits):
            other = flip(row, 1 << b)
            mine = bit_of(b) == 0
            row = jnp.concatenate(
                [jnp.where(mine, row, other), jnp.where(mine, other, row)], 0
            )
        return row

    cot_view = cotangent.reshape(frames, groups, here, width)

    def cot_piece(j):
        part = lax.dynamic_index_in_dim(cot_view, jnp.bitwise_xor(wide_at, j), 1, keepdims=False)
        return part.reshape(frames, chunks, per_chunk, width)

    cots = [cot_piece(0)] + [flip(cot_piece(j), j) for j in range(1, groups)]

    times = gather_narrow(timestep.astype(F32).reshape(1, 1))
    silu_all = silu_of(time_features(times[:, 0], width)).astype(BF).astype(F32)
    mine = width // devices
    silu_rows = lax.dynamic_slice_in_dim(silu_all, index * mine, mine, 1)

    silu_time = silu_of(time_features(timestep.astype(F32), width)).astype(BF)
    mod = mm(silu_time, ada_weight)
    text_flat = text_states.reshape(text_rows, width)
    text_flat = jnp.pad(text_flat, ((0, text_pad - text_rows), (0, 0)))
    text_proj = mm(text_flat, cross_kv_weight).astype(BF)

    video_view = video.reshape(frames, groups, here, width)

    def own_patches(j):
        return pl.BlockSpec(
            (1, 1, here, width), lambda f, w: (f, jnp.bitwise_xor(w[0], j), 0, 0)
        )

    def frame_piece():
        return pl.BlockSpec((1, chunks, per_chunk, width), lambda f, *_: (f, 0, 0, 0))

    def chunk_piece():
        return pl.BlockSpec((frames, 1, per_chunk, width), lambda k, *_: (0, k, 0, 0))

    def row_block(cols):
        return pl.BlockSpec((ROWS, cols), lambda f, *_: (f, 0))

    piece_shape = jax.ShapeDtypeStruct((frames, chunks, per_chunk, width), BF)

    def rows_of(cols, dtype=BF):
        return jax.ShapeDtypeStruct((tokens, cols), dtype)

    mod_spec = fixed(mod.shape)
    outs = pl.pallas_call(
        functools.partial(spatial_forward, groups=groups, width=width),
        grid_spec=pltpu.PrefetchScalarGridSpec(
            num_scalar_prefetch=1,
            grid=(frames,),
            in_specs=[own_patches(j) for j in range(groups)]
            + [mod_spec, fixed(spatial_qkv_weight.shape), fixed(spatial_out_weight.shape)],
            out_specs=[row_block(width), row_block(3 * width), row_block(width), row_block(width)]
            + [frame_piece()] * groups,
        ),
        out_shape=[rows_of(width), rows_of(3 * width), rows_of(width), rows_of(width)]
        + [piece_shape] * groups,
        compiler_params=params(),
        cost_estimate=cost(8 * tokens * width * width, 10e6, tokens * patches * 12),
        name="spatial_forward",
    )(place, *[video_view] * groups, mod, spatial_qkv_weight, spatial_out_weight)
    spatial_in, spatial_proj, spatial_mix, spatial_branch = outs[:4]
    firsts = [outs[4]] + [flip(outs[4 + j], j) for j in range(1, groups)]

    def two_scalars(grid, in_specs, out_specs, scratch=()):
        return pltpu.PrefetchScalarGridSpec(
            num_scalar_prefetch=2,
            grid=grid,
            in_specs=in_specs,
            out_specs=out_specs,
            scratch_shapes=scratch,
        )

    outs = pl.pallas_call(
        functools.partial(middle_forward, groups=groups, width=width, per_chunk=per_chunk),
        grid_spec=two_scalars(
            (chunks,),
            [chunk_piece() for _ in range(groups)]
            + [
                mod_spec,
                fixed(temporal_qkv_weight.shape),
                fixed(temporal_out_weight.shape),
                fixed(cross_query_weight.shape),
                fixed(text_proj.shape),
                fixed(cross_out_weight.shape),
            ],
            [
                row_block(width),
                row_block(3 * width),
                row_block(width),
                row_block(width),
                row_block(width),
                row_block(width),
                row_block(width),
                row_block(width),
                row_block(width),
            ],
        ),
        out_shape=[
            rows_of(width),
            rows_of(3 * width),
            rows_of(width),
            rows_of(width),
            rows_of(width),
            rows_of(width),
            rows_of(width),
            rows_of(width, F32),
            rows_of(width, F32),
        ],
        compiler_params=params(),
        cost_estimate=cost(12 * tokens * width * width, 20e6, tokens * ROWS * 18),
        name="middle_forward",
    )(
        text_length,
        motion_free,
        *firsts,
        mod,
        temporal_qkv_weight,
        temporal_out_weight,
        cross_query_weight,
        text_proj,
        cross_out_weight,
    )
    temporal_in, temporal_proj, temporal_mix, cross_in, cross_q, cross_mix, mlp_in, mid, third = outs

    steps = 4
    wide_h = hidden // steps

    def hidden_at(step, core_ref):
        half = steps // 2
        first_half = lax.div(step, half)
        side = jnp.where(first_half == 0, 1 - core_ref[0], core_ref[0])
        return side * half + lax.rem(step, half)

    whole_piece = fixed((frames, chunks, per_chunk, width))
    outs = pl.pallas_call(
        functools.partial(mlp_both, groups=groups, width=width, steps=steps),
        grid_spec=pltpu.PrefetchScalarGridSpec(
            num_scalar_prefetch=1,
            grid=(steps,),
            in_specs=[whole_piece] * groups
            + [
                fixed(mlp_in.shape),
                fixed(third.shape),
                mod_spec,
                pl.BlockSpec((width, wide_h), lambda s, c: (0, hidden_at(s, c))),
                pl.BlockSpec((wide_h, width), lambda s, c: (hidden_at(s, c), 0)),
            ],
            out_specs=[
                pl.BlockSpec((width, wide_h), lambda s, c: (0, jnp.minimum(s, steps // 2 - 1))),
                pl.BlockSpec((width, wide_h), lambda s, c: (0, jnp.maximum(s - steps // 2, 0))),
                pl.BlockSpec((wide_h, width // 2), lambda s, c: (hidden_at(s, c), 0)),
                pl.BlockSpec((wide_h, width // 2), lambda s, c: (hidden_at(s, c), 0)),
                fixed((tokens, width)),
                fixed((1, width)),
            ]
            + [whole_piece] * groups,
            scratch_shapes=[
                pltpu.VMEM((width, tokens), BF),
                pltpu.VMEM((tokens, width), BF),
                pltpu.VMEM((tokens, width), F32),
            ],
        ),
        out_shape=[
            jax.ShapeDtypeStruct((width, hidden // 2), BF),
            jax.ShapeDtypeStruct((width, hidden // 2), BF),
            jax.ShapeDtypeStruct((hidden, width // 2), BF),
            jax.ShapeDtypeStruct((hidden, width // 2), BF),
            rows_of(width, F32),
            jax.ShapeDtypeStruct((1, width), F32),
        ]
        + [piece_shape] * groups,
        compiler_params=params(),
        cost_estimate=cost(12 * tokens * width * hidden, 25e6, tokens * hidden),
        name="mlp_both",
    )(core_arr, *cots, mlp_in, third, mod, mlp_in_weight, mlp_out_weight)
    send_in, keep_in, send_out, keep_out, d_mlp_in, d_gate_two = outs[:6]
    results = [outs[6]] + [flip(outs[6 + j], j) for j in range(1, groups)]

    outs = pl.pallas_call(
        functools.partial(middle_backward, groups=groups, width=width, per_chunk=per_chunk),
        grid_spec=two_scalars(
            (chunks,),
            [chunk_piece() for _ in range(groups)]
            + [
                row_block(width),
                row_block(width),
                row_block(width),
                mod_spec,
                row_block(width),
                row_block(3 * width),
                row_block(width),
                fixed(text_proj.shape),
                fixed(cross_out_weight.shape),
                fixed(cross_query_weight.shape),
                fixed(temporal_out_weight.shape),
                fixed(temporal_qkv_weight.shape),
            ]
            + [chunk_piece() for _ in range(groups)],
            [
                row_block(width),
                row_block(width),
                fixed((text_pad, 2 * width)),
                row_block(width),
                row_block(3 * width),
                fixed((2, width)),
            ]
            + [chunk_piece() for _ in range(groups)],
            [pltpu.VMEM((text_pad, 2 * width), F32), pltpu.VMEM((ROWS, width), BF)],
        ),
        out_shape=[
            rows_of(width),
            rows_of(width),
            jax.ShapeDtypeStruct((text_pad, 2 * width), BF),
            rows_of(width),
            rows_of(3 * width),
            jax.ShapeDtypeStruct((2, width), F32),
        ]
        + [piece_shape] * groups,
        compiler_params=params(),
        cost_estimate=cost(20 * tokens * width * width, 25e6, tokens * ROWS * 18),
        name="middle_backward",
    )(
        text_length,
        motion_free,
        *cots,
        d_mlp_in,
        third,
        mid,
        mod,
        temporal_in,
        temporal_proj,
        cross_q,
        text_proj,
        cross_out_weight,
        cross_query_weight,
        temporal_out_weight,
        temporal_qkv_weight,
        *firsts,
    )
    d_cross_branch, d_cross_q, d_text, d_temporal_branch, d_temporal_proj, d_mod_two = outs[:6]
    d_firsts = [outs[6]] + [flip(outs[6 + j], j) for j in range(1, groups)]

    cross_send, cross_keep = weight_grads_call(
        core_arr,
        [(cross_in, d_cross_q), (text_flat, d_text), (cross_mix, d_cross_branch)],
    )
    temporal_send, temporal_keep = weight_grads_call(
        core_arr,
        [(temporal_in, d_temporal_proj), (temporal_mix, d_temporal_branch)],
    )

    d_spatial_branch, d_spatial_proj, d_gate_one = pl.pallas_call(
        functools.partial(spatial_backward, groups=groups, width=width),
        grid=(frames,),
        in_specs=[frame_piece() for _ in range(groups)]
        + [mod_spec, row_block(width), row_block(3 * width), fixed(spatial_out_weight.shape)],
        out_specs=[row_block(width), row_block(3 * width), fixed((1, width))],
        out_shape=[rows_of(width), rows_of(3 * width), jax.ShapeDtypeStruct((1, width), F32)],
        scratch_shapes=[pltpu.VMEM((ROWS, width), BF)],
        compiler_params=params(),
        cost_estimate=cost(8 * tokens * width * width, 10e6, tokens * patches * 12),
        name="spatial_backward",
    )(*d_firsts, mod, spatial_branch, spatial_proj, spatial_out_weight)

    spatial_send, spatial_keep = weight_grads_call(
        core_arr,
        [(spatial_in, d_spatial_proj), (spatial_mix, d_spatial_branch)],
    )

    out_block = pl.BlockSpec((1, groups, here, width), lambda f, *_: (f, 0, 0, 0))
    video_grad, result, d_mod_one = pl.pallas_call(
        functools.partial(video_backward, groups=groups, width=width),
        grid_spec=pltpu.PrefetchScalarGridSpec(
            num_scalar_prefetch=1,
            grid=(frames,),
            in_specs=[own_patches(j) for j in range(groups)]
            + [frame_piece() for _ in range(2 * groups)]
            + [mod_spec, row_block(3 * width), fixed(spatial_qkv_weight.shape)],
            out_specs=[out_block, out_block, fixed((2, width))],
        ),
        out_shape=[
            jax.ShapeDtypeStruct((frames, groups, here, width), F32),
            jax.ShapeDtypeStruct((frames, groups, here, width), BF),
            jax.ShapeDtypeStruct((2, width), F32),
        ],
        compiler_params=params(),
        cost_estimate=cost(6 * tokens * width * width, 12e6),
        name="video_backward",
    )(place, *[video_view] * groups, *d_firsts, *results, mod, d_spatial_proj, spatial_qkv_weight)
    video_grad = video_grad.reshape(video.shape)
    result = result.reshape(video.shape)

    d_mod = jnp.concatenate([d_mod_one, d_gate_one, d_mod_two, d_gate_two], 0)
    for b in range(wide_bits):
        d_mod = d_mod + flip(d_mod, 1 << b)
    d_mod_all = gather_narrow(d_mod[None])
    ada_rows = jnp.sum(silu_rows[:, :, None, None] * d_mod_all[:, None, :, :], 0)
    ada_grad = ada_rows.reshape(-1)

    chip_bits = list(range(1, bits))
    first_x = [wide_bits, 1]
    rest = [b for b in chip_bits if b not in first_x]
    order_a = first_x + rest
    order_b = first_x[::-1] + rest

    def reduce_scatter(send, keep, order):
        cols = keep.shape[1]
        recv = flip(send, 1)
        cur = keep.astype(F32) + recv.astype(F32)
        axes = sorted(chip_bits, reverse=True)
        for b in order:
            cur = cur.astype(BF)
            at = axes.index(b)
            view = cur.reshape(1 << at, 2, 1 << (len(axes) - at - 1), -1, cols)
            out = lax.dynamic_index_in_dim(view, 1 - bit_of(b), 1, keepdims=False)
            own = lax.dynamic_index_in_dim(view, bit_of(b), 1, keepdims=False)
            cur = own.astype(F32) + flip(out, 1 << b).astype(F32)
            axes.remove(b)
        cur = cur.reshape(2, -1, cols)
        own = lax.dynamic_index_in_dim(cur, core, 0, keepdims=False)
        other = flip(lax.dynamic_index_in_dim(cur, 1 - core, 0, keepdims=False), 1)
        low = jnp.where(core == 0, own, other)
        high = jnp.where(core == 0, other, own)
        return low, high

    def unpack(pair, widths):
        low, high = pair
        start, out = 0, []
        for w in widths:
            half = w // 2
            cols = slice(start, start + half)
            out.append(jnp.concatenate([low[:, cols], high[:, cols]], 1).reshape(-1))
            start += half
        return out

    mlp_out_grad = unpack(reduce_scatter(send_out, keep_out, order_a), [width])[0]
    mlp_in_grad = unpack(reduce_scatter(send_in, keep_in, order_b), [hidden])[0]
    cross_query_grad, cross_kv_grad, cross_out_grad = unpack(
        reduce_scatter(cross_send, cross_keep, order_a), [width, 2 * width, width]
    )
    temporal_qkv_grad, temporal_out_grad = unpack(
        reduce_scatter(temporal_send, temporal_keep, order_b), [3 * width, width]
    )
    spatial_qkv_grad, spatial_out_grad = unpack(
        reduce_scatter(spatial_send, spatial_keep, order_a), [3 * width, width]
    )
    return (
        result,
        video_grad,
        ada_grad,
        spatial_qkv_grad,
        spatial_out_grad,
        temporal_qkv_grad,
        temporal_out_grad,
        cross_query_grad,
        cross_kv_grad,
        cross_out_grad,
        mlp_in_grad,
        mlp_out_grad,
    )


def solution(mesh):
    tokens_spec = P("narrow", "wide", None, None)
    in_specs = (
        (tokens_spec, P("narrow", None, None), P("narrow"), P("narrow"), P("narrow"))
        + (P(),) * 10
        + (tokens_spec,)
    )
    out_specs = (tokens_spec, tokens_spec) + (P(AXES),) * 10
    return jax.shard_map(
        functools.partial(shards, mesh_shape=dict(mesh.shape)),
        mesh=mesh,
        in_specs=in_specs,
        out_specs=out_specs,
        check_vma=False,
    )
```

```python
import functools
import math

import jax
import jax.numpy as jnp
from jax import lax
from jax.experimental import pallas as pl
from jax.experimental.pallas import tpu as pltpu
from jax.sharding import PartitionSpec as P

HEAD_DIM = 64
SLAB = 2 * HEAD_DIM
SCALE = HEAD_DIM ** (-0.5)
EPSILON = 1e-06
NEG_LARGE = -1e30
BF = jnp.bfloat16
F32 = jnp.float32
AXES = ("narrow", "wide")
ROWS = 256
MESH = pl.DeviceIdType.MESH
VMEM_LIMIT = 60 * 1024 * 1024


def time_features(time_value, width):
    half = width // 2
    freqs = jnp.exp(-math.log(10000.0) * jnp.arange(half, dtype=F32) / half)
    angles = time_value[..., None] * freqs
    return jnp.concatenate([jnp.cos(angles), jnp.sin(angles)], axis=-1)


def silu_of(values):
    return values / (1.0 + jnp.exp(-values))


def normalize(values):
    mean = jnp.mean(values, -1, keepdims=True)
    centred = values - mean
    variance = jnp.mean(centred * centred, -1, keepdims=True)
    inv_std = lax.rsqrt(variance + EPSILON)
    return centred * inv_std, inv_std


def norm_back(grad_norm, normed, inv_std):
    return inv_std * (
        grad_norm
        - jnp.mean(grad_norm, -1, keepdims=True)
        - normed * jnp.mean(grad_norm * normed, -1, keepdims=True)
    )


def mm(left, right):
    return jnp.dot(left, right, preferred_element_type=F32)


def mm_nt(left, right):
    return lax.dot_general(left, right, (((1,), (1,)), ((), ())), preferred_element_type=F32)


def mm_tn(left, right):
    return lax.dot_general(left, right, (((0,), (0,)), ((), ())), preferred_element_type=F32)


def head_masks():
    lane = lax.broadcasted_iota(jnp.int32, (1, SLAB), 1)
    low = (lane < HEAD_DIM).astype(F32)
    return low.astype(BF), (1.0 - low).astype(BF)


def softmax_rows(scores):
    peak = jnp.max(scores, -1, keepdims=True)
    expd = jnp.exp(scores - peak)
    return expd * (1.0 / jnp.sum(expd, -1, keepdims=True))


def attend_slab(query, key, value, bias):
    mixed = None
    for mask in head_masks():
        scores = mm_nt(query * mask, key) * SCALE
        if bias is not None:
            scores = jnp.where(bias, scores, NEG_LARGE)
        probs = softmax_rows(scores).astype(BF)
        part = mm(probs, value * mask)
        mixed = part if mixed is None else mixed + part
    return mixed


def attend_slab_back(query, key, value, grad, bias):
    grad_query = grad_key = grad_value = 0.0
    for mask in head_masks():
        query_part = query * mask
        grad_part = grad * mask
        scores = mm_nt(query_part, key) * SCALE
        if bias is not None:
            scores = jnp.where(bias, scores, NEG_LARGE)
        probs = softmax_rows(scores)
        grad_probs = mm_nt(grad_part, value)
        inner = jnp.sum(grad_probs * probs, -1, keepdims=True)
        grad_scores = (probs * (grad_probs - inner)).astype(BF)
        grad_value = grad_value + mm_tn(probs.astype(BF), grad_part)
        grad_query = grad_query + mm(grad_scores, key * mask)
        grad_key = grad_key + mm_tn(grad_scores, query_part)
    return grad_query * SCALE, grad_key * SCALE, grad_value


def slab_at(index, offset=0):
    return pl.ds(pl.multiple_of(index * SLAB + offset, SLAB), SLAB)


def frame_mask(rows, per_chunk):
    row = lax.broadcasted_iota(jnp.int32, (rows, rows), 0)
    col = lax.broadcasted_iota(jnp.int32, (rows, rows), 1)
    return lax.rem(row, per_chunk) == lax.rem(col, per_chunk)


def part_of(mod, index, width):
    return mod[:, index * width : (index + 1) * width]


def cost(flops, bytes_accessed, transcendentals=0):
    return pl.CostEstimate(
        flops=int(flops), bytes_accessed=int(bytes_accessed), transcendentals=int(transcendentals)
    )


def params(**extra):
    return pltpu.CompilerParams(vmem_limit_bytes=VMEM_LIMIT, **extra)


def fixed(shape):
    rank = len(shape)
    return pl.BlockSpec(shape, lambda *_: (0,) * rank, pipeline_mode=pl.Buffered(1))


def partner(mask):
    wide = lax.axis_size("wide")
    me = lax.axis_index("narrow") * wide + lax.axis_index("wide")
    other = jnp.bitwise_xor(me, mask)
    return (lax.div(other, wide), lax.rem(other, wide))


def greet(masks):
    barrier = pltpu.get_barrier_semaphore()
    for mask in masks:
        pl.semaphore_signal(barrier, inc=1, device_id=partner(mask), device_id_type=MESH)
    pl.semaphore_wait(barrier, len(masks))


def send(src, dst, send_sem, recv_sem, mask):
    return pltpu.make_async_remote_copy(
        src_ref=src,
        dst_ref=dst,
        send_sem=send_sem,
        recv_sem=recv_sem,
        device_id=partner(mask),
        device_id_type=MESH,
    )


def spatial_forward(*refs, groups, width, frames):
    videos, refs = refs[:groups], refs[groups:]
    cot_own, cot_all, mod_ref, qkv_ref, out_ref, refs = refs[0], refs[1], refs[2], refs[3], refs[4], refs[5:]
    in_ref, proj_ref, mix_ref, branch_ref, refs = refs[0], refs[1], refs[2], refs[3], refs[4:]
    first_own, firsts, refs = refs[0], refs[1:groups], refs[groups:]
    cot_out, cots, refs = refs[0], refs[1:groups], refs[groups:]
    out_buf, cot_sems, first_sems = refs
    frame = pl.program_id(0)
    place = lax.axis_index("wide")
    others = range(1, groups)

    def cot_copy(j):
        return send(
            cot_all.at[:, jnp.bitwise_xor(place, j)],
            cots[j - 1],
            cot_sems.at[0, j - 1],
            cot_sems.at[1, j - 1],
            j,
        )

    def first_copy(j, f):
        return send(
            out_buf.at[j - 1, f],
            firsts[j - 1].at[f],
            first_sems.at[0, j - 1, f],
            first_sems.at[1, j - 1, f],
            j,
        )

    @pl.when(frame == 0)
    def _():
        greet(list(others))
        for j in others:
            cot_copy(j).start()

    cot_out[...] = cot_own[...].reshape(cot_out.shape)
    mod = mod_ref[...]
    video = jnp.concatenate([v[...].reshape(-1, width) for v in videos], 0).astype(F32)
    normed, _ = normalize(video)
    entry = (normed * (1.0 + part_of(mod, 1, width)) + part_of(mod, 0, width)).astype(BF)
    in_ref[...] = entry
    proj_ref[...] = mm(entry, qkv_ref[...]).astype(BF)

    def pair(index, carry):
        mixed = attend_slab(
            proj_ref[:, slab_at(index)],
            proj_ref[:, slab_at(index, width)],
            proj_ref[:, slab_at(index, 2 * width)],
            None,
        )
        mix_ref[:, slab_at(index)] = mixed.astype(BF)
        return carry

    lax.fori_loop(0, width // SLAB, pair, 0)
    branch = mm(mix_ref[...], out_ref[...])
    first = (video + part_of(mod, 2, width) * branch).astype(BF)
    share = first.shape[0] // groups
    for j in others:
        out_buf[j - 1, frame] = first[j * share : (j + 1) * share]
    first_own[...] = first[:share].reshape(first_own.shape)
    branch_ref[...] = branch.astype(BF)
    for j in others:
        first_copy(j, frame).start()

    @pl.when(frame == frames - 1)
    def _():
        for j in others:
            cot_copy(j).wait()
            for f in range(frames):
                first_copy(j, f).wait()


def middle_forward(length_ref, keep_ref, *refs, groups, width, per_chunk):
    pieces, refs = refs[:groups], refs[groups:]
    mod_ref, qkv_ref, tout_ref, cq_ref, text_ref, cout_ref = refs[:6]
    tin_ref, tproj_ref, tmix_ref, cin_ref, cq_out, cmix_ref, mlp_ref, mid_ref, third_ref = refs[6:]
    mod = mod_ref[...]
    first = jnp.concatenate([p[...].reshape(-1, width) for p in pieces], 0).astype(F32)
    rows = first.shape[0]
    normed, _ = normalize(first)
    entry = normed.astype(BF)
    tin_ref[...] = entry
    tproj_ref[...] = mm(entry, qkv_ref[...]).astype(BF)
    same = frame_mask(rows, per_chunk)

    def pair(index, carry):
        mixed = attend_slab(
            tproj_ref[:, slab_at(index)],
            tproj_ref[:, slab_at(index, width)],
            tproj_ref[:, slab_at(index, 2 * width)],
            same,
        )
        tmix_ref[:, slab_at(index)] = mixed.astype(BF)
        return carry

    lax.fori_loop(0, width // SLAB, pair, 0)
    keep = (1 - keep_ref[0]).astype(F32)
    mid = first + keep * mm(tmix_ref[...], tout_ref[...])
    mid_ref[...] = mid
    normed, _ = normalize(mid)
    entry = normed.astype(BF)
    cin_ref[...] = entry
    cq_out[...] = mm(entry, cq_ref[...]).astype(BF)
    keys = text_ref.shape[0]
    valid = lax.broadcasted_iota(jnp.int32, (rows, keys), 1) < length_ref[0]

    def cross_pair(index, carry):
        mixed = attend_slab(
            cq_out[:, slab_at(index)],
            text_ref[:, slab_at(index)],
            text_ref[:, slab_at(index, width)],
            valid,
        )
        cmix_ref[:, slab_at(index)] = mixed.astype(BF)
        return carry

    lax.fori_loop(0, width // SLAB, cross_pair, 0)
    third = mid + mm(cmix_ref[...], cout_ref[...])
    third_ref[...] = third
    normed, _ = normalize(third)
    mlp_ref[...] = (normed * (1.0 + part_of(mod, 4, width)) + part_of(mod, 3, width)).astype(BF)


def mlp_both(*refs, groups, width, steps):
    cots, refs = refs[:groups], refs[groups:]
    mlp_ref, third_ref, mod_ref, win_ref, wout_ref = refs[:5]
    sum_in, sum_out, dmlp_ref, dgate_ref = refs[5:9]
    results, scratch = refs[9 : 9 + groups], refs[9 + groups :]
    mlp_t, dbranch, branch, send_in, recv_in, send_out, keep_out, recv_out, in_sems, out_sems = scratch
    step = pl.program_id(0)
    half = steps // 2
    core = jnp.bitwise_and(lax.axis_index("wide"), 1)
    mod = mod_ref[...]
    gate = part_of(mod, 5, width)
    tokens = mlp_ref.shape[0]
    chunks = tokens // ROWS
    share = ROWS // groups

    def block_at(s):
        side = jnp.where(s < half, 1 - core, core)
        return side * half + lax.rem(s, half)

    def in_copy(s):
        return send(send_in.at[s], recv_in.at[s], in_sems.at[0, s], in_sems.at[1, s], 1)

    def out_copy(s):
        block = block_at(s)
        return send(
            send_out.at[block], recv_out.at[block], out_sems.at[0, block], out_sems.at[1, block], 1
        )

    @pl.when(step == 0)
    def _():
        greet([1])
        mlp_t[...] = mlp_ref[...].T
        for k in range(chunks):
            for j in range(groups):
                rows = pl.ds(k * ROWS + j * share, share)
                cot = cots[j][:, k].reshape(share, width).astype(F32)
                dbranch[rows, :] = (gate * cot).astype(BF)
        branch[...] = jnp.zeros_like(branch)
        dmlp_ref[...] = jnp.zeros_like(dmlp_ref)

    @pl.when(step >= 1)
    def _():
        out_copy(step - 1).start()

    @pl.when(jnp.logical_and(step >= 1, step <= half))
    def _():
        in_copy(step - 1).start()

    pre = mm(mlp_ref[...], win_ref[...])
    d_hidden = mm_nt(dbranch[...], wout_ref[...])
    square = pre * pre
    bend = jnp.tanh(0.7978845608 * pre * (1.0 + 0.044715 * square))
    ramp = 0.5 * (1.0 + bend)
    hidden = (pre * ramp).astype(BF)
    slope = ramp + 0.5 * pre * (1.0 - bend * bend) * (
        0.7978845608 * (1.0 + (3.0 * 0.044715) * square)
    )
    d_pre = (d_hidden * slope).astype(BF)
    hidden_t = hidden.T
    side = width // 2
    block = block_at(step)
    send_out[block] = mm(
        hidden_t, dbranch[:, pl.ds(pl.multiple_of((1 - core) * side, 128), side)]
    ).astype(BF)
    keep_out[block] = mm(
        hidden_t, dbranch[:, pl.ds(pl.multiple_of(core * side, 128), side)]
    ).astype(BF)
    grad_in = mm(mlp_t[...], d_pre)

    @pl.when(step < half)
    def _():
        send_in[step] = grad_in.astype(BF)

    @pl.when(step >= half)
    def _():
        in_copy(step - half).wait_recv()
        sum_in[...] = (grad_in + recv_in[step - half].astype(F32)).astype(BF)

    branch[...] += mm(hidden, wout_ref[...])
    dmlp_ref[...] += mm_nt(d_pre, win_ref[...])

    @pl.when(step == steps - 1)
    def _():
        out_copy(steps - 1).start()
        total = jnp.zeros((1, width), F32)
        for k in range(chunks):
            for j in range(groups):
                rows = pl.ds(k * ROWS + j * share, share)
                cot = cots[j][:, k].reshape(share, width).astype(F32)
                piece = branch[rows, :]
                total = total + jnp.sum(cot * piece, 0, keepdims=True)
                out = (third_ref[rows, :] + gate * piece).astype(BF)
                results[j][:, k] = out.reshape(results[j][:, k].shape)
        dgate_ref[...] = total
        for s in range(half):
            in_copy(s).wait_send()
        deep = send_out.shape[1]
        for s in range(steps):
            out_copy(s).wait_send()
            out_copy((s + half) % steps).wait_recv()
            block = block_at((s + half) % steps)
            rows = pl.ds(pl.multiple_of(block * deep, 16), deep)
            sum_out[rows, :] = (
                keep_out[block].astype(F32) + recv_out[block].astype(F32)
            ).astype(BF)


def middle_backward(length_ref, keep_ref, *refs, groups, width, per_chunk):
    cots, refs = refs[:groups], refs[groups:]
    dmlp_ref, third_ref, mid_ref, mod_ref = refs[:4]
    tin_ref, tproj_ref, cq_in, text_ref = refs[4:8]
    cout_ref, cq_ref, tout_ref, tqkv_ref = refs[8:12]
    first_refs, refs = refs[12 : 12 + groups], refs[12 + groups :]
    dcb_ref, dcq_ref, dtext_ref, dtb_ref, dtp_ref, dmod_ref = refs[:6]
    dfirsts = refs[6 : 6 + groups]
    text_acc, work = refs[6 + groups :]
    chunk = pl.program_id(0)
    mod = mod_ref[...]

    @pl.when(chunk == 0)
    def _():
        text_acc[...] = jnp.zeros_like(text_acc)
        dmod_ref[...] = jnp.zeros_like(dmod_ref)

    cot = jnp.concatenate([p[...].reshape(-1, width) for p in cots], 0).astype(F32)
    rows = cot.shape[0]
    d_mlp = dmlp_ref[...]
    normed, inv_std = normalize(third_ref[...])
    dmod_ref[0:1, :] += jnp.sum(d_mlp, 0, keepdims=True)
    dmod_ref[1:2, :] += jnp.sum(d_mlp * normed, 0, keepdims=True)
    d_third = cot + norm_back(d_mlp * (1.0 + part_of(mod, 4, width)), normed, inv_std)
    d_branch = d_third.astype(BF)
    dcb_ref[...] = d_branch
    work[...] = mm_nt(d_branch, cout_ref[...]).astype(BF)
    keys = text_ref.shape[0]
    valid = lax.broadcasted_iota(jnp.int32, (rows, keys), 1) < length_ref[0]

    def cross_pair(index, carry):
        at, after = slab_at(index), slab_at(index, width)
        grad_q, grad_k, grad_v = attend_slab_back(
            cq_in[:, at], text_ref[:, at], text_ref[:, after], work[:, at], valid
        )
        dcq_ref[:, at] = grad_q.astype(BF)
        text_acc[:, at] += grad_k
        text_acc[:, after] += grad_v
        return carry

    lax.fori_loop(0, width // SLAB, cross_pair, 0)
    dtext_ref[...] = text_acc[...].astype(BF)
    normed, inv_std = normalize(mid_ref[...])
    d_mid = d_third + norm_back(mm_nt(dcq_ref[...], cq_ref[...]), normed, inv_std)
    keep = (1 - keep_ref[0]).astype(F32)
    d_branch = (keep * d_mid).astype(BF)
    dtb_ref[...] = d_branch
    work[...] = mm_nt(d_branch, tout_ref[...]).astype(BF)
    same = frame_mask(rows, per_chunk)

    def pair(index, carry):
        at, after, last = slab_at(index), slab_at(index, width), slab_at(index, 2 * width)
        grad_q, grad_k, grad_v = attend_slab_back(
            tproj_ref[:, at], tproj_ref[:, after], tproj_ref[:, last], work[:, at], same
        )
        dtp_ref[:, at] = grad_q.astype(BF)
        dtp_ref[:, after] = grad_k.astype(BF)
        dtp_ref[:, last] = grad_v.astype(BF)
        return carry

    lax.fori_loop(0, width // SLAB, pair, 0)
    first = jnp.concatenate([p[...].reshape(-1, width) for p in first_refs], 0).astype(F32)
    normed, inv_std = normalize(first)
    d_first = d_mid + norm_back(mm_nt(dtp_ref[...], tqkv_ref[...]), normed, inv_std)
    d_first = d_first.astype(BF)
    share = rows // groups
    for j, ref in enumerate(dfirsts):
        ref[...] = d_first[j * share : (j + 1) * share].reshape(ref.shape)


def spatial_backward(*refs, groups, width):
    dfirsts, refs = refs[:groups], refs[groups:]
    mod_ref, branch_ref, proj_ref, out_ref = refs[:4]
    dsb_ref, dproj_ref, dgate_ref, work = refs[4:]
    frame = pl.program_id(0)
    mod = mod_ref[...]

    @pl.when(frame == 0)
    def _():
        dgate_ref[...] = jnp.zeros_like(dgate_ref)

    d_first = jnp.concatenate([p[...].reshape(-1, width) for p in dfirsts], 0).astype(F32)
    dgate_ref[...] += jnp.sum(d_first * branch_ref[...].astype(F32), 0, keepdims=True)
    d_branch = (part_of(mod, 2, width) * d_first).astype(BF)
    dsb_ref[...] = d_branch
    work[...] = mm_nt(d_branch, out_ref[...]).astype(BF)

    def pair(index, carry):
        at, after, last = slab_at(index), slab_at(index, width), slab_at(index, 2 * width)
        grad_q, grad_k, grad_v = attend_slab_back(
            proj_ref[:, at], proj_ref[:, after], proj_ref[:, last], work[:, at], None
        )
        dproj_ref[:, at] = grad_q.astype(BF)
        dproj_ref[:, after] = grad_k.astype(BF)
        dproj_ref[:, last] = grad_v.astype(BF)
        return carry

    lax.fori_loop(0, width // SLAB, pair, 0)


def video_backward(where_ref, *refs, groups, width):
    videos, refs = refs[:groups], refs[groups:]
    dfirsts, refs = refs[:groups], refs[groups:]
    results, refs = refs[:groups], refs[groups:]
    mod_ref, dproj_ref, qkv_ref, grad_ref, result_ref, dmod_ref = refs
    frame = pl.program_id(0)
    place = where_ref[0]
    mod = mod_ref[...]

    @pl.when(frame == 0)
    def _():
        dmod_ref[...] = jnp.zeros_like(dmod_ref)

    video = jnp.concatenate([v[...].reshape(-1, width) for v in videos], 0).astype(F32)
    d_first = jnp.concatenate([p[...].reshape(-1, width) for p in dfirsts], 0).astype(F32)
    normed, inv_std = normalize(video)
    d_in = mm_nt(dproj_ref[...], qkv_ref[...])
    dmod_ref[0:1, :] += jnp.sum(d_in, 0, keepdims=True)
    dmod_ref[1:2, :] += jnp.sum(d_in * normed, 0, keepdims=True)
    grad = d_first + norm_back(d_in * (1.0 + part_of(mod, 1, width)), normed, inv_std)
    share = grad.shape[0] // groups
    for j in range(groups):
        slot = jnp.bitwise_xor(place, j)
        grad_ref[0, slot] = grad[j * share : (j + 1) * share]
        result_ref[0, slot] = results[j][...].reshape(share, width)


def weight_grads(core_ref, *refs, count):
    pairs, outs = refs[: 2 * count], refs[2 * count :]
    core = core_ref[0]
    for sign, out in enumerate(outs):
        side = 1 - core if sign == 0 else core
        start = 0
        for k in range(count):
            left, right = pairs[2 * k], pairs[2 * k + 1]
            part = right.shape[1] // 2
            cols = pl.ds(pl.multiple_of(side * part, 128), part)
            out[:, start : start + part] = mm_tn(left[...], right[:, cols]).astype(BF)
            start += part


def weight_grads_call(core, pairs):
    depth = pairs[0][0].shape[1]
    total = sum(right.shape[1] for _, right in pairs)
    tile = 256
    specs = []
    for left, right in pairs:
        specs.append(pl.BlockSpec((left.shape[0], tile), lambda m, _: (0, m)))
        specs.append(fixed(right.shape))
    shape = jax.ShapeDtypeStruct((depth, total // 2), BF)
    flops = sum(2 * left.shape[0] * depth * right.shape[1] for left, right in pairs)
    return pl.pallas_call(
        functools.partial(weight_grads, count=len(pairs)),
        grid_spec=pltpu.PrefetchScalarGridSpec(
            num_scalar_prefetch=1,
            grid=(depth // tile,),
            in_specs=specs,
            out_specs=[pl.BlockSpec((tile, total // 2), lambda m, _: (m, 0))] * 2,
        ),
        out_shape=[shape, shape],
        compiler_params=params(),
        cost_estimate=cost(flops, 8e6),
        name="weight_grads",
    )(core, *[a for pair in pairs for a in pair])


def shards(
    video,
    text_states,
    text_length,
    timestep,
    motion_free,
    ada_weight,
    spatial_qkv_weight,
    spatial_out_weight,
    temporal_qkv_weight,
    temporal_out_weight,
    cross_query_weight,
    cross_kv_weight,
    cross_out_weight,
    mlp_in_weight,
    mlp_out_weight,
    cotangent,
    *,
    mesh_shape,
):
    clips, frames, patches, width = video.shape
    if clips != 1 or patches != ROWS:
        raise ValueError("unsupported shard")
    wide, narrow = mesh_shape["wide"], mesh_shape["narrow"]
    devices = wide * narrow
    groups = wide
    here = patches // groups
    tokens = frames * patches
    chunks = tokens // ROWS
    per_chunk = here // chunks
    hidden = mlp_in_weight.shape[1]
    text_rows = text_states.shape[1]
    text_pad = -(-text_rows // 128) * 128

    wide_at = lax.axis_index("wide")
    narrow_at = lax.axis_index("narrow")
    index = narrow_at * wide + wide_at
    core = jnp.bitwise_and(wide_at, 1)
    place = wide_at.reshape(1).astype(jnp.int32)
    core_arr = core.reshape(1).astype(jnp.int32)
    wide_bits = wide.bit_length() - 1
    bits = devices.bit_length() - 1

    def flip(value, mask):
        return lax.ppermute(value, AXES, [(i, i ^ mask) for i in range(devices)])

    def bit_of(b):
        return jnp.bitwise_and(lax.shift_right_logical(index, b), 1)

    def gather_narrow(row):
        for b in range(wide_bits, bits):
            other = flip(row, 1 << b)
            mine = bit_of(b) == 0
            row = jnp.concatenate(
                [jnp.where(mine, row, other), jnp.where(mine, other, row)], 0
            )
        return row

    cot_view = cotangent.reshape(frames, groups, here, width)

    times = gather_narrow(timestep.astype(F32).reshape(1, 1))
    silu_all = silu_of(time_features(times[:, 0], width)).astype(BF).astype(F32)
    mine = width // devices
    silu_rows = lax.dynamic_slice_in_dim(silu_all, index * mine, mine, 1)

    silu_time = silu_of(time_features(timestep.astype(F32), width)).astype(BF)
    mod = mm(silu_time, ada_weight)
    text_flat = text_states.reshape(text_rows, width)
    text_flat = jnp.pad(text_flat, ((0, text_pad - text_rows), (0, 0)))
    text_proj = mm(text_flat, cross_kv_weight).astype(BF)

    video_view = video.reshape(frames, groups, here, width)

    def own_patches(j):
        return pl.BlockSpec(
            (1, 1, here, width),
            lambda f, *_: (f, jnp.bitwise_xor(lax.axis_index("wide"), j), 0, 0),
        )

    def frame_piece():
        return pl.BlockSpec((1, chunks, per_chunk, width), lambda f, *_: (f, 0, 0, 0))

    def chunk_piece():
        return pl.BlockSpec((frames, 1, per_chunk, width), lambda k, *_: (0, k, 0, 0))

    def row_block(cols):
        return pl.BlockSpec((ROWS, cols), lambda f, *_: (f, 0))

    piece_shape = jax.ShapeDtypeStruct((frames, chunks, per_chunk, width), BF)

    def rows_of(cols, dtype=BF):
        return jax.ShapeDtypeStruct((tokens, cols), dtype)

    mod_spec = fixed(mod.shape)
    anywhere = pl.BlockSpec(memory_space=pl.ANY)
    own_piece = jax.ShapeDtypeStruct((frames, here, width), BF)
    outs = pl.pallas_call(
        functools.partial(spatial_forward, groups=groups, width=width, frames=frames),
        grid_spec=pltpu.PrefetchScalarGridSpec(
            num_scalar_prefetch=0,
            grid=(frames,),
            in_specs=[own_patches(j) for j in range(groups)]
            + [own_patches(0), anywhere]
            + [mod_spec, fixed(spatial_qkv_weight.shape), fixed(spatial_out_weight.shape)],
            out_specs=[row_block(width), row_block(3 * width), row_block(width), row_block(width)]
            + ([pl.BlockSpec((1, here, width), lambda f, *_: (f, 0, 0))] + [anywhere] * (groups - 1)) * 2,
            scratch_shapes=[
                pltpu.VMEM((groups - 1, frames, here, width), BF),
                pltpu.SemaphoreType.DMA((2, groups - 1)),
                pltpu.SemaphoreType.DMA((2, groups - 1, frames)),
            ],
        ),
        out_shape=[rows_of(width), rows_of(3 * width), rows_of(width), rows_of(width)]
        + [own_piece] * (2 * groups),
        compiler_params=params(collective_id=0, has_side_effects=True),
        cost_estimate=cost(8 * tokens * width * width, 10e6, tokens * patches * 12),
        name="spatial_forward",
    )(*[video_view] * groups, cot_view, cot_view, mod, spatial_qkv_weight, spatial_out_weight)
    spatial_in, spatial_proj, spatial_mix, spatial_branch = outs[:4]
    firsts = [p.reshape(piece_shape.shape) for p in outs[4 : 4 + groups]]
    cots = [p.reshape(piece_shape.shape) for p in outs[4 + groups :]]

    def two_scalars(grid, in_specs, out_specs, scratch=()):
        return pltpu.PrefetchScalarGridSpec(
            num_scalar_prefetch=2,
            grid=grid,
            in_specs=in_specs,
            out_specs=out_specs,
            scratch_shapes=scratch,
        )

    outs = pl.pallas_call(
        functools.partial(middle_forward, groups=groups, width=width, per_chunk=per_chunk),
        grid_spec=two_scalars(
            (chunks,),
            [chunk_piece() for _ in range(groups)]
            + [
                mod_spec,
                fixed(temporal_qkv_weight.shape),
                fixed(temporal_out_weight.shape),
                fixed(cross_query_weight.shape),
                fixed(text_proj.shape),
                fixed(cross_out_weight.shape),
            ],
            [
                row_block(width),
                row_block(3 * width),
                row_block(width),
                row_block(width),
                row_block(width),
                row_block(width),
                row_block(width),
                row_block(width),
                row_block(width),
            ],
        ),
        out_shape=[
            rows_of(width),
            rows_of(3 * width),
            rows_of(width),
            rows_of(width),
            rows_of(width),
            rows_of(width),
            rows_of(width),
            rows_of(width, F32),
            rows_of(width, F32),
        ],
        compiler_params=params(),
        cost_estimate=cost(12 * tokens * width * width, 20e6, tokens * ROWS * 18),
        name="middle_forward",
    )(
        text_length,
        motion_free,
        *firsts,
        mod,
        temporal_qkv_weight,
        temporal_out_weight,
        cross_query_weight,
        text_proj,
        cross_out_weight,
    )
    temporal_in, temporal_proj, temporal_mix, cross_in, cross_q, cross_mix, mlp_in, mid, third = outs

    steps = 4
    wide_h = hidden // steps

    def hidden_at(step):
        half = steps // 2
        side_bit = jnp.bitwise_and(lax.axis_index("wide"), 1)
        side = jnp.where(step < half, 1 - side_bit, side_bit)
        return side * half + lax.rem(step, half)

    whole_piece = fixed((frames, chunks, per_chunk, width))
    outs = pl.pallas_call(
        functools.partial(mlp_both, groups=groups, width=width, steps=steps),
        grid_spec=pltpu.PrefetchScalarGridSpec(
            num_scalar_prefetch=0,
            grid=(steps,),
            in_specs=[whole_piece] * groups
            + [
                fixed(mlp_in.shape),
                fixed(third.shape),
                mod_spec,
                pl.BlockSpec((width, wide_h), lambda s: (0, hidden_at(s))),
                pl.BlockSpec((wide_h, width), lambda s: (hidden_at(s), 0)),
            ],
            out_specs=[
                pl.BlockSpec((width, wide_h), lambda s: (0, jnp.maximum(s - steps // 2, 0))),
                fixed((hidden, width // 2)),
                fixed((tokens, width)),
                fixed((1, width)),
            ]
            + [whole_piece] * groups,
            scratch_shapes=[
                pltpu.VMEM((width, tokens), BF),
                pltpu.VMEM((tokens, width), BF),
                pltpu.VMEM((tokens, width), F32),
                pltpu.VMEM((steps // 2, width, wide_h), BF),
                pltpu.VMEM((steps // 2, width, wide_h), BF),
                pltpu.VMEM((steps, wide_h, width // 2), BF),
                pltpu.VMEM((steps, wide_h, width // 2), BF),
                pltpu.VMEM((steps, wide_h, width // 2), BF),
                pltpu.SemaphoreType.DMA((2, steps // 2)),
                pltpu.SemaphoreType.DMA((2, steps)),
            ],
        ),
        out_shape=[
            jax.ShapeDtypeStruct((width, hidden // 2), BF),
            jax.ShapeDtypeStruct((hidden, width // 2), BF),
            rows_of(width, F32),
            jax.ShapeDtypeStruct((1, width), F32),
        ]
        + [piece_shape] * groups,
        compiler_params=params(collective_id=1, has_side_effects=True),
        cost_estimate=cost(12 * tokens * width * hidden, 25e6, tokens * hidden),
        name="mlp_both",
    )(*cots, mlp_in, third, mod, mlp_in_weight, mlp_out_weight)
    sum_in, sum_out, d_mlp_in, d_gate_two = outs[:4]
    results = [outs[4]] + [flip(outs[4 + j], j) for j in range(1, groups)]

    outs = pl.pallas_call(
        functools.partial(middle_backward, groups=groups, width=width, per_chunk=per_chunk),
        grid_spec=two_scalars(
            (chunks,),
            [chunk_piece() for _ in range(groups)]
            + [
                row_block(width),
                row_block(width),
                row_block(width),
                mod_spec,
                row_block(width),
                row_block(3 * width),
                row_block(width),
                fixed(text_proj.shape),
                fixed(cross_out_weight.shape),
                fixed(cross_query_weight.shape),
                fixed(temporal_out_weight.shape),
                fixed(temporal_qkv_weight.shape),
            ]
            + [chunk_piece() for _ in range(groups)],
            [
                row_block(width),
                row_block(width),
                fixed((text_pad, 2 * width)),
                row_block(width),
                row_block(3 * width),
                fixed((2, width)),
            ]
            + [chunk_piece() for _ in range(groups)],
            [pltpu.VMEM((text_pad, 2 * width), F32), pltpu.VMEM((ROWS, width), BF)],
        ),
        out_shape=[
            rows_of(width),
            rows_of(width),
            jax.ShapeDtypeStruct((text_pad, 2 * width), BF),
            rows_of(width),
            rows_of(3 * width),
            jax.ShapeDtypeStruct((2, width), F32),
        ]
        + [piece_shape] * groups,
        compiler_params=params(),
        cost_estimate=cost(20 * tokens * width * width, 25e6, tokens * ROWS * 18),
        name="middle_backward",
    )(
        text_length,
        motion_free,
        *cots,
        d_mlp_in,
        third,
        mid,
        mod,
        temporal_in,
        temporal_proj,
        cross_q,
        text_proj,
        cross_out_weight,
        cross_query_weight,
        temporal_out_weight,
        temporal_qkv_weight,
        *firsts,
    )
    d_cross_branch, d_cross_q, d_text, d_temporal_branch, d_temporal_proj, d_mod_two = outs[:6]
    d_firsts = [outs[6]] + [flip(outs[6 + j], j) for j in range(1, groups)]

    cross_send, cross_keep = weight_grads_call(
        core_arr,
        [(cross_in, d_cross_q), (text_flat, d_text), (cross_mix, d_cross_branch)],
    )
    temporal_send, temporal_keep = weight_grads_call(
        core_arr,
        [(temporal_in, d_temporal_proj), (temporal_mix, d_temporal_branch)],
    )

    d_spatial_branch, d_spatial_proj, d_gate_one = pl.pallas_call(
        functools.partial(spatial_backward, groups=groups, width=width),
        grid=(frames,),
        in_specs=[frame_piece() for _ in range(groups)]
        + [mod_spec, row_block(width), row_block(3 * width), fixed(spatial_out_weight.shape)],
        out_specs=[row_block(width), row_block(3 * width), fixed((1, width))],
        out_shape=[rows_of(width), rows_of(3 * width), jax.ShapeDtypeStruct((1, width), F32)],
        scratch_shapes=[pltpu.VMEM((ROWS, width), BF)],
        compiler_params=params(),
        cost_estimate=cost(8 * tokens * width * width, 10e6, tokens * patches * 12),
        name="spatial_backward",
    )(*d_firsts, mod, spatial_branch, spatial_proj, spatial_out_weight)

    spatial_send, spatial_keep = weight_grads_call(
        core_arr,
        [(spatial_in, d_spatial_proj), (spatial_mix, d_spatial_branch)],
    )

    out_block = pl.BlockSpec((1, groups, here, width), lambda f, *_: (f, 0, 0, 0))
    video_grad, result, d_mod_one = pl.pallas_call(
        functools.partial(video_backward, groups=groups, width=width),
        grid_spec=pltpu.PrefetchScalarGridSpec(
            num_scalar_prefetch=1,
            grid=(frames,),
            in_specs=[own_patches(j) for j in range(groups)]
            + [frame_piece() for _ in range(2 * groups)]
            + [mod_spec, row_block(3 * width), fixed(spatial_qkv_weight.shape)],
            out_specs=[out_block, out_block, fixed((2, width))],
        ),
        out_shape=[
            jax.ShapeDtypeStruct((frames, groups, here, width), F32),
            jax.ShapeDtypeStruct((frames, groups, here, width), BF),
            jax.ShapeDtypeStruct((2, width), F32),
        ],
        compiler_params=params(),
        cost_estimate=cost(6 * tokens * width * width, 12e6),
        name="video_backward",
    )(place, *[video_view] * groups, *d_firsts, *results, mod, d_spatial_proj, spatial_qkv_weight)
    video_grad = video_grad.reshape(video.shape)
    result = result.reshape(video.shape)

    d_mod = jnp.concatenate([d_mod_one, d_gate_one, d_mod_two, d_gate_two], 0)
    for b in range(wide_bits):
        d_mod = d_mod + flip(d_mod, 1 << b)
    d_mod_all = gather_narrow(d_mod[None])
    ada_rows = jnp.sum(silu_rows[:, :, None, None] * d_mod_all[:, None, :, :], 0)
    ada_grad = ada_rows.reshape(-1)

    chip_bits = list(range(1, bits))
    first_x = [wide_bits, 1]
    rest = [b for b in chip_bits if b not in first_x]
    order_a = first_x + rest
    order_b = first_x[::-1] + rest

    def join(send, keep):
        return keep.astype(F32) + flip(send, 1).astype(F32)

    def reduce_scatter(cur, order):
        cols = cur.shape[1]
        axes = sorted(chip_bits, reverse=True)
        for b in order:
            cur = cur.astype(BF)
            at = axes.index(b)
            view = cur.reshape(1 << at, 2, 1 << (len(axes) - at - 1), -1, cols)
            out = lax.dynamic_index_in_dim(view, 1 - bit_of(b), 1, keepdims=False)
            own = lax.dynamic_index_in_dim(view, bit_of(b), 1, keepdims=False)
            cur = own.astype(F32) + flip(out, 1 << b).astype(F32)
            axes.remove(b)
        cur = cur.reshape(2, -1, cols)
        own = lax.dynamic_index_in_dim(cur, core, 0, keepdims=False)
        other = flip(lax.dynamic_index_in_dim(cur, 1 - core, 0, keepdims=False), 1)
        low = jnp.where(core == 0, own, other)
        high = jnp.where(core == 0, other, own)
        return low, high

    def unpack(pair, widths):
        low, high = pair
        start, out = 0, []
        for w in widths:
            half = w // 2
            cols = slice(start, start + half)
            out.append(jnp.concatenate([low[:, cols], high[:, cols]], 1).reshape(-1))
            start += half
        return out

    mlp_out_grad = unpack(reduce_scatter(sum_out, order_a), [width])[0]
    mlp_in_grad = unpack(reduce_scatter(sum_in, order_b), [hidden])[0]
    cross_query_grad, cross_kv_grad, cross_out_grad = unpack(
        reduce_scatter(join(cross_send, cross_keep), order_a), [width, 2 * width, width]
    )
    temporal_qkv_grad, temporal_out_grad = unpack(
        reduce_scatter(join(temporal_send, temporal_keep), order_b), [3 * width, width]
    )
    spatial_qkv_grad, spatial_out_grad = unpack(
        reduce_scatter(join(spatial_send, spatial_keep), order_a), [3 * width, width]
    )
    return (
        result,
        video_grad,
        ada_grad,
        spatial_qkv_grad,
        spatial_out_grad,
        temporal_qkv_grad,
        temporal_out_grad,
        cross_query_grad,
        cross_kv_grad,
        cross_out_grad,
        mlp_in_grad,
        mlp_out_grad,
    )


def solution(mesh):
    tokens_spec = P("narrow", "wide", None, None)
    in_specs = (
        (tokens_spec, P("narrow", None, None), P("narrow"), P("narrow"), P("narrow"))
        + (P(),) * 10
        + (tokens_spec,)
    )
    out_specs = (tokens_spec, tokens_spec) + (P(AXES),) * 10
    return jax.shard_map(
        functools.partial(shards, mesh_shape=dict(mesh.shape)),
        mesh=mesh,
        in_specs=in_specs,
        out_specs=out_specs,
        check_vma=False,
    )
```

```python
import functools
import itertools
import math

import jax
import jax.numpy as jnp
from jax import lax
from jax.experimental import pallas as pl
from jax.experimental.pallas import tpu as pltpu
from jax.sharding import PartitionSpec as P

HEAD_DIM = 64
SLAB = 2 * HEAD_DIM
SCALE = HEAD_DIM ** (-0.5)
EPSILON = 1e-06
NEG_LARGE = -1e30
BF = jnp.bfloat16
F32 = jnp.float32
AXES = ("narrow", "wide")
ROWS = 256
MESH = pl.DeviceIdType.MESH
VMEM_LIMIT = 60 * 1024 * 1024


def time_features(time_value, width):
    half = width // 2
    freqs = jnp.exp(-math.log(10000.0) * jnp.arange(half, dtype=F32) / half)
    angles = time_value[..., None] * freqs
    return jnp.concatenate([jnp.cos(angles), jnp.sin(angles)], axis=-1)


def silu_of(values):
    return values / (1.0 + jnp.exp(-values))


def normalize(values):
    mean = jnp.mean(values, -1, keepdims=True)
    centred = values - mean
    variance = jnp.mean(centred * centred, -1, keepdims=True)
    inv_std = lax.rsqrt(variance + EPSILON)
    return centred * inv_std, inv_std


def norm_back(grad_norm, normed, inv_std):
    return inv_std * (
        grad_norm
        - jnp.mean(grad_norm, -1, keepdims=True)
        - normed * jnp.mean(grad_norm * normed, -1, keepdims=True)
    )


def mm(left, right):
    return jnp.dot(left, right, preferred_element_type=F32)


def mm_nt(left, right):
    return lax.dot_general(left, right, (((1,), (1,)), ((), ())), preferred_element_type=F32)


def mm_tn(left, right):
    return lax.dot_general(left, right, (((0,), (0,)), ((), ())), preferred_element_type=F32)


def head_masks():
    lane = lax.broadcasted_iota(jnp.int32, (1, SLAB), 1)
    low = (lane < HEAD_DIM).astype(F32)
    return low.astype(BF), (1.0 - low).astype(BF)


def softmax_rows(scores):
    peak = jnp.max(scores, -1, keepdims=True)
    expd = jnp.exp(scores - peak)
    return expd * (1.0 / jnp.sum(expd, -1, keepdims=True))


def attend_slab(query, key, value, bias):
    mixed = None
    for mask in head_masks():
        scores = mm_nt(query * mask, key) * SCALE
        if bias is not None:
            scores = jnp.where(bias, scores, NEG_LARGE)
        probs = softmax_rows(scores).astype(BF)
        part = mm(probs, value * mask)
        mixed = part if mixed is None else mixed + part
    return mixed


def attend_slab_back(query, key, value, grad, bias):
    grad_query = grad_key = grad_value = 0.0
    for mask in head_masks():
        query_part = query * mask
        grad_part = grad * mask
        scores = mm_nt(query_part, key) * SCALE
        if bias is not None:
            scores = jnp.where(bias, scores, NEG_LARGE)
        probs = softmax_rows(scores)
        grad_probs = mm_nt(grad_part, value)
        inner = jnp.sum(grad_probs * probs, -1, keepdims=True)
        grad_scores = (probs * (grad_probs - inner)).astype(BF)
        grad_value = grad_value + mm_tn(probs.astype(BF), grad_part)
        grad_query = grad_query + mm(grad_scores, key * mask)
        grad_key = grad_key + mm_tn(grad_scores, query_part)
    return grad_query * SCALE, grad_key * SCALE, grad_value


def slab_at(index, offset=0):
    return pl.ds(pl.multiple_of(index * SLAB + offset, SLAB), SLAB)


def frame_mask(rows, per_chunk):
    row = lax.broadcasted_iota(jnp.int32, (rows, rows), 0)
    col = lax.broadcasted_iota(jnp.int32, (rows, rows), 1)
    return lax.rem(row, per_chunk) == lax.rem(col, per_chunk)


def part_of(mod, index, width):
    return mod[:, index * width : (index + 1) * width]


def cost(flops, bytes_accessed, transcendentals=0):
    return pl.CostEstimate(
        flops=int(flops), bytes_accessed=int(bytes_accessed), transcendentals=int(transcendentals)
    )


def params(**extra):
    return pltpu.CompilerParams(vmem_limit_bytes=VMEM_LIMIT, **extra)


def fixed(shape):
    rank = len(shape)
    return pl.BlockSpec(shape, lambda *_: (0,) * rank, pipeline_mode=pl.Buffered(1))


def partner(mask):
    wide = lax.axis_size("wide")
    me = lax.axis_index("narrow") * wide + lax.axis_index("wide")
    other = jnp.bitwise_xor(me, mask)
    return (lax.div(other, wide), lax.rem(other, wide))


def greet(masks):
    barrier = pltpu.get_barrier_semaphore()
    for mask in masks:
        pl.semaphore_signal(barrier, inc=1, device_id=partner(mask), device_id_type=MESH)
    pl.semaphore_wait(barrier, len(masks))


def send(src, dst, send_sem, recv_sem, mask):
    return pltpu.make_async_remote_copy(
        src_ref=src,
        dst_ref=dst,
        send_sem=send_sem,
        recv_sem=recv_sem,
        device_id=partner(mask),
        device_id_type=MESH,
    )


def spatial_forward(*refs, groups, width, frames):
    videos, refs = refs[:groups], refs[groups:]
    cot_own, cot_all, mod_ref, qkv_ref, out_ref, refs = refs[0], refs[1], refs[2], refs[3], refs[4], refs[5:]
    in_ref, proj_ref, mix_ref, branch_ref, refs = refs[0], refs[1], refs[2], refs[3], refs[4:]
    first_own, firsts, refs = refs[0], refs[1:groups], refs[groups:]
    cot_out, cots, refs = refs[0], refs[1:groups], refs[groups:]
    out_buf, cot_sems, first_sems = refs
    frame = pl.program_id(0)
    place = lax.axis_index("wide")
    others = range(1, groups)

    def cot_copy(j):
        return send(
            cot_all.at[:, jnp.bitwise_xor(place, j)],
            cots[j - 1],
            cot_sems.at[0, j - 1],
            cot_sems.at[1, j - 1],
            j,
        )

    def first_copy(j, f):
        return send(
            out_buf.at[j - 1, f],
            firsts[j - 1].at[f],
            first_sems.at[0, j - 1, f],
            first_sems.at[1, j - 1, f],
            j,
        )

    @pl.when(frame == 0)
    def _():
        greet(list(others))
        for j in others:
            cot_copy(j).start()

    cot_out[...] = cot_own[...].reshape(cot_out.shape)
    mod = mod_ref[...]
    video = jnp.concatenate([v[...].reshape(-1, width) for v in videos], 0).astype(F32)
    normed, _ = normalize(video)
    entry = (normed * (1.0 + part_of(mod, 1, width)) + part_of(mod, 0, width)).astype(BF)
    in_ref[...] = entry
    proj_ref[...] = mm(entry, qkv_ref[...]).astype(BF)

    def pair(index, carry):
        mixed = attend_slab(
            proj_ref[:, slab_at(index)],
            proj_ref[:, slab_at(index, width)],
            proj_ref[:, slab_at(index, 2 * width)],
            None,
        )
        mix_ref[:, slab_at(index)] = mixed.astype(BF)
        return carry

    lax.fori_loop(0, width // SLAB, pair, 0)
    branch = mm(mix_ref[...], out_ref[...])
    first = (video + part_of(mod, 2, width) * branch).astype(BF)
    share = first.shape[0] // groups
    for j in others:
        out_buf[j - 1, frame] = first[j * share : (j + 1) * share]
    first_own[...] = first[:share].reshape(first_own.shape)
    branch_ref[...] = branch.astype(BF)
    for j in others:
        first_copy(j, frame).start()

    @pl.when(frame == frames - 1)
    def _():
        for j in others:
            cot_copy(j).wait()
            for f in range(frames):
                first_copy(j, f).wait()


def middle_forward(length_ref, keep_ref, *refs, groups, width, per_chunk):
    pieces, refs = refs[:groups], refs[groups:]
    mod_ref, qkv_ref, tout_ref, cq_ref, text_ref, cout_ref = refs[:6]
    tin_ref, tproj_ref, tmix_ref, cin_ref, cq_out, cmix_ref, mlp_ref, mid_ref, third_ref = refs[6:]
    mod = mod_ref[...]
    first = jnp.concatenate([p[...].reshape(-1, width) for p in pieces], 0).astype(F32)
    rows = first.shape[0]
    normed, _ = normalize(first)
    entry = normed.astype(BF)
    tin_ref[...] = entry
    tproj_ref[...] = mm(entry, qkv_ref[...]).astype(BF)
    same = frame_mask(rows, per_chunk)

    def pair(index, carry):
        mixed = attend_slab(
            tproj_ref[:, slab_at(index)],
            tproj_ref[:, slab_at(index, width)],
            tproj_ref[:, slab_at(index, 2 * width)],
            same,
        )
        tmix_ref[:, slab_at(index)] = mixed.astype(BF)
        return carry

    lax.fori_loop(0, width // SLAB, pair, 0)
    keep = (1 - keep_ref[0]).astype(F32)
    mid = first + keep * mm(tmix_ref[...], tout_ref[...])
    mid_ref[...] = mid
    normed, _ = normalize(mid)
    entry = normed.astype(BF)
    cin_ref[...] = entry
    cq_out[...] = mm(entry, cq_ref[...]).astype(BF)
    keys = text_ref.shape[0]
    valid = lax.broadcasted_iota(jnp.int32, (rows, keys), 1) < length_ref[0]

    def cross_pair(index, carry):
        mixed = attend_slab(
            cq_out[:, slab_at(index)],
            text_ref[:, slab_at(index)],
            text_ref[:, slab_at(index, width)],
            valid,
        )
        cmix_ref[:, slab_at(index)] = mixed.astype(BF)
        return carry

    lax.fori_loop(0, width // SLAB, cross_pair, 0)
    third = mid + mm(cmix_ref[...], cout_ref[...])
    third_ref[...] = third
    normed, _ = normalize(third)
    mlp_ref[...] = (normed * (1.0 + part_of(mod, 4, width)) + part_of(mod, 3, width)).astype(BF)


def mlp_both(*refs, groups, width, steps):
    cots, refs = refs[:groups], refs[groups:]
    mlp_ref, third_ref, mod_ref, win_ref, wout_ref = refs[:5]
    sum_in, sum_out, dmlp_ref, dgate_ref = refs[5:9]
    results, scratch = refs[9 : 9 + groups], refs[9 + groups :]
    mlp_t, dbranch, branch, send_in, recv_in, send_out, keep_out, recv_out, in_sems, out_sems = scratch
    step = pl.program_id(0)
    half = steps // 2
    core = jnp.bitwise_and(lax.axis_index("wide"), 1)
    mod = mod_ref[...]
    gate = part_of(mod, 5, width)
    tokens = mlp_ref.shape[0]
    chunks = tokens // ROWS
    share = ROWS // groups

    def block_at(s):
        side = jnp.where(s < half, 1 - core, core)
        return side * half + lax.rem(s, half)

    def in_copy(s):
        return send(send_in.at[s], recv_in.at[s], in_sems.at[0, s], in_sems.at[1, s], 1)

    def out_copy(s):
        block = block_at(s)
        return send(
            send_out.at[block], recv_out.at[block], out_sems.at[0, block], out_sems.at[1, block], 1
        )

    @pl.when(step == 0)
    def _():
        greet([1])
        mlp_t[...] = mlp_ref[...].T
        for k in range(chunks):
            for j in range(groups):
                rows = pl.ds(k * ROWS + j * share, share)
                cot = cots[j][:, k].reshape(share, width).astype(F32)
                dbranch[rows, :] = (gate * cot).astype(BF)
        branch[...] = jnp.zeros_like(branch)
        dmlp_ref[...] = jnp.zeros_like(dmlp_ref)

    @pl.when(step >= 1)
    def _():
        out_copy(step - 1).start()

    @pl.when(jnp.logical_and(step >= 1, step <= half))
    def _():
        in_copy(step - 1).start()

    pre = mm(mlp_ref[...], win_ref[...])
    d_hidden = mm_nt(dbranch[...], wout_ref[...])
    square = pre * pre
    bend = jnp.tanh(0.7978845608 * pre * (1.0 + 0.044715 * square))
    ramp = 0.5 * (1.0 + bend)
    hidden = (pre * ramp).astype(BF)
    slope = ramp + 0.5 * pre * (1.0 - bend * bend) * (
        0.7978845608 * (1.0 + (3.0 * 0.044715) * square)
    )
    d_pre = (d_hidden * slope).astype(BF)
    hidden_t = hidden.T
    side = width // 2
    block = block_at(step)
    send_out[block] = mm(
        hidden_t, dbranch[:, pl.ds(pl.multiple_of((1 - core) * side, 128), side)]
    ).astype(BF)
    keep_out[block] = mm(
        hidden_t, dbranch[:, pl.ds(pl.multiple_of(core * side, 128), side)]
    ).astype(BF)
    grad_in = mm(mlp_t[...], d_pre)

    @pl.when(step < half)
    def _():
        send_in[step] = grad_in.astype(BF)

    @pl.when(step >= half)
    def _():
        in_copy(step - half).wait_recv()
        sum_in[...] = (grad_in + recv_in[step - half].astype(F32)).astype(BF)

    branch[...] += mm(hidden, wout_ref[...])
    dmlp_ref[...] += mm_nt(d_pre, win_ref[...])

    @pl.when(step == steps - 1)
    def _():
        out_copy(steps - 1).start()
        total = jnp.zeros((1, width), F32)
        for k in range(chunks):
            for j in range(groups):
                rows = pl.ds(k * ROWS + j * share, share)
                cot = cots[j][:, k].reshape(share, width).astype(F32)
                piece = branch[rows, :]
                total = total + jnp.sum(cot * piece, 0, keepdims=True)
                out = (third_ref[rows, :] + gate * piece).astype(BF)
                results[j][:, k] = out.reshape(results[j][:, k].shape)
        dgate_ref[...] = total
        for s in range(half):
            in_copy(s).wait_send()
        deep = send_out.shape[1]
        for s in range(steps):
            out_copy(s).wait_send()
            out_copy((s + half) % steps).wait_recv()
            block = block_at((s + half) % steps)
            rows = pl.ds(pl.multiple_of(block * deep, 16), deep)
            sum_out[rows, :] = (
                keep_out[block].astype(F32) + recv_out[block].astype(F32)
            ).astype(BF)


def middle_backward(length_ref, keep_ref, *refs, groups, width, per_chunk):
    cots, refs = refs[:groups], refs[groups:]
    dmlp_ref, third_ref, mid_ref, mod_ref = refs[:4]
    tin_ref, tproj_ref, cq_in, text_ref = refs[4:8]
    cout_ref, cq_ref, tout_ref, tqkv_ref = refs[8:12]
    first_refs, refs = refs[12 : 12 + groups], refs[12 + groups :]
    dcb_ref, dcq_ref, dtext_ref, dtb_ref, dtp_ref, dmod_ref = refs[:6]
    dfirsts = refs[6 : 6 + groups]
    text_acc, work = refs[6 + groups :]
    chunk = pl.program_id(0)
    mod = mod_ref[...]

    @pl.when(chunk == 0)
    def _():
        text_acc[...] = jnp.zeros_like(text_acc)
        dmod_ref[...] = jnp.zeros_like(dmod_ref)

    cot = jnp.concatenate([p[...].reshape(-1, width) for p in cots], 0).astype(F32)
    rows = cot.shape[0]
    d_mlp = dmlp_ref[...]
    normed, inv_std = normalize(third_ref[...])
    dmod_ref[0:1, :] += jnp.sum(d_mlp, 0, keepdims=True)
    dmod_ref[1:2, :] += jnp.sum(d_mlp * normed, 0, keepdims=True)
    d_third = cot + norm_back(d_mlp * (1.0 + part_of(mod, 4, width)), normed, inv_std)
    d_branch = d_third.astype(BF)
    dcb_ref[...] = d_branch
    work[...] = mm_nt(d_branch, cout_ref[...]).astype(BF)
    keys = text_ref.shape[0]
    valid = lax.broadcasted_iota(jnp.int32, (rows, keys), 1) < length_ref[0]

    def cross_pair(index, carry):
        at, after = slab_at(index), slab_at(index, width)
        grad_q, grad_k, grad_v = attend_slab_back(
            cq_in[:, at], text_ref[:, at], text_ref[:, after], work[:, at], valid
        )
        dcq_ref[:, at] = grad_q.astype(BF)
        text_acc[:, at] += grad_k
        text_acc[:, after] += grad_v
        return carry

    lax.fori_loop(0, width // SLAB, cross_pair, 0)
    dtext_ref[...] = text_acc[...].astype(BF)
    normed, inv_std = normalize(mid_ref[...])
    d_mid = d_third + norm_back(mm_nt(dcq_ref[...], cq_ref[...]), normed, inv_std)
    keep = (1 - keep_ref[0]).astype(F32)
    d_branch = (keep * d_mid).astype(BF)
    dtb_ref[...] = d_branch
    work[...] = mm_nt(d_branch, tout_ref[...]).astype(BF)
    same = frame_mask(rows, per_chunk)

    def pair(index, carry):
        at, after, last = slab_at(index), slab_at(index, width), slab_at(index, 2 * width)
        grad_q, grad_k, grad_v = attend_slab_back(
            tproj_ref[:, at], tproj_ref[:, after], tproj_ref[:, last], work[:, at], same
        )
        dtp_ref[:, at] = grad_q.astype(BF)
        dtp_ref[:, after] = grad_k.astype(BF)
        dtp_ref[:, last] = grad_v.astype(BF)
        return carry

    lax.fori_loop(0, width // SLAB, pair, 0)
    first = jnp.concatenate([p[...].reshape(-1, width) for p in first_refs], 0).astype(F32)
    normed, inv_std = normalize(first)
    d_first = d_mid + norm_back(mm_nt(dtp_ref[...], tqkv_ref[...]), normed, inv_std)
    d_first = d_first.astype(BF)
    share = rows // groups
    for j, ref in enumerate(dfirsts):
        ref[...] = d_first[j * share : (j + 1) * share].reshape(ref.shape)


def spatial_backward(*refs, groups, width):
    dfirsts, refs = refs[:groups], refs[groups:]
    mod_ref, branch_ref, proj_ref, out_ref = refs[:4]
    dsb_ref, dproj_ref, dgate_ref, work = refs[4:]
    frame = pl.program_id(0)
    mod = mod_ref[...]

    @pl.when(frame == 0)
    def _():
        dgate_ref[...] = jnp.zeros_like(dgate_ref)

    d_first = jnp.concatenate([p[...].reshape(-1, width) for p in dfirsts], 0).astype(F32)
    dgate_ref[...] += jnp.sum(d_first * branch_ref[...].astype(F32), 0, keepdims=True)
    d_branch = (part_of(mod, 2, width) * d_first).astype(BF)
    dsb_ref[...] = d_branch
    work[...] = mm_nt(d_branch, out_ref[...]).astype(BF)

    def pair(index, carry):
        at, after, last = slab_at(index), slab_at(index, width), slab_at(index, 2 * width)
        grad_q, grad_k, grad_v = attend_slab_back(
            proj_ref[:, at], proj_ref[:, after], proj_ref[:, last], work[:, at], None
        )
        dproj_ref[:, at] = grad_q.astype(BF)
        dproj_ref[:, after] = grad_k.astype(BF)
        dproj_ref[:, last] = grad_v.astype(BF)
        return carry

    lax.fori_loop(0, width // SLAB, pair, 0)


def video_backward(where_ref, *refs, groups, width):
    videos, refs = refs[:groups], refs[groups:]
    dfirsts, refs = refs[:groups], refs[groups:]
    results, refs = refs[:groups], refs[groups:]
    mod_ref, dproj_ref, qkv_ref, grad_ref, result_ref, dmod_ref = refs
    frame = pl.program_id(0)
    place = where_ref[0]
    mod = mod_ref[...]

    @pl.when(frame == 0)
    def _():
        dmod_ref[...] = jnp.zeros_like(dmod_ref)

    video = jnp.concatenate([v[...].reshape(-1, width) for v in videos], 0).astype(F32)
    d_first = jnp.concatenate([p[...].reshape(-1, width) for p in dfirsts], 0).astype(F32)
    normed, inv_std = normalize(video)
    d_in = mm_nt(dproj_ref[...], qkv_ref[...])
    dmod_ref[0:1, :] += jnp.sum(d_in, 0, keepdims=True)
    dmod_ref[1:2, :] += jnp.sum(d_in * normed, 0, keepdims=True)
    grad = d_first + norm_back(d_in * (1.0 + part_of(mod, 1, width)), normed, inv_std)
    share = grad.shape[0] // groups
    for j in range(groups):
        slot = jnp.bitwise_xor(place, j)
        grad_ref[0, slot] = grad[j * share : (j + 1) * share]
        result_ref[0, slot] = results[j][...].reshape(share, width)


class Stream:
    def __init__(self, cur, recv, sems, bits, order, cols, source=None, begin=0):
        self.cur, self.recv, self.sems, self.begin = cur, recv, sems, begin
        self.bits, self.order, self.cols = bits, order, cols
        self.source = source
        wide = lax.axis_size("wide")
        me = lax.axis_index("narrow") * wide + lax.axis_index("wide")
        self.mine = {b: jnp.bitwise_and(lax.shift_right_logical(me, b), 1) for b in bits}

    def where(self, stage, side):
        spots = []
        for b in self.bits:
            at = self.order.index(b)
            if at < stage:
                spots.append(self.mine[b])
            elif at == stage:
                spots.append(self.mine[b] if side == 0 else 1 - self.mine[b])
            else:
                spots.append(slice(None))
        return tuple(spots) + (slice(None), self.cols)

    def copy(self, stage):
        base = self.cur if stage > self.begin or self.source is None else self.source
        return send(
            base.at[self.where(stage, 1)],
            self.recv[stage],
            self.sems.at[0, stage],
            self.sems.at[1, stage],
            1 << self.order[stage],
        )

    def start(self, stage):
        self.copy(stage).start()

    def add(self, stage):
        self.copy(stage).wait()
        left = [b for b in self.bits if self.order.index(b) > stage]
        for combo in itertools.product(range(2), repeat=len(left)):
            place = dict(zip(left, combo))
            spot = tuple(place.get(b, self.mine[b]) for b in self.bits) + (slice(None), self.cols)
            here = self.cur[spot].astype(F32) + self.recv[stage][combo].astype(F32)
            if not left:
                return here
            self.cur[spot] = here.astype(BF)
        return None


def stream_scratch(rows, cols, bits):
    shapes = [pltpu.VMEM((2,) * k + (rows, cols), BF) for k in range(bits - 1, -1, -1)]
    return shapes + [pltpu.SemaphoreType.DMA((2, bits))]


def make_stream(scratch, cur, bits, order, cols, source=None, begin=0):
    return Stream(cur, scratch[:-1], scratch[-1], bits, order, cols, source, begin)


def share_out(final, out, widths, start, sems, begin):
    core = jnp.bitwise_and(lax.axis_index("wide"), 1)
    for k, width in enumerate(widths):
        half = width // 2
        cols = slice(start, start + half)
        target = pl.ds(pl.multiple_of(core * half, 128), half)
        copy = send(
            final.at[1 - core, :, cols], out[k].at[:, target], sems.at[0, k], sems.at[1, k], 1
        )
        if begin:
            out[k][:, target] = final[core, :, cols]
            copy.start()
        else:
            copy.wait()
        start += half


def grads_half(pairs, side, dest, extra=None):
    start = 0
    for left, right in pairs:
        part = right.shape[1] // 2
        cols = pl.ds(pl.multiple_of(side * part, 128), part)
        for m in range(left.shape[1] // ROWS):
            rows = slice(m * ROWS, (m + 1) * ROWS)
            value = mm_tn(left[:, rows], right[:, cols])
            spot = (slice(m * ROWS, (m + 1) * ROWS), slice(start, start + part))
            if extra is not None:
                value = value + extra[spot].astype(F32)
            dest[spot] = value.astype(BF)
        start += part


def flat_rows(ref):
    return ref.reshape(-1, ref.shape[-1])


def with_scratch(body, scratch):
    form = jax.tree.structure(scratch)
    count = form.num_leaves

    def kernel(*refs):
        body(*refs[:-count], **jax.tree.unflatten(form, refs[-count:]))

    return kernel


def all_bits():
    total = lax.axis_size("wide") * lax.axis_size("narrow")
    return total.bit_length() - 1


def piece_rows(ref, chunk):
    groups = ref.shape[0]
    width = ref.shape[-1]
    return jnp.concatenate([ref[j, :, chunk].reshape(-1, width) for j in range(groups)], 0)


def back_one(length_ref, keep_ref, ins, outs, **scr):
    groups = len(ins["cots"])
    width = ins["dmlp"].shape[1]
    tokens = ins["dmlp"].shape[0]
    chunks = tokens // ROWS
    bits = list(range(all_bits() - 1, 0, -1))
    core = jnp.bitwise_and(lax.axis_index("wide"), 1)
    wide_bits = lax.axis_size("wide").bit_length() - 1
    others = range(1, groups)
    sem = scr["local"]
    loads = {}

    def load(name, src, dst):
        loads[name] = pltpu.make_async_copy(src, dst, sem.at[len(loads)])
        loads[name].start()

    for j in range(groups):
        load(f"cot{j}", ins["cots"][j], scr["cots"].at[j])
    for name in ("dmlp", "third", "cout", "cq", "text", "mid", "cwq", "tout", "tproj"):
        load(name, ins[name], scr[name])
    for j in range(groups):
        load(f"first{j}", ins["firsts"][j], scr["firsts"].at[j])
    for name in ("tqkv", "cin", "cmix", "words", "tin", "tmix"):
        load(name, ins[name], scr[name])

    x_bit, y_bit, z_bits = wide_bits, 1, [b for b in reversed(bits) if b not in (wide_bits, 1)]
    order_a = [x_bit, y_bit] + z_bits
    order_b = [y_bit, x_bit] + z_bits
    order_c = z_bits + [x_bit, y_bit]
    full = slice(None)
    s_out = make_stream(scr["so"], scr["cur_out"], bits, order_a, full, ins["sum_out"])
    s_in = make_stream(scr["si"], scr["cur_in"], bits, order_b, full, ins["sum_in"])
    keeps = []
    for stream, k in ((s_out, 0), (s_in, 1)):
        spot = stream.where(0, 0)
        keeps.append(
            pltpu.make_async_copy(
                stream.source.at[spot], stream.cur.at[spot], scr["keep_sems"].at[k]
            )
        )
    greet(list(others) + [1 << b for b in range(wide_bits, len(bits) + 1)])
    s_out.start(0)
    s_in.start(0)
    for k in keeps:
        k.start()

    def result_copy(j):
        sems = scr["result_sems"]
        return send(ins["results"][j - 1], outs["results"][j - 1], sems.at[0, j - 1], sems.at[1, j - 1], j)

    for j in others:
        result_copy(j).start()

    keys = scr["text"].shape[0]
    valid = lax.broadcasted_iota(jnp.int32, (ROWS, keys), 1) < length_ref[0]
    mod_scale = ins["mod"][:, 4 * width : 5 * width]
    text_acc, work = scr["text_acc"], scr["work"]
    text_acc[...] = jnp.zeros_like(text_acc)
    for j in range(groups):
        loads[f"cot{j}"].wait()
    for name in ("dmlp", "third", "cout", "cq", "text"):
        loads[name].wait()
    sums = [jnp.zeros((1, width), F32)] * 2
    for k in range(chunks):
        rows = slice(k * ROWS, (k + 1) * ROWS)
        cot = piece_rows(scr["cots"], k).astype(F32)
        d_mlp = scr["dmlp"][rows, :]
        normed, inv_std = normalize(scr["third"][rows, :])
        sums[0] = sums[0] + jnp.sum(d_mlp, 0, keepdims=True)
        sums[1] = sums[1] + jnp.sum(d_mlp * normed, 0, keepdims=True)
        d_third = cot + norm_back(d_mlp * (1.0 + mod_scale), normed, inv_std)
        scr["dmlp"][rows, :] = d_third
        d_branch = d_third.astype(BF)
        scr["dcb"][rows, :] = d_branch
        work[...] = mm_nt(d_branch, scr["cout"][...]).astype(BF)

        def cross_pair(index, carry):
            at, after = slab_at(index), slab_at(index, width)
            grad_q, grad_k, grad_v = attend_slab_back(
                scr["cq"][rows, at], scr["text"][:, at], scr["text"][:, after], work[:, at], valid
            )
            scr["dcq"][rows, at] = grad_q.astype(BF)
            text_acc[:, at] += grad_k
            text_acc[:, after] += grad_v
            return carry

        lax.fori_loop(0, width // SLAB, cross_pair, 0)
    outs["dmod"][0:1, :] = sums[0]
    outs["dmod"][1:2, :] = sums[1]
    scr["dtext"][...] = text_acc[...].astype(BF)

    for name in ("cin", "cmix", "words"):
        loads[name].wait()
    pairs_c = [(scr["cin"], scr["dcq"]), (scr["words"], scr["dtext"]), (scr["cmix"], scr["dcb"])]
    grads_half(pairs_c, 1 - core, scr["send_c"])

    def core_copy(name, k):
        return send(
            scr["send_" + name], flat_rows(scr["cur_" + name]),
            scr["core_sems"].at[0, k], scr["core_sems"].at[1, k], 1,
        )

    for name in ("mid", "cwq", "tout", "tproj"):
        loads[name].wait()
    for j in range(groups):
        loads[f"first{j}"].wait()
    keep = (1 - keep_ref[0]).astype(F32)
    same = frame_mask(ROWS, ins["firsts"][0].shape[2])
    tproj, dtp = scr["tproj"], scr["dtp"]

    def temporal(k, before_norm=None):
        rows = slice(k * ROWS, (k + 1) * ROWS)
        normed, inv_std = normalize(scr["mid"][rows, :])
        d_mid = scr["dmlp"][rows, :] + norm_back(
            mm_nt(scr["dcq"][rows, :], scr["cwq"][...]), normed, inv_std
        )
        d_branch = (keep * d_mid).astype(BF)
        scr["dtb"][rows, :] = d_branch
        work[...] = mm_nt(d_branch, scr["tout"][...]).astype(BF)

        def pair(index, carry):
            at, after, last = slab_at(index), slab_at(index, width), slab_at(index, 2 * width)
            grad_q, grad_k, grad_v = attend_slab_back(
                tproj[rows, at], tproj[rows, after], tproj[rows, last], work[:, at], same
            )
            dtp[rows, at] = grad_q.astype(BF)
            dtp[rows, after] = grad_k.astype(BF)
            dtp[rows, last] = grad_v.astype(BF)
            return carry

        lax.fori_loop(0, width // SLAB, pair, 0)
        first = piece_rows(scr["firsts"], k).astype(F32)
        normed, inv_std = normalize(first)
        if k == 0:
            loads["tqkv"].wait()
        d_first = d_mid + norm_back(mm_nt(dtp[rows, :], scr["tqkv"][...]), normed, inv_std)
        d_first = d_first.astype(BF)
        share = ROWS // groups
        buf = scr["dfirst"]
        for j in range(groups):
            buf[j, :, k] = d_first[j * share : (j + 1) * share].reshape(buf.shape[1:2] + buf.shape[3:])

    def first_copy(j, k):
        src, dst = scr["dfirst"].at[j, :, k], outs["dfirsts"][j].at[:, k]
        sems = scr["first_sems"]
        if j == 0:
            return pltpu.make_async_copy(src, dst, sems.at[0, j, k])
        return send(src, dst, sems.at[0, j, k], sems.at[1, j, k], j)

    core_copy("c", 0).start()
    temporal(0)
    core_copy("c", 0).wait()
    cur_c = flat_rows(scr["cur_c"])
    grads_half(pairs_c, core, cur_c, cur_c)
    for j in range(groups):
        first_copy(j, 0).start()
    for k in keeps:
        k.wait()
    s_out.add(0)
    s_in.add(0)
    s_out.start(1)
    s_in.start(1)
    temporal(1)
    loads["tin"].wait()
    loads["tmix"].wait()
    pairs_t = [(scr["tin"], dtp), (scr["tmix"], scr["dtb"])]
    for j in range(groups):
        first_copy(j, 1).start()
    s_c = make_stream(scr["sc"], scr["cur_c"], bits, order_c, full)
    s_c.start(0)
    grads_half(pairs_t, 1 - core, scr["send_t"])
    s_out.add(1)
    s_in.add(1)
    core_copy("t", 1).start()
    s_out.start(2)
    s_in.start(2)
    last = len(bits) - 1
    for stage in range(2, last):
        s_out.add(stage)
        s_in.add(stage)
        s_out.start(stage + 1)
        s_in.start(stage + 1)
    core_copy("t", 1).wait()
    cur_t = flat_rows(scr["cur_t"])
    grads_half(pairs_t, core, cur_t, cur_t)
    for final, stream, name, widths in (
        (scr["fin_out"], s_out, "mlp_out", [width]),
        (scr["fin_in"], s_in, "mlp_in", [2 * scr["fin_in"].shape[2]]),
    ):
        final[...] = stream.add(last).reshape(final.shape)
        share_out(final, [outs[name]], widths, 0, scr[name + "_sems"], True)
    s_c.add(0)
    hold = [
        pltpu.make_async_copy(scr["cur_c"], outs["cur_c"], scr["keep_sems"].at[2]),
        pltpu.make_async_copy(scr["cur_t"], outs["cur_t"], scr["keep_sems"].at[3]),
    ]
    for h in hold:
        h.start()
    share_out(scr["fin_out"], [outs["mlp_out"]], [width], 0, scr["mlp_out_sems"], False)
    share_out(
        scr["fin_in"], [outs["mlp_in"]], [2 * scr["fin_in"].shape[2]], 0, scr["mlp_in_sems"], False
    )
    for j in others:
        result_copy(j).wait()
    for j in range(groups):
        for k in range(chunks):
            first_copy(j, k).wait()
    for h in hold:
        h.wait()


def back_two(ins, outs, **scr):
    groups = len(ins["dfirsts"])
    frames, _, _, width = ins["video"].shape
    bits = list(range(all_bits() - 1, 0, -1))
    place = lax.axis_index("wide")
    core = jnp.bitwise_and(place, 1)
    wide_bits = lax.axis_size("wide").bit_length() - 1
    sem = scr["local"]
    loads = {}

    def load(name, src, dst):
        loads[name] = pltpu.make_async_copy(src, dst, sem.at[len(loads)])
        loads[name].start()

    for j in range(groups):
        load(f"dfirst{j}", ins["dfirsts"][j], scr["dfirsts"].at[j])
    for name in ("sbranch", "sout", "sproj", "sin", "smix", "sqkv"):
        load(name, ins[name], scr[name])
    for j in range(groups):
        load(f"video{j}", ins["video"].at[:, jnp.bitwise_xor(place, j)], scr["video"].at[j])
        load(f"result{j}", ins["results"][j], scr["results"].at[j])

    x_bit, y_bit, z_bits = wide_bits, 1, [b for b in reversed(bits) if b not in (wide_bits, 1)]
    order_a = [x_bit, y_bit] + z_bits
    order_b = [y_bit, x_bit] + z_bits
    order_c = z_bits + [x_bit, y_bit]
    cols = scr["cur_t"].shape[-1]
    mid_col = cols // 2
    lo, hi = slice(0, mid_col), slice(mid_col, cols)
    full = slice(None)
    s_c = make_stream(scr["sc"], scr["cur_c"], bits, order_c, full, ins["cur_c"], 1)
    s_ta = make_stream(scr["sta"], scr["cur_t"], bits, order_a, lo, ins["cur_t"])
    s_tb = make_stream(scr["stb"], scr["cur_t"], bits, order_b, hi, ins["cur_t"])
    keeps = []
    for stream, stage in ((s_c, 1), (s_ta, 0), (s_tb, 0)):
        spot = stream.where(stage, 0)
        keeps.append(
            pltpu.make_async_copy(
                stream.source.at[spot], stream.cur.at[spot], scr["keep_sems"].at[len(keeps)]
            )
        )
    greet([1] + [1 << b for b in range(1, len(bits) + 1)])
    s_ta.start(0)
    s_tb.start(0)
    s_c.start(1)
    for k in keeps:
        k.start()

    gate = ins["mod"][:, 2 * width : 3 * width]
    scale = ins["mod"][:, width : 2 * width]
    for j in range(groups):
        loads[f"dfirst{j}"].wait()
    for name in ("sbranch", "sout", "sproj"):
        loads[name].wait()
    work, dsp, sproj = scr["work"], scr["dsp"], scr["sproj"]

    def frame_rows(ref, f):
        return jnp.concatenate([ref[j, f].reshape(-1, width) for j in range(groups)], 0)

    gate_sum = jnp.zeros((1, width), F32)
    for f in range(frames):
        rows = slice(f * ROWS, (f + 1) * ROWS)
        d_first = frame_rows(scr["dfirsts"], f).astype(F32)
        gate_sum = gate_sum + jnp.sum(
            d_first * scr["sbranch"][rows, :].astype(F32), 0, keepdims=True
        )
        d_branch = (gate * d_first).astype(BF)
        scr["dsb"][rows, :] = d_branch
        work[...] = mm_nt(d_branch, scr["sout"][...]).astype(BF)

        def pair(index, carry):
            at, after, last = slab_at(index), slab_at(index, width), slab_at(index, 2 * width)
            grad_q, grad_k, grad_v = attend_slab_back(
                sproj[rows, at], sproj[rows, after], sproj[rows, last], work[:, at], None
            )
            dsp[rows, at] = grad_q.astype(BF)
            dsp[rows, after] = grad_k.astype(BF)
            dsp[rows, last] = grad_v.astype(BF)
            return carry

        lax.fori_loop(0, width // SLAB, pair, 0)
    for name in ("sin", "smix"):
        loads[name].wait()
    pairs_s = [(scr["sin"], dsp), (scr["smix"], scr["dsb"])]
    grads_half(pairs_s, 1 - core, scr["send_s"])
    cur_s = flat_rows(scr["cur_s"])
    core_copy = send(scr["send_s"], cur_s, scr["core_sems"].at[0, 0], scr["core_sems"].at[1, 0], 1)
    core_copy.start()
    for k in keeps:
        k.wait()
    s_ta.add(0)
    s_tb.add(0)
    s_ta.start(1)
    s_tb.start(1)
    core_copy.wait()
    grads_half(pairs_s, core, cur_s, cur_s)
    s_a = make_stream(scr["ssa"], scr["cur_s"], bits, order_a, lo)
    s_b = make_stream(scr["ssb"], scr["cur_s"], bits, order_b, hi)
    s_a.start(0)
    s_b.start(0)

    for name in ["sqkv"] + [f"video{j}" for j in range(groups)] + [f"result{j}" for j in range(groups)]:
        loads[name].wait()
    sums = [jnp.zeros((1, width), F32)] * 2
    share = ROWS // groups
    for f in range(frames):
        rows = slice(f * ROWS, (f + 1) * ROWS)
        video = frame_rows(scr["video"], f).astype(F32)
        d_first = frame_rows(scr["dfirsts"], f).astype(F32)
        normed, inv_std = normalize(video)
        d_in = mm_nt(dsp[rows, :], scr["sqkv"][...])
        sums[0] = sums[0] + jnp.sum(d_in, 0, keepdims=True)
        sums[1] = sums[1] + jnp.sum(d_in * normed, 0, keepdims=True)
        grad = d_first + norm_back(d_in * (1.0 + scale), normed, inv_std)
        for j in range(groups):
            slot = jnp.bitwise_xor(place, j)
            outs["video_grad"][f, slot] = grad[j * share : (j + 1) * share]
            outs["result"][f, slot] = scr["results"][j, f].reshape(share, width)

    mod_sum, mod_in = scr["mod_sum"], scr["mod_in"]
    mod_sum[...] = jnp.concatenate(
        [sums[0], sums[1], gate_sum, ins["dmod_two"][...], ins["dgate_two"][...],
         jnp.zeros((2, width), F32)], 0,
    )

    def mod_copy(b):
        return send(
            mod_sum, mod_in.at[b], scr["mod_sems"].at[0, b], scr["mod_sems"].at[1, b], 1 << b
        )

    def gather_copy(b, slots):
        span = mod_all.at[slots]
        return send(span, span, scr["mod_sems"].at[0, b], scr["mod_sems"].at[1, b], 1 << b)

    mod_all = outs["dmod_all"]
    narrow_at = lax.axis_index("narrow")

    def slots_of(b):
        size = 1 << (b - wide_bits)
        start = lax.div(narrow_at, size) * size
        return pl.ds(start, size)

    def mod_start(b):
        if b < wide_bits:
            mod_copy(b).start()
        else:
            gather_copy(b, slots_of(b)).start()

    def mod_finish(b):
        if b < wide_bits:
            mod_copy(b).wait()
            mod_sum[...] = mod_sum[...] + mod_in[b]
        else:
            gather_copy(b, slots_of(b)).wait()
        if b == wide_bits - 1:
            mod_all[narrow_at] = mod_sum[...]

    last = len(bits) - 1
    mod_start(0)
    s_ta.add(1)
    s_tb.add(1)
    s_ta.start(2)
    s_tb.start(2)
    mod_finish(0)
    mod_start(1)
    s_c.add(1)
    s_c.start(2)
    mod_finish(1)
    mod_start(2)
    for stage in range(2, last):
        s_ta.add(stage)
        s_tb.add(stage)
        s_ta.start(stage + 1)
        s_tb.start(stage + 1)
    mod_finish(2)
    mod_start(3)
    s_a.add(0)
    s_b.add(0)
    s_a.start(1)
    s_b.start(1)
    for stage in range(2, last):
        s_c.add(stage)
        s_c.start(stage + 1)
    mod_finish(3)
    mod_start(4)
    widths_t, widths_c = [3 * width, width], [width, 2 * width, width]
    fin = scr["fin_t"]
    fin[:, :, lo] = s_ta.add(last).reshape(2, -1, mid_col)
    fin[:, :, hi] = s_tb.add(last).reshape(2, -1, mid_col)
    share_out(fin, outs["temporal"], widths_t, 0, scr["t_sems"], True)
    s_a.add(1)
    s_b.add(1)
    s_a.start(2)
    s_b.start(2)
    mod_finish(4)
    fin_c = scr["fin_c"]
    fin_c[...] = s_c.add(last).reshape(fin_c.shape)
    share_out(fin_c, outs["cross"], widths_c, 0, scr["c_sems"], True)
    for stage in range(2, last):
        s_a.add(stage)
        s_b.add(stage)
        s_a.start(stage + 1)
        s_b.start(stage + 1)
    share_out(fin, outs["temporal"], widths_t, 0, scr["t_sems"], False)
    share_out(fin_c, outs["cross"], widths_c, 0, scr["c_sems"], False)
    fin_s = scr["fin_s"]
    fin_s[:, :, lo] = s_a.add(last).reshape(2, -1, mid_col)
    fin_s[:, :, hi] = s_b.add(last).reshape(2, -1, mid_col)
    share_out(fin_s, outs["spatial"], widths_t, 0, scr["s_sems"], True)
    share_out(fin_s, outs["spatial"], widths_t, 0, scr["s_sems"], False)


def weight_grads(core_ref, *refs, count):
    pairs, outs = refs[: 2 * count], refs[2 * count :]
    core = core_ref[0]
    for sign, out in enumerate(outs):
        side = 1 - core if sign == 0 else core
        start = 0
        for k in range(count):
            left, right = pairs[2 * k], pairs[2 * k + 1]
            part = right.shape[1] // 2
            cols = pl.ds(pl.multiple_of(side * part, 128), part)
            out[:, start : start + part] = mm_tn(left[...], right[:, cols]).astype(BF)
            start += part


def weight_grads_call(core, pairs):
    depth = pairs[0][0].shape[1]
    total = sum(right.shape[1] for _, right in pairs)
    tile = 256
    specs = []
    for left, right in pairs:
        specs.append(pl.BlockSpec((left.shape[0], tile), lambda m, _: (0, m)))
        specs.append(fixed(right.shape))
    shape = jax.ShapeDtypeStruct((depth, total // 2), BF)
    flops = sum(2 * left.shape[0] * depth * right.shape[1] for left, right in pairs)
    return pl.pallas_call(
        functools.partial(weight_grads, count=len(pairs)),
        grid_spec=pltpu.PrefetchScalarGridSpec(
            num_scalar_prefetch=1,
            grid=(depth // tile,),
            in_specs=specs,
            out_specs=[pl.BlockSpec((tile, total // 2), lambda m, _: (m, 0))] * 2,
        ),
        out_shape=[shape, shape],
        compiler_params=params(),
        cost_estimate=cost(flops, 8e6),
        name="weight_grads",
    )(core, *[a for pair in pairs for a in pair])


def shards(
    video,
    text_states,
    text_length,
    timestep,
    motion_free,
    ada_weight,
    spatial_qkv_weight,
    spatial_out_weight,
    temporal_qkv_weight,
    temporal_out_weight,
    cross_query_weight,
    cross_kv_weight,
    cross_out_weight,
    mlp_in_weight,
    mlp_out_weight,
    cotangent,
    *,
    mesh_shape,
):
    clips, frames, patches, width = video.shape
    if clips != 1 or patches != ROWS:
        raise ValueError("unsupported shard")
    wide, narrow = mesh_shape["wide"], mesh_shape["narrow"]
    devices = wide * narrow
    groups = wide
    here = patches // groups
    tokens = frames * patches
    chunks = tokens // ROWS
    per_chunk = here // chunks
    hidden = mlp_in_weight.shape[1]
    text_rows = text_states.shape[1]
    text_pad = -(-text_rows // 128) * 128

    wide_at = lax.axis_index("wide")
    narrow_at = lax.axis_index("narrow")
    index = narrow_at * wide + wide_at
    core = jnp.bitwise_and(wide_at, 1)
    place = wide_at.reshape(1).astype(jnp.int32)
    core_arr = core.reshape(1).astype(jnp.int32)
    wide_bits = wide.bit_length() - 1
    bits = devices.bit_length() - 1

    def flip(value, mask):
        return lax.ppermute(value, AXES, [(i, i ^ mask) for i in range(devices)])

    def bit_of(b):
        return jnp.bitwise_and(lax.shift_right_logical(index, b), 1)

    def gather_narrow(row):
        for b in range(wide_bits, bits):
            other = flip(row, 1 << b)
            mine = bit_of(b) == 0
            row = jnp.concatenate(
                [jnp.where(mine, row, other), jnp.where(mine, other, row)], 0
            )
        return row

    cot_view = cotangent.reshape(frames, groups, here, width)

    times = gather_narrow(timestep.astype(F32).reshape(1, 1))
    silu_all = silu_of(time_features(times[:, 0], width)).astype(BF).astype(F32)
    mine = width // devices
    silu_rows = lax.dynamic_slice_in_dim(silu_all, index * mine, mine, 1)

    silu_time = silu_of(time_features(timestep.astype(F32), width)).astype(BF)
    mod = mm(silu_time, ada_weight)
    text_flat = text_states.reshape(text_rows, width)
    text_flat = jnp.pad(text_flat, ((0, text_pad - text_rows), (0, 0)))
    text_proj = mm(text_flat, cross_kv_weight).astype(BF)

    video_view = video.reshape(frames, groups, here, width)

    def own_patches(j):
        return pl.BlockSpec(
            (1, 1, here, width),
            lambda f, *_: (f, jnp.bitwise_xor(lax.axis_index("wide"), j), 0, 0),
        )

    def frame_piece():
        return pl.BlockSpec((1, chunks, per_chunk, width), lambda f, *_: (f, 0, 0, 0))

    def chunk_piece():
        return pl.BlockSpec((frames, 1, per_chunk, width), lambda k, *_: (0, k, 0, 0))

    def row_block(cols):
        return pl.BlockSpec((ROWS, cols), lambda f, *_: (f, 0))

    piece_shape = jax.ShapeDtypeStruct((frames, chunks, per_chunk, width), BF)

    def rows_of(cols, dtype=BF):
        return jax.ShapeDtypeStruct((tokens, cols), dtype)

    mod_spec = fixed(mod.shape)
    anywhere = pl.BlockSpec(memory_space=pl.ANY)
    own_piece = jax.ShapeDtypeStruct((frames, here, width), BF)
    outs = pl.pallas_call(
        functools.partial(spatial_forward, groups=groups, width=width, frames=frames),
        grid_spec=pltpu.PrefetchScalarGridSpec(
            num_scalar_prefetch=0,
            grid=(frames,),
            in_specs=[own_patches(j) for j in range(groups)]
            + [own_patches(0), anywhere]
            + [mod_spec, fixed(spatial_qkv_weight.shape), fixed(spatial_out_weight.shape)],
            out_specs=[row_block(width), row_block(3 * width), row_block(width), row_block(width)]
            + ([pl.BlockSpec((1, here, width), lambda f, *_: (f, 0, 0))] + [anywhere] * (groups - 1)) * 2,
            scratch_shapes=[
                pltpu.VMEM((groups - 1, frames, here, width), BF),
                pltpu.SemaphoreType.DMA((2, groups - 1)),
                pltpu.SemaphoreType.DMA((2, groups - 1, frames)),
            ],
        ),
        out_shape=[rows_of(width), rows_of(3 * width), rows_of(width), rows_of(width)]
        + [own_piece] * (2 * groups),
        compiler_params=params(collective_id=0, has_side_effects=True),
        cost_estimate=cost(8 * tokens * width * width, 10e6, tokens * patches * 12),
        name="spatial_forward",
    )(*[video_view] * groups, cot_view, cot_view, mod, spatial_qkv_weight, spatial_out_weight)
    spatial_in, spatial_proj, spatial_mix, spatial_branch = outs[:4]
    firsts = [p.reshape(piece_shape.shape) for p in outs[4 : 4 + groups]]
    cots = [p.reshape(piece_shape.shape) for p in outs[4 + groups :]]

    def two_scalars(grid, in_specs, out_specs, scratch=()):
        return pltpu.PrefetchScalarGridSpec(
            num_scalar_prefetch=2,
            grid=grid,
            in_specs=in_specs,
            out_specs=out_specs,
            scratch_shapes=scratch,
        )

    outs = pl.pallas_call(
        functools.partial(middle_forward, groups=groups, width=width, per_chunk=per_chunk),
        grid_spec=two_scalars(
            (chunks,),
            [chunk_piece() for _ in range(groups)]
            + [
                mod_spec,
                fixed(temporal_qkv_weight.shape),
                fixed(temporal_out_weight.shape),
                fixed(cross_query_weight.shape),
                fixed(text_proj.shape),
                fixed(cross_out_weight.shape),
            ],
            [
                row_block(width),
                row_block(3 * width),
                row_block(width),
                row_block(width),
                row_block(width),
                row_block(width),
                row_block(width),
                row_block(width),
                row_block(width),
            ],
        ),
        out_shape=[
            rows_of(width),
            rows_of(3 * width),
            rows_of(width),
            rows_of(width),
            rows_of(width),
            rows_of(width),
            rows_of(width),
            rows_of(width, F32),
            rows_of(width, F32),
        ],
        compiler_params=params(),
        cost_estimate=cost(12 * tokens * width * width, 20e6, tokens * ROWS * 18),
        name="middle_forward",
    )(
        text_length,
        motion_free,
        *firsts,
        mod,
        temporal_qkv_weight,
        temporal_out_weight,
        cross_query_weight,
        text_proj,
        cross_out_weight,
    )
    temporal_in, temporal_proj, temporal_mix, cross_in, cross_q, cross_mix, mlp_in, mid, third = outs

    steps = 4
    wide_h = hidden // steps

    def hidden_at(step):
        half = steps // 2
        side_bit = jnp.bitwise_and(lax.axis_index("wide"), 1)
        side = jnp.where(step < half, 1 - side_bit, side_bit)
        return side * half + lax.rem(step, half)

    whole_piece = fixed((frames, chunks, per_chunk, width))
    outs = pl.pallas_call(
        functools.partial(mlp_both, groups=groups, width=width, steps=steps),
        grid_spec=pltpu.PrefetchScalarGridSpec(
            num_scalar_prefetch=0,
            grid=(steps,),
            in_specs=[whole_piece] * groups
            + [
                fixed(mlp_in.shape),
                fixed(third.shape),
                mod_spec,
                pl.BlockSpec((width, wide_h), lambda s: (0, hidden_at(s))),
                pl.BlockSpec((wide_h, width), lambda s: (hidden_at(s), 0)),
            ],
            out_specs=[
                pl.BlockSpec((width, wide_h), lambda s: (0, jnp.maximum(s - steps // 2, 0))),
                fixed((hidden, width // 2)),
                fixed((tokens, width)),
                fixed((1, width)),
            ]
            + [whole_piece] * groups,
            scratch_shapes=[
                pltpu.VMEM((width, tokens), BF),
                pltpu.VMEM((tokens, width), BF),
                pltpu.VMEM((tokens, width), F32),
                pltpu.VMEM((steps // 2, width, wide_h), BF),
                pltpu.VMEM((steps // 2, width, wide_h), BF),
                pltpu.VMEM((steps, wide_h, width // 2), BF),
                pltpu.VMEM((steps, wide_h, width // 2), BF),
                pltpu.VMEM((steps, wide_h, width // 2), BF),
                pltpu.SemaphoreType.DMA((2, steps // 2)),
                pltpu.SemaphoreType.DMA((2, steps)),
            ],
        ),
        out_shape=[
            jax.ShapeDtypeStruct((width, hidden // 2), BF),
            jax.ShapeDtypeStruct((hidden, width // 2), BF),
            rows_of(width, F32),
            jax.ShapeDtypeStruct((1, width), F32),
        ]
        + [piece_shape] * groups,
        compiler_params=params(collective_id=1, has_side_effects=True),
        cost_estimate=cost(12 * tokens * width * hidden, 25e6, tokens * hidden),
        name="mlp_both",
    )(*cots, mlp_in, third, mod, mlp_in_weight, mlp_out_weight)
    sum_in, sum_out, d_mlp_in, d_gate_two = outs[:4]
    if (2 * width // devices) % 16 == 0:
        chip = (2,) * (bits - 1)
        nb = bits - 1
        rows_in, rows_out = 2 * width // devices, 2 * hidden // devices
        cols_in, cols_out = hidden // 2, width // 2
        vm, sems = pltpu.VMEM, pltpu.SemaphoreType.DMA
        half_in = cols_in // 2
        act = lambda cols, dtype=BF: vm((tokens, cols), dtype)
        group = vm(chip + (rows_in, cols_in), BF)
        pieces = vm((groups, frames, chunks, per_chunk, width), BF)
        ins = dict(
            cots=tuple(cots),
            dmlp=d_mlp_in,
            third=third,
            mid=mid,
            mod=mod,
            cq=cross_q,
            text=text_proj,
            tproj=temporal_proj,
            cout=cross_out_weight,
            cwq=cross_query_weight,
            tout=temporal_out_weight,
            tqkv=temporal_qkv_weight,
            firsts=tuple(firsts),
            cin=cross_in,
            cmix=cross_mix,
            words=text_flat,
            tin=temporal_in,
            tmix=temporal_mix,
            sum_out=sum_out.reshape(chip + (rows_out, cols_out)),
            sum_in=sum_in.reshape(chip + (rows_in, cols_in)),
            results=tuple(outs[5 : 4 + groups]),
        )
        in_specs = jax.tree.map(lambda _: anywhere, ins)
        in_specs["mod"] = mod_spec
        out_shape = dict(
            results=(piece_shape,) * (groups - 1),
            dfirsts=(piece_shape,) * groups,
            dmod=jax.ShapeDtypeStruct((2, width), F32),
            mlp_out=jax.ShapeDtypeStruct((rows_out // 2, width), F32),
            mlp_in=jax.ShapeDtypeStruct((rows_in // 2, hidden), F32),
            cur_c=jax.ShapeDtypeStruct(chip + (rows_in, cols_in), BF),
            cur_t=jax.ShapeDtypeStruct(chip + (rows_in, cols_in), BF),
        )
        out_specs = jax.tree.map(lambda _: anywhere, out_shape)
        for name in ("dmod", "mlp_out", "mlp_in"):
            out_specs[name] = fixed(out_shape[name].shape)
        scratch = dict(
            local=sems((40,)),
            cots=pieces,
            firsts=pieces,
            dfirst=pieces,
            dmlp=act(width, F32),
            third=act(width, F32),
            mid=act(width, F32),
            cq=act(width),
            text=vm(text_proj.shape, BF),
            tproj=act(3 * width),
            cout=vm((width, width), BF),
            cwq=vm((width, width), BF),
            tout=vm((width, width), BF),
            tqkv=vm((width, 3 * width), BF),
            cin=act(width),
            cmix=act(width),
            words=vm(text_flat.shape, BF),
            tin=act(width),
            tmix=act(width),
            so=stream_scratch(rows_out, cols_out, nb),
            si=stream_scratch(rows_in, cols_in, nb),
            sc=stream_scratch(rows_in, cols_in, nb),
            cur_out=vm(chip + (rows_out, cols_out), BF),
            cur_in=group,
            cur_c=group,
            cur_t=group,
            send_c=vm((width, cols_in), BF),
            send_t=vm((width, cols_in), BF),
            keep_sems=sems((4,)),
            core_sems=sems((2, 2)),
            result_sems=sems((2, groups - 1)),
            first_sems=sems((2, groups, chunks)),
            mlp_out_sems=sems((2, 1)),
            mlp_in_sems=sems((2, 1)),
            text_acc=vm(text_proj.shape, F32),
            work=vm((ROWS, width), BF),
            dcb=act(width),
            dcq=act(width),
            dtext=vm(text_proj.shape, BF),
            dtb=act(width),
            dtp=act(3 * width),
            fin_out=vm((2, rows_out // 2, cols_out), F32),
            fin_in=vm((2, rows_in // 2, cols_in), F32),
        )
        one = pl.pallas_call(
            with_scratch(back_one, scratch),
            grid_spec=pltpu.PrefetchScalarGridSpec(
                num_scalar_prefetch=2,
                grid=(1,),
                in_specs=[in_specs],
                out_specs=out_specs,
                scratch_shapes=jax.tree.leaves(scratch),
            ),
            out_shape=out_shape,
            compiler_params=params(collective_id=2, has_side_effects=True),
            cost_estimate=cost(44 * tokens * width * width, 40e6, tokens * ROWS * 18),
            name="back_one",
        )(text_length, motion_free, ins)

        ins = dict(
            dfirsts=one["dfirsts"],
            results=(outs[4],) + tuple(one["results"]),
            video=video_view.reshape(frames, groups, here, width),
            sbranch=spatial_branch,
            sout=spatial_out_weight,
            sproj=spatial_proj,
            sin=spatial_in,
            smix=spatial_mix,
            sqkv=spatial_qkv_weight,
            mod=mod,
            dmod_two=one["dmod"],
            dgate_two=d_gate_two,
            cur_c=one["cur_c"],
            cur_t=one["cur_t"],
        )
        in_specs = jax.tree.map(lambda _: anywhere, ins)
        for name in ("mod", "dmod_two", "dgate_two"):
            in_specs[name] = fixed(ins[name].shape)
        mine_rows = rows_in // 2

        def grad_shapes(widths):
            return tuple(jax.ShapeDtypeStruct((mine_rows, w), F32) for w in widths)

        out_shape = dict(
            video_grad=jax.ShapeDtypeStruct((frames, groups, here, width), F32),
            result=jax.ShapeDtypeStruct((frames, groups, here, width), BF),
            dmod_all=jax.ShapeDtypeStruct((narrow, 8, width), F32),
            spatial=grad_shapes([3 * width, width]),
            temporal=grad_shapes([3 * width, width]),
            cross=grad_shapes([width, 2 * width, width]),
        )
        out_specs = jax.tree.map(lambda leaf: fixed(leaf.shape), out_shape)
        final = vm((2, mine_rows, cols_in), F32)
        scratch = dict(
            local=sems((32,)),
            dfirsts=pieces,
            sbranch=act(width),
            sout=vm((width, width), BF),
            sproj=act(3 * width),
            sin=act(width),
            smix=act(width),
            sqkv=vm((width, 3 * width), BF),
            video=vm((groups, frames, here, width), BF),
            results=pieces,
            cur_c=group,
            cur_t=group,
            cur_s=group,
            sc=stream_scratch(rows_in, cols_in, nb),
            sta=stream_scratch(rows_in, half_in, nb),
            stb=stream_scratch(rows_in, half_in, nb),
            ssa=stream_scratch(rows_in, half_in, nb),
            ssb=stream_scratch(rows_in, half_in, nb),
            send_s=vm((width, cols_in), BF),
            keep_sems=sems((3,)),
            core_sems=sems((2, 1)),
            mod_sems=sems((2, bits)),
            t_sems=sems((2, 2)),
            c_sems=sems((2, 3)),
            s_sems=sems((2, 2)),
            work=vm((ROWS, width), BF),
            dsb=act(width),
            dsp=act(3 * width),
            mod_sum=vm((8, width), F32),
            mod_in=vm((wide_bits, 8, width), F32),
            fin_t=final,
            fin_c=final,
            fin_s=final,
        )
        two = pl.pallas_call(
            with_scratch(back_two, scratch),
            grid_spec=pltpu.PrefetchScalarGridSpec(
                num_scalar_prefetch=0,
                grid=(1,),
                in_specs=[in_specs],
                out_specs=out_specs,
                scratch_shapes=jax.tree.leaves(scratch),
            ),
            out_shape=out_shape,
            compiler_params=params(collective_id=3, has_side_effects=True),
            cost_estimate=cost(30 * tokens * width * width, 30e6, tokens * patches * 12),
            name="back_two",
        )(ins)
        d_mod_all = two["dmod_all"][:, :6]
        ada_rows = jnp.sum(silu_rows[:, :, None, None] * d_mod_all[:, None, :, :], 0)
        grads = (
            [ada_rows]
            + list(two["spatial"])
            + list(two["temporal"])
            + list(two["cross"])
            + [one["mlp_in"], one["mlp_out"]]
        )
        return (
            two["result"].reshape(video.shape),
            two["video_grad"].reshape(video.shape),
        ) + tuple(g.reshape(-1) for g in grads)

    results = [outs[4]] + [flip(outs[4 + j], j) for j in range(1, groups)]

    outs = pl.pallas_call(
        functools.partial(middle_backward, groups=groups, width=width, per_chunk=per_chunk),
        grid_spec=two_scalars(
            (chunks,),
            [chunk_piece() for _ in range(groups)]
            + [
                row_block(width),
                row_block(width),
                row_block(width),
                mod_spec,
                row_block(width),
                row_block(3 * width),
                row_block(width),
                fixed(text_proj.shape),
                fixed(cross_out_weight.shape),
                fixed(cross_query_weight.shape),
                fixed(temporal_out_weight.shape),
                fixed(temporal_qkv_weight.shape),
            ]
            + [chunk_piece() for _ in range(groups)],
            [
                row_block(width),
                row_block(width),
                fixed((text_pad, 2 * width)),
                row_block(width),
                row_block(3 * width),
                fixed((2, width)),
            ]
            + [chunk_piece() for _ in range(groups)],
            [pltpu.VMEM((text_pad, 2 * width), F32), pltpu.VMEM((ROWS, width), BF)],
        ),
        out_shape=[
            rows_of(width),
            rows_of(width),
            jax.ShapeDtypeStruct((text_pad, 2 * width), BF),
            rows_of(width),
            rows_of(3 * width),
            jax.ShapeDtypeStruct((2, width), F32),
        ]
        + [piece_shape] * groups,
        compiler_params=params(),
        cost_estimate=cost(20 * tokens * width * width, 25e6, tokens * ROWS * 18),
        name="middle_backward",
    )(
        text_length,
        motion_free,
        *cots,
        d_mlp_in,
        third,
        mid,
        mod,
        temporal_in,
        temporal_proj,
        cross_q,
        text_proj,
        cross_out_weight,
        cross_query_weight,
        temporal_out_weight,
        temporal_qkv_weight,
        *firsts,
    )
    d_cross_branch, d_cross_q, d_text, d_temporal_branch, d_temporal_proj, d_mod_two = outs[:6]
    d_firsts = [outs[6]] + [flip(outs[6 + j], j) for j in range(1, groups)]

    cross_send, cross_keep = weight_grads_call(
        core_arr,
        [(cross_in, d_cross_q), (text_flat, d_text), (cross_mix, d_cross_branch)],
    )
    temporal_send, temporal_keep = weight_grads_call(
        core_arr,
        [(temporal_in, d_temporal_proj), (temporal_mix, d_temporal_branch)],
    )

    d_spatial_branch, d_spatial_proj, d_gate_one = pl.pallas_call(
        functools.partial(spatial_backward, groups=groups, width=width),
        grid=(frames,),
        in_specs=[frame_piece() for _ in range(groups)]
        + [mod_spec, row_block(width), row_block(3 * width), fixed(spatial_out_weight.shape)],
        out_specs=[row_block(width), row_block(3 * width), fixed((1, width))],
        out_shape=[rows_of(width), rows_of(3 * width), jax.ShapeDtypeStruct((1, width), F32)],
        scratch_shapes=[pltpu.VMEM((ROWS, width), BF)],
        compiler_params=params(),
        cost_estimate=cost(8 * tokens * width * width, 10e6, tokens * patches * 12),
        name="spatial_backward",
    )(*d_firsts, mod, spatial_branch, spatial_proj, spatial_out_weight)

    spatial_send, spatial_keep = weight_grads_call(
        core_arr,
        [(spatial_in, d_spatial_proj), (spatial_mix, d_spatial_branch)],
    )

    out_block = pl.BlockSpec((1, groups, here, width), lambda f, *_: (f, 0, 0, 0))
    video_grad, result, d_mod_one = pl.pallas_call(
        functools.partial(video_backward, groups=groups, width=width),
        grid_spec=pltpu.PrefetchScalarGridSpec(
            num_scalar_prefetch=1,
            grid=(frames,),
            in_specs=[own_patches(j) for j in range(groups)]
            + [frame_piece() for _ in range(2 * groups)]
            + [mod_spec, row_block(3 * width), fixed(spatial_qkv_weight.shape)],
            out_specs=[out_block, out_block, fixed((2, width))],
        ),
        out_shape=[
            jax.ShapeDtypeStruct((frames, groups, here, width), F32),
            jax.ShapeDtypeStruct((frames, groups, here, width), BF),
            jax.ShapeDtypeStruct((2, width), F32),
        ],
        compiler_params=params(),
        cost_estimate=cost(6 * tokens * width * width, 12e6),
        name="video_backward",
    )(place, *[video_view] * groups, *d_firsts, *results, mod, d_spatial_proj, spatial_qkv_weight)
    video_grad = video_grad.reshape(video.shape)
    result = result.reshape(video.shape)

    d_mod = jnp.concatenate([d_mod_one, d_gate_one, d_mod_two, d_gate_two], 0)
    for b in range(wide_bits):
        d_mod = d_mod + flip(d_mod, 1 << b)
    d_mod_all = gather_narrow(d_mod[None])
    ada_rows = jnp.sum(silu_rows[:, :, None, None] * d_mod_all[:, None, :, :], 0)
    ada_grad = ada_rows.reshape(-1)

    chip_bits = list(range(1, bits))
    first_x = [wide_bits, 1]
    rest = [b for b in chip_bits if b not in first_x]
    order_a = first_x + rest
    order_b = first_x[::-1] + rest

    def join(send, keep):
        return keep.astype(F32) + flip(send, 1).astype(F32)

    def reduce_scatter(cur, order):
        cols = cur.shape[1]
        axes = sorted(chip_bits, reverse=True)
        for b in order:
            cur = cur.astype(BF)
            at = axes.index(b)
            view = cur.reshape(1 << at, 2, 1 << (len(axes) - at - 1), -1, cols)
            out = lax.dynamic_index_in_dim(view, 1 - bit_of(b), 1, keepdims=False)
            own = lax.dynamic_index_in_dim(view, bit_of(b), 1, keepdims=False)
            cur = own.astype(F32) + flip(out, 1 << b).astype(F32)
            axes.remove(b)
        cur = cur.reshape(2, -1, cols)
        own = lax.dynamic_index_in_dim(cur, core, 0, keepdims=False)
        other = flip(lax.dynamic_index_in_dim(cur, 1 - core, 0, keepdims=False), 1)
        low = jnp.where(core == 0, own, other)
        high = jnp.where(core == 0, other, own)
        return low, high

    def unpack(pair, widths):
        low, high = pair
        start, out = 0, []
        for w in widths:
            half = w // 2
            cols = slice(start, start + half)
            out.append(jnp.concatenate([low[:, cols], high[:, cols]], 1).reshape(-1))
            start += half
        return out

    mlp_out_grad = unpack(reduce_scatter(sum_out, order_a), [width])[0]
    mlp_in_grad = unpack(reduce_scatter(sum_in, order_b), [hidden])[0]
    cross_query_grad, cross_kv_grad, cross_out_grad = unpack(
        reduce_scatter(join(cross_send, cross_keep), order_a), [width, 2 * width, width]
    )
    temporal_qkv_grad, temporal_out_grad = unpack(
        reduce_scatter(join(temporal_send, temporal_keep), order_b), [3 * width, width]
    )
    spatial_qkv_grad, spatial_out_grad = unpack(
        reduce_scatter(join(spatial_send, spatial_keep), order_a), [3 * width, width]
    )
    return (
        result,
        video_grad,
        ada_grad,
        spatial_qkv_grad,
        spatial_out_grad,
        temporal_qkv_grad,
        temporal_out_grad,
        cross_query_grad,
        cross_kv_grad,
        cross_out_grad,
        mlp_in_grad,
        mlp_out_grad,
    )


def solution(mesh):
    tokens_spec = P("narrow", "wide", None, None)
    in_specs = (
        (tokens_spec, P("narrow", None, None), P("narrow"), P("narrow"), P("narrow"))
        + (P(),) * 10
        + (tokens_spec,)
    )
    out_specs = (tokens_spec, tokens_spec) + (P(AXES),) * 10
    return jax.shard_map(
        functools.partial(shards, mesh_shape=dict(mesh.shape)),
        mesh=mesh,
        in_specs=in_specs,
        out_specs=out_specs,
        check_vma=False,
    )
```

```python
import functools
import itertools
import math
import types

import jax
import jax.numpy as jnp
from jax import lax
from jax.experimental import pallas as pl
from jax.experimental.pallas import tpu as pltpu
from jax.sharding import PartitionSpec as P

HEAD_DIM = 64
SLAB = 2 * HEAD_DIM
SCALE = HEAD_DIM ** (-0.5)
EPSILON = 1e-06
NEG_LARGE = -1e30
BF = jnp.bfloat16
F32 = jnp.float32
AXES = ("narrow", "wide")
ROWS = 256
MESH = pl.DeviceIdType.MESH
VMEM_LIMIT = 60 * 1024 * 1024
Names = types.SimpleNamespace


def time_features(time_value, width):
    half = width // 2
    freqs = jnp.exp(-math.log(10000.0) * jnp.arange(half, dtype=F32) / half)
    angles = time_value[..., None] * freqs
    return jnp.concatenate([jnp.cos(angles), jnp.sin(angles)], axis=-1)


def silu_of(values):
    return values / (1.0 + jnp.exp(-values))


def normalize(values):
    mean = jnp.mean(values, -1, keepdims=True)
    centred = values - mean
    variance = jnp.mean(centred * centred, -1, keepdims=True)
    inv_std = lax.rsqrt(variance + EPSILON)
    return centred * inv_std, inv_std


def norm_back(grad_norm, normed, inv_std):
    return inv_std * (
        grad_norm
        - jnp.mean(grad_norm, -1, keepdims=True)
        - normed * jnp.mean(grad_norm * normed, -1, keepdims=True)
    )


def mm(left, right):
    return jnp.dot(left, right, preferred_element_type=F32)


def mm_nt(left, right):
    return lax.dot_general(left, right, (((1,), (1,)), ((), ())), preferred_element_type=F32)


def mm_tn(left, right):
    return lax.dot_general(left, right, (((0,), (0,)), ((), ())), preferred_element_type=F32)


def head_masks():
    lane = lax.broadcasted_iota(jnp.int32, (1, SLAB), 1)
    low = (lane < HEAD_DIM).astype(F32)
    return low.astype(BF), (1.0 - low).astype(BF)


def softmax_rows(scores):
    peak = jnp.max(scores, -1, keepdims=True)
    expd = jnp.exp(scores - peak)
    return expd * (1.0 / jnp.sum(expd, -1, keepdims=True))


def attend_slab(query, key, value, bias):
    mixed = None
    for mask in head_masks():
        scores = mm_nt(query * mask, key) * SCALE
        if bias is not None:
            scores = jnp.where(bias, scores, NEG_LARGE)
        probs = softmax_rows(scores).astype(BF)
        part = mm(probs, value * mask)
        mixed = part if mixed is None else mixed + part
    return mixed


def attend_slab_back(query, key, value, grad, bias):
    grad_query = grad_key = grad_value = 0.0
    for mask in head_masks():
        query_part = query * mask
        grad_part = grad * mask
        scores = mm_nt(query_part, key) * SCALE
        if bias is not None:
            scores = jnp.where(bias, scores, NEG_LARGE)
        probs = softmax_rows(scores)
        grad_probs = mm_nt(grad_part, value)
        inner = jnp.sum(grad_probs * probs, -1, keepdims=True)
        grad_scores = (probs * (grad_probs - inner)).astype(BF)
        grad_value = grad_value + mm_tn(probs.astype(BF), grad_part)
        grad_query = grad_query + mm(grad_scores, key * mask)
        grad_key = grad_key + mm_tn(grad_scores, query_part)
    return grad_query * SCALE, grad_key * SCALE, grad_value


def slab_at(index, offset=0):
    return pl.ds(pl.multiple_of(index * SLAB + offset, SLAB), SLAB)


def frame_mask(rows, per_chunk):
    row = lax.broadcasted_iota(jnp.int32, (rows, rows), 0)
    col = lax.broadcasted_iota(jnp.int32, (rows, rows), 1)
    return lax.rem(row, per_chunk) == lax.rem(col, per_chunk)


def part_of(mod, index, width):
    return mod[:, index * width : (index + 1) * width]


def cost(flops, bytes_accessed, transcendentals=0):
    return pl.CostEstimate(
        flops=int(flops), bytes_accessed=int(bytes_accessed), transcendentals=int(transcendentals)
    )


def params(**extra):
    return pltpu.CompilerParams(vmem_limit_bytes=VMEM_LIMIT, **extra)


def fixed(shape):
    rank = len(shape)
    return pl.BlockSpec(shape, lambda *_: (0,) * rank, pipeline_mode=pl.Buffered(1))


def partner(mask):
    wide = lax.axis_size("wide")
    me = lax.axis_index("narrow") * wide + lax.axis_index("wide")
    other = jnp.bitwise_xor(me, mask)
    return (lax.div(other, wide), lax.rem(other, wide))


def greet(masks):
    barrier = pltpu.get_barrier_semaphore()
    for mask in masks:
        pl.semaphore_signal(barrier, inc=1, device_id=partner(mask), device_id_type=MESH)
    pl.semaphore_wait(barrier, len(masks))


def send(src, dst, send_sem, recv_sem, mask):
    return pltpu.make_async_remote_copy(
        src_ref=src,
        dst_ref=dst,
        send_sem=send_sem,
        recv_sem=recv_sem,
        device_id=partner(mask),
        device_id_type=MESH,
    )


def spatial_forward(*refs, groups, width, frames):
    videos, refs = refs[:groups], refs[groups:]
    cot_own, cot_all, mod_ref, qkv_ref, out_ref, refs = refs[0], refs[1], refs[2], refs[3], refs[4], refs[5:]
    in_ref, proj_ref, mix_ref, branch_ref, refs = refs[0], refs[1], refs[2], refs[3], refs[4:]
    first_own, firsts, refs = refs[0], refs[1:groups], refs[groups:]
    cot_out, cots, refs = refs[0], refs[1:groups], refs[groups:]
    out_buf, cot_sems, first_sems = refs
    frame = pl.program_id(0)
    place = lax.axis_index("wide")
    others = range(1, groups)

    def cot_copy(j):
        return send(
            cot_all.at[:, jnp.bitwise_xor(place, j)],
            cots[j - 1],
            cot_sems.at[0, j - 1],
            cot_sems.at[1, j - 1],
            j,
        )

    def first_copy(j, f):
        return send(
            out_buf.at[j - 1, f],
            firsts[j - 1].at[f],
            first_sems.at[0, j - 1, f],
            first_sems.at[1, j - 1, f],
            j,
        )

    @pl.when(frame == 0)
    def _():
        greet(list(others))
        for j in others:
            cot_copy(j).start()

    cot_out[...] = cot_own[...].reshape(cot_out.shape)
    mod = mod_ref[...]
    video = jnp.concatenate([v[...].reshape(-1, width) for v in videos], 0).astype(F32)
    normed, _ = normalize(video)
    entry = (normed * (1.0 + part_of(mod, 1, width)) + part_of(mod, 0, width)).astype(BF)
    in_ref[...] = entry
    proj_ref[...] = mm(entry, qkv_ref[...]).astype(BF)

    def pair(index, carry):
        mixed = attend_slab(
            proj_ref[:, slab_at(index)],
            proj_ref[:, slab_at(index, width)],
            proj_ref[:, slab_at(index, 2 * width)],
            None,
        )
        mix_ref[:, slab_at(index)] = mixed.astype(BF)
        return carry

    lax.fori_loop(0, width // SLAB, pair, 0)
    branch = mm(mix_ref[...], out_ref[...])
    first = (video + part_of(mod, 2, width) * branch).astype(BF)
    share = first.shape[0] // groups
    for j in others:
        out_buf[j - 1, frame] = first[j * share : (j + 1) * share]
    first_own[...] = first[:share].reshape(first_own.shape)
    branch_ref[...] = branch.astype(BF)
    for j in others:
        first_copy(j, frame).start()

    @pl.when(frame == frames - 1)
    def _():
        for j in others:
            cot_copy(j).wait()
            for f in range(frames):
                first_copy(j, f).wait()


def middle_forward(length_ref, keep_ref, *refs, groups, width, per_chunk):
    pieces, refs = refs[:groups], refs[groups:]
    mod_ref, qkv_ref, tout_ref, cq_ref, text_ref, cout_ref = refs[:6]
    tin_ref, tproj_ref, tmix_ref, cin_ref, cq_out, cmix_ref, mlp_ref, mid_ref, third_ref = refs[6:]
    mod = mod_ref[...]
    first = jnp.concatenate([p[...].reshape(-1, width) for p in pieces], 0).astype(F32)
    rows = first.shape[0]
    normed, _ = normalize(first)
    entry = normed.astype(BF)
    tin_ref[...] = entry
    tproj_ref[...] = mm(entry, qkv_ref[...]).astype(BF)
    same = frame_mask(rows, per_chunk)

    def pair(index, carry):
        mixed = attend_slab(
            tproj_ref[:, slab_at(index)],
            tproj_ref[:, slab_at(index, width)],
            tproj_ref[:, slab_at(index, 2 * width)],
            same,
        )
        tmix_ref[:, slab_at(index)] = mixed.astype(BF)
        return carry

    lax.fori_loop(0, width // SLAB, pair, 0)
    keep = (1 - keep_ref[0]).astype(F32)
    mid = first + keep * mm(tmix_ref[...], tout_ref[...])
    mid_ref[...] = mid
    normed, _ = normalize(mid)
    entry = normed.astype(BF)
    cin_ref[...] = entry
    cq_out[...] = mm(entry, cq_ref[...]).astype(BF)
    keys = text_ref.shape[0]
    valid = lax.broadcasted_iota(jnp.int32, (rows, keys), 1) < length_ref[0]

    def cross_pair(index, carry):
        mixed = attend_slab(
            cq_out[:, slab_at(index)],
            text_ref[:, slab_at(index)],
            text_ref[:, slab_at(index, width)],
            valid,
        )
        cmix_ref[:, slab_at(index)] = mixed.astype(BF)
        return carry

    lax.fori_loop(0, width // SLAB, cross_pair, 0)
    third = mid + mm(cmix_ref[...], cout_ref[...])
    third_ref[...] = third
    normed, _ = normalize(third)
    mlp_ref[...] = (normed * (1.0 + part_of(mod, 4, width)) + part_of(mod, 3, width)).astype(BF)


def mlp_both(*refs, groups, width, steps):
    cots, refs = refs[:groups], refs[groups:]
    mlp_ref, third_ref, mod_ref, win_ref, wout_ref = refs[:5]
    sum_in, sum_out, dmlp_ref, dgate_ref = refs[5:9]
    results, scratch = refs[9 : 9 + groups], refs[9 + groups :]
    mlp_t, dbranch, branch, send_in, recv_in, send_out, keep_out, recv_out, in_sems, out_sems = scratch
    step = pl.program_id(0)
    half = steps // 2
    core = jnp.bitwise_and(lax.axis_index("wide"), 1)
    mod = mod_ref[...]
    gate = part_of(mod, 5, width)
    tokens = mlp_ref.shape[0]
    chunks = tokens // ROWS
    share = ROWS // groups

    def block_at(s):
        side = jnp.where(s < half, 1 - core, core)
        return side * half + lax.rem(s, half)

    def in_copy(s):
        return send(send_in.at[s], recv_in.at[s], in_sems.at[0, s], in_sems.at[1, s], 1)

    def out_copy(s):
        block = block_at(s)
        return send(
            send_out.at[block], recv_out.at[block], out_sems.at[0, block], out_sems.at[1, block], 1
        )

    @pl.when(step == 0)
    def _():
        greet([1])
        mlp_t[...] = mlp_ref[...].T
        for k in range(chunks):
            for j in range(groups):
                rows = pl.ds(k * ROWS + j * share, share)
                cot = cots[j][:, k].reshape(share, width).astype(F32)
                dbranch[rows, :] = (gate * cot).astype(BF)
        branch[...] = jnp.zeros_like(branch)
        dmlp_ref[...] = jnp.zeros_like(dmlp_ref)

    @pl.when(step >= 1)
    def _():
        out_copy(step - 1).start()

    @pl.when(jnp.logical_and(step >= 1, step <= half))
    def _():
        in_copy(step - 1).start()

    pre = mm(mlp_ref[...], win_ref[...])
    d_hidden = mm_nt(dbranch[...], wout_ref[...])
    square = pre * pre
    bend = jnp.tanh(0.7978845608 * pre * (1.0 + 0.044715 * square))
    ramp = 0.5 * (1.0 + bend)
    hidden = (pre * ramp).astype(BF)
    slope = ramp + 0.5 * pre * (1.0 - bend * bend) * (
        0.7978845608 * (1.0 + (3.0 * 0.044715) * square)
    )
    d_pre = (d_hidden * slope).astype(BF)
    hidden_t = hidden.T
    side = width // 2
    block = block_at(step)
    send_out[block] = mm(
        hidden_t, dbranch[:, pl.ds(pl.multiple_of((1 - core) * side, 128), side)]
    ).astype(BF)
    keep_out[block] = mm(
        hidden_t, dbranch[:, pl.ds(pl.multiple_of(core * side, 128), side)]
    ).astype(BF)
    grad_in = mm(mlp_t[...], d_pre)

    @pl.when(step < half)
    def _():
        send_in[step] = grad_in.astype(BF)

    @pl.when(step >= half)
    def _():
        in_copy(step - half).wait_recv()
        sum_in[...] = (grad_in + recv_in[step - half].astype(F32)).astype(BF)

    branch[...] += mm(hidden, wout_ref[...])
    dmlp_ref[...] += mm_nt(d_pre, win_ref[...])

    @pl.when(step == steps - 1)
    def _():
        out_copy(steps - 1).start()
        total = jnp.zeros((1, width), F32)
        for k in range(chunks):
            for j in range(groups):
                rows = pl.ds(k * ROWS + j * share, share)
                cot = cots[j][:, k].reshape(share, width).astype(F32)
                piece = branch[rows, :]
                total = total + jnp.sum(cot * piece, 0, keepdims=True)
                out = (third_ref[rows, :] + gate * piece).astype(BF)
                results[j][:, k] = out.reshape(results[j][:, k].shape)
        dgate_ref[...] = total
        for s in range(half):
            in_copy(s).wait_send()
        deep = send_out.shape[1]
        for s in range(steps):
            out_copy(s).wait_send()
            out_copy((s + half) % steps).wait_recv()
            block = block_at((s + half) % steps)
            rows = pl.ds(pl.multiple_of(block * deep, 16), deep)
            sum_out[rows, :] = (
                keep_out[block].astype(F32) + recv_out[block].astype(F32)
            ).astype(BF)


def middle_backward(length_ref, keep_ref, *refs, groups, width, per_chunk):
    cots, refs = refs[:groups], refs[groups:]
    dmlp_ref, third_ref, mid_ref, mod_ref = refs[:4]
    tin_ref, tproj_ref, cq_in, text_ref = refs[4:8]
    cout_ref, cq_ref, tout_ref, tqkv_ref = refs[8:12]
    first_refs, refs = refs[12 : 12 + groups], refs[12 + groups :]
    dcb_ref, dcq_ref, dtext_ref, dtb_ref, dtp_ref, dmod_ref = refs[:6]
    dfirsts = refs[6 : 6 + groups]
    text_acc, work = refs[6 + groups :]
    chunk = pl.program_id(0)
    mod = mod_ref[...]

    @pl.when(chunk == 0)
    def _():
        text_acc[...] = jnp.zeros_like(text_acc)
        dmod_ref[...] = jnp.zeros_like(dmod_ref)

    cot = jnp.concatenate([p[...].reshape(-1, width) for p in cots], 0).astype(F32)
    rows = cot.shape[0]
    d_mlp = dmlp_ref[...]
    normed, inv_std = normalize(third_ref[...])
    dmod_ref[0:1, :] += jnp.sum(d_mlp, 0, keepdims=True)
    dmod_ref[1:2, :] += jnp.sum(d_mlp * normed, 0, keepdims=True)
    d_third = cot + norm_back(d_mlp * (1.0 + part_of(mod, 4, width)), normed, inv_std)
    d_branch = d_third.astype(BF)
    dcb_ref[...] = d_branch
    work[...] = mm_nt(d_branch, cout_ref[...]).astype(BF)
    keys = text_ref.shape[0]
    valid = lax.broadcasted_iota(jnp.int32, (rows, keys), 1) < length_ref[0]

    def cross_pair(index, carry):
        at, after = slab_at(index), slab_at(index, width)
        grad_q, grad_k, grad_v = attend_slab_back(
            cq_in[:, at], text_ref[:, at], text_ref[:, after], work[:, at], valid
        )
        dcq_ref[:, at] = grad_q.astype(BF)
        text_acc[:, at] += grad_k
        text_acc[:, after] += grad_v
        return carry

    lax.fori_loop(0, width // SLAB, cross_pair, 0)
    dtext_ref[...] = text_acc[...].astype(BF)
    normed, inv_std = normalize(mid_ref[...])
    d_mid = d_third + norm_back(mm_nt(dcq_ref[...], cq_ref[...]), normed, inv_std)
    keep = (1 - keep_ref[0]).astype(F32)
    d_branch = (keep * d_mid).astype(BF)
    dtb_ref[...] = d_branch
    work[...] = mm_nt(d_branch, tout_ref[...]).astype(BF)
    same = frame_mask(rows, per_chunk)

    def pair(index, carry):
        at, after, last = slab_at(index), slab_at(index, width), slab_at(index, 2 * width)
        grad_q, grad_k, grad_v = attend_slab_back(
            tproj_ref[:, at], tproj_ref[:, after], tproj_ref[:, last], work[:, at], same
        )
        dtp_ref[:, at] = grad_q.astype(BF)
        dtp_ref[:, after] = grad_k.astype(BF)
        dtp_ref[:, last] = grad_v.astype(BF)
        return carry

    lax.fori_loop(0, width // SLAB, pair, 0)
    first = jnp.concatenate([p[...].reshape(-1, width) for p in first_refs], 0).astype(F32)
    normed, inv_std = normalize(first)
    d_first = d_mid + norm_back(mm_nt(dtp_ref[...], tqkv_ref[...]), normed, inv_std)
    d_first = d_first.astype(BF)
    share = rows // groups
    for j, ref in enumerate(dfirsts):
        ref[...] = d_first[j * share : (j + 1) * share].reshape(ref.shape)


def spatial_backward(*refs, groups, width):
    dfirsts, refs = refs[:groups], refs[groups:]
    mod_ref, branch_ref, proj_ref, out_ref = refs[:4]
    dsb_ref, dproj_ref, dgate_ref, work = refs[4:]
    frame = pl.program_id(0)
    mod = mod_ref[...]

    @pl.when(frame == 0)
    def _():
        dgate_ref[...] = jnp.zeros_like(dgate_ref)

    d_first = jnp.concatenate([p[...].reshape(-1, width) for p in dfirsts], 0).astype(F32)
    dgate_ref[...] += jnp.sum(d_first * branch_ref[...].astype(F32), 0, keepdims=True)
    d_branch = (part_of(mod, 2, width) * d_first).astype(BF)
    dsb_ref[...] = d_branch
    work[...] = mm_nt(d_branch, out_ref[...]).astype(BF)

    def pair(index, carry):
        at, after, last = slab_at(index), slab_at(index, width), slab_at(index, 2 * width)
        grad_q, grad_k, grad_v = attend_slab_back(
            proj_ref[:, at], proj_ref[:, after], proj_ref[:, last], work[:, at], None
        )
        dproj_ref[:, at] = grad_q.astype(BF)
        dproj_ref[:, after] = grad_k.astype(BF)
        dproj_ref[:, last] = grad_v.astype(BF)
        return carry

    lax.fori_loop(0, width // SLAB, pair, 0)


def video_backward(where_ref, *refs, groups, width):
    videos, refs = refs[:groups], refs[groups:]
    dfirsts, refs = refs[:groups], refs[groups:]
    results, refs = refs[:groups], refs[groups:]
    mod_ref, dproj_ref, qkv_ref, grad_ref, result_ref, dmod_ref = refs
    frame = pl.program_id(0)
    place = where_ref[0]
    mod = mod_ref[...]

    @pl.when(frame == 0)
    def _():
        dmod_ref[...] = jnp.zeros_like(dmod_ref)

    video = jnp.concatenate([v[...].reshape(-1, width) for v in videos], 0).astype(F32)
    d_first = jnp.concatenate([p[...].reshape(-1, width) for p in dfirsts], 0).astype(F32)
    normed, inv_std = normalize(video)
    d_in = mm_nt(dproj_ref[...], qkv_ref[...])
    dmod_ref[0:1, :] += jnp.sum(d_in, 0, keepdims=True)
    dmod_ref[1:2, :] += jnp.sum(d_in * normed, 0, keepdims=True)
    grad = d_first + norm_back(d_in * (1.0 + part_of(mod, 1, width)), normed, inv_std)
    share = grad.shape[0] // groups
    for j in range(groups):
        slot = jnp.bitwise_xor(place, j)
        grad_ref[0, slot] = grad[j * share : (j + 1) * share]
        result_ref[0, slot] = results[j][...].reshape(share, width)


class Stream:
    def __init__(self, cur, recv, sems, order, cols, fin, source=None):
        self.cur, self.recv, self.sems, self.fin = cur, recv, sems, fin
        self.order, self.cols, self.source = order, cols, source
        self.bits = sorted(order, reverse=True)
        wide = lax.axis_size("wide")
        me = lax.axis_index("narrow") * wide + lax.axis_index("wide")
        self.mine = {b: jnp.bitwise_and(lax.shift_right_logical(me, b), 1) for b in order}

    def where(self, stage):
        spots = []
        for b in self.bits:
            at = self.order.index(b)
            if at < stage:
                spots.append(self.mine[b])
            elif at == stage:
                spots.append(1 - self.mine[b])
            else:
                spots.append(slice(None))
        return tuple(spots) + (slice(None), self.cols)

    def copy(self, stage):
        base = self.cur if stage > 0 or self.source is None else self.source
        return send(
            base.at[self.where(stage)],
            self.recv[stage],
            self.sems.at[0, stage],
            self.sems.at[1, stage],
            1 << self.order[stage],
        )

    def add(self, stage):
        self.copy(stage).wait()
        left = [b for b in self.bits if self.order.index(b) > stage]
        count = len(left)

        def summed(place):
            spot = tuple(place.get(b, self.mine[b]) for b in self.bits) + (slice(None), self.cols)
            inner = tuple(place[b] for b in left)
            return spot, self.cur[spot].astype(F32) + self.recv[stage][inner].astype(F32)

        if not left:
            _, total = summed({})
            self.fin[:, :, self.cols] = total.reshape(self.fin.shape[0], -1, total.shape[1])
            return

        def body(i, carry):
            place = {
                b: jnp.bitwise_and(lax.shift_right_logical(i, count - 1 - k), 1)
                for k, b in enumerate(left)
            }
            spot, total = summed(place)
            self.cur[spot] = total.astype(BF)
            return carry

        lax.fori_loop(0, 1 << count, body, 0)


def stream_scratch(rows, cols, bits, parts):
    cols = cols // parts
    shapes = [pltpu.VMEM((2,) * k + (rows, cols), BF) for k in range(bits - 1, -1, -1)]
    return [shapes + [pltpu.SemaphoreType.DMA((2, bits))] for _ in range(parts)]


def stream_orders(wide_bits, bits):
    z_bits = [b for b in range(2, bits + 1) if b != wide_bits]
    return [
        [wide_bits, 1] + z_bits,
        [1, z_bits[0], wide_bits] + z_bits[1:],
        [z_bits[0], wide_bits, 1] + z_bits[1:],
    ]


def forward_stage(streams, stage):
    for stream in streams:
        stream.add(stage)
        if stage + 1 < len(stream.order):
            stream.copy(stage + 1).start()


def store_flat(out, value, first, pitch):
    for t in range(value.shape[1] // 128):
        out[pl.ds(first + t, value.shape[0], stride=pitch), :] = value[:, t * 128 : (t + 1) * 128]


class Finish:
    def __init__(self, fin, fin_in, sems, flats, outs):
        self.fin, self.fin_in, self.sems, self.flats, self.outs = fin, fin_in, sems, flats, outs
        self.core = jnp.bitwise_and(lax.axis_index("wide"), 1)

    def swap(self):
        return send(
            self.fin.at[1 - self.core], self.fin_in, self.sems.at[0], self.sems.at[1], 1
        )

    def writes(self):
        return [
            pltpu.make_async_copy(flat, out, self.sems.at[2 + k])
            for k, (flat, out) in enumerate(zip(self.flats, self.outs))
        ]

    def store(self):
        self.swap().wait()
        own, other = self.fin[self.core], self.fin_in[...]
        low = jnp.where(self.core == 0, own, other)
        high = jnp.where(self.core == 0, other, own)
        start = 0
        for flat in self.flats:
            pitch = flat.shape[0] // own.shape[0]
            half = pitch * 128 // 2
            store_flat(flat, low[:, start : start + half], 0, pitch)
            store_flat(flat, high[:, start : start + half], pitch // 2, pitch)
            start += half
        for write in self.writes():
            write.start()

    def wait(self):
        for write in self.writes():
            write.wait()


def grads_half(pairs, side, dest, extra=None):
    start = 0
    for left, right in pairs:
        part = right.shape[1] // 2
        cols = pl.ds(pl.multiple_of(side * part, 128), part)
        for m in range(left.shape[1] // ROWS):
            rows = slice(m * ROWS, (m + 1) * ROWS)
            value = mm_tn(left[:, rows], right[:, cols])
            spot = (slice(m * ROWS, (m + 1) * ROWS), slice(start, start + part))
            if extra is not None:
                value = value + extra[spot].astype(F32)
            dest[spot] = value.astype(BF)
        start += part


def flat_rows(ref):
    return ref.reshape(-1, ref.shape[-1])


def with_scratch(body, scratch):
    form = jax.tree.structure(scratch)
    count = form.num_leaves

    def kernel(*refs):
        body(*refs[:-count], jax.tree.unflatten(form, refs[-count:]))

    return kernel


def all_bits():
    total = lax.axis_size("wide") * lax.axis_size("narrow")
    return total.bit_length() - 1


def piece_rows(ref, chunk):
    groups = ref.shape[0]
    width = ref.shape[-1]
    return jnp.concatenate([ref[j, :, chunk].reshape(-1, width) for j in range(groups)], 0)


def frame_rows(ref, frame):
    width = ref.shape[-1]
    return jnp.concatenate([ref[j, frame].reshape(-1, width) for j in range(ref.shape[0])], 0)


def backward(length_ref, keep_ref, ins, outs, scratch):
    a, o, s = Names(**ins), Names(**outs), Names(**scratch)
    groups = len(a.cots)
    tokens, width = a.dmlp.shape
    chunks = tokens // ROWS
    frames = a.video.shape[0]
    share = ROWS // groups
    bits = all_bits() - 1
    wide_bits = lax.axis_size("wide").bit_length() - 1
    place, narrow_at = lax.axis_index("wide"), lax.axis_index("narrow")
    core = jnp.bitwise_and(place, 1)
    others = range(1, groups)
    counter = itertools.count()

    def load(src, dst):
        copy = pltpu.make_async_copy(src, dst, s.local.at[next(counter)])
        copy.start()
        return copy

    def wait_all(copies):
        for copy in copies:
            copy.wait()

    cross_loads = [load(a.cots[j], s.cots.at[j]) for j in range(groups)]
    cross_loads += [load(a.dmlp, s.dmlp), load(a.third, s.third), load(a.cout, s.cout)]
    cross_loads += [load(a.cq, s.cq), load(a.text, s.text)]
    cross_grad_loads = [load(a.cin, s.cin), load(a.words, s.words), load(a.cmix, s.cmix)]
    temporal_loads = [load(a.mid, s.mid), load(a.cwq, s.cwq), load(a.tout, s.tout)]
    temporal_loads += [load(a.tproj, s.tproj), load(a.tqkv, s.tqkv)]
    temporal_loads += [load(a.firsts[j], s.firsts.at[j]) for j in range(groups)]
    sum_loads = [load(a.sum_out, s.cur_out), load(a.sum_in, s.cur_in)]

    orders = stream_orders(wide_bits, bits)

    def split(cur, parts, fin, source=None):
        third = cur.shape[-1] // len(orders)
        return [
            Stream(cur, part[:-1], part[-1], order, slice(i * third, (i + 1) * third), fin, source)
            for i, (part, order) in enumerate(zip(parts, orders))
        ]

    mlp = split(s.cur_out, s.st_out, s.fin_out, a.sum_out)
    mlp += split(s.cur_in, s.st_in, s.fin_in, a.sum_in)
    cross = split(s.cur_c, s.st_c, s.fin_c)
    temporal = split(s.cur_t, s.st_t, s.fin_t)
    spatial = split(s.cur_s, s.st_s, s.fin_s)
    ends = [
        Finish(s.fin_out, s.fin_out_in, s.end_out, s.flat_out, o.mlp_out),
        Finish(s.fin_in, s.fin_in_in, s.end_in, s.flat_in, o.mlp_in),
        Finish(s.fin_c, s.fin_c_in, s.end_c, s.flat_c, o.cross),
        Finish(s.fin_t, s.fin_t_in, s.end_t, s.flat_t, o.temporal),
        Finish(s.fin_s, s.fin_s_in, s.end_s, s.flat_s, o.spatial),
    ]
    greet(list(others) + [1 << b for b in range(wide_bits, bits + 1)])
    for stream in mlp:
        stream.copy(0).start()

    def result_copy(j):
        target = o.result.at[:, place]
        if j == 0:
            return pltpu.make_async_copy(a.results[0], target, s.result_sems.at[0, 0])
        return send(a.results[j], target, s.result_sems.at[0, j], s.result_sems.at[1, j], j)

    keys = s.text.shape[0]
    valid = lax.broadcasted_iota(jnp.int32, (ROWS, keys), 1) < length_ref[0]
    mod_scale = a.mod[:, 4 * width : 5 * width]
    work = s.work
    s.text_acc[...] = jnp.zeros_like(s.text_acc)
    s.mod_sum[...] = jnp.zeros_like(s.mod_sum)
    wait_all(cross_loads)

    def cross_chunk(k, carry):
        rows = pl.ds(pl.multiple_of(k * ROWS, ROWS), ROWS)
        cot = piece_rows(s.cots, k).astype(F32)
        d_mlp = s.dmlp[rows, :]
        normed, inv_std = normalize(s.third[rows, :])
        s.mod_sum[3:4, :] += jnp.sum(d_mlp, 0, keepdims=True)
        s.mod_sum[4:5, :] += jnp.sum(d_mlp * normed, 0, keepdims=True)
        d_third = cot + norm_back(d_mlp * (1.0 + mod_scale), normed, inv_std)
        s.dmlp[rows, :] = d_third
        d_branch = d_third.astype(BF)
        s.dcb[rows, :] = d_branch
        work[...] = mm_nt(d_branch, s.cout[...]).astype(BF)

        def pair(index, inner):
            at, after = slab_at(index), slab_at(index, width)
            grad_q, grad_k, grad_v = attend_slab_back(
                s.cq[rows, at], s.text[:, at], s.text[:, after], work[:, at], valid
            )
            s.dcq[rows, at] = grad_q.astype(BF)
            s.text_acc[:, at] += grad_k
            s.text_acc[:, after] += grad_v
            return inner

        lax.fori_loop(0, width // SLAB, pair, 0)
        return carry

    lax.fori_loop(0, chunks, cross_chunk, 0)
    s.dtext[...] = s.text_acc[...].astype(BF)
    video_loads = [load(a.video.at[:, jnp.bitwise_xor(place, j)], s.cots.at[j]) for j in range(groups)]
    late_loads = [load(a.sout, s.cout), load(a.sbranch, s.cq)]

    wait_all(cross_grad_loads)
    pairs_c = [(s.cin, s.dcq), (s.words, s.dtext), (s.cmix, s.dcb)]
    grads_half(pairs_c, 1 - core, s.send)

    def core_copy(src, cur, k):
        return send(src, flat_rows(cur), s.core_sems.at[0, k], s.core_sems.at[1, k], 1)

    copy_c = core_copy(s.send, s.cur_c, 0)
    copy_c.start()

    wait_all(temporal_loads)
    keep = (1 - keep_ref[0]).astype(F32)
    same = frame_mask(ROWS, a.firsts[0].shape[2])
    tproj, dtp = s.tproj, s.dtp

    def temporal_chunk(k):
        rows = slice(k * ROWS, (k + 1) * ROWS)
        normed, inv_std = normalize(s.mid[rows, :])
        d_mid = s.dmlp[rows, :] + norm_back(
            mm_nt(s.dcq[rows, :], s.cwq[...]), normed, inv_std
        )
        d_branch = (keep * d_mid).astype(BF)
        s.dtb[rows, :] = d_branch
        work[...] = mm_nt(d_branch, s.tout[...]).astype(BF)

        def pair(index, carry):
            at, after, last = slab_at(index), slab_at(index, width), slab_at(index, 2 * width)
            grad_q, grad_k, grad_v = attend_slab_back(
                tproj[rows, at], tproj[rows, after], tproj[rows, last], work[:, at], same
            )
            dtp[rows, at] = grad_q.astype(BF)
            dtp[rows, after] = grad_k.astype(BF)
            dtp[rows, last] = grad_v.astype(BF)
            return carry

        lax.fori_loop(0, width // SLAB, pair, 0)
        normed, inv_std = normalize(piece_rows(s.firsts, k).astype(F32))
        d_first = d_mid + norm_back(mm_nt(dtp[rows, :], s.tqkv[...]), normed, inv_std)
        d_first = d_first.astype(BF)
        for j in range(groups):
            buf = s.dfirsts if j == 0 else s.firsts
            buf[j, :, k] = d_first[j * share : (j + 1) * share].reshape(
                buf.shape[1:2] + buf.shape[3:]
            )

    def first_copy(j, k):
        return send(
            s.firsts.at[j, :, k], s.dfirsts.at[j, :, k],
            s.first_sems.at[0, j, k], s.first_sems.at[1, j, k], j,
        )

    temporal_chunk(0)
    for j in others:
        first_copy(j, 0).start()
    wait_all(sum_loads)
    forward_stage(mlp, 0)
    copy_c.wait()
    cur_c = flat_rows(s.cur_c)
    grads_half(pairs_c, core, cur_c, cur_c)
    for stream in cross:
        stream.copy(0).start()
    temporal_grad_loads = [load(a.tin, s.cin), load(a.tmix, s.cmix)]
    for k in range(1, chunks):
        temporal_chunk(k)
        for j in others:
            first_copy(j, k).start()
    late_loads += [load(a.sproj, s.tproj), load(a.sqkv, s.tqkv)]
    forward_stage(mlp, 1)
    for j in range(groups):
        result_copy(j).start()
    wait_all(temporal_grad_loads)
    pairs_t = [(s.cin, dtp), (s.cmix, s.dtb)]
    grads_half(pairs_t, 1 - core, s.send)
    copy_t = core_copy(s.send, s.cur_t, 1)
    copy_t.start()
    forward_stage(mlp, 2)
    forward_stage(cross, 0)
    copy_t.wait()
    cur_t = flat_rows(s.cur_t)
    grads_half(pairs_t, core, cur_t, cur_t)
    spatial_grad_loads = [load(a.sin, s.cin), load(a.smix, s.cmix)]
    for stream in temporal:
        stream.copy(0).start()

    for j in others:
        for k in range(chunks):
            first_copy(j, k).wait()
    wait_all(late_loads)
    gate = a.mod[:, 2 * width : 3 * width]
    scale = a.mod[:, width : 2 * width]

    def spatial_frame(f):
        rows = slice(f * ROWS, (f + 1) * ROWS)
        d_first = frame_rows(s.dfirsts, f).astype(F32)
        s.mod_sum[2:3, :] += jnp.sum(d_first * s.cq[rows, :].astype(F32), 0, keepdims=True)
        d_branch = (gate * d_first).astype(BF)
        s.dcb[rows, :] = d_branch
        work[...] = mm_nt(d_branch, s.cout[...]).astype(BF)

        def pair(index, carry):
            at, after, last = slab_at(index), slab_at(index, width), slab_at(index, 2 * width)
            grad_q, grad_k, grad_v = attend_slab_back(
                tproj[rows, at], tproj[rows, after], tproj[rows, last], work[:, at], None
            )
            dtp[rows, at] = grad_q.astype(BF)
            dtp[rows, after] = grad_k.astype(BF)
            dtp[rows, last] = grad_v.astype(BF)
            return carry

        lax.fori_loop(0, width // SLAB, pair, 0)

    spatial_frame(0)
    forward_stage(mlp, 3)
    for end in ends[:2]:
        end.swap().start()
    forward_stage(cross, 1)
    forward_stage(temporal, 0)
    for f in range(1, frames):
        spatial_frame(f)
    forward_stage(cross, 2)
    forward_stage(temporal, 1)
    wait_all(spatial_grad_loads)
    pairs_s = [(s.cin, dtp), (s.cmix, s.dcb)]
    grads_half(pairs_s, 1 - core, s.send)
    copy_s = core_copy(s.send, s.cur_s, 2)
    copy_s.start()
    for end in ends[:2]:
        end.store()
    forward_stage(temporal, 2)
    copy_s.wait()
    cur_s = flat_rows(s.cur_s)
    grads_half(pairs_s, core, cur_s, cur_s)
    for stream in spatial:
        stream.copy(0).start()
    forward_stage(cross, 3)
    ends[2].swap().start()

    wait_all(video_loads)
    grad_writes = []
    for f in range(frames):
        rows = slice(f * ROWS, (f + 1) * ROWS)
        video = frame_rows(s.cots, f).astype(F32)
        d_first = frame_rows(s.dfirsts, f).astype(F32)
        normed, inv_std = normalize(video)
        d_in = mm_nt(dtp[rows, :], s.tqkv[...])
        s.mod_sum[0:1, :] += jnp.sum(d_in, 0, keepdims=True)
        s.mod_sum[1:2, :] += jnp.sum(d_in * normed, 0, keepdims=True)
        grad = d_first + norm_back(d_in * (1.0 + scale), normed, inv_std)
        for j in range(groups):
            slot = jnp.bitwise_xor(place, j)
            at = pl.ds(pl.multiple_of(f * ROWS + slot * share, share), share)
            s.third[at, :] = grad[j * share : (j + 1) * share]
        grad_writes.append(load(s.third.at[rows, :], o.video_grad.at[f]))

    s.mod_sum[5:6, :] = a.dgate_two[...]
    mod_all = s.mod_all

    def mod_copy(b):
        sems = s.mod_sems.at[0, b], s.mod_sems.at[1, b]
        if b < wide_bits:
            return send(s.mod_sum, s.mod_in.at[b], *sems, 1 << b)
        size = 1 << (b - wide_bits)
        span = mod_all.at[pl.ds(lax.div(narrow_at, size) * size, size)]
        return send(span, span, *sems, 1 << b)

    def mod_step(b):
        mod_copy(b).wait()
        if b < wide_bits:
            s.mod_sum[...] = s.mod_sum[...] + s.mod_in[b]
        if b == wide_bits - 1:
            mod_all[narrow_at] = s.mod_sum[...]
            mod_all[narrow_at, 6:7, :] = a.silu[...]
        if b < bits:
            mod_copy(b + 1).start()

    mod_copy(0).start()
    ends[2].store()
    forward_stage(temporal, 3)
    ends[3].swap().start()
    mod_step(0)
    forward_stage(spatial, 0)
    mod_step(1)
    ends[3].store()
    mod_step(2)
    forward_stage(spatial, 1)
    mod_step(3)
    forward_stage(spatial, 2)
    for b in range(4, bits + 1):
        mod_step(b)
    mine = o.ada.shape[0] // (6 * width // 128)
    me = narrow_at * lax.axis_size("wide") + place
    row = lax.broadcasted_iota(jnp.int32, (mine, width), 0)
    col = lax.broadcasted_iota(jnp.int32, (mine, width), 1)
    picks = (col == me * mine + row).astype(F32).astype(BF)
    silu_mine = mm_nt(picks, mod_all[:, 6, :].astype(BF))
    pitch = 6 * width // 128
    for part in range(6):
        rows = 0.0
        for c in range(mod_all.shape[0]):
            rows = rows + silu_mine[:, c : c + 1] * mod_all[c, part : part + 1, :]
        store_flat(s.flat_ada, rows, part * width // 128, pitch)
    ada_write = load(s.flat_ada, o.ada)
    forward_stage(spatial, 3)
    ends[4].swap().start()
    for j in range(groups):
        result_copy(j).wait()
    wait_all(grad_writes)
    for end in ends[:4]:
        end.wait()
    ends[4].store()
    ada_write.wait()
    ends[4].wait()


def copy_out(ins, outs, sems):
    copies = [
        pltpu.make_async_copy(src, dst, sems.at[k])
        for k, (src, dst) in enumerate(zip(jax.tree.leaves(ins), jax.tree.leaves(outs)))
    ]
    for copy in copies:
        copy.start()
    for copy in copies:
        copy.wait()


def weight_grads(core_ref, *refs, count):
    pairs, outs = refs[: 2 * count], refs[2 * count :]
    core = core_ref[0]
    for sign, out in enumerate(outs):
        side = 1 - core if sign == 0 else core
        start = 0
        for k in range(count):
            left, right = pairs[2 * k], pairs[2 * k + 1]
            part = right.shape[1] // 2
            cols = pl.ds(pl.multiple_of(side * part, 128), part)
            out[:, start : start + part] = mm_tn(left[...], right[:, cols]).astype(BF)
            start += part


def weight_grads_call(core, pairs):
    depth = pairs[0][0].shape[1]
    total = sum(right.shape[1] for _, right in pairs)
    tile = 256
    specs = []
    for left, right in pairs:
        specs.append(pl.BlockSpec((left.shape[0], tile), lambda m, _: (0, m)))
        specs.append(fixed(right.shape))
    shape = jax.ShapeDtypeStruct((depth, total // 2), BF)
    flops = sum(2 * left.shape[0] * depth * right.shape[1] for left, right in pairs)
    return pl.pallas_call(
        functools.partial(weight_grads, count=len(pairs)),
        grid_spec=pltpu.PrefetchScalarGridSpec(
            num_scalar_prefetch=1,
            grid=(depth // tile,),
            in_specs=specs,
            out_specs=[pl.BlockSpec((tile, total // 2), lambda m, _: (m, 0))] * 2,
        ),
        out_shape=[shape, shape],
        compiler_params=params(),
        cost_estimate=cost(flops, 8e6),
        name="weight_grads",
    )(core, *[a for pair in pairs for a in pair])


def shards(
    video,
    text_states,
    text_length,
    timestep,
    motion_free,
    ada_weight,
    spatial_qkv_weight,
    spatial_out_weight,
    temporal_qkv_weight,
    temporal_out_weight,
    cross_query_weight,
    cross_kv_weight,
    cross_out_weight,
    mlp_in_weight,
    mlp_out_weight,
    cotangent,
    *,
    mesh_shape,
):
    clips, frames, patches, width = video.shape
    if clips != 1 or patches != ROWS:
        raise ValueError("unsupported shard")
    wide, narrow = mesh_shape["wide"], mesh_shape["narrow"]
    devices = wide * narrow
    groups = wide
    here = patches // groups
    tokens = frames * patches
    chunks = tokens // ROWS
    per_chunk = here // chunks
    hidden = mlp_in_weight.shape[1]
    text_rows = text_states.shape[1]
    text_pad = -(-text_rows // 128) * 128

    wide_at = lax.axis_index("wide")
    narrow_at = lax.axis_index("narrow")
    index = narrow_at * wide + wide_at
    core = jnp.bitwise_and(wide_at, 1)
    place = wide_at.reshape(1).astype(jnp.int32)
    core_arr = core.reshape(1).astype(jnp.int32)
    wide_bits = wide.bit_length() - 1
    bits = devices.bit_length() - 1

    cot_view = cotangent.reshape(frames, groups, here, width)

    silu_time = silu_of(time_features(timestep.astype(F32), width)).astype(BF)
    mod = mm(silu_time, ada_weight)
    text_flat = text_states.reshape(text_rows, width)
    text_flat = jnp.pad(text_flat, ((0, text_pad - text_rows), (0, 0)))
    text_proj = mm(text_flat, cross_kv_weight).astype(BF)

    video_view = video.reshape(frames, groups, here, width)

    def own_patches(j):
        return pl.BlockSpec(
            (1, 1, here, width),
            lambda f, *_: (f, jnp.bitwise_xor(lax.axis_index("wide"), j), 0, 0),
        )

    def frame_piece():
        return pl.BlockSpec((1, chunks, per_chunk, width), lambda f, *_: (f, 0, 0, 0))

    def chunk_piece():
        return pl.BlockSpec((frames, 1, per_chunk, width), lambda k, *_: (0, k, 0, 0))

    def row_block(cols):
        return pl.BlockSpec((ROWS, cols), lambda f, *_: (f, 0))

    piece_shape = jax.ShapeDtypeStruct((frames, chunks, per_chunk, width), BF)

    def rows_of(cols, dtype=BF):
        return jax.ShapeDtypeStruct((tokens, cols), dtype)

    mod_spec = fixed(mod.shape)
    anywhere = pl.BlockSpec(memory_space=pl.ANY)
    own_piece = jax.ShapeDtypeStruct((frames, here, width), BF)
    outs = pl.pallas_call(
        functools.partial(spatial_forward, groups=groups, width=width, frames=frames),
        grid_spec=pltpu.PrefetchScalarGridSpec(
            num_scalar_prefetch=0,
            grid=(frames,),
            in_specs=[own_patches(j) for j in range(groups)]
            + [own_patches(0), anywhere]
            + [mod_spec, fixed(spatial_qkv_weight.shape), fixed(spatial_out_weight.shape)],
            out_specs=[row_block(width), row_block(3 * width), row_block(width), row_block(width)]
            + ([pl.BlockSpec((1, here, width), lambda f, *_: (f, 0, 0))] + [anywhere] * (groups - 1)) * 2,
            scratch_shapes=[
                pltpu.VMEM((groups - 1, frames, here, width), BF),
                pltpu.SemaphoreType.DMA((2, groups - 1)),
                pltpu.SemaphoreType.DMA((2, groups - 1, frames)),
            ],
        ),
        out_shape=[rows_of(width), rows_of(3 * width), rows_of(width), rows_of(width)]
        + [own_piece] * (2 * groups),
        compiler_params=params(collective_id=0, has_side_effects=True),
        cost_estimate=cost(8 * tokens * width * width, 10e6, tokens * patches * 12),
        name="spatial_forward",
    )(*[video_view] * groups, cot_view, cot_view, mod, spatial_qkv_weight, spatial_out_weight)
    spatial_in, spatial_proj, spatial_mix, spatial_branch = outs[:4]
    firsts = [p.reshape(piece_shape.shape) for p in outs[4 : 4 + groups]]
    cots = [p.reshape(piece_shape.shape) for p in outs[4 + groups :]]

    def two_scalars(grid, in_specs, out_specs, scratch=()):
        return pltpu.PrefetchScalarGridSpec(
            num_scalar_prefetch=2,
            grid=grid,
            in_specs=in_specs,
            out_specs=out_specs,
            scratch_shapes=scratch,
        )

    outs = pl.pallas_call(
        functools.partial(middle_forward, groups=groups, width=width, per_chunk=per_chunk),
        grid_spec=two_scalars(
            (chunks,),
            [chunk_piece() for _ in range(groups)]
            + [
                mod_spec,
                fixed(temporal_qkv_weight.shape),
                fixed(temporal_out_weight.shape),
                fixed(cross_query_weight.shape),
                fixed(text_proj.shape),
                fixed(cross_out_weight.shape),
            ],
            [
                row_block(width),
                row_block(3 * width),
                row_block(width),
                row_block(width),
                row_block(width),
                row_block(width),
                row_block(width),
                row_block(width),
                row_block(width),
            ],
        ),
        out_shape=[
            rows_of(width),
            rows_of(3 * width),
            rows_of(width),
            rows_of(width),
            rows_of(width),
            rows_of(width),
            rows_of(width),
            rows_of(width, F32),
            rows_of(width, F32),
        ],
        compiler_params=params(),
        cost_estimate=cost(12 * tokens * width * width, 20e6, tokens * ROWS * 18),
        name="middle_forward",
    )(
        text_length,
        motion_free,
        *firsts,
        mod,
        temporal_qkv_weight,
        temporal_out_weight,
        cross_query_weight,
        text_proj,
        cross_out_weight,
    )
    temporal_in, temporal_proj, temporal_mix, cross_in, cross_q, cross_mix, mlp_in, mid, third = outs

    steps = 4
    wide_h = hidden // steps

    def hidden_at(step):
        half = steps // 2
        side_bit = jnp.bitwise_and(lax.axis_index("wide"), 1)
        side = jnp.where(step < half, 1 - side_bit, side_bit)
        return side * half + lax.rem(step, half)

    whole_piece = fixed((frames, chunks, per_chunk, width))
    outs = pl.pallas_call(
        functools.partial(mlp_both, groups=groups, width=width, steps=steps),
        grid_spec=pltpu.PrefetchScalarGridSpec(
            num_scalar_prefetch=0,
            grid=(steps,),
            in_specs=[whole_piece] * groups
            + [
                fixed(mlp_in.shape),
                fixed(third.shape),
                mod_spec,
                pl.BlockSpec((width, wide_h), lambda s: (0, hidden_at(s))),
                pl.BlockSpec((wide_h, width), lambda s: (hidden_at(s), 0)),
            ],
            out_specs=[
                pl.BlockSpec((width, wide_h), lambda s: (0, jnp.maximum(s - steps // 2, 0))),
                fixed((hidden, width // 2)),
                fixed((tokens, width)),
                fixed((1, width)),
            ]
            + [whole_piece] * groups,
            scratch_shapes=[
                pltpu.VMEM((width, tokens), BF),
                pltpu.VMEM((tokens, width), BF),
                pltpu.VMEM((tokens, width), F32),
                pltpu.VMEM((steps // 2, width, wide_h), BF),
                pltpu.VMEM((steps // 2, width, wide_h), BF),
                pltpu.VMEM((steps, wide_h, width // 2), BF),
                pltpu.VMEM((steps, wide_h, width // 2), BF),
                pltpu.VMEM((steps, wide_h, width // 2), BF),
                pltpu.SemaphoreType.DMA((2, steps // 2)),
                pltpu.SemaphoreType.DMA((2, steps)),
            ],
        ),
        out_shape=[
            jax.ShapeDtypeStruct((width, hidden // 2), BF),
            jax.ShapeDtypeStruct((hidden, width // 2), BF),
            rows_of(width, F32),
            jax.ShapeDtypeStruct((1, width), F32),
        ]
        + [piece_shape] * groups,
        compiler_params=params(collective_id=1, has_side_effects=True),
        cost_estimate=cost(12 * tokens * width * hidden, 25e6, tokens * hidden),
        name="mlp_both",
    )(*cots, mlp_in, third, mod, mlp_in_weight, mlp_out_weight)
    sum_in, sum_out, d_mlp_in, d_gate_two = outs[:4]
    if (2 * width // devices) % 16 == 0 and width % 768 == 0 and hidden % 768 == 0:
        chip = (2,) * (bits - 1)
        nb = bits - 1
        rows_in, rows_out = 2 * width // devices, 2 * hidden // devices
        cols_in, cols_out = hidden // 2, width // 2
        vm, sems = pltpu.VMEM, pltpu.SemaphoreType.DMA
        act = lambda cols, dtype=BF: vm((tokens, cols), dtype)
        group = vm(chip + (rows_in, cols_in), BF)
        pieces = vm((groups, frames, chunks, per_chunk, width), BF)
        ins = dict(
            cots=tuple(cots),
            dmlp=d_mlp_in,
            third=third,
            mid=mid,
            mod=mod,
            silu=silu_time.astype(F32),
            dgate_two=d_gate_two,
            cq=cross_q,
            text=text_proj,
            tproj=temporal_proj,
            cout=cross_out_weight,
            cwq=cross_query_weight,
            tout=temporal_out_weight,
            tqkv=temporal_qkv_weight,
            firsts=tuple(firsts),
            cin=cross_in,
            cmix=cross_mix,
            words=text_flat,
            tin=temporal_in,
            tmix=temporal_mix,
            sum_out=sum_out.reshape(chip + (rows_out, cols_out)),
            sum_in=sum_in.reshape(chip + (rows_in, cols_in)),
            results=tuple(p.reshape(frames, here, width) for p in outs[4 : 4 + groups]),
            video=video.reshape(frames, groups, chunks, per_chunk, width),
            sbranch=spatial_branch,
            sout=spatial_out_weight,
            sproj=spatial_proj,
            sin=spatial_in,
            smix=spatial_mix,
            sqkv=spatial_qkv_weight,
        )
        in_specs = jax.tree.map(lambda _: anywhere, ins)
        for name in ("mod", "silu", "dgate_two"):
            in_specs[name] = fixed(ins[name].shape)

        def flat_shapes(elements):
            return tuple(jax.ShapeDtypeStruct((n // devices // 128, 128), F32) for n in elements)

        square = width * width
        out_shape = dict(
            result=jax.ShapeDtypeStruct((frames, groups, here, width), BF),
            video_grad=jax.ShapeDtypeStruct((frames, patches, width), F32),
            ada=flat_shapes([6 * square])[0],
            spatial=flat_shapes([3 * square, square]),
            temporal=flat_shapes([3 * square, square]),
            cross=flat_shapes([square, 2 * square, square]),
            mlp_in=flat_shapes([width * hidden]),
            mlp_out=flat_shapes([width * hidden]),
        )
        in_hbm = pl.BlockSpec(memory_space=pltpu.HBM)
        out_specs = jax.tree.map(lambda _: in_hbm, out_shape)
        flats = jax.tree.map(lambda leaf: vm(leaf.shape, F32), out_shape)

        def streams_in():
            return stream_scratch(rows_in, cols_in, nb, 3)

        def fin(rows, cols, count):
            return vm((2, rows // 2, cols), F32), vm((rows // 2, cols), F32), sems((2 + count,))

        fin_out, fin_out_in, end_out = fin(rows_out, cols_out, 1)
        fin_in, fin_in_in, end_in = fin(rows_in, cols_in, 1)
        fin_c, fin_c_in, end_c = fin(rows_in, cols_in, 3)
        fin_t, fin_t_in, end_t = fin(rows_in, cols_in, 2)
        scratch = dict(
            local=sems((64,)),
            cots=pieces,
            firsts=pieces,
            dfirsts=pieces,
            dmlp=act(width, F32),
            third=act(width, F32),
            mid=act(width, F32),
            cq=act(width),
            text=vm(text_proj.shape, BF),
            tproj=act(3 * width),
            cout=vm((width, width), BF),
            cwq=vm((width, width), BF),
            tout=vm((width, width), BF),
            tqkv=vm((width, 3 * width), BF),
            cin=act(width),
            cmix=act(width),
            words=vm(text_flat.shape, BF),
            st_out=stream_scratch(rows_out, cols_out, nb, 3),
            st_in=streams_in(),
            st_c=streams_in(),
            st_t=streams_in(),
            st_s=streams_in(),
            cur_out=vm(chip + (rows_out, cols_out), BF),
            cur_in=group,
            cur_c=group,
            cur_t=group,
            cur_s=group,
            send=vm((width, cols_in), BF),
            fin_out=fin_out,
            fin_in=fin_in,
            fin_c=fin_c,
            fin_t=fin_t,
            fin_s=fin_t,
            fin_out_in=fin_out_in,
            fin_in_in=fin_in_in,
            fin_c_in=fin_c_in,
            fin_t_in=fin_t_in,
            fin_s_in=fin_t_in,
            end_out=end_out,
            end_in=end_in,
            end_c=end_c,
            end_t=end_t,
            end_s=end_t,
            flat_out=flats["mlp_out"],
            flat_in=flats["mlp_in"],
            flat_c=flats["cross"],
            flat_t=flats["temporal"],
            flat_s=flats["spatial"],
            flat_ada=flats["ada"],
            core_sems=sems((2, 3)),
            result_sems=sems((2, groups)),
            first_sems=sems((2, groups, chunks)),
            mod_sems=sems((2, bits)),
            text_acc=vm(text_proj.shape, F32),
            work=vm((ROWS, width), BF),
            dcb=act(width),
            dcq=act(width),
            dtext=vm(text_proj.shape, BF),
            dtb=act(width),
            dtp=act(3 * width),
            mod_sum=vm((8, width), F32),
            mod_in=vm((wide_bits, 8, width), F32),
            mod_all=vm((narrow, 8, width), F32),
        )
        back = pl.pallas_call(
            with_scratch(backward, scratch),
            grid_spec=pltpu.PrefetchScalarGridSpec(
                num_scalar_prefetch=2,
                grid=(1,),
                in_specs=[in_specs],
                out_specs=out_specs,
                scratch_shapes=jax.tree.leaves(scratch),
            ),
            out_shape=out_shape,
            compiler_params=params(collective_id=2, has_side_effects=True),
            cost_estimate=cost(74 * tokens * width * width, 70e6, tokens * ROWS * 30),
            name="backward",
        )(text_length, motion_free, ins)
        back = pl.pallas_call(
            copy_out,
            grid=(),
            in_specs=[jax.tree.map(lambda _: anywhere, out_shape)],
            out_specs=out_specs,
            out_shape=out_shape,
            scratch_shapes=[sems((len(jax.tree.leaves(out_shape)),))],
            compiler_params=params(),
            cost_estimate=cost(0, 9e6),
            name="copy_out",
        )(back)
        grads = (
            [back["ada"]]
            + list(back["spatial"])
            + list(back["temporal"])
            + list(back["cross"])
            + list(back["mlp_in"])
            + list(back["mlp_out"])
        )
        return (
            back["result"].reshape(video.shape),
            back["video_grad"].reshape(video.shape),
        ) + tuple(g.reshape(-1) for g in grads)

    def flip(value, mask):
        return lax.ppermute(value, AXES, [(i, i ^ mask) for i in range(devices)])

    def bit_of(b):
        return jnp.bitwise_and(lax.shift_right_logical(index, b), 1)

    def gather_narrow(row):
        for b in range(wide_bits, bits):
            other = flip(row, 1 << b)
            mine = bit_of(b) == 0
            row = jnp.concatenate(
                [jnp.where(mine, row, other), jnp.where(mine, other, row)], 0
            )
        return row

    times = gather_narrow(timestep.astype(F32).reshape(1, 1))
    silu_all = silu_of(time_features(times[:, 0], width)).astype(BF).astype(F32)
    mine = width // devices
    silu_rows = lax.dynamic_slice_in_dim(silu_all, index * mine, mine, 1)

    results = [outs[4]] + [flip(outs[4 + j], j) for j in range(1, groups)]

    outs = pl.pallas_call(
        functools.partial(middle_backward, groups=groups, width=width, per_chunk=per_chunk),
        grid_spec=two_scalars(
            (chunks,),
            [chunk_piece() for _ in range(groups)]
            + [
                row_block(width),
                row_block(width),
                row_block(width),
                mod_spec,
                row_block(width),
                row_block(3 * width),
                row_block(width),
                fixed(text_proj.shape),
                fixed(cross_out_weight.shape),
                fixed(cross_query_weight.shape),
                fixed(temporal_out_weight.shape),
                fixed(temporal_qkv_weight.shape),
            ]
            + [chunk_piece() for _ in range(groups)],
            [
                row_block(width),
                row_block(width),
                fixed((text_pad, 2 * width)),
                row_block(width),
                row_block(3 * width),
                fixed((2, width)),
            ]
            + [chunk_piece() for _ in range(groups)],
            [pltpu.VMEM((text_pad, 2 * width), F32), pltpu.VMEM((ROWS, width), BF)],
        ),
        out_shape=[
            rows_of(width),
            rows_of(width),
            jax.ShapeDtypeStruct((text_pad, 2 * width), BF),
            rows_of(width),
            rows_of(3 * width),
            jax.ShapeDtypeStruct((2, width), F32),
        ]
        + [piece_shape] * groups,
        compiler_params=params(),
        cost_estimate=cost(20 * tokens * width * width, 25e6, tokens * ROWS * 18),
        name="middle_backward",
    )(
        text_length,
        motion_free,
        *cots,
        d_mlp_in,
        third,
        mid,
        mod,
        temporal_in,
        temporal_proj,
        cross_q,
        text_proj,
        cross_out_weight,
        cross_query_weight,
        temporal_out_weight,
        temporal_qkv_weight,
        *firsts,
    )
    d_cross_branch, d_cross_q, d_text, d_temporal_branch, d_temporal_proj, d_mod_two = outs[:6]
    d_firsts = [outs[6]] + [flip(outs[6 + j], j) for j in range(1, groups)]

    cross_send, cross_keep = weight_grads_call(
        core_arr,
        [(cross_in, d_cross_q), (text_flat, d_text), (cross_mix, d_cross_branch)],
    )
    temporal_send, temporal_keep = weight_grads_call(
        core_arr,
        [(temporal_in, d_temporal_proj), (temporal_mix, d_temporal_branch)],
    )

    d_spatial_branch, d_spatial_proj, d_gate_one = pl.pallas_call(
        functools.partial(spatial_backward, groups=groups, width=width),
        grid=(frames,),
        in_specs=[frame_piece() for _ in range(groups)]
        + [mod_spec, row_block(width), row_block(3 * width), fixed(spatial_out_weight.shape)],
        out_specs=[row_block(width), row_block(3 * width), fixed((1, width))],
        out_shape=[rows_of(width), rows_of(3 * width), jax.ShapeDtypeStruct((1, width), F32)],
        scratch_shapes=[pltpu.VMEM((ROWS, width), BF)],
        compiler_params=params(),
        cost_estimate=cost(8 * tokens * width * width, 10e6, tokens * patches * 12),
        name="spatial_backward",
    )(*d_firsts, mod, spatial_branch, spatial_proj, spatial_out_weight)

    spatial_send, spatial_keep = weight_grads_call(
        core_arr,
        [(spatial_in, d_spatial_proj), (spatial_mix, d_spatial_branch)],
    )

    out_block = pl.BlockSpec((1, groups, here, width), lambda f, *_: (f, 0, 0, 0))
    video_grad, result, d_mod_one = pl.pallas_call(
        functools.partial(video_backward, groups=groups, width=width),
        grid_spec=pltpu.PrefetchScalarGridSpec(
            num_scalar_prefetch=1,
            grid=(frames,),
            in_specs=[own_patches(j) for j in range(groups)]
            + [frame_piece() for _ in range(2 * groups)]
            + [mod_spec, row_block(3 * width), fixed(spatial_qkv_weight.shape)],
            out_specs=[out_block, out_block, fixed((2, width))],
        ),
        out_shape=[
            jax.ShapeDtypeStruct((frames, groups, here, width), F32),
            jax.ShapeDtypeStruct((frames, groups, here, width), BF),
            jax.ShapeDtypeStruct((2, width), F32),
        ],
        compiler_params=params(),
        cost_estimate=cost(6 * tokens * width * width, 12e6),
        name="video_backward",
    )(place, *[video_view] * groups, *d_firsts, *results, mod, d_spatial_proj, spatial_qkv_weight)
    video_grad = video_grad.reshape(video.shape)
    result = result.reshape(video.shape)

    d_mod = jnp.concatenate([d_mod_one, d_gate_one, d_mod_two, d_gate_two], 0)
    for b in range(wide_bits):
        d_mod = d_mod + flip(d_mod, 1 << b)
    d_mod_all = gather_narrow(d_mod[None])
    ada_rows = jnp.sum(silu_rows[:, :, None, None] * d_mod_all[:, None, :, :], 0)
    ada_grad = ada_rows.reshape(-1)

    chip_bits = list(range(1, bits))
    first_x = [wide_bits, 1]
    rest = [b for b in chip_bits if b not in first_x]
    order_a = first_x + rest
    order_b = first_x[::-1] + rest

    def join(send, keep):
        return keep.astype(F32) + flip(send, 1).astype(F32)

    def reduce_scatter(cur, order):
        cols = cur.shape[1]
        axes = sorted(chip_bits, reverse=True)
        for b in order:
            cur = cur.astype(BF)
            at = axes.index(b)
            view = cur.reshape(1 << at, 2, 1 << (len(axes) - at - 1), -1, cols)
            out = lax.dynamic_index_in_dim(view, 1 - bit_of(b), 1, keepdims=False)
            own = lax.dynamic_index_in_dim(view, bit_of(b), 1, keepdims=False)
            cur = own.astype(F32) + flip(out, 1 << b).astype(F32)
            axes.remove(b)
        cur = cur.reshape(2, -1, cols)
        own = lax.dynamic_index_in_dim(cur, core, 0, keepdims=False)
        other = flip(lax.dynamic_index_in_dim(cur, 1 - core, 0, keepdims=False), 1)
        low = jnp.where(core == 0, own, other)
        high = jnp.where(core == 0, other, own)
        return low, high

    def unpack(pair, widths):
        low, high = pair
        start, out = 0, []
        for w in widths:
            half = w // 2
            cols = slice(start, start + half)
            out.append(jnp.concatenate([low[:, cols], high[:, cols]], 1).reshape(-1))
            start += half
        return out

    mlp_out_grad = unpack(reduce_scatter(sum_out, order_a), [width])[0]
    mlp_in_grad = unpack(reduce_scatter(sum_in, order_b), [hidden])[0]
    cross_query_grad, cross_kv_grad, cross_out_grad = unpack(
        reduce_scatter(join(cross_send, cross_keep), order_a), [width, 2 * width, width]
    )
    temporal_qkv_grad, temporal_out_grad = unpack(
        reduce_scatter(join(temporal_send, temporal_keep), order_b), [3 * width, width]
    )
    spatial_qkv_grad, spatial_out_grad = unpack(
        reduce_scatter(join(spatial_send, spatial_keep), order_a), [3 * width, width]
    )
    return (
        result,
        video_grad,
        ada_grad,
        spatial_qkv_grad,
        spatial_out_grad,
        temporal_qkv_grad,
        temporal_out_grad,
        cross_query_grad,
        cross_kv_grad,
        cross_out_grad,
        mlp_in_grad,
        mlp_out_grad,
    )


def solution(mesh):
    tokens_spec = P("narrow", "wide", None, None)
    in_specs = (
        (tokens_spec, P("narrow", None, None), P("narrow"), P("narrow"), P("narrow"))
        + (P(),) * 10
        + (tokens_spec,)
    )
    out_specs = (tokens_spec, tokens_spec) + (P(AXES),) * 10
    return jax.shard_map(
        functools.partial(shards, mesh_shape=dict(mesh.shape)),
        mesh=mesh,
        in_specs=in_specs,
        out_specs=out_specs,
        check_vma=False,
    )
```

```python
import functools
import itertools
import math
import types

import jax
import jax.numpy as jnp
from jax import lax
from jax.experimental import pallas as pl
from jax.experimental.pallas import tpu as pltpu
from jax.sharding import PartitionSpec as P

HEAD_DIM = 64
SLAB = 2 * HEAD_DIM
SCALE = HEAD_DIM ** (-0.5)
EPSILON = 1e-06
NEG_LARGE = -1e30
BF = jnp.bfloat16
F32 = jnp.float32
AXES = ("narrow", "wide")
ROWS = 256
MESH = pl.DeviceIdType.MESH
VMEM_LIMIT = 60 * 1024 * 1024
Names = types.SimpleNamespace


def time_features(time_value, width):
    half = width // 2
    freqs = jnp.exp(-math.log(10000.0) * jnp.arange(half, dtype=F32) / half)
    angles = time_value[..., None] * freqs
    return jnp.concatenate([jnp.cos(angles), jnp.sin(angles)], axis=-1)


def silu_of(values):
    return values / (1.0 + jnp.exp(-values))


def normalize(values):
    mean = jnp.mean(values, -1, keepdims=True)
    centred = values - mean
    variance = jnp.mean(centred * centred, -1, keepdims=True)
    inv_std = lax.rsqrt(variance + EPSILON)
    return centred * inv_std, inv_std


def norm_back(grad_norm, normed, inv_std):
    return inv_std * (
        grad_norm
        - jnp.mean(grad_norm, -1, keepdims=True)
        - normed * jnp.mean(grad_norm * normed, -1, keepdims=True)
    )


def mm(left, right):
    return jnp.dot(left, right, preferred_element_type=F32)


def mm_nt(left, right):
    return lax.dot_general(left, right, (((1,), (1,)), ((), ())), preferred_element_type=F32)


def mm_tn(left, right):
    return lax.dot_general(left, right, (((0,), (0,)), ((), ())), preferred_element_type=F32)


def head_masks():
    lane = lax.broadcasted_iota(jnp.int32, (1, SLAB), 1)
    low = (lane < HEAD_DIM).astype(F32)
    return low.astype(BF), (1.0 - low).astype(BF)


def softmax_rows(scores):
    peak = jnp.max(scores, -1, keepdims=True)
    expd = jnp.exp(scores - peak)
    return expd * (1.0 / jnp.sum(expd, -1, keepdims=True))


def attend_slab(query, key, value, bias):
    mixed = None
    for mask in head_masks():
        scores = mm_nt(query * mask, key) * SCALE
        if bias is not None:
            scores = jnp.where(bias, scores, NEG_LARGE)
        probs = softmax_rows(scores).astype(BF)
        part = mm(probs, value * mask)
        mixed = part if mixed is None else mixed + part
    return mixed


def attend_slab_back(query, key, value, grad, bias):
    grad_query = grad_key = grad_value = 0.0
    for mask in head_masks():
        query_part = query * mask
        grad_part = grad * mask
        scores = mm_nt(query_part, key) * SCALE
        if bias is not None:
            scores = jnp.where(bias, scores, NEG_LARGE)
        probs = softmax_rows(scores)
        grad_probs = mm_nt(grad_part, value)
        inner = jnp.sum(grad_probs * probs, -1, keepdims=True)
        grad_scores = (probs * (grad_probs - inner)).astype(BF)
        grad_value = grad_value + mm_tn(probs.astype(BF), grad_part)
        grad_query = grad_query + mm(grad_scores, key * mask)
        grad_key = grad_key + mm_tn(grad_scores, query_part)
    return grad_query * SCALE, grad_key * SCALE, grad_value


def slab_at(index, offset=0):
    return pl.ds(pl.multiple_of(index * SLAB + offset, SLAB), SLAB)


def frame_mask(rows, per_chunk):
    row = lax.broadcasted_iota(jnp.int32, (rows, rows), 0)
    col = lax.broadcasted_iota(jnp.int32, (rows, rows), 1)
    return lax.rem(row, per_chunk) == lax.rem(col, per_chunk)


def part_of(mod, index, width):
    return mod[:, index * width : (index + 1) * width]


def cost(flops, bytes_accessed, transcendentals=0):
    return pl.CostEstimate(
        flops=int(flops), bytes_accessed=int(bytes_accessed), transcendentals=int(transcendentals)
    )


def params(**extra):
    return pltpu.CompilerParams(vmem_limit_bytes=VMEM_LIMIT, **extra)


def fixed(shape):
    rank = len(shape)
    return pl.BlockSpec(shape, lambda *_: (0,) * rank, pipeline_mode=pl.Buffered(1))


def partner(mask):
    wide = lax.axis_size("wide")
    me = lax.axis_index("narrow") * wide + lax.axis_index("wide")
    other = jnp.bitwise_xor(me, mask)
    return (lax.div(other, wide), lax.rem(other, wide))


def greet(masks):
    barrier = pltpu.get_barrier_semaphore()
    for mask in masks:
        pl.semaphore_signal(barrier, inc=1, device_id=partner(mask), device_id_type=MESH)
    pl.semaphore_wait(barrier, len(masks))


def send(src, dst, send_sem, recv_sem, mask):
    return pltpu.make_async_remote_copy(
        src_ref=src,
        dst_ref=dst,
        send_sem=send_sem,
        recv_sem=recv_sem,
        device_id=partner(mask),
        device_id_type=MESH,
    )


def spatial_forward(*refs, groups, width, frames):
    videos, refs = refs[:groups], refs[groups:]
    cot_ins, refs = refs[:groups], refs[groups:]
    mod_ref, qkv_ref, out_ref, refs = refs[0], refs[1], refs[2], refs[3:]
    in_ref, proj_ref, mix_ref, branch_ref, refs = refs[0], refs[1], refs[2], refs[3], refs[4:]
    first_own, firsts, refs = refs[0], refs[1:groups], refs[groups:]
    cot_out, cots, refs = refs[0], refs[1:groups], refs[groups:]
    out_buf, cot_buf, cot_sems, first_sems = refs
    frame = pl.program_id(0)
    place = lax.axis_index("wide")
    others = range(1, groups)

    def cot_copy(j, f):
        return send(
            cot_buf.at[j - 1, f],
            cots[j - 1].at[f],
            cot_sems.at[0, j - 1, f],
            cot_sems.at[1, j - 1, f],
            j,
        )

    def first_copy(j, f):
        return send(
            out_buf.at[j - 1, f],
            firsts[j - 1].at[f],
            first_sems.at[0, j - 1, f],
            first_sems.at[1, j - 1, f],
            j,
        )

    @pl.when(frame == 0)
    def _():
        greet(list(others))

    cot_out[...] = cot_ins[0][...].reshape(cot_out.shape)
    for j in others:
        cot_buf[j - 1, frame] = cot_ins[j][...].reshape(cot_buf.shape[2:])
    for j in others:
        cot_copy(j, frame).start()
    mod = mod_ref[...]
    video = jnp.concatenate([v[...].reshape(-1, width) for v in videos], 0).astype(F32)
    normed, _ = normalize(video)
    entry = (normed * (1.0 + part_of(mod, 1, width)) + part_of(mod, 0, width)).astype(BF)
    in_ref[...] = entry
    proj_ref[...] = mm(entry, qkv_ref[...]).astype(BF)

    def pair(index, carry):
        mixed = attend_slab(
            proj_ref[:, slab_at(index)],
            proj_ref[:, slab_at(index, width)],
            proj_ref[:, slab_at(index, 2 * width)],
            None,
        )
        mix_ref[:, slab_at(index)] = mixed.astype(BF)
        return carry

    lax.fori_loop(0, width // SLAB, pair, 0)
    branch = mm(mix_ref[...], out_ref[...])
    first = (video + part_of(mod, 2, width) * branch).astype(BF)
    share = first.shape[0] // groups
    for j in others:
        out_buf[j - 1, frame] = first[j * share : (j + 1) * share]
    first_own[...] = first[:share].reshape(first_own.shape)
    branch_ref[...] = branch.astype(BF)
    for j in others:
        first_copy(j, frame).start()

    @pl.when(frame == frames - 1)
    def _():
        for j in others:
            for f in range(frames):
                cot_copy(j, f).wait()
                first_copy(j, f).wait()


def middle_forward(length_ref, keep_ref, *refs, groups, width, per_chunk):
    pieces, refs = refs[:groups], refs[groups:]
    mod_ref, qkv_ref, tout_ref, cq_ref, text_ref, cout_ref = refs[:6]
    tin_ref, tproj_ref, tmix_ref, cin_ref, cq_out, cmix_ref, mlp_ref, mid_ref, third_ref = refs[6:]
    mod = mod_ref[...]
    first = jnp.concatenate([p[...].reshape(-1, width) for p in pieces], 0).astype(F32)
    rows = first.shape[0]
    normed, _ = normalize(first)
    entry = normed.astype(BF)
    tin_ref[...] = entry
    tproj_ref[...] = mm(entry, qkv_ref[...]).astype(BF)
    same = frame_mask(rows, per_chunk)

    def pair(index, carry):
        mixed = attend_slab(
            tproj_ref[:, slab_at(index)],
            tproj_ref[:, slab_at(index, width)],
            tproj_ref[:, slab_at(index, 2 * width)],
            same,
        )
        tmix_ref[:, slab_at(index)] = mixed.astype(BF)
        return carry

    lax.fori_loop(0, width // SLAB, pair, 0)
    keep = (1 - keep_ref[0]).astype(F32)
    mid = first + keep * mm(tmix_ref[...], tout_ref[...])
    mid_ref[...] = mid
    normed, _ = normalize(mid)
    entry = normed.astype(BF)
    cin_ref[...] = entry
    cq_out[...] = mm(entry, cq_ref[...]).astype(BF)
    keys = text_ref.shape[0]
    valid = lax.broadcasted_iota(jnp.int32, (rows, keys), 1) < length_ref[0]

    def cross_pair(index, carry):
        mixed = attend_slab(
            cq_out[:, slab_at(index)],
            text_ref[:, slab_at(index)],
            text_ref[:, slab_at(index, width)],
            valid,
        )
        cmix_ref[:, slab_at(index)] = mixed.astype(BF)
        return carry

    lax.fori_loop(0, width // SLAB, cross_pair, 0)
    third = mid + mm(cmix_ref[...], cout_ref[...])
    third_ref[...] = third
    normed, _ = normalize(third)
    mlp_ref[...] = (normed * (1.0 + part_of(mod, 4, width)) + part_of(mod, 3, width)).astype(BF)


def mlp_both(*refs, groups, width, steps):
    cots, refs = refs[:groups], refs[groups:]
    mlp_ref, third_ref, mod_ref, win_ref, wout_ref = refs[:5]
    sum_in, sum_out, dmlp_ref, dgate_ref = refs[5:9]
    results, scratch = refs[9 : 9 + groups], refs[9 + groups :]
    mlp_t, dbranch, branch, send_in, recv_in, send_out, keep_out, recv_out, in_sems, out_sems = scratch
    step = pl.program_id(0)
    half = steps // 2
    core = jnp.bitwise_and(lax.axis_index("wide"), 1)
    mod = mod_ref[...]
    gate = part_of(mod, 5, width)
    tokens = mlp_ref.shape[0]
    chunks = tokens // ROWS
    share = ROWS // groups

    def block_at(s):
        side = jnp.where(s < half, 1 - core, core)
        return side * half + lax.rem(s, half)

    def in_copy(s):
        return send(send_in.at[s], recv_in.at[s], in_sems.at[0, s], in_sems.at[1, s], 1)

    def out_copy(s):
        block = block_at(s)
        return send(
            send_out.at[block], recv_out.at[block], out_sems.at[0, block], out_sems.at[1, block], 1
        )

    @pl.when(step == 0)
    def _():
        greet([1])
        mlp_t[...] = mlp_ref[...].T
        for k in range(chunks):
            for j in range(groups):
                rows = pl.ds(k * ROWS + j * share, share)
                cot = cots[j][:, k].reshape(share, width).astype(F32)
                dbranch[rows, :] = (gate * cot).astype(BF)
        branch[...] = jnp.zeros_like(branch)
        dmlp_ref[...] = jnp.zeros_like(dmlp_ref)

    @pl.when(step >= 1)
    def _():
        out_copy(step - 1).start()

    @pl.when(jnp.logical_and(step >= 1, step <= half))
    def _():
        in_copy(step - 1).start()

    pre = mm(mlp_ref[...], win_ref[...])
    d_hidden = mm_nt(dbranch[...], wout_ref[...])
    square = pre * pre
    bend = jnp.tanh(0.7978845608 * pre * (1.0 + 0.044715 * square))
    ramp = 0.5 * (1.0 + bend)
    hidden = (pre * ramp).astype(BF)
    slope = ramp + 0.5 * pre * (1.0 - bend * bend) * (
        0.7978845608 * (1.0 + (3.0 * 0.044715) * square)
    )
    d_pre = (d_hidden * slope).astype(BF)
    hidden_t = hidden.T
    side = width // 2
    block = block_at(step)
    send_out[block] = mm(
        hidden_t, dbranch[:, pl.ds(pl.multiple_of((1 - core) * side, 128), side)]
    ).astype(BF)
    keep_out[block] = mm(
        hidden_t, dbranch[:, pl.ds(pl.multiple_of(core * side, 128), side)]
    ).astype(BF)
    grad_in = mm(mlp_t[...], d_pre)

    @pl.when(step < half)
    def _():
        send_in[step] = grad_in.astype(BF)

    @pl.when(step >= half)
    def _():
        in_copy(step - half).wait_recv()
        sum_in[...] = (grad_in + recv_in[step - half].astype(F32)).astype(BF)

    branch[...] += mm(hidden, wout_ref[...])
    dmlp_ref[...] += mm_nt(d_pre, win_ref[...])

    @pl.when(step == steps - 1)
    def _():
        out_copy(steps - 1).start()
        total = jnp.zeros((1, width), F32)
        for k in range(chunks):
            for j in range(groups):
                rows = pl.ds(k * ROWS + j * share, share)
                cot = cots[j][:, k].reshape(share, width).astype(F32)
                piece = branch[rows, :]
                total = total + jnp.sum(cot * piece, 0, keepdims=True)
                out = (third_ref[rows, :] + gate * piece).astype(BF)
                results[j][:, k] = out.reshape(results[j][:, k].shape)
        dgate_ref[...] = total
        for s in range(half):
            in_copy(s).wait_send()
        deep = send_out.shape[1]
        for s in range(steps):
            out_copy(s).wait_send()
            out_copy((s + half) % steps).wait_recv()
            block = block_at((s + half) % steps)
            rows = pl.ds(pl.multiple_of(block * deep, 16), deep)
            sum_out[rows, :] = (
                keep_out[block].astype(F32) + recv_out[block].astype(F32)
            ).astype(BF)


def middle_backward(length_ref, keep_ref, *refs, groups, width, per_chunk):
    cots, refs = refs[:groups], refs[groups:]
    dmlp_ref, third_ref, mid_ref, mod_ref = refs[:4]
    tin_ref, tproj_ref, cq_in, text_ref = refs[4:8]
    cout_ref, cq_ref, tout_ref, tqkv_ref = refs[8:12]
    first_refs, refs = refs[12 : 12 + groups], refs[12 + groups :]
    dcb_ref, dcq_ref, dtext_ref, dtb_ref, dtp_ref, dmod_ref = refs[:6]
    dfirsts = refs[6 : 6 + groups]
    text_acc, work = refs[6 + groups :]
    chunk = pl.program_id(0)
    mod = mod_ref[...]

    @pl.when(chunk == 0)
    def _():
        text_acc[...] = jnp.zeros_like(text_acc)
        dmod_ref[...] = jnp.zeros_like(dmod_ref)

    cot = jnp.concatenate([p[...].reshape(-1, width) for p in cots], 0).astype(F32)
    rows = cot.shape[0]
    d_mlp = dmlp_ref[...]
    normed, inv_std = normalize(third_ref[...])
    dmod_ref[0:1, :] += jnp.sum(d_mlp, 0, keepdims=True)
    dmod_ref[1:2, :] += jnp.sum(d_mlp * normed, 0, keepdims=True)
    d_third = cot + norm_back(d_mlp * (1.0 + part_of(mod, 4, width)), normed, inv_std)
    d_branch = d_third.astype(BF)
    dcb_ref[...] = d_branch
    work[...] = mm_nt(d_branch, cout_ref[...]).astype(BF)
    keys = text_ref.shape[0]
    valid = lax.broadcasted_iota(jnp.int32, (rows, keys), 1) < length_ref[0]

    def cross_pair(index, carry):
        at, after = slab_at(index), slab_at(index, width)
        grad_q, grad_k, grad_v = attend_slab_back(
            cq_in[:, at], text_ref[:, at], text_ref[:, after], work[:, at], valid
        )
        dcq_ref[:, at] = grad_q.astype(BF)
        text_acc[:, at] += grad_k
        text_acc[:, after] += grad_v
        return carry

    lax.fori_loop(0, width // SLAB, cross_pair, 0)
    dtext_ref[...] = text_acc[...].astype(BF)
    normed, inv_std = normalize(mid_ref[...])
    d_mid = d_third + norm_back(mm_nt(dcq_ref[...], cq_ref[...]), normed, inv_std)
    keep = (1 - keep_ref[0]).astype(F32)
    d_branch = (keep * d_mid).astype(BF)
    dtb_ref[...] = d_branch
    work[...] = mm_nt(d_branch, tout_ref[...]).astype(BF)
    same = frame_mask(rows, per_chunk)

    def pair(index, carry):
        at, after, last = slab_at(index), slab_at(index, width), slab_at(index, 2 * width)
        grad_q, grad_k, grad_v = attend_slab_back(
            tproj_ref[:, at], tproj_ref[:, after], tproj_ref[:, last], work[:, at], same
        )
        dtp_ref[:, at] = grad_q.astype(BF)
        dtp_ref[:, after] = grad_k.astype(BF)
        dtp_ref[:, last] = grad_v.astype(BF)
        return carry

    lax.fori_loop(0, width // SLAB, pair, 0)
    first = jnp.concatenate([p[...].reshape(-1, width) for p in first_refs], 0).astype(F32)
    normed, inv_std = normalize(first)
    d_first = d_mid + norm_back(mm_nt(dtp_ref[...], tqkv_ref[...]), normed, inv_std)
    d_first = d_first.astype(BF)
    share = rows // groups
    for j, ref in enumerate(dfirsts):
        ref[...] = d_first[j * share : (j + 1) * share].reshape(ref.shape)


def spatial_backward(*refs, groups, width):
    dfirsts, refs = refs[:groups], refs[groups:]
    mod_ref, branch_ref, proj_ref, out_ref = refs[:4]
    dsb_ref, dproj_ref, dgate_ref, work = refs[4:]
    frame = pl.program_id(0)
    mod = mod_ref[...]

    @pl.when(frame == 0)
    def _():
        dgate_ref[...] = jnp.zeros_like(dgate_ref)

    d_first = jnp.concatenate([p[...].reshape(-1, width) for p in dfirsts], 0).astype(F32)
    dgate_ref[...] += jnp.sum(d_first * branch_ref[...].astype(F32), 0, keepdims=True)
    d_branch = (part_of(mod, 2, width) * d_first).astype(BF)
    dsb_ref[...] = d_branch
    work[...] = mm_nt(d_branch, out_ref[...]).astype(BF)

    def pair(index, carry):
        at, after, last = slab_at(index), slab_at(index, width), slab_at(index, 2 * width)
        grad_q, grad_k, grad_v = attend_slab_back(
            proj_ref[:, at], proj_ref[:, after], proj_ref[:, last], work[:, at], None
        )
        dproj_ref[:, at] = grad_q.astype(BF)
        dproj_ref[:, after] = grad_k.astype(BF)
        dproj_ref[:, last] = grad_v.astype(BF)
        return carry

    lax.fori_loop(0, width // SLAB, pair, 0)


def video_backward(where_ref, *refs, groups, width):
    videos, refs = refs[:groups], refs[groups:]
    dfirsts, refs = refs[:groups], refs[groups:]
    results, refs = refs[:groups], refs[groups:]
    mod_ref, dproj_ref, qkv_ref, grad_ref, result_ref, dmod_ref = refs
    frame = pl.program_id(0)
    place = where_ref[0]
    mod = mod_ref[...]

    @pl.when(frame == 0)
    def _():
        dmod_ref[...] = jnp.zeros_like(dmod_ref)

    video = jnp.concatenate([v[...].reshape(-1, width) for v in videos], 0).astype(F32)
    d_first = jnp.concatenate([p[...].reshape(-1, width) for p in dfirsts], 0).astype(F32)
    normed, inv_std = normalize(video)
    d_in = mm_nt(dproj_ref[...], qkv_ref[...])
    dmod_ref[0:1, :] += jnp.sum(d_in, 0, keepdims=True)
    dmod_ref[1:2, :] += jnp.sum(d_in * normed, 0, keepdims=True)
    grad = d_first + norm_back(d_in * (1.0 + part_of(mod, 1, width)), normed, inv_std)
    share = grad.shape[0] // groups
    for j in range(groups):
        slot = jnp.bitwise_xor(place, j)
        grad_ref[0, slot] = grad[j * share : (j + 1) * share]
        result_ref[0, slot] = results[j][...].reshape(share, width)


class Stream:
    def __init__(self, cur, recv, sems, order, cols, fin, source=None):
        self.cur, self.recv, self.sems, self.fin = cur, recv, sems, fin
        self.order, self.cols, self.source = order, cols, source
        self.bits = sorted(order, reverse=True)
        wide = lax.axis_size("wide")
        me = lax.axis_index("narrow") * wide + lax.axis_index("wide")
        self.mine = {b: jnp.bitwise_and(lax.shift_right_logical(me, b), 1) for b in order}

    def where(self, stage):
        spots = []
        for b in self.bits:
            at = self.order.index(b)
            if at < stage:
                spots.append(self.mine[b])
            elif at == stage:
                spots.append(1 - self.mine[b])
            else:
                spots.append(slice(None))
        return tuple(spots) + (slice(None), self.cols)

    def copy(self, stage):
        base = self.cur if stage > 0 or self.source is None else self.source
        return send(
            base.at[self.where(stage)],
            self.recv[stage],
            self.sems.at[0, stage],
            self.sems.at[1, stage],
            1 << self.order[stage],
        )

    def add(self, stage):
        self.copy(stage).wait()
        left = [b for b in self.bits if self.order.index(b) > stage]
        count = len(left)

        def summed(place):
            spot = tuple(place.get(b, self.mine[b]) for b in self.bits) + (slice(None), self.cols)
            inner = tuple(place[b] for b in left)
            return spot, self.cur[spot].astype(F32) + self.recv[stage][inner].astype(F32)

        if not left:
            _, total = summed({})
            self.fin[:, :, self.cols] = total.reshape(self.fin.shape[0], -1, total.shape[1])
            return

        def body(i, carry):
            place = {
                b: jnp.bitwise_and(lax.shift_right_logical(i, count - 1 - k), 1)
                for k, b in enumerate(left)
            }
            spot, total = summed(place)
            self.cur[spot] = total.astype(BF)
            return carry

        lax.fori_loop(0, 1 << count, body, 0)


def stream_scratch(rows, cols, bits, parts):
    cols = cols // parts
    shapes = [pltpu.VMEM((2,) * k + (rows, cols), BF) for k in range(bits - 1, -1, -1)]
    return [shapes + [pltpu.SemaphoreType.DMA((2, bits))] for _ in range(parts)]


def stream_orders(wide_bits, bits):
    z_bits = [b for b in range(2, bits + 1) if b != wide_bits]
    return [
        [wide_bits, 1] + z_bits,
        [1, z_bits[0], wide_bits] + z_bits[1:],
        [z_bits[0], wide_bits, 1] + z_bits[1:],
    ]


def forward_stage(streams, stage):
    for stream in streams:
        stream.add(stage)
        if stage + 1 < len(stream.order):
            stream.copy(stage + 1).start()


def store_flat(out, value, first, pitch):
    for t in range(value.shape[1] // 128):
        out[pl.ds(first + t, value.shape[0], stride=pitch), :] = value[:, t * 128 : (t + 1) * 128]


class Finish:
    def __init__(self, fin, fin_in, sems, flats, outs):
        self.fin, self.fin_in, self.sems, self.flats, self.outs = fin, fin_in, sems, flats, outs
        self.core = jnp.bitwise_and(lax.axis_index("wide"), 1)

    def swap(self):
        return send(
            self.fin.at[1 - self.core], self.fin_in, self.sems.at[0], self.sems.at[1], 1
        )

    def writes(self):
        return [
            pltpu.make_async_copy(flat, out, self.sems.at[2 + k])
            for k, (flat, out) in enumerate(zip(self.flats, self.outs))
        ]

    def store(self):
        self.swap().wait()
        own, other = self.fin[self.core], self.fin_in[...]
        low = jnp.where(self.core == 0, own, other)
        high = jnp.where(self.core == 0, other, own)
        start = 0
        for flat in self.flats:
            pitch = flat.shape[0] // own.shape[0]
            half = pitch * 128 // 2
            store_flat(flat, low[:, start : start + half], 0, pitch)
            store_flat(flat, high[:, start : start + half], pitch // 2, pitch)
            start += half
        for write in self.writes():
            write.start()

    def wait(self):
        for write in self.writes():
            write.wait()


def grads_half(pairs, side, dest, extra=None):
    start = 0
    for left, right in pairs:
        part = right.shape[1] // 2
        cols = pl.ds(pl.multiple_of(side * part, 128), part)
        for m in range(left.shape[1] // ROWS):
            rows = slice(m * ROWS, (m + 1) * ROWS)
            value = mm_tn(left[:, rows], right[:, cols])
            spot = (slice(m * ROWS, (m + 1) * ROWS), slice(start, start + part))
            if extra is not None:
                value = value + extra[spot].astype(F32)
            dest[spot] = value.astype(BF)
        start += part


def flat_rows(ref):
    return ref.reshape(-1, ref.shape[-1])


def with_scratch(body, scratch):
    form = jax.tree.structure(scratch)
    count = form.num_leaves

    def kernel(*refs):
        body(*refs[:-count], jax.tree.unflatten(form, refs[-count:]))

    return kernel


def all_bits():
    total = lax.axis_size("wide") * lax.axis_size("narrow")
    return total.bit_length() - 1


def piece_rows(ref, chunk):
    groups = ref.shape[0]
    width = ref.shape[-1]
    return jnp.concatenate([ref[j, :, chunk].reshape(-1, width) for j in range(groups)], 0)


def frame_rows(ref, frame):
    width = ref.shape[-1]
    return jnp.concatenate([ref[j, frame].reshape(-1, width) for j in range(ref.shape[0])], 0)


def backward(length_ref, keep_ref, ins, outs, scratch):
    a, o, s = Names(**ins), Names(**outs), Names(**scratch)
    groups = len(a.cots)
    tokens, width = a.dmlp.shape
    chunks = tokens // ROWS
    frames = a.video.shape[0]
    share = ROWS // groups
    bits = all_bits() - 1
    wide_bits = lax.axis_size("wide").bit_length() - 1
    place, narrow_at = lax.axis_index("wide"), lax.axis_index("narrow")
    core = jnp.bitwise_and(place, 1)
    others = range(1, groups)
    counter = itertools.count()

    def load(src, dst):
        copy = pltpu.make_async_copy(src, dst, s.local.at[next(counter)])
        copy.start()
        return copy

    def wait_all(copies):
        for copy in copies:
            copy.wait()

    cross_loads = [load(a.cots[j], s.cots.at[j]) for j in range(groups)]
    cross_loads += [load(a.dmlp, s.dmlp), load(a.third, s.third), load(a.cout, s.cout)]
    cross_loads += [load(a.cq, s.cq), load(a.text, s.text)]
    cross_grad_loads = [load(a.cin, s.cin), load(a.words, s.words), load(a.cmix, s.cmix)]
    temporal_loads = [load(a.mid, s.mid), load(a.cwq, s.cwq), load(a.tout, s.tout)]
    temporal_loads += [load(a.tproj, s.tproj), load(a.tqkv, s.tqkv)]
    temporal_loads += [load(a.firsts[j], s.firsts.at[j]) for j in range(groups)]
    sum_loads = [load(a.sum_out, s.cur_out), load(a.sum_in, s.cur_in)]

    orders = stream_orders(wide_bits, bits)

    def split(cur, parts, fin, source=None):
        third = cur.shape[-1] // len(orders)
        return [
            Stream(cur, part[:-1], part[-1], order, slice(i * third, (i + 1) * third), fin, source)
            for i, (part, order) in enumerate(zip(parts, orders))
        ]

    mlp = split(s.cur_out, s.st_out, s.fin_out, a.sum_out)
    mlp += split(s.cur_in, s.st_in, s.fin_in, a.sum_in)
    cross = split(s.cur_c, s.st_c, s.fin_c)
    temporal = split(s.cur_t, s.st_t, s.fin_t)
    spatial = split(s.cur_s, s.st_s, s.fin_s)
    ends = [
        Finish(s.fin_out, s.fin_out_in, s.end_out, s.flat_out, o.mlp_out),
        Finish(s.fin_in, s.fin_in_in, s.end_in, s.flat_in, o.mlp_in),
        Finish(s.fin_c, s.fin_c_in, s.end_c, s.flat_c, o.cross),
        Finish(s.fin_t, s.fin_t_in, s.end_t, s.flat_t, o.temporal),
        Finish(s.fin_s, s.fin_s_in, s.end_s, s.flat_s, o.spatial),
    ]
    greet(list(others) + [1 << b for b in range(wide_bits, bits + 1)])
    for stream in mlp:
        stream.copy(0).start()

    def result_copy(j):
        target = o.result.at[:, place]
        held = s.dcq.reshape(groups, *a.results[0].shape).at[j]
        if j == 0:
            return pltpu.make_async_copy(held, target, s.result_sems.at[0, 0])
        return send(held, target, s.result_sems.at[0, j], s.result_sems.at[1, j], j)

    keys = s.text.shape[0]
    valid = lax.broadcasted_iota(jnp.int32, (ROWS, keys), 1) < length_ref[0]
    mod_scale = a.mod[:, 4 * width : 5 * width]
    work = s.work
    s.text_acc[...] = jnp.zeros_like(s.text_acc)
    s.mod_sum[...] = jnp.zeros_like(s.mod_sum)
    wait_all(cross_loads)

    def cross_chunk(k, carry):
        rows = pl.ds(pl.multiple_of(k * ROWS, ROWS), ROWS)
        cot = piece_rows(s.cots, k).astype(F32)
        d_mlp = s.dmlp[rows, :]
        normed, inv_std = normalize(s.third[rows, :])
        s.mod_sum[3:4, :] += jnp.sum(d_mlp, 0, keepdims=True)
        s.mod_sum[4:5, :] += jnp.sum(d_mlp * normed, 0, keepdims=True)
        d_third = cot + norm_back(d_mlp * (1.0 + mod_scale), normed, inv_std)
        s.dmlp[rows, :] = d_third
        d_branch = d_third.astype(BF)
        s.dcb[rows, :] = d_branch
        work[...] = mm_nt(d_branch, s.cout[...]).astype(BF)

        def pair(index, inner):
            at, after = slab_at(index), slab_at(index, width)
            grad_q, grad_k, grad_v = attend_slab_back(
                s.cq[rows, at], s.text[:, at], s.text[:, after], work[:, at], valid
            )
            s.dcq[rows, at] = grad_q.astype(BF)
            s.text_acc[:, at] += grad_k
            s.text_acc[:, after] += grad_v
            return inner

        lax.fori_loop(0, width // SLAB, pair, 0)
        return carry

    lax.fori_loop(0, chunks, cross_chunk, 0)
    s.dtext[...] = s.text_acc[...].astype(BF)
    video_loads = [load(a.video.at[:, jnp.bitwise_xor(place, j)], s.cots.at[j]) for j in range(groups)]
    late_loads = [load(a.sout, s.cout), load(a.sbranch, s.cq)]

    wait_all(cross_grad_loads)
    pairs_c = [(s.cin, s.dcq), (s.words, s.dtext), (s.cmix, s.dcb)]
    grads_half(pairs_c, 1 - core, s.send)

    def core_copy(src, cur, k):
        return send(src, flat_rows(cur), s.core_sems.at[0, k], s.core_sems.at[1, k], 1)

    copy_c = core_copy(s.send, s.cur_c, 0)
    copy_c.start()

    wait_all(temporal_loads)
    keep = (1 - keep_ref[0]).astype(F32)
    same = frame_mask(ROWS, a.firsts[0].shape[2])
    tproj, dtp = s.tproj, s.dtp

    def temporal_chunk(k):
        rows = slice(k * ROWS, (k + 1) * ROWS)
        normed, inv_std = normalize(s.mid[rows, :])
        d_mid = s.dmlp[rows, :] + norm_back(
            mm_nt(s.dcq[rows, :], s.cwq[...]), normed, inv_std
        )
        d_branch = (keep * d_mid).astype(BF)
        s.dtb[rows, :] = d_branch
        work[...] = mm_nt(d_branch, s.tout[...]).astype(BF)

        def pair(index, carry):
            at, after, last = slab_at(index), slab_at(index, width), slab_at(index, 2 * width)
            grad_q, grad_k, grad_v = attend_slab_back(
                tproj[rows, at], tproj[rows, after], tproj[rows, last], work[:, at], same
            )
            dtp[rows, at] = grad_q.astype(BF)
            dtp[rows, after] = grad_k.astype(BF)
            dtp[rows, last] = grad_v.astype(BF)
            return carry

        lax.fori_loop(0, width // SLAB, pair, 0)
        normed, inv_std = normalize(piece_rows(s.firsts, k).astype(F32))
        d_first = d_mid + norm_back(mm_nt(dtp[rows, :], s.tqkv[...]), normed, inv_std)
        d_first = d_first.astype(BF)
        for j in range(groups):
            buf = s.dfirsts if j == 0 else s.firsts
            buf[j, :, k] = d_first[j * share : (j + 1) * share].reshape(
                buf.shape[1:2] + buf.shape[3:]
            )

    def first_copy(j, k):
        return send(
            s.firsts.at[j, :, k], s.dfirsts.at[j, :, k],
            s.first_sems.at[0, j, k], s.first_sems.at[1, j, k], j,
        )

    temporal_chunk(0)
    for j in others:
        first_copy(j, 0).start()
    wait_all(sum_loads)
    forward_stage(mlp, 0)
    copy_c.wait()
    cur_c = flat_rows(s.cur_c)
    grads_half(pairs_c, core, cur_c, cur_c)
    for stream in cross:
        stream.copy(0).start()
    temporal_grad_loads = [load(a.tin, s.cin), load(a.tmix, s.cmix)]
    for k in range(1, chunks):
        temporal_chunk(k)
        for j in others:
            first_copy(j, k).start()
    late_loads += [load(a.sproj, s.tproj), load(a.sqkv, s.tqkv)]
    held = s.dcq.reshape(groups, *a.results[0].shape)
    result_loads = [load(a.results[j], held.at[j]) for j in range(groups)]
    forward_stage(mlp, 1)
    wait_all(result_loads)
    for j in range(groups):
        result_copy(j).start()
    wait_all(temporal_grad_loads)
    pairs_t = [(s.cin, dtp), (s.cmix, s.dtb)]
    grads_half(pairs_t, 1 - core, s.send)
    copy_t = core_copy(s.send, s.cur_t, 1)
    copy_t.start()
    forward_stage(mlp, 2)
    forward_stage(cross, 0)
    copy_t.wait()
    cur_t = flat_rows(s.cur_t)
    grads_half(pairs_t, core, cur_t, cur_t)
    spatial_grad_loads = [load(a.sin, s.cin), load(a.smix, s.cmix)]
    for stream in temporal:
        stream.copy(0).start()

    for j in others:
        for k in range(chunks):
            first_copy(j, k).wait()
    wait_all(late_loads)
    gate = a.mod[:, 2 * width : 3 * width]
    scale = a.mod[:, width : 2 * width]

    def spatial_frame(f):
        rows = slice(f * ROWS, (f + 1) * ROWS)
        d_first = frame_rows(s.dfirsts, f).astype(F32)
        s.mod_sum[2:3, :] += jnp.sum(d_first * s.cq[rows, :].astype(F32), 0, keepdims=True)
        d_branch = (gate * d_first).astype(BF)
        s.dcb[rows, :] = d_branch
        work[...] = mm_nt(d_branch, s.cout[...]).astype(BF)

        def pair(index, carry):
            at, after, last = slab_at(index), slab_at(index, width), slab_at(index, 2 * width)
            grad_q, grad_k, grad_v = attend_slab_back(
                tproj[rows, at], tproj[rows, after], tproj[rows, last], work[:, at], None
            )
            dtp[rows, at] = grad_q.astype(BF)
            dtp[rows, after] = grad_k.astype(BF)
            dtp[rows, last] = grad_v.astype(BF)
            return carry

        lax.fori_loop(0, width // SLAB, pair, 0)

    spatial_frame(0)
    forward_stage(mlp, 3)
    for end in ends[:2]:
        end.swap().start()
    forward_stage(cross, 1)
    forward_stage(temporal, 0)
    for f in range(1, frames):
        spatial_frame(f)
    forward_stage(cross, 2)
    forward_stage(temporal, 1)
    wait_all(spatial_grad_loads)
    pairs_s = [(s.cin, dtp), (s.cmix, s.dcb)]
    grads_half(pairs_s, 1 - core, s.send)
    copy_s = core_copy(s.send, s.cur_s, 2)
    copy_s.start()
    for end in ends[:2]:
        end.store()
    forward_stage(temporal, 2)
    copy_s.wait()
    cur_s = flat_rows(s.cur_s)
    grads_half(pairs_s, core, cur_s, cur_s)
    for stream in spatial:
        stream.copy(0).start()
    forward_stage(cross, 3)
    ends[2].swap().start()

    wait_all(video_loads)
    grad_writes = []
    for f in range(frames):
        rows = slice(f * ROWS, (f + 1) * ROWS)
        video = frame_rows(s.cots, f).astype(F32)
        d_first = frame_rows(s.dfirsts, f).astype(F32)
        normed, inv_std = normalize(video)
        d_in = mm_nt(dtp[rows, :], s.tqkv[...])
        s.mod_sum[0:1, :] += jnp.sum(d_in, 0, keepdims=True)
        s.mod_sum[1:2, :] += jnp.sum(d_in * normed, 0, keepdims=True)
        grad = d_first + norm_back(d_in * (1.0 + scale), normed, inv_std)
        for j in range(groups):
            slot = jnp.bitwise_xor(place, j)
            at = pl.ds(pl.multiple_of(f * ROWS + slot * share, share), share)
            s.third[at, :] = grad[j * share : (j + 1) * share]
        grad_writes.append(load(s.third.at[rows, :], o.video_grad.at[f]))

    s.mod_sum[5:6, :] = a.dgate_two[...]
    mod_all = s.mod_all

    def mod_copy(b):
        sems = s.mod_sems.at[0, b], s.mod_sems.at[1, b]
        if b < wide_bits:
            return send(s.mod_sum, s.mod_in.at[b], *sems, 1 << b)
        size = 1 << (b - wide_bits)
        span = mod_all.at[pl.ds(lax.div(narrow_at, size) * size, size)]
        return send(span, span, *sems, 1 << b)

    def mod_step(b):
        mod_copy(b).wait()
        if b < wide_bits:
            s.mod_sum[...] = s.mod_sum[...] + s.mod_in[b]
        if b == wide_bits - 1:
            mod_all[narrow_at] = s.mod_sum[...]
            mod_all[narrow_at, 6:7, :] = a.silu[...]
        if b < bits:
            mod_copy(b + 1).start()

    mod_copy(0).start()
    ends[2].store()
    forward_stage(temporal, 3)
    ends[3].swap().start()
    mod_step(0)
    forward_stage(spatial, 0)
    mod_step(1)
    ends[3].store()
    mod_step(2)
    forward_stage(spatial, 1)
    mod_step(3)
    forward_stage(spatial, 2)
    for b in range(4, bits + 1):
        mod_step(b)
    mine = o.ada.shape[0] // (6 * width // 128)
    me = narrow_at * lax.axis_size("wide") + place
    row = lax.broadcasted_iota(jnp.int32, (mine, width), 0)
    col = lax.broadcasted_iota(jnp.int32, (mine, width), 1)
    picks = (col == me * mine + row).astype(F32).astype(BF)
    silu_mine = mm_nt(picks, mod_all[:, 6, :].astype(BF))
    pitch = 6 * width // 128
    for part in range(6):
        rows = 0.0
        for c in range(mod_all.shape[0]):
            rows = rows + silu_mine[:, c : c + 1] * mod_all[c, part : part + 1, :]
        store_flat(s.flat_ada, rows, part * width // 128, pitch)
    ada_write = load(s.flat_ada, o.ada)
    forward_stage(spatial, 3)
    ends[4].swap().start()
    for j in range(groups):
        result_copy(j).wait()
    wait_all(grad_writes)
    for end in ends[:4]:
        end.wait()
    ends[4].store()
    ada_write.wait()
    ends[4].wait()


def copy_out(ins, outs, bufs, in_sems, out_sems):
    ins, outs, bufs = jax.tree.leaves(ins), jax.tree.leaves(outs), jax.tree.leaves(bufs)
    reads = [
        pltpu.make_async_copy(src, buf, in_sems.at[k])
        for k, (src, buf) in enumerate(zip(ins, bufs))
    ]
    writes = [
        pltpu.make_async_copy(buf, dst, out_sems.at[k])
        for k, (buf, dst) in enumerate(zip(bufs, outs))
    ]
    for read in reads:
        read.start()
    for read, write in zip(reads, writes):
        read.wait()
        write.start()
    for write in writes:
        write.wait()


def weight_grads(core_ref, *refs, count):
    pairs, outs = refs[: 2 * count], refs[2 * count :]
    core = core_ref[0]
    for sign, out in enumerate(outs):
        side = 1 - core if sign == 0 else core
        start = 0
        for k in range(count):
            left, right = pairs[2 * k], pairs[2 * k + 1]
            part = right.shape[1] // 2
            cols = pl.ds(pl.multiple_of(side * part, 128), part)
            out[:, start : start + part] = mm_tn(left[...], right[:, cols]).astype(BF)
            start += part


def weight_grads_call(core, pairs):
    depth = pairs[0][0].shape[1]
    total = sum(right.shape[1] for _, right in pairs)
    tile = 256
    specs = []
    for left, right in pairs:
        specs.append(pl.BlockSpec((left.shape[0], tile), lambda m, _: (0, m)))
        specs.append(fixed(right.shape))
    shape = jax.ShapeDtypeStruct((depth, total // 2), BF)
    flops = sum(2 * left.shape[0] * depth * right.shape[1] for left, right in pairs)
    return pl.pallas_call(
        functools.partial(weight_grads, count=len(pairs)),
        grid_spec=pltpu.PrefetchScalarGridSpec(
            num_scalar_prefetch=1,
            grid=(depth // tile,),
            in_specs=specs,
            out_specs=[pl.BlockSpec((tile, total // 2), lambda m, _: (m, 0))] * 2,
        ),
        out_shape=[shape, shape],
        compiler_params=params(),
        cost_estimate=cost(flops, 8e6),
        name="weight_grads",
    )(core, *[a for pair in pairs for a in pair])


def shards(
    video,
    text_states,
    text_length,
    timestep,
    motion_free,
    ada_weight,
    spatial_qkv_weight,
    spatial_out_weight,
    temporal_qkv_weight,
    temporal_out_weight,
    cross_query_weight,
    cross_kv_weight,
    cross_out_weight,
    mlp_in_weight,
    mlp_out_weight,
    cotangent,
    *,
    mesh_shape,
):
    clips, frames, patches, width = video.shape
    if clips != 1 or patches != ROWS:
        raise ValueError("unsupported shard")
    wide, narrow = mesh_shape["wide"], mesh_shape["narrow"]
    devices = wide * narrow
    groups = wide
    here = patches // groups
    tokens = frames * patches
    chunks = tokens // ROWS
    per_chunk = here // chunks
    hidden = mlp_in_weight.shape[1]
    text_rows = text_states.shape[1]
    text_pad = -(-text_rows // 128) * 128

    wide_at = lax.axis_index("wide")
    narrow_at = lax.axis_index("narrow")
    index = narrow_at * wide + wide_at
    core = jnp.bitwise_and(wide_at, 1)
    place = wide_at.reshape(1).astype(jnp.int32)
    core_arr = core.reshape(1).astype(jnp.int32)
    wide_bits = wide.bit_length() - 1
    bits = devices.bit_length() - 1

    cot_view = cotangent.reshape(frames, groups, here, width)

    silu_time = silu_of(time_features(timestep.astype(F32), width)).astype(BF)
    mod = mm(silu_time, ada_weight)
    text_flat = text_states.reshape(text_rows, width)
    text_flat = jnp.pad(text_flat, ((0, text_pad - text_rows), (0, 0)))
    text_proj = mm(text_flat, cross_kv_weight).astype(BF)

    video_view = video.reshape(frames, groups, here, width)

    def own_patches(j):
        return pl.BlockSpec(
            (1, 1, here, width),
            lambda f, *_: (f, jnp.bitwise_xor(lax.axis_index("wide"), j), 0, 0),
        )

    def frame_piece():
        return pl.BlockSpec((1, chunks, per_chunk, width), lambda f, *_: (f, 0, 0, 0))

    def chunk_piece():
        return pl.BlockSpec((frames, 1, per_chunk, width), lambda k, *_: (0, k, 0, 0))

    def row_block(cols):
        return pl.BlockSpec((ROWS, cols), lambda f, *_: (f, 0))

    piece_shape = jax.ShapeDtypeStruct((frames, chunks, per_chunk, width), BF)

    def rows_of(cols, dtype=BF):
        return jax.ShapeDtypeStruct((tokens, cols), dtype)

    mod_spec = fixed(mod.shape)
    anywhere = pl.BlockSpec(memory_space=pl.ANY)
    own_piece = jax.ShapeDtypeStruct((frames, here, width), BF)
    outs = pl.pallas_call(
        functools.partial(spatial_forward, groups=groups, width=width, frames=frames),
        grid_spec=pltpu.PrefetchScalarGridSpec(
            num_scalar_prefetch=0,
            grid=(frames,),
            in_specs=[own_patches(j) for j in range(groups)]
            + [own_patches(j) for j in range(groups)]
            + [mod_spec, fixed(spatial_qkv_weight.shape), fixed(spatial_out_weight.shape)],
            out_specs=[row_block(width), row_block(3 * width), row_block(width), row_block(width)]
            + ([pl.BlockSpec((1, here, width), lambda f, *_: (f, 0, 0))] + [anywhere] * (groups - 1)) * 2,
            scratch_shapes=[
                pltpu.VMEM((groups - 1, frames, here, width), BF),
                pltpu.VMEM((groups - 1, frames, here, width), BF),
                pltpu.SemaphoreType.DMA((2, groups - 1, frames)),
                pltpu.SemaphoreType.DMA((2, groups - 1, frames)),
            ],
        ),
        out_shape=[rows_of(width), rows_of(3 * width), rows_of(width), rows_of(width)]
        + [own_piece] * (2 * groups),
        compiler_params=params(collective_id=0, has_side_effects=True),
        cost_estimate=cost(8 * tokens * width * width, 10e6, tokens * patches * 12),
        name="spatial_forward",
    )(*[video_view] * groups, *[cot_view] * groups, mod, spatial_qkv_weight, spatial_out_weight)
    spatial_in, spatial_proj, spatial_mix, spatial_branch = outs[:4]
    firsts = [p.reshape(piece_shape.shape) for p in outs[4 : 4 + groups]]
    cots = [p.reshape(piece_shape.shape) for p in outs[4 + groups :]]

    def two_scalars(grid, in_specs, out_specs, scratch=()):
        return pltpu.PrefetchScalarGridSpec(
            num_scalar_prefetch=2,
            grid=grid,
            in_specs=in_specs,
            out_specs=out_specs,
            scratch_shapes=scratch,
        )

    outs = pl.pallas_call(
        functools.partial(middle_forward, groups=groups, width=width, per_chunk=per_chunk),
        grid_spec=two_scalars(
            (chunks,),
            [chunk_piece() for _ in range(groups)]
            + [
                mod_spec,
                fixed(temporal_qkv_weight.shape),
                fixed(temporal_out_weight.shape),
                fixed(cross_query_weight.shape),
                fixed(text_proj.shape),
                fixed(cross_out_weight.shape),
            ],
            [
                row_block(width),
                row_block(3 * width),
                row_block(width),
                row_block(width),
                row_block(width),
                row_block(width),
                row_block(width),
                row_block(width),
                row_block(width),
            ],
        ),
        out_shape=[
            rows_of(width),
            rows_of(3 * width),
            rows_of(width),
            rows_of(width),
            rows_of(width),
            rows_of(width),
            rows_of(width),
            rows_of(width, F32),
            rows_of(width, F32),
        ],
        compiler_params=params(),
        cost_estimate=cost(12 * tokens * width * width, 20e6, tokens * ROWS * 18),
        name="middle_forward",
    )(
        text_length,
        motion_free,
        *firsts,
        mod,
        temporal_qkv_weight,
        temporal_out_weight,
        cross_query_weight,
        text_proj,
        cross_out_weight,
    )
    temporal_in, temporal_proj, temporal_mix, cross_in, cross_q, cross_mix, mlp_in, mid, third = outs

    steps = 4
    wide_h = hidden // steps

    def hidden_at(step):
        half = steps // 2
        side_bit = jnp.bitwise_and(lax.axis_index("wide"), 1)
        side = jnp.where(step < half, 1 - side_bit, side_bit)
        return side * half + lax.rem(step, half)

    whole_piece = fixed((frames, chunks, per_chunk, width))
    outs = pl.pallas_call(
        functools.partial(mlp_both, groups=groups, width=width, steps=steps),
        grid_spec=pltpu.PrefetchScalarGridSpec(
            num_scalar_prefetch=0,
            grid=(steps,),
            in_specs=[whole_piece] * groups
            + [
                fixed(mlp_in.shape),
                fixed(third.shape),
                mod_spec,
                pl.BlockSpec((width, wide_h), lambda s: (0, hidden_at(s))),
                pl.BlockSpec((wide_h, width), lambda s: (hidden_at(s), 0)),
            ],
            out_specs=[
                pl.BlockSpec((width, wide_h), lambda s: (0, jnp.maximum(s - steps // 2, 0))),
                fixed((hidden, width // 2)),
                fixed((tokens, width)),
                fixed((1, width)),
            ]
            + [whole_piece] * groups,
            scratch_shapes=[
                pltpu.VMEM((width, tokens), BF),
                pltpu.VMEM((tokens, width), BF),
                pltpu.VMEM((tokens, width), F32),
                pltpu.VMEM((steps // 2, width, wide_h), BF),
                pltpu.VMEM((steps // 2, width, wide_h), BF),
                pltpu.VMEM((steps, wide_h, width // 2), BF),
                pltpu.VMEM((steps, wide_h, width // 2), BF),
                pltpu.VMEM((steps, wide_h, width // 2), BF),
                pltpu.SemaphoreType.DMA((2, steps // 2)),
                pltpu.SemaphoreType.DMA((2, steps)),
            ],
        ),
        out_shape=[
            jax.ShapeDtypeStruct((width, hidden // 2), BF),
            jax.ShapeDtypeStruct((hidden, width // 2), BF),
            rows_of(width, F32),
            jax.ShapeDtypeStruct((1, width), F32),
        ]
        + [piece_shape] * groups,
        compiler_params=params(collective_id=1, has_side_effects=True),
        cost_estimate=cost(12 * tokens * width * hidden, 25e6, tokens * hidden),
        name="mlp_both",
    )(*cots, mlp_in, third, mod, mlp_in_weight, mlp_out_weight)
    sum_in, sum_out, d_mlp_in, d_gate_two = outs[:4]
    if (2 * width // devices) % 16 == 0 and width % 768 == 0 and hidden % 768 == 0:
        chip = (2,) * (bits - 1)
        nb = bits - 1
        rows_in, rows_out = 2 * width // devices, 2 * hidden // devices
        cols_in, cols_out = hidden // 2, width // 2
        vm, sems = pltpu.VMEM, pltpu.SemaphoreType.DMA
        act = lambda cols, dtype=BF: vm((tokens, cols), dtype)
        group = vm(chip + (rows_in, cols_in), BF)
        pieces = vm((groups, frames, chunks, per_chunk, width), BF)
        ins = dict(
            cots=tuple(cots),
            dmlp=d_mlp_in,
            third=third,
            mid=mid,
            mod=mod,
            silu=silu_time.astype(F32),
            dgate_two=d_gate_two,
            cq=cross_q,
            text=text_proj,
            tproj=temporal_proj,
            cout=cross_out_weight,
            cwq=cross_query_weight,
            tout=temporal_out_weight,
            tqkv=temporal_qkv_weight,
            firsts=tuple(firsts),
            cin=cross_in,
            cmix=cross_mix,
            words=text_flat,
            tin=temporal_in,
            tmix=temporal_mix,
            sum_out=sum_out.reshape(chip + (rows_out, cols_out)),
            sum_in=sum_in.reshape(chip + (rows_in, cols_in)),
            results=tuple(p.reshape(frames, here, width) for p in outs[4 : 4 + groups]),
            video=video.reshape(frames, groups, chunks, per_chunk, width),
            sbranch=spatial_branch,
            sout=spatial_out_weight,
            sproj=spatial_proj,
            sin=spatial_in,
            smix=spatial_mix,
            sqkv=spatial_qkv_weight,
        )
        in_specs = jax.tree.map(lambda _: anywhere, ins)
        for name in ("mod", "silu", "dgate_two"):
            in_specs[name] = fixed(ins[name].shape)

        def flat_shapes(elements):
            return tuple(jax.ShapeDtypeStruct((n // devices // 128, 128), F32) for n in elements)

        square = width * width
        out_shape = dict(
            result=jax.ShapeDtypeStruct((frames, groups, here, width), BF),
            video_grad=jax.ShapeDtypeStruct((frames, patches, width), F32),
            ada=flat_shapes([6 * square])[0],
            spatial=flat_shapes([3 * square, square]),
            temporal=flat_shapes([3 * square, square]),
            cross=flat_shapes([square, 2 * square, square]),
            mlp_in=flat_shapes([width * hidden]),
            mlp_out=flat_shapes([width * hidden]),
        )
        in_hbm = pl.BlockSpec(memory_space=pltpu.HBM)
        out_specs = jax.tree.map(lambda _: in_hbm, out_shape)
        flats = jax.tree.map(lambda leaf: vm(leaf.shape, F32), out_shape)

        def streams_in():
            return stream_scratch(rows_in, cols_in, nb, 3)

        def fin(rows, cols, count):
            return vm((2, rows // 2, cols), F32), vm((rows // 2, cols), F32), sems((2 + count,))

        fin_out, fin_out_in, end_out = fin(rows_out, cols_out, 1)
        fin_in, fin_in_in, end_in = fin(rows_in, cols_in, 1)
        fin_c, fin_c_in, end_c = fin(rows_in, cols_in, 3)
        fin_t, fin_t_in, end_t = fin(rows_in, cols_in, 2)
        scratch = dict(
            local=sems((64,)),
            cots=pieces,
            firsts=pieces,
            dfirsts=pieces,
            dmlp=act(width, F32),
            third=act(width, F32),
            mid=act(width, F32),
            cq=act(width),
            text=vm(text_proj.shape, BF),
            tproj=act(3 * width),
            cout=vm((width, width), BF),
            cwq=vm((width, width), BF),
            tout=vm((width, width), BF),
            tqkv=vm((width, 3 * width), BF),
            cin=act(width),
            cmix=act(width),
            words=vm(text_flat.shape, BF),
            st_out=stream_scratch(rows_out, cols_out, nb, 3),
            st_in=streams_in(),
            st_c=streams_in(),
            st_t=streams_in(),
            st_s=streams_in(),
            cur_out=vm(chip + (rows_out, cols_out), BF),
            cur_in=group,
            cur_c=group,
            cur_t=group,
            cur_s=group,
            send=vm((width, cols_in), BF),
            fin_out=fin_out,
            fin_in=fin_in,
            fin_c=fin_c,
            fin_t=fin_t,
            fin_s=fin_t,
            fin_out_in=fin_out_in,
            fin_in_in=fin_in_in,
            fin_c_in=fin_c_in,
            fin_t_in=fin_t_in,
            fin_s_in=fin_t_in,
            end_out=end_out,
            end_in=end_in,
            end_c=end_c,
            end_t=end_t,
            end_s=end_t,
            flat_out=flats["mlp_out"],
            flat_in=flats["mlp_in"],
            flat_c=flats["cross"],
            flat_t=flats["temporal"],
            flat_s=flats["spatial"],
            flat_ada=flats["ada"],
            core_sems=sems((2, 3)),
            result_sems=sems((2, groups)),
            first_sems=sems((2, groups, chunks)),
            mod_sems=sems((2, bits)),
            text_acc=vm(text_proj.shape, F32),
            work=vm((ROWS, width), BF),
            dcb=act(width),
            dcq=act(width),
            dtext=vm(text_proj.shape, BF),
            dtb=act(width),
            dtp=act(3 * width),
            mod_sum=vm((8, width), F32),
            mod_in=vm((wide_bits, 8, width), F32),
            mod_all=vm((narrow, 8, width), F32),
        )
        back = pl.pallas_call(
            with_scratch(backward, scratch),
            grid_spec=pltpu.PrefetchScalarGridSpec(
                num_scalar_prefetch=2,
                grid=(1,),
                in_specs=[in_specs],
                out_specs=out_specs,
                scratch_shapes=jax.tree.leaves(scratch),
            ),
            out_shape=out_shape,
            compiler_params=params(collective_id=2, has_side_effects=True),
            cost_estimate=cost(74 * tokens * width * width, 70e6, tokens * ROWS * 30),
            name="backward",
        )(text_length, motion_free, ins)
        back = pl.pallas_call(
            copy_out,
            grid=(),
            in_specs=[jax.tree.map(lambda _: anywhere, out_shape)],
            out_specs=out_specs,
            out_shape=out_shape,
            scratch_shapes=[
                jax.tree.map(lambda leaf: vm(leaf.shape, leaf.dtype), out_shape),
                sems((len(jax.tree.leaves(out_shape)),)),
                sems((len(jax.tree.leaves(out_shape)),)),
            ],
            compiler_params=params(),
            cost_estimate=cost(0, 9e6),
            name="copy_out",
        )(back)
        grads = (
            [back["ada"]]
            + list(back["spatial"])
            + list(back["temporal"])
            + list(back["cross"])
            + list(back["mlp_in"])
            + list(back["mlp_out"])
        )
        return (
            back["result"].reshape(video.shape),
            back["video_grad"].reshape(video.shape),
        ) + tuple(g.reshape(-1) for g in grads)

    def flip(value, mask):
        return lax.ppermute(value, AXES, [(i, i ^ mask) for i in range(devices)])

    def bit_of(b):
        return jnp.bitwise_and(lax.shift_right_logical(index, b), 1)

    def gather_narrow(row):
        for b in range(wide_bits, bits):
            other = flip(row, 1 << b)
            mine = bit_of(b) == 0
            row = jnp.concatenate(
                [jnp.where(mine, row, other), jnp.where(mine, other, row)], 0
            )
        return row

    times = gather_narrow(timestep.astype(F32).reshape(1, 1))
    silu_all = silu_of(time_features(times[:, 0], width)).astype(BF).astype(F32)
    mine = width // devices
    silu_rows = lax.dynamic_slice_in_dim(silu_all, index * mine, mine, 1)

    results = [outs[4]] + [flip(outs[4 + j], j) for j in range(1, groups)]

    outs = pl.pallas_call(
        functools.partial(middle_backward, groups=groups, width=width, per_chunk=per_chunk),
        grid_spec=two_scalars(
            (chunks,),
            [chunk_piece() for _ in range(groups)]
            + [
                row_block(width),
                row_block(width),
                row_block(width),
                mod_spec,
                row_block(width),
                row_block(3 * width),
                row_block(width),
                fixed(text_proj.shape),
                fixed(cross_out_weight.shape),
                fixed(cross_query_weight.shape),
                fixed(temporal_out_weight.shape),
                fixed(temporal_qkv_weight.shape),
            ]
            + [chunk_piece() for _ in range(groups)],
            [
                row_block(width),
                row_block(width),
                fixed((text_pad, 2 * width)),
                row_block(width),
                row_block(3 * width),
                fixed((2, width)),
            ]
            + [chunk_piece() for _ in range(groups)],
            [pltpu.VMEM((text_pad, 2 * width), F32), pltpu.VMEM((ROWS, width), BF)],
        ),
        out_shape=[
            rows_of(width),
            rows_of(width),
            jax.ShapeDtypeStruct((text_pad, 2 * width), BF),
            rows_of(width),
            rows_of(3 * width),
            jax.ShapeDtypeStruct((2, width), F32),
        ]
        + [piece_shape] * groups,
        compiler_params=params(),
        cost_estimate=cost(20 * tokens * width * width, 25e6, tokens * ROWS * 18),
        name="middle_backward",
    )(
        text_length,
        motion_free,
        *cots,
        d_mlp_in,
        third,
        mid,
        mod,
        temporal_in,
        temporal_proj,
        cross_q,
        text_proj,
        cross_out_weight,
        cross_query_weight,
        temporal_out_weight,
        temporal_qkv_weight,
        *firsts,
    )
    d_cross_branch, d_cross_q, d_text, d_temporal_branch, d_temporal_proj, d_mod_two = outs[:6]
    d_firsts = [outs[6]] + [flip(outs[6 + j], j) for j in range(1, groups)]

    cross_send, cross_keep = weight_grads_call(
        core_arr,
        [(cross_in, d_cross_q), (text_flat, d_text), (cross_mix, d_cross_branch)],
    )
    temporal_send, temporal_keep = weight_grads_call(
        core_arr,
        [(temporal_in, d_temporal_proj), (temporal_mix, d_temporal_branch)],
    )

    d_spatial_branch, d_spatial_proj, d_gate_one = pl.pallas_call(
        functools.partial(spatial_backward, groups=groups, width=width),
        grid=(frames,),
        in_specs=[frame_piece() for _ in range(groups)]
        + [mod_spec, row_block(width), row_block(3 * width), fixed(spatial_out_weight.shape)],
        out_specs=[row_block(width), row_block(3 * width), fixed((1, width))],
        out_shape=[rows_of(width), rows_of(3 * width), jax.ShapeDtypeStruct((1, width), F32)],
        scratch_shapes=[pltpu.VMEM((ROWS, width), BF)],
        compiler_params=params(),
        cost_estimate=cost(8 * tokens * width * width, 10e6, tokens * patches * 12),
        name="spatial_backward",
    )(*d_firsts, mod, spatial_branch, spatial_proj, spatial_out_weight)

    spatial_send, spatial_keep = weight_grads_call(
        core_arr,
        [(spatial_in, d_spatial_proj), (spatial_mix, d_spatial_branch)],
    )

    out_block = pl.BlockSpec((1, groups, here, width), lambda f, *_: (f, 0, 0, 0))
    video_grad, result, d_mod_one = pl.pallas_call(
        functools.partial(video_backward, groups=groups, width=width),
        grid_spec=pltpu.PrefetchScalarGridSpec(
            num_scalar_prefetch=1,
            grid=(frames,),
            in_specs=[own_patches(j) for j in range(groups)]
            + [frame_piece() for _ in range(2 * groups)]
            + [mod_spec, row_block(3 * width), fixed(spatial_qkv_weight.shape)],
            out_specs=[out_block, out_block, fixed((2, width))],
        ),
        out_shape=[
            jax.ShapeDtypeStruct((frames, groups, here, width), F32),
            jax.ShapeDtypeStruct((frames, groups, here, width), BF),
            jax.ShapeDtypeStruct((2, width), F32),
        ],
        compiler_params=params(),
        cost_estimate=cost(6 * tokens * width * width, 12e6),
        name="video_backward",
    )(place, *[video_view] * groups, *d_firsts, *results, mod, d_spatial_proj, spatial_qkv_weight)
    video_grad = video_grad.reshape(video.shape)
    result = result.reshape(video.shape)

    d_mod = jnp.concatenate([d_mod_one, d_gate_one, d_mod_two, d_gate_two], 0)
    for b in range(wide_bits):
        d_mod = d_mod + flip(d_mod, 1 << b)
    d_mod_all = gather_narrow(d_mod[None])
    ada_rows = jnp.sum(silu_rows[:, :, None, None] * d_mod_all[:, None, :, :], 0)
    ada_grad = ada_rows.reshape(-1)

    chip_bits = list(range(1, bits))
    first_x = [wide_bits, 1]
    rest = [b for b in chip_bits if b not in first_x]
    order_a = first_x + rest
    order_b = first_x[::-1] + rest

    def join(send, keep):
        return keep.astype(F32) + flip(send, 1).astype(F32)

    def reduce_scatter(cur, order):
        cols = cur.shape[1]
        axes = sorted(chip_bits, reverse=True)
        for b in order:
            cur = cur.astype(BF)
            at = axes.index(b)
            view = cur.reshape(1 << at, 2, 1 << (len(axes) - at - 1), -1, cols)
            out = lax.dynamic_index_in_dim(view, 1 - bit_of(b), 1, keepdims=False)
            own = lax.dynamic_index_in_dim(view, bit_of(b), 1, keepdims=False)
            cur = own.astype(F32) + flip(out, 1 << b).astype(F32)
            axes.remove(b)
        cur = cur.reshape(2, -1, cols)
        own = lax.dynamic_index_in_dim(cur, core, 0, keepdims=False)
        other = flip(lax.dynamic_index_in_dim(cur, 1 - core, 0, keepdims=False), 1)
        low = jnp.where(core == 0, own, other)
        high = jnp.where(core == 0, other, own)
        return low, high

    def unpack(pair, widths):
        low, high = pair
        start, out = 0, []
        for w in widths:
            half = w // 2
            cols = slice(start, start + half)
            out.append(jnp.concatenate([low[:, cols], high[:, cols]], 1).reshape(-1))
            start += half
        return out

    mlp_out_grad = unpack(reduce_scatter(sum_out, order_a), [width])[0]
    mlp_in_grad = unpack(reduce_scatter(sum_in, order_b), [hidden])[0]
    cross_query_grad, cross_kv_grad, cross_out_grad = unpack(
        reduce_scatter(join(cross_send, cross_keep), order_a), [width, 2 * width, width]
    )
    temporal_qkv_grad, temporal_out_grad = unpack(
        reduce_scatter(join(temporal_send, temporal_keep), order_b), [3 * width, width]
    )
    spatial_qkv_grad, spatial_out_grad = unpack(
        reduce_scatter(join(spatial_send, spatial_keep), order_a), [3 * width, width]
    )
    return (
        result,
        video_grad,
        ada_grad,
        spatial_qkv_grad,
        spatial_out_grad,
        temporal_qkv_grad,
        temporal_out_grad,
        cross_query_grad,
        cross_kv_grad,
        cross_out_grad,
        mlp_in_grad,
        mlp_out_grad,
    )


def solution(mesh):
    tokens_spec = P("narrow", "wide", None, None)
    in_specs = (
        (tokens_spec, P("narrow", None, None), P("narrow"), P("narrow"), P("narrow"))
        + (P(),) * 10
        + (tokens_spec,)
    )
    out_specs = (tokens_spec, tokens_spec) + (P(AXES),) * 10
    return jax.shard_map(
        functools.partial(shards, mesh_shape=dict(mesh.shape)),
        mesh=mesh,
        in_specs=in_specs,
        out_specs=out_specs,
        check_vma=False,
    )
```

```python
import functools
import itertools
import math
import types

import jax
import jax.numpy as jnp
from jax import lax
from jax.experimental import pallas as pl
from jax.experimental.pallas import tpu as pltpu
from jax.sharding import PartitionSpec as P

HEAD_DIM = 64
SLAB = 2 * HEAD_DIM
SCALE = HEAD_DIM ** (-0.5)
EPSILON = 1e-06
NEG_LARGE = -1e30
BF = jnp.bfloat16
F32 = jnp.float32
AXES = ("narrow", "wide")
ROWS = 256
MESH = pl.DeviceIdType.MESH
VMEM_LIMIT = 60 * 1024 * 1024
Names = types.SimpleNamespace


def time_features(time_value, width):
    half = width // 2
    freqs = jnp.exp(-math.log(10000.0) * jnp.arange(half, dtype=F32) / half)
    angles = time_value[..., None] * freqs
    return jnp.concatenate([jnp.cos(angles), jnp.sin(angles)], axis=-1)


def silu_of(values):
    return values / (1.0 + jnp.exp(-values))


def normalize(values):
    mean = jnp.mean(values, -1, keepdims=True)
    centred = values - mean
    variance = jnp.mean(centred * centred, -1, keepdims=True)
    inv_std = lax.rsqrt(variance + EPSILON)
    return centred * inv_std, inv_std


def norm_back(grad_norm, normed, inv_std):
    return inv_std * (
        grad_norm
        - jnp.mean(grad_norm, -1, keepdims=True)
        - normed * jnp.mean(grad_norm * normed, -1, keepdims=True)
    )


def mm(left, right):
    return jnp.dot(left, right, preferred_element_type=F32)


def mm_nt(left, right):
    return lax.dot_general(left, right, (((1,), (1,)), ((), ())), preferred_element_type=F32)


def mm_tn(left, right):
    return lax.dot_general(left, right, (((0,), (0,)), ((), ())), preferred_element_type=F32)


def head_masks():
    lane = lax.broadcasted_iota(jnp.int32, (1, SLAB), 1)
    low = (lane < HEAD_DIM).astype(F32)
    return low.astype(BF), (1.0 - low).astype(BF)


def softmax_rows(scores):
    peak = jnp.max(scores, -1, keepdims=True)
    expd = jnp.exp(scores - peak)
    return expd * (1.0 / jnp.sum(expd, -1, keepdims=True))


def attend_slab(query, key, value, bias):
    mixed = None
    for mask in head_masks():
        scores = mm_nt(query * mask, key) * SCALE
        if bias is not None:
            scores = jnp.where(bias, scores, NEG_LARGE)
        probs = softmax_rows(scores).astype(BF)
        part = mm(probs, value * mask)
        mixed = part if mixed is None else mixed + part
    return mixed


def attend_slab_back(query, key, value, grad, bias):
    grad_query = grad_key = grad_value = 0.0
    for mask in head_masks():
        query_part = query * mask
        grad_part = grad * mask
        scores = mm_nt(query_part, key) * SCALE
        if bias is not None:
            scores = jnp.where(bias, scores, NEG_LARGE)
        probs = softmax_rows(scores)
        grad_probs = mm_nt(grad_part, value)
        inner = jnp.sum(grad_probs * probs, -1, keepdims=True)
        grad_scores = (probs * (grad_probs - inner)).astype(BF)
        grad_value = grad_value + mm_tn(probs.astype(BF), grad_part)
        grad_query = grad_query + mm(grad_scores, key * mask)
        grad_key = grad_key + mm_tn(grad_scores, query_part)
    return grad_query * SCALE, grad_key * SCALE, grad_value


def slab_at(index, offset=0):
    return pl.ds(pl.multiple_of(index * SLAB + offset, SLAB), SLAB)


def frame_mask(rows, per_chunk):
    row = lax.broadcasted_iota(jnp.int32, (rows, rows), 0)
    col = lax.broadcasted_iota(jnp.int32, (rows, rows), 1)
    return lax.rem(row, per_chunk) == lax.rem(col, per_chunk)


def part_of(mod, index, width):
    return mod[:, index * width : (index + 1) * width]


def cost(flops, bytes_accessed, transcendentals=0):
    return pl.CostEstimate(
        flops=int(flops), bytes_accessed=int(bytes_accessed), transcendentals=int(transcendentals)
    )


def params(**extra):
    return pltpu.CompilerParams(vmem_limit_bytes=VMEM_LIMIT, **extra)


def fixed(shape):
    rank = len(shape)
    return pl.BlockSpec(shape, lambda *_: (0,) * rank, pipeline_mode=pl.Buffered(1))


def partner(mask):
    wide = lax.axis_size("wide")
    me = lax.axis_index("narrow") * wide + lax.axis_index("wide")
    other = jnp.bitwise_xor(me, mask)
    return (lax.div(other, wide), lax.rem(other, wide))


def greet(masks):
    barrier = pltpu.get_barrier_semaphore()
    for mask in masks:
        pl.semaphore_signal(barrier, inc=1, device_id=partner(mask), device_id_type=MESH)
    pl.semaphore_wait(barrier, len(masks))


def send(src, dst, send_sem, recv_sem, mask):
    return pltpu.make_async_remote_copy(
        src_ref=src,
        dst_ref=dst,
        send_sem=send_sem,
        recv_sem=recv_sem,
        device_id=partner(mask),
        device_id_type=MESH,
    )


def spatial_forward(*refs, groups, width, frames):
    videos, refs = refs[:groups], refs[groups:]
    mod_ref, qkv_ref, out_ref, refs = refs[0], refs[1], refs[2], refs[3:]
    in_ref, proj_ref, mix_ref, branch_ref, refs = refs[0], refs[1], refs[2], refs[3], refs[4:]
    first_own, firsts, refs = refs[0], refs[1:groups], refs[groups:]
    out_buf, first_sems = refs
    frame = pl.program_id(0)
    others = range(1, groups)

    def first_copy(j, f):
        return send(
            out_buf.at[j - 1, f],
            firsts[j - 1].at[f],
            first_sems.at[0, j - 1, f],
            first_sems.at[1, j - 1, f],
            j,
        )

    @pl.when(frame == 0)
    def _():
        greet(list(others))

    mod = mod_ref[...]
    video = jnp.concatenate([v[...].reshape(-1, width) for v in videos], 0).astype(F32)
    normed, _ = normalize(video)
    entry = (normed * (1.0 + part_of(mod, 1, width)) + part_of(mod, 0, width)).astype(BF)
    in_ref[...] = entry
    proj_ref[...] = mm(entry, qkv_ref[...]).astype(BF)
    half = video.shape[0] // 2
    share = video.shape[0] // groups
    for part in (1, 0):
        rows = slice(part * half, (part + 1) * half)

        def pair(index, carry):
            mixed = attend_slab(
                proj_ref[rows, slab_at(index)],
                proj_ref[:, slab_at(index, width)],
                proj_ref[:, slab_at(index, 2 * width)],
                None,
            )
            mix_ref[rows, slab_at(index)] = mixed.astype(BF)
            return carry

        lax.fori_loop(0, width // SLAB, pair, 0)
        branch = mm(mix_ref[rows, :], out_ref[...])
        first = (video[rows] + part_of(mod, 2, width) * branch).astype(BF)
        branch_ref[rows, :] = branch.astype(BF)
        for j in range(part * groups // 2, (part + 1) * groups // 2):
            piece = first[j * share - part * half : (j + 1) * share - part * half]
            if j == 0:
                first_own[...] = piece.reshape(first_own.shape)
            else:
                out_buf[j - 1, frame] = piece
                first_copy(j, frame).start()

    @pl.when(frame == frames - 1)
    def _():
        for j in others:
            for f in range(frames):
                first_copy(j, f).wait()


def middle_forward(length_ref, keep_ref, *refs, groups, width, per_chunk, chunks):
    pieces, cot_all, refs = refs[:groups], refs[groups], refs[groups + 1 :]
    mod_ref, qkv_ref, tout_ref, cq_ref, text_ref, cout_ref = refs[:6]
    tin_ref, tproj_ref, tmix_ref, cin_ref, cq_out, cmix_ref, mlp_ref, mid_ref, third_ref = refs[6:15]
    cots, (cot_buf, load_sems, cot_sems) = refs[15 : 15 + groups], refs[15 + groups :]
    place = lax.axis_index("wide")

    def cot_load(j):
        source = cot_all.at[:, jnp.bitwise_xor(place, j)]
        return pltpu.make_async_copy(source, cot_buf.at[j], load_sems.at[j])

    def cot_copy(j):
        if j == 0:
            return pltpu.make_async_copy(cot_buf.at[0], cots[0], cot_sems.at[0, 0])
        return send(cot_buf.at[j], cots[j], cot_sems.at[0, j], cot_sems.at[1, j], j)

    @pl.when(pl.program_id(0) == 0)
    def _():
        for j in range(groups):
            cot_load(j).start()
        greet(list(range(1, groups)))
        for j in range(groups):
            cot_load(j).wait()
            cot_copy(j).start()

    mod = mod_ref[...]
    first = jnp.concatenate([p[...].reshape(-1, width) for p in pieces], 0).astype(F32)
    rows = first.shape[0]
    normed, _ = normalize(first)
    entry = normed.astype(BF)
    tin_ref[...] = entry
    tproj_ref[...] = mm(entry, qkv_ref[...]).astype(BF)
    same = frame_mask(rows, per_chunk)

    def pair(index, carry):
        mixed = attend_slab(
            tproj_ref[:, slab_at(index)],
            tproj_ref[:, slab_at(index, width)],
            tproj_ref[:, slab_at(index, 2 * width)],
            same,
        )
        tmix_ref[:, slab_at(index)] = mixed.astype(BF)
        return carry

    lax.fori_loop(0, width // SLAB, pair, 0)
    keep = (1 - keep_ref[0]).astype(F32)
    mid = first + keep * mm(tmix_ref[...], tout_ref[...])
    mid_ref[...] = mid
    normed, _ = normalize(mid)
    entry = normed.astype(BF)
    cin_ref[...] = entry
    cq_out[...] = mm(entry, cq_ref[...]).astype(BF)
    keys = text_ref.shape[0]
    valid = lax.broadcasted_iota(jnp.int32, (rows, keys), 1) < length_ref[0]

    def cross_pair(index, carry):
        mixed = attend_slab(
            cq_out[:, slab_at(index)],
            text_ref[:, slab_at(index)],
            text_ref[:, slab_at(index, width)],
            valid,
        )
        cmix_ref[:, slab_at(index)] = mixed.astype(BF)
        return carry

    lax.fori_loop(0, width // SLAB, cross_pair, 0)
    third = mid + mm(cmix_ref[...], cout_ref[...])
    third_ref[...] = third
    normed, _ = normalize(third)
    mlp_ref[...] = (normed * (1.0 + part_of(mod, 4, width)) + part_of(mod, 3, width)).astype(BF)

    @pl.when(pl.program_id(0) == chunks - 1)
    def _():
        for j in range(groups):
            cot_copy(j).wait()


def mlp_both(*refs, groups, width, steps):
    cots, refs = refs[:groups], refs[groups:]
    mlp_ref, third_ref, mod_ref, win_ref, wout_ref = refs[:5]
    sum_in, sum_out, dmlp_ref, dgate_ref = refs[5:9]
    results, scratch = refs[9 : 9 + groups], refs[9 + groups :]
    mlp_t, dbranch, branch, send_in, recv_in, send_out, keep_out, recv_out, in_sems, out_sems = scratch
    step = pl.program_id(0)
    half = steps // 2
    core = jnp.bitwise_and(lax.axis_index("wide"), 1)
    mod = mod_ref[...]
    gate = part_of(mod, 5, width)
    tokens = mlp_ref.shape[0]
    chunks = tokens // ROWS
    share = ROWS // groups

    def block_at(s):
        side = jnp.where(s < half, 1 - core, core)
        return side * half + lax.rem(s, half)

    def in_copy(s):
        return send(send_in.at[s], recv_in.at[s], in_sems.at[0, s], in_sems.at[1, s], 1)

    def out_copy(s):
        block = block_at(s)
        return send(
            send_out.at[block], recv_out.at[block], out_sems.at[0, block], out_sems.at[1, block], 1
        )

    @pl.when(step == 0)
    def _():
        greet([1])
        mlp_t[...] = mlp_ref[...].T
        for k in range(chunks):
            for j in range(groups):
                rows = pl.ds(k * ROWS + j * share, share)
                cot = cots[j][:, k].reshape(share, width).astype(F32)
                dbranch[rows, :] = (gate * cot).astype(BF)
        branch[...] = jnp.zeros_like(branch)
        dmlp_ref[...] = jnp.zeros_like(dmlp_ref)

    @pl.when(step >= 1)
    def _():
        out_copy(step - 1).start()

    @pl.when(jnp.logical_and(step >= 1, step <= half))
    def _():
        in_copy(step - 1).start()

    pre = mm(mlp_ref[...], win_ref[...])
    d_hidden = mm_nt(dbranch[...], wout_ref[...])
    square = pre * pre
    bend = jnp.tanh(0.7978845608 * pre * (1.0 + 0.044715 * square))
    ramp = 0.5 * (1.0 + bend)
    hidden = (pre * ramp).astype(BF)
    slope = ramp + 0.5 * pre * (1.0 - bend * bend) * (
        0.7978845608 * (1.0 + (3.0 * 0.044715) * square)
    )
    d_pre = (d_hidden * slope).astype(BF)
    hidden_t = hidden.T
    side = width // 2
    block = block_at(step)
    send_out[block] = mm(
        hidden_t, dbranch[:, pl.ds(pl.multiple_of((1 - core) * side, 128), side)]
    ).astype(BF)
    keep_out[block] = mm(
        hidden_t, dbranch[:, pl.ds(pl.multiple_of(core * side, 128), side)]
    ).astype(BF)
    grad_in = mm(mlp_t[...], d_pre)

    @pl.when(step < half)
    def _():
        send_in[step] = grad_in.astype(BF)

    @pl.when(step >= half)
    def _():
        in_copy(step - half).wait_recv()
        sum_in[...] = (grad_in + recv_in[step - half].astype(F32)).astype(BF)

    branch[...] += mm(hidden, wout_ref[...])
    dmlp_ref[...] += mm_nt(d_pre, win_ref[...])

    @pl.when(step == steps - 1)
    def _():
        out_copy(steps - 1).start()
        total = jnp.zeros((1, width), F32)
        for k in range(chunks):
            for j in range(groups):
                rows = pl.ds(k * ROWS + j * share, share)
                cot = cots[j][:, k].reshape(share, width).astype(F32)
                piece = branch[rows, :]
                total = total + jnp.sum(cot * piece, 0, keepdims=True)
                out = (third_ref[rows, :] + gate * piece).astype(BF)
                results[j][:, k] = out.reshape(results[j][:, k].shape)
        dgate_ref[...] = total
        for s in range(half):
            in_copy(s).wait_send()
        deep = send_out.shape[1]
        for s in range(steps):
            out_copy(s).wait_send()
            out_copy((s + half) % steps).wait_recv()
            block = block_at((s + half) % steps)
            rows = pl.ds(pl.multiple_of(block * deep, 16), deep)
            sum_out[rows, :] = (
                keep_out[block].astype(F32) + recv_out[block].astype(F32)
            ).astype(BF)


def middle_backward(length_ref, keep_ref, *refs, groups, width, per_chunk):
    cots, refs = refs[:groups], refs[groups:]
    dmlp_ref, third_ref, mid_ref, mod_ref = refs[:4]
    tin_ref, tproj_ref, cq_in, text_ref = refs[4:8]
    cout_ref, cq_ref, tout_ref, tqkv_ref = refs[8:12]
    first_refs, refs = refs[12 : 12 + groups], refs[12 + groups :]
    dcb_ref, dcq_ref, dtext_ref, dtb_ref, dtp_ref, dmod_ref = refs[:6]
    dfirsts = refs[6 : 6 + groups]
    text_acc, work = refs[6 + groups :]
    chunk = pl.program_id(0)
    mod = mod_ref[...]

    @pl.when(chunk == 0)
    def _():
        text_acc[...] = jnp.zeros_like(text_acc)
        dmod_ref[...] = jnp.zeros_like(dmod_ref)

    cot = jnp.concatenate([p[...].reshape(-1, width) for p in cots], 0).astype(F32)
    rows = cot.shape[0]
    d_mlp = dmlp_ref[...]
    normed, inv_std = normalize(third_ref[...])
    dmod_ref[0:1, :] += jnp.sum(d_mlp, 0, keepdims=True)
    dmod_ref[1:2, :] += jnp.sum(d_mlp * normed, 0, keepdims=True)
    d_third = cot + norm_back(d_mlp * (1.0 + part_of(mod, 4, width)), normed, inv_std)
    d_branch = d_third.astype(BF)
    dcb_ref[...] = d_branch
    work[...] = mm_nt(d_branch, cout_ref[...]).astype(BF)
    keys = text_ref.shape[0]
    valid = lax.broadcasted_iota(jnp.int32, (rows, keys), 1) < length_ref[0]

    def cross_pair(index, carry):
        at, after = slab_at(index), slab_at(index, width)
        grad_q, grad_k, grad_v = attend_slab_back(
            cq_in[:, at], text_ref[:, at], text_ref[:, after], work[:, at], valid
        )
        dcq_ref[:, at] = grad_q.astype(BF)
        text_acc[:, at] += grad_k
        text_acc[:, after] += grad_v
        return carry

    lax.fori_loop(0, width // SLAB, cross_pair, 0)
    dtext_ref[...] = text_acc[...].astype(BF)
    normed, inv_std = normalize(mid_ref[...])
    d_mid = d_third + norm_back(mm_nt(dcq_ref[...], cq_ref[...]), normed, inv_std)
    keep = (1 - keep_ref[0]).astype(F32)
    d_branch = (keep * d_mid).astype(BF)
    dtb_ref[...] = d_branch
    work[...] = mm_nt(d_branch, tout_ref[...]).astype(BF)
    same = frame_mask(rows, per_chunk)

    def pair(index, carry):
        at, after, last = slab_at(index), slab_at(index, width), slab_at(index, 2 * width)
        grad_q, grad_k, grad_v = attend_slab_back(
            tproj_ref[:, at], tproj_ref[:, after], tproj_ref[:, last], work[:, at], same
        )
        dtp_ref[:, at] = grad_q.astype(BF)
        dtp_ref[:, after] = grad_k.astype(BF)
        dtp_ref[:, last] = grad_v.astype(BF)
        return carry

    lax.fori_loop(0, width // SLAB, pair, 0)
    first = jnp.concatenate([p[...].reshape(-1, width) for p in first_refs], 0).astype(F32)
    normed, inv_std = normalize(first)
    d_first = d_mid + norm_back(mm_nt(dtp_ref[...], tqkv_ref[...]), normed, inv_std)
    d_first = d_first.astype(BF)
    share = rows // groups
    for j, ref in enumerate(dfirsts):
        ref[...] = d_first[j * share : (j + 1) * share].reshape(ref.shape)


def spatial_backward(*refs, groups, width):
    dfirsts, refs = refs[:groups], refs[groups:]
    mod_ref, branch_ref, proj_ref, out_ref = refs[:4]
    dsb_ref, dproj_ref, dgate_ref, work = refs[4:]
    frame = pl.program_id(0)
    mod = mod_ref[...]

    @pl.when(frame == 0)
    def _():
        dgate_ref[...] = jnp.zeros_like(dgate_ref)

    d_first = jnp.concatenate([p[...].reshape(-1, width) for p in dfirsts], 0).astype(F32)
    dgate_ref[...] += jnp.sum(d_first * branch_ref[...].astype(F32), 0, keepdims=True)
    d_branch = (part_of(mod, 2, width) * d_first).astype(BF)
    dsb_ref[...] = d_branch
    work[...] = mm_nt(d_branch, out_ref[...]).astype(BF)

    def pair(index, carry):
        at, after, last = slab_at(index), slab_at(index, width), slab_at(index, 2 * width)
        grad_q, grad_k, grad_v = attend_slab_back(
            proj_ref[:, at], proj_ref[:, after], proj_ref[:, last], work[:, at], None
        )
        dproj_ref[:, at] = grad_q.astype(BF)
        dproj_ref[:, after] = grad_k.astype(BF)
        dproj_ref[:, last] = grad_v.astype(BF)
        return carry

    lax.fori_loop(0, width // SLAB, pair, 0)


def video_backward(where_ref, *refs, groups, width):
    videos, refs = refs[:groups], refs[groups:]
    dfirsts, refs = refs[:groups], refs[groups:]
    results, refs = refs[:groups], refs[groups:]
    mod_ref, dproj_ref, qkv_ref, grad_ref, result_ref, dmod_ref = refs
    frame = pl.program_id(0)
    place = where_ref[0]
    mod = mod_ref[...]

    @pl.when(frame == 0)
    def _():
        dmod_ref[...] = jnp.zeros_like(dmod_ref)

    video = jnp.concatenate([v[...].reshape(-1, width) for v in videos], 0).astype(F32)
    d_first = jnp.concatenate([p[...].reshape(-1, width) for p in dfirsts], 0).astype(F32)
    normed, inv_std = normalize(video)
    d_in = mm_nt(dproj_ref[...], qkv_ref[...])
    dmod_ref[0:1, :] += jnp.sum(d_in, 0, keepdims=True)
    dmod_ref[1:2, :] += jnp.sum(d_in * normed, 0, keepdims=True)
    grad = d_first + norm_back(d_in * (1.0 + part_of(mod, 1, width)), normed, inv_std)
    share = grad.shape[0] // groups
    for j in range(groups):
        slot = jnp.bitwise_xor(place, j)
        grad_ref[0, slot] = grad[j * share : (j + 1) * share]
        result_ref[0, slot] = results[j][...].reshape(share, width)


class Stream:
    def __init__(self, cur, recv, sems, order, cols, fin, source=None):
        self.cur, self.recv, self.sems, self.fin = cur, recv, sems, fin
        self.order, self.cols, self.source = order, cols, source
        self.bits = sorted(order, reverse=True)
        wide = lax.axis_size("wide")
        me = lax.axis_index("narrow") * wide + lax.axis_index("wide")
        self.mine = {b: jnp.bitwise_and(lax.shift_right_logical(me, b), 1) for b in order}

    def where(self, stage):
        spots = []
        for b in self.bits:
            at = self.order.index(b)
            if at < stage:
                spots.append(self.mine[b])
            elif at == stage:
                spots.append(1 - self.mine[b])
            else:
                spots.append(slice(None))
        return tuple(spots) + (slice(None), self.cols)

    def copy(self, stage):
        base = self.cur if stage > 0 or self.source is None else self.source
        return send(
            base.at[self.where(stage)],
            self.recv[stage],
            self.sems.at[0, stage],
            self.sems.at[1, stage],
            1 << self.order[stage],
        )

    def add(self, stage):
        self.copy(stage).wait()
        left = [b for b in self.bits if self.order.index(b) > stage]
        count = len(left)

        def summed(place):
            spot = tuple(place.get(b, self.mine[b]) for b in self.bits) + (slice(None), self.cols)
            inner = tuple(place[b] for b in left)
            return spot, self.cur[spot].astype(F32) + self.recv[stage][inner].astype(F32)

        if not left:
            _, total = summed({})
            self.fin[:, :, self.cols] = total.reshape(self.fin.shape[0], -1, total.shape[1])
            return

        def body(i, carry):
            place = {
                b: jnp.bitwise_and(lax.shift_right_logical(i, count - 1 - k), 1)
                for k, b in enumerate(left)
            }
            spot, total = summed(place)
            self.cur[spot] = total.astype(BF)
            return carry

        lax.fori_loop(0, 1 << count, body, 0)

    def step(self, stage):
        self.add(stage)
        if stage + 1 < len(self.order):
            self.copy(stage + 1).start()


def stream_scratch(rows, cols, bits, parts):
    cols = cols // parts
    shapes = [pltpu.VMEM((2,) * k + (rows, cols), BF) for k in range(bits - 1, -1, -1)]
    return [shapes + [pltpu.SemaphoreType.DMA((2, bits))] for _ in range(parts)]


def stream_orders(wide_bits, bits):
    z_bits = [b for b in range(2, bits + 1) if b != wide_bits]
    return [
        [wide_bits, 1] + z_bits,
        [1, z_bits[0], wide_bits] + z_bits[1:],
        [z_bits[0], wide_bits, 1] + z_bits[1:],
    ]


def store_flat(out, value, first, pitch):
    for t in range(value.shape[1] // 128):
        out[pl.ds(first + t, value.shape[0], stride=pitch), :] = value[:, t * 128 : (t + 1) * 128]


class Finish:
    def __init__(self, fin, fin_in, sems, flats, outs):
        self.fin, self.fin_in, self.sems, self.flats, self.outs = fin, fin_in, sems, flats, outs
        self.core = jnp.bitwise_and(lax.axis_index("wide"), 1)

    def swap(self):
        return send(
            self.fin.at[1 - self.core], self.fin_in, self.sems.at[0], self.sems.at[1], 1
        )

    def writes(self):
        return [
            pltpu.make_async_copy(flat, out, self.sems.at[2 + k])
            for k, (flat, out) in enumerate(zip(self.flats, self.outs))
        ]

    def store(self):
        self.swap().wait()
        own, other = self.fin[self.core], self.fin_in[...]
        low = jnp.where(self.core == 0, own, other)
        high = jnp.where(self.core == 0, other, own)
        start = 0
        for flat in self.flats:
            pitch = flat.shape[0] // own.shape[0]
            half = pitch * 128 // 2
            store_flat(flat, low[:, start : start + half], 0, pitch)
            store_flat(flat, high[:, start : start + half], pitch // 2, pitch)
            start += half
        for write in self.writes():
            write.start()

    def wait(self):
        for write in self.writes():
            write.wait()


def grads_rows(pairs, side, part_at, dest, extra=None):
    rows = pl.ds(pl.multiple_of(part_at * ROWS, ROWS), ROWS)
    start = 0
    for left, right in pairs:
        part = right.shape[1] // 2
        cols = pl.ds(pl.multiple_of(side * part, 128), part)
        value = mm_tn(left[:, rows], right[:, cols])
        spot = (rows, slice(start, start + part))
        if extra is not None:
            value = value + extra[spot].astype(F32)
        dest[spot] = value.astype(BF)
        start += part


def flat_rows(ref):
    return ref.reshape(-1, ref.shape[-1])


def with_scratch(body, scratch):
    form = jax.tree.structure(scratch)
    count = form.num_leaves

    def kernel(*refs):
        body(*refs[:-count], jax.tree.unflatten(form, refs[-count:]))

    return kernel


def all_bits():
    total = lax.axis_size("wide") * lax.axis_size("narrow")
    return total.bit_length() - 1


def piece_rows(ref, chunk):
    groups = ref.shape[0]
    width = ref.shape[-1]
    return jnp.concatenate([ref[j, :, chunk].reshape(-1, width) for j in range(groups)], 0)


def frame_rows(ref, frame):
    width = ref.shape[-1]
    return jnp.concatenate([ref[j, frame].reshape(-1, width) for j in range(ref.shape[0])], 0)


def backward(length_ref, keep_ref, ins, outs, scratch):
    a, o, s = Names(**ins), Names(**outs), Names(**scratch)
    groups = len(a.cots)
    tokens, width = a.dmlp.shape
    chunks = tokens // ROWS
    frames = a.video.shape[0]
    share = ROWS // groups
    bits = all_bits() - 1
    wide_bits = lax.axis_size("wide").bit_length() - 1
    place, narrow_at = lax.axis_index("wide"), lax.axis_index("narrow")
    core = jnp.bitwise_and(place, 1)
    others = range(1, groups)
    counter = itertools.count()

    def load(src, dst):
        copy = pltpu.make_async_copy(src, dst, s.local.at[next(counter)])
        copy.start()
        return copy

    def wait_all(copies):
        for copy in copies:
            copy.wait()

    cross_loads = [load(a.cots[j], s.cots.at[j]) for j in range(groups)]
    cross_loads += [load(a.dmlp, s.dmlp), load(a.third, s.third), load(a.cout, s.cout)]
    cross_loads += [load(a.cq, s.cq), load(a.text, s.text)]
    cross_grad_loads = [load(a.cin, s.cin), load(a.words, s.words), load(a.cmix, s.cmix)]
    temporal_loads = [load(a.mid, s.mid), load(a.cwq, s.cwq), load(a.tout, s.tout)]
    temporal_loads += [load(a.tproj, s.tproj), load(a.tqkv, s.tqkv)]
    temporal_loads += [load(a.firsts[j], s.firsts.at[j]) for j in range(groups)]
    sum_loads = [load(a.sum_out, s.cur_out), load(a.sum_in, s.cur_in)]

    orders = stream_orders(wide_bits, bits)

    def split(cur, parts, fin, source=None):
        third = cur.shape[-1] // len(orders)
        return [
            Stream(cur, part[:-1], part[-1], order, slice(i * third, (i + 1) * third), fin, source)
            for i, (part, order) in enumerate(zip(parts, orders))
        ]

    r_out = split(s.cur_out, s.st_out, s.fin_out, a.sum_out)
    r_in = split(s.cur_in, s.st_in, s.fin_in, a.sum_in)
    r_c = split(s.cur_c, s.st_c, s.fin_c)
    r_t = split(s.cur_t, s.st_t, s.fin_t)
    r_s = split(s.cur_s, s.st_s, s.fin_s)
    e_out = Finish(s.fin_out, s.fin_out_in, s.end_out, s.flat_out, o.mlp_out)
    e_in = Finish(s.fin_in, s.fin_in_in, s.end_in, s.flat_in, o.mlp_in)
    e_c = Finish(s.fin_c, s.fin_c_in, s.end_c, s.flat_c, o.cross)
    e_t = Finish(s.fin_t, s.fin_t_in, s.end_t, s.flat_t, o.temporal)
    e_s = Finish(s.fin_s, s.fin_s_in, s.end_s, s.flat_s, o.spatial)
    greet(list(others) + [1 << b for b in range(wide_bits, bits + 1)])
    r_out[2].copy(0).start()
    r_in[1].copy(0).start()
    r_in[2].copy(0).start()
    r_out[1].copy(0).start()
    r_in[0].copy(0).start()

    def result_copy(j):
        target = o.result.at[:, place]
        held = s.dcq.reshape(groups, *a.results[0].shape).at[j]
        if j == 0:
            return pltpu.make_async_copy(held, target, s.result_sems.at[0, 0])
        return send(held, target, s.result_sems.at[0, j], s.result_sems.at[1, j], j)

    keys = s.text.shape[0]
    valid = lax.broadcasted_iota(jnp.int32, (ROWS, keys), 1) < length_ref[0]
    mod_scale = a.mod[:, 4 * width : 5 * width]
    work = s.work
    s.text_acc[...] = jnp.zeros_like(s.text_acc)
    s.mod_sum[...] = jnp.zeros_like(s.mod_sum)
    wait_all(cross_loads)

    def cross_chunk(k, carry):
        rows = pl.ds(pl.multiple_of(k * ROWS, ROWS), ROWS)
        cot = piece_rows(s.cots, k).astype(F32)
        d_mlp = s.dmlp[rows, :]
        normed, inv_std = normalize(s.third[rows, :])
        s.mod_sum[3:4, :] += jnp.sum(d_mlp, 0, keepdims=True)
        s.mod_sum[4:5, :] += jnp.sum(d_mlp * normed, 0, keepdims=True)
        d_third = cot + norm_back(d_mlp * (1.0 + mod_scale), normed, inv_std)
        s.dmlp[rows, :] = d_third
        d_branch = d_third.astype(BF)
        s.dcb[rows, :] = d_branch
        work[...] = mm_nt(d_branch, s.cout[...]).astype(BF)

        def pair(index, inner):
            at, after = slab_at(index), slab_at(index, width)
            grad_q, grad_k, grad_v = attend_slab_back(
                s.cq[rows, at], s.text[:, at], s.text[:, after], work[:, at], valid
            )
            s.dcq[rows, at] = grad_q.astype(BF)
            s.text_acc[:, at] += grad_k
            s.text_acc[:, after] += grad_v
            return inner

        lax.fori_loop(0, width // SLAB, pair, 0)
        return carry

    lax.fori_loop(0, chunks, cross_chunk, 0)
    s.dtext[...] = s.text_acc[...].astype(BF)
    wait_all(sum_loads)
    video_loads = [load(a.video.at[:, jnp.bitwise_xor(place, j)], s.cots.at[j]) for j in range(groups)]
    late_loads = [load(a.sout, s.cout), load(a.sbranch, s.cq)]

    wait_all(cross_grad_loads)
    pairs_c = [(s.cin, s.dcq), (s.words, s.dtext), (s.cmix, s.dcb)]

    def core_copy(cur, k, m):
        rows = pl.ds(pl.multiple_of(m * ROWS, ROWS), ROWS)
        return send(
            s.send.at[rows], flat_rows(cur).at[rows],
            s.core_sems.at[0, k, m], s.core_sems.at[1, k, m], 1,
        )

    def other_half(pairs, cur, k):
        def body(m, carry):
            grads_rows(pairs, 1 - core, m, s.send)
            core_copy(cur, k, m).start()
            return carry

        lax.fori_loop(0, width // ROWS, body, 0)

    def own_half(pairs, cur, k):
        def body(m, carry):
            core_copy(cur, k, m).wait()
            grads_rows(pairs, core, m, flat_rows(cur), flat_rows(cur))
            return carry

        lax.fori_loop(0, width // ROWS, body, 0)

    wait_all(temporal_loads)
    keep = (1 - keep_ref[0]).astype(F32)
    same = frame_mask(ROWS, a.firsts[0].shape[2])
    tproj, dtp = s.tproj, s.dtp

    def temporal_chunk(k):
        rows = slice(k * ROWS, (k + 1) * ROWS)
        normed, inv_std = normalize(s.mid[rows, :])
        d_mid = s.dmlp[rows, :] + norm_back(
            mm_nt(s.dcq[rows, :], s.cwq[...]), normed, inv_std
        )
        d_branch = (keep * d_mid).astype(BF)
        s.dtb[rows, :] = d_branch
        work[...] = mm_nt(d_branch, s.tout[...]).astype(BF)

        def pair(index, carry):
            at, after, last = slab_at(index), slab_at(index, width), slab_at(index, 2 * width)
            grad_q, grad_k, grad_v = attend_slab_back(
                tproj[rows, at], tproj[rows, after], tproj[rows, last], work[:, at], same
            )
            dtp[rows, at] = grad_q.astype(BF)
            dtp[rows, after] = grad_k.astype(BF)
            dtp[rows, last] = grad_v.astype(BF)
            return carry

        lax.fori_loop(0, width // SLAB, pair, 0)
        normed, inv_std = normalize(piece_rows(s.firsts, k).astype(F32))
        d_first = d_mid + norm_back(mm_nt(dtp[rows, :], s.tqkv[...]), normed, inv_std)
        d_first = d_first.astype(BF)
        for j in range(groups):
            buf = s.dfirsts if j == 0 else s.firsts
            buf[j, :, k] = d_first[j * share : (j + 1) * share].reshape(
                buf.shape[1:2] + buf.shape[3:]
            )

    def first_copy(j, k):
        return send(
            s.firsts.at[j, :, k], s.dfirsts.at[j, :, k],
            s.first_sems.at[0, j, k], s.first_sems.at[1, j, k], j,
        )

    gate = a.mod[:, 2 * width : 3 * width]
    scale = a.mod[:, width : 2 * width]

    def spatial_frame(f):
        rows = slice(f * ROWS, (f + 1) * ROWS)
        d_first = frame_rows(s.dfirsts, f).astype(F32)
        s.mod_sum[2:3, :] += jnp.sum(d_first * s.cq[rows, :].astype(F32), 0, keepdims=True)
        d_branch = (gate * d_first).astype(BF)
        s.dcb[rows, :] = d_branch
        work[...] = mm_nt(d_branch, s.cout[...]).astype(BF)

        def pair(index, carry):
            at, after, last = slab_at(index), slab_at(index, width), slab_at(index, 2 * width)
            grad_q, grad_k, grad_v = attend_slab_back(
                tproj[rows, at], tproj[rows, after], tproj[rows, last], work[:, at], None
            )
            dtp[rows, at] = grad_q.astype(BF)
            dtp[rows, after] = grad_k.astype(BF)
            dtp[rows, last] = grad_v.astype(BF)
            return carry

        lax.fori_loop(0, width // SLAB, pair, 0)

    def video_frame(f, carry):
        rows = pl.ds(pl.multiple_of(f * ROWS, ROWS), ROWS)
        video = frame_rows(s.cots, f).astype(F32)
        d_first = frame_rows(s.dfirsts, f).astype(F32)
        normed, inv_std = normalize(video)
        d_in = mm_nt(dtp[rows, :], s.tqkv[...])
        s.mod_sum[0:1, :] += jnp.sum(d_in, 0, keepdims=True)
        s.mod_sum[1:2, :] += jnp.sum(d_in * normed, 0, keepdims=True)
        grad = d_first + norm_back(d_in * (1.0 + scale), normed, inv_std)
        for j in range(groups):
            slot = jnp.bitwise_xor(place, j)
            at = pl.ds(pl.multiple_of(f * ROWS + slot * share, share), share)
            s.third[at, :] = grad[j * share : (j + 1) * share]
        return carry

    mod_all = s.mod_all

    def mod_copy(b):
        sems = s.mod_sems.at[0, b], s.mod_sems.at[1, b]
        if b < wide_bits:
            return send(s.mod_sum, s.mod_in.at[b], *sems, 1 << b)
        size = 1 << (b - wide_bits)
        span = mod_all.at[pl.ds(lax.div(narrow_at, size) * size, size)]
        return send(span, span, *sems, 1 << b)

    def mod_step(b):
        mod_copy(b).wait()
        if b < wide_bits:
            s.mod_sum[...] = s.mod_sum[...] + s.mod_in[b]
        if b == wide_bits - 1:
            mod_all[narrow_at] = s.mod_sum[...]
            mod_all[narrow_at, 6:7, :] = a.silu[...]
        if b < bits:
            mod_copy(b + 1).start()

    def ada_rows():
        mine = o.ada.shape[0] // (6 * width // 128)
        me = narrow_at * lax.axis_size("wide") + place
        row = lax.broadcasted_iota(jnp.int32, (mine, width), 0)
        col = lax.broadcasted_iota(jnp.int32, (mine, width), 1)
        picks = (col == me * mine + row).astype(F32).astype(BF)
        silu_mine = mm_nt(picks, mod_all[:, 6, :].astype(BF))
        pitch = 6 * width // 128
        for part in range(6):
            rows = 0.0
            for c in range(mod_all.shape[0]):
                rows = rows + silu_mine[:, c : c + 1] * mod_all[c, part : part + 1, :]
            store_flat(s.flat_ada, rows, part * width // 128, pitch)
        return load(s.flat_ada, o.ada)

    r_in[0].step(0)
    r_out[0].copy(0).start()
    r_in[1].step(0)
    other_half(pairs_c, s.cur_c, 0)
    temporal_chunk(0)
    for j in others:
        first_copy(j, 0).start()
    r_out[1].step(0)
    r_out[2].step(0)
    own_half(pairs_c, s.cur_c, 0)
    temporal_grad_loads = [load(a.tin, s.cin), load(a.tmix, s.cmix)]
    r_c[1].copy(0).start()
    r_c[2].copy(0).start()
    r_c[0].copy(0).start()
    r_in[0].step(1)
    temporal_chunk(1)
    late_loads += [load(a.sproj, s.tproj), load(a.sqkv, s.tqkv)]
    held = s.dcq.reshape(groups, *a.results[0].shape)
    result_loads = [load(a.results[j], held.at[j]) for j in range(groups)]
    for j in others:
        first_copy(j, 1).start()
    wait_all(temporal_grad_loads)
    pairs_t = [(s.cin, dtp), (s.cmix, s.dtb)]
    other_half(pairs_t, s.cur_t, 1)
    r_out[2].step(1)
    r_in[1].step(1)
    r_out[0].step(0)
    r_out[1].step(1)
    r_in[2].step(0)
    for j in others:
        first_copy(j, 0).wait()
    r_c[1].step(0)
    r_c[2].step(0)
    r_c[0].step(0)
    own_half(pairs_t, s.cur_t, 1)
    spatial_grad_loads = [load(a.sin, s.cin), load(a.smix, s.cmix)]
    r_t[2].copy(0).start()
    r_t[0].copy(0).start()
    for j in others:
        first_copy(j, 1).wait()
    wait_all(late_loads)
    spatial_frame(0)
    r_out[2].step(2)
    r_out[0].step(1)
    r_in[0].step(2)
    r_in[1].step(2)
    r_c[1].step(1)
    r_t[1].copy(0).start()
    r_out[1].step(2)
    r_in[2].step(1)
    spatial_frame(1)
    r_out[0].step(2)
    r_c[0].step(1)
    wait_all(spatial_grad_loads)
    pairs_s = [(s.cin, dtp), (s.cmix, s.dcb)]
    other_half(pairs_s, s.cur_s, 2)
    r_t[1].step(0)
    r_t[0].step(0)
    r_t[2].step(0)
    own_half(pairs_s, s.cur_s, 2)
    r_s[0].copy(0).start()
    r_s[1].copy(0).start()
    r_s[2].copy(0).start()
    r_c[2].step(1)
    r_c[1].step(2)
    r_t[1].step(1)
    r_c[0].step(2)
    r_out[1].step(3)
    r_t[0].step(1)
    r_t[2].step(1)
    r_c[1].step(3)
    wait_all(video_loads)
    lax.fori_loop(0, frames, video_frame, 0)
    grad_write = load(s.third, o.video_grad)
    s.mod_sum[5:6, :] = a.dgate_two[...]
    mod_copy(0).start()
    r_s[2].step(0)
    r_s[1].step(0)
    r_in[2].step(2)
    r_c[2].step(2)
    r_s[0].step(0)
    mod_step(0)
    r_t[1].step(2)
    r_in[2].step(3)
    r_in[1].step(3)
    r_t[2].step(2)
    r_s[2].step(1)
    mod_step(1)
    r_out[2].step(3)
    r_s[1].step(1)
    r_c[2].step(3)
    r_in[0].step(3)
    wait_all(result_loads)
    for j in range(groups):
        result_copy(j).start()
    r_s[0].step(1)
    mod_step(2)
    r_t[0].step(2)
    r_out[0].step(3)
    r_s[2].step(2)
    r_t[2].step(3)
    r_t[1].step(3)
    mod_step(3)
    r_s[1].step(2)
    e_in.swap().start()
    r_s[0].step(2)
    r_s[2].step(3)
    e_out.swap().start()
    e_in.store()
    r_c[0].step(3)
    r_s[1].step(3)
    mod_step(4)
    ada_write = ada_rows()
    r_t[0].step(3)
    e_out.store()
    e_t.swap().start()
    e_c.swap().start()
    r_s[0].step(3)
    e_t.store()
    e_s.swap().start()
    e_c.store()
    for j in range(groups):
        result_copy(j).wait()
    grad_write.wait()
    e_out.wait()
    e_in.wait()
    e_c.wait()
    e_t.wait()
    e_s.store()
    ada_write.wait()
    e_s.wait()


def copy_out(ins, outs, bufs, in_sems, out_sems):
    ins, outs, bufs = jax.tree.leaves(ins), jax.tree.leaves(outs), jax.tree.leaves(bufs)
    reads = [
        pltpu.make_async_copy(src, buf, in_sems.at[k])
        for k, (src, buf) in enumerate(zip(ins, bufs))
    ]
    writes = [
        pltpu.make_async_copy(buf, dst, out_sems.at[k])
        for k, (buf, dst) in enumerate(zip(bufs, outs))
    ]
    for read in reads:
        read.start()
    for read, write in zip(reads, writes):
        read.wait()
        write.start()
    for write in writes:
        write.wait()


def weight_grads(core_ref, *refs, count):
    pairs, outs = refs[: 2 * count], refs[2 * count :]
    core = core_ref[0]
    for sign, out in enumerate(outs):
        side = 1 - core if sign == 0 else core
        start = 0
        for k in range(count):
            left, right = pairs[2 * k], pairs[2 * k + 1]
            part = right.shape[1] // 2
            cols = pl.ds(pl.multiple_of(side * part, 128), part)
            out[:, start : start + part] = mm_tn(left[...], right[:, cols]).astype(BF)
            start += part


def weight_grads_call(core, pairs):
    depth = pairs[0][0].shape[1]
    total = sum(right.shape[1] for _, right in pairs)
    tile = 256
    specs = []
    for left, right in pairs:
        specs.append(pl.BlockSpec((left.shape[0], tile), lambda m, _: (0, m)))
        specs.append(fixed(right.shape))
    shape = jax.ShapeDtypeStruct((depth, total // 2), BF)
    flops = sum(2 * left.shape[0] * depth * right.shape[1] for left, right in pairs)
    return pl.pallas_call(
        functools.partial(weight_grads, count=len(pairs)),
        grid_spec=pltpu.PrefetchScalarGridSpec(
            num_scalar_prefetch=1,
            grid=(depth // tile,),
            in_specs=specs,
            out_specs=[pl.BlockSpec((tile, total // 2), lambda m, _: (m, 0))] * 2,
        ),
        out_shape=[shape, shape],
        compiler_params=params(),
        cost_estimate=cost(flops, 8e6),
        name="weight_grads",
    )(core, *[a for pair in pairs for a in pair])


def shards(
    video,
    text_states,
    text_length,
    timestep,
    motion_free,
    ada_weight,
    spatial_qkv_weight,
    spatial_out_weight,
    temporal_qkv_weight,
    temporal_out_weight,
    cross_query_weight,
    cross_kv_weight,
    cross_out_weight,
    mlp_in_weight,
    mlp_out_weight,
    cotangent,
    *,
    mesh_shape,
):
    clips, frames, patches, width = video.shape
    if clips != 1 or patches != ROWS:
        raise ValueError("unsupported shard")
    wide, narrow = mesh_shape["wide"], mesh_shape["narrow"]
    devices = wide * narrow
    groups = wide
    here = patches // groups
    tokens = frames * patches
    chunks = tokens // ROWS
    per_chunk = here // chunks
    hidden = mlp_in_weight.shape[1]
    text_rows = text_states.shape[1]
    text_pad = -(-text_rows // 128) * 128

    wide_at = lax.axis_index("wide")
    narrow_at = lax.axis_index("narrow")
    index = narrow_at * wide + wide_at
    core = jnp.bitwise_and(wide_at, 1)
    place = wide_at.reshape(1).astype(jnp.int32)
    core_arr = core.reshape(1).astype(jnp.int32)
    wide_bits = wide.bit_length() - 1
    bits = devices.bit_length() - 1

    cot_view = cotangent.reshape(frames, groups, here, width)

    silu_time = silu_of(time_features(timestep.astype(F32), width)).astype(BF)
    mod = mm(silu_time, ada_weight)
    text_flat = text_states.reshape(text_rows, width)
    text_flat = jnp.pad(text_flat, ((0, text_pad - text_rows), (0, 0)))
    text_proj = mm(text_flat, cross_kv_weight).astype(BF)

    video_view = video.reshape(frames, groups, here, width)

    def own_patches(j):
        return pl.BlockSpec(
            (1, 1, here, width),
            lambda f, *_: (f, jnp.bitwise_xor(lax.axis_index("wide"), j), 0, 0),
        )

    def frame_piece():
        return pl.BlockSpec((1, chunks, per_chunk, width), lambda f, *_: (f, 0, 0, 0))

    def chunk_piece():
        return pl.BlockSpec((frames, 1, per_chunk, width), lambda k, *_: (0, k, 0, 0))

    def row_block(cols):
        return pl.BlockSpec((ROWS, cols), lambda f, *_: (f, 0))

    piece_shape = jax.ShapeDtypeStruct((frames, chunks, per_chunk, width), BF)

    def rows_of(cols, dtype=BF):
        return jax.ShapeDtypeStruct((tokens, cols), dtype)

    mod_spec = fixed(mod.shape)
    anywhere = pl.BlockSpec(memory_space=pl.ANY)
    own_piece = jax.ShapeDtypeStruct((frames, here, width), BF)
    outs = pl.pallas_call(
        functools.partial(spatial_forward, groups=groups, width=width, frames=frames),
        grid_spec=pltpu.PrefetchScalarGridSpec(
            num_scalar_prefetch=0,
            grid=(frames,),
            in_specs=[own_patches(j) for j in range(groups)]
            + [mod_spec, fixed(spatial_qkv_weight.shape), fixed(spatial_out_weight.shape)],
            out_specs=[row_block(width), row_block(3 * width), row_block(width), row_block(width)]
            + [pl.BlockSpec((1, here, width), lambda f, *_: (f, 0, 0))]
            + [anywhere] * (groups - 1),
            scratch_shapes=[
                pltpu.VMEM((groups - 1, frames, here, width), BF),
                pltpu.SemaphoreType.DMA((2, groups - 1, frames)),
            ],
        ),
        out_shape=[rows_of(width), rows_of(3 * width), rows_of(width), rows_of(width)]
        + [own_piece] * groups,
        compiler_params=params(collective_id=0, has_side_effects=True),
        cost_estimate=cost(8 * tokens * width * width, 10e6, tokens * patches * 12),
        name="spatial_forward",
    )(*[video_view] * groups, mod, spatial_qkv_weight, spatial_out_weight)
    spatial_in, spatial_proj, spatial_mix, spatial_branch = outs[:4]
    firsts = [p.reshape(piece_shape.shape) for p in outs[4 : 4 + groups]]

    def two_scalars(grid, in_specs, out_specs, scratch=()):
        return pltpu.PrefetchScalarGridSpec(
            num_scalar_prefetch=2,
            grid=grid,
            in_specs=in_specs,
            out_specs=out_specs,
            scratch_shapes=scratch,
        )

    outs = pl.pallas_call(
        functools.partial(
            middle_forward, groups=groups, width=width, per_chunk=per_chunk, chunks=chunks
        ),
        grid_spec=two_scalars(
            (chunks,),
            [chunk_piece() for _ in range(groups)]
            + [
                anywhere,
                mod_spec,
                fixed(temporal_qkv_weight.shape),
                fixed(temporal_out_weight.shape),
                fixed(cross_query_weight.shape),
                fixed(text_proj.shape),
                fixed(cross_out_weight.shape),
            ],
            [
                row_block(width),
                row_block(3 * width),
                row_block(width),
                row_block(width),
                row_block(width),
                row_block(width),
                row_block(width),
                row_block(width),
                row_block(width),
            ]
            + [anywhere] * groups,
            [
                pltpu.VMEM((groups, frames, here, width), BF),
                pltpu.SemaphoreType.DMA((groups,)),
                pltpu.SemaphoreType.DMA((2, groups)),
            ],
        ),
        out_shape=[
            rows_of(width),
            rows_of(3 * width),
            rows_of(width),
            rows_of(width),
            rows_of(width),
            rows_of(width),
            rows_of(width),
            rows_of(width, F32),
            rows_of(width, F32),
        ]
        + [own_piece] * groups,
        compiler_params=params(collective_id=4, has_side_effects=True),
        cost_estimate=cost(12 * tokens * width * width, 20e6, tokens * ROWS * 18),
        name="middle_forward",
    )(
        text_length,
        motion_free,
        *firsts,
        cot_view,
        mod,
        temporal_qkv_weight,
        temporal_out_weight,
        cross_query_weight,
        text_proj,
        cross_out_weight,
    )
    temporal_in, temporal_proj, temporal_mix, cross_in, cross_q, cross_mix, mlp_in, mid, third = outs[:9]
    cots = [p.reshape(piece_shape.shape) for p in outs[9:]]

    steps = 4
    wide_h = hidden // steps

    def hidden_at(step):
        half = steps // 2
        side_bit = jnp.bitwise_and(lax.axis_index("wide"), 1)
        side = jnp.where(step < half, 1 - side_bit, side_bit)
        return side * half + lax.rem(step, half)

    whole_piece = fixed((frames, chunks, per_chunk, width))
    outs = pl.pallas_call(
        functools.partial(mlp_both, groups=groups, width=width, steps=steps),
        grid_spec=pltpu.PrefetchScalarGridSpec(
            num_scalar_prefetch=0,
            grid=(steps,),
            in_specs=[whole_piece] * groups
            + [
                fixed(mlp_in.shape),
                fixed(third.shape),
                mod_spec,
                pl.BlockSpec((width, wide_h), lambda s: (0, hidden_at(s))),
                pl.BlockSpec((wide_h, width), lambda s: (hidden_at(s), 0)),
            ],
            out_specs=[
                pl.BlockSpec((width, wide_h), lambda s: (0, jnp.maximum(s - steps // 2, 0))),
                fixed((hidden, width // 2)),
                fixed((tokens, width)),
                fixed((1, width)),
            ]
            + [whole_piece] * groups,
            scratch_shapes=[
                pltpu.VMEM((width, tokens), BF),
                pltpu.VMEM((tokens, width), BF),
                pltpu.VMEM((tokens, width), F32),
                pltpu.VMEM((steps // 2, width, wide_h), BF),
                pltpu.VMEM((steps // 2, width, wide_h), BF),
                pltpu.VMEM((steps, wide_h, width // 2), BF),
                pltpu.VMEM((steps, wide_h, width // 2), BF),
                pltpu.VMEM((steps, wide_h, width // 2), BF),
                pltpu.SemaphoreType.DMA((2, steps // 2)),
                pltpu.SemaphoreType.DMA((2, steps)),
            ],
        ),
        out_shape=[
            jax.ShapeDtypeStruct((width, hidden // 2), BF),
            jax.ShapeDtypeStruct((hidden, width // 2), BF),
            rows_of(width, F32),
            jax.ShapeDtypeStruct((1, width), F32),
        ]
        + [piece_shape] * groups,
        compiler_params=params(collective_id=1, has_side_effects=True),
        cost_estimate=cost(12 * tokens * width * hidden, 25e6, tokens * hidden),
        name="mlp_both",
    )(*cots, mlp_in, third, mod, mlp_in_weight, mlp_out_weight)
    sum_in, sum_out, d_mlp_in, d_gate_two = outs[:4]
    if bits == 5 and frames == 2 and width == 768 and hidden % 768 == 0:
        chip = (2,) * (bits - 1)
        nb = bits - 1
        rows_in, rows_out = 2 * width // devices, 2 * hidden // devices
        cols_in, cols_out = hidden // 2, width // 2
        vm, sems = pltpu.VMEM, pltpu.SemaphoreType.DMA
        act = lambda cols, dtype=BF: vm((tokens, cols), dtype)
        group = vm(chip + (rows_in, cols_in), BF)
        pieces = vm((groups, frames, chunks, per_chunk, width), BF)
        ins = dict(
            cots=tuple(cots),
            dmlp=d_mlp_in,
            third=third,
            mid=mid,
            mod=mod,
            silu=silu_time.astype(F32),
            dgate_two=d_gate_two,
            cq=cross_q,
            text=text_proj,
            tproj=temporal_proj,
            cout=cross_out_weight,
            cwq=cross_query_weight,
            tout=temporal_out_weight,
            tqkv=temporal_qkv_weight,
            firsts=tuple(firsts),
            cin=cross_in,
            cmix=cross_mix,
            words=text_flat,
            tin=temporal_in,
            tmix=temporal_mix,
            sum_out=sum_out.reshape(chip + (rows_out, cols_out)),
            sum_in=sum_in.reshape(chip + (rows_in, cols_in)),
            results=tuple(p.reshape(frames, here, width) for p in outs[4 : 4 + groups]),
            video=video.reshape(frames, groups, chunks, per_chunk, width),
            sbranch=spatial_branch,
            sout=spatial_out_weight,
            sproj=spatial_proj,
            sin=spatial_in,
            smix=spatial_mix,
            sqkv=spatial_qkv_weight,
        )
        in_specs = jax.tree.map(lambda _: anywhere, ins)
        for name in ("mod", "silu", "dgate_two"):
            in_specs[name] = fixed(ins[name].shape)

        def flat_shapes(elements):
            return tuple(jax.ShapeDtypeStruct((n // devices // 128, 128), F32) for n in elements)

        square = width * width
        out_shape = dict(
            result=jax.ShapeDtypeStruct((frames, groups, here, width), BF),
            video_grad=jax.ShapeDtypeStruct((tokens, width), F32),
            ada=flat_shapes([6 * square])[0],
            spatial=flat_shapes([3 * square, square]),
            temporal=flat_shapes([3 * square, square]),
            cross=flat_shapes([square, 2 * square, square]),
            mlp_in=flat_shapes([width * hidden]),
            mlp_out=flat_shapes([width * hidden]),
        )
        in_hbm = pl.BlockSpec(memory_space=pltpu.HBM)
        out_specs = jax.tree.map(lambda _: in_hbm, out_shape)
        flats = jax.tree.map(lambda leaf: vm(leaf.shape, F32), out_shape)

        def streams_in():
            return stream_scratch(rows_in, cols_in, nb, 3)

        def fin(rows, cols, count):
            return vm((2, rows // 2, cols), F32), vm((rows // 2, cols), F32), sems((2 + count,))

        fin_out, fin_out_in, end_out = fin(rows_out, cols_out, 1)
        fin_in, fin_in_in, end_in = fin(rows_in, cols_in, 1)
        fin_c, fin_c_in, end_c = fin(rows_in, cols_in, 3)
        fin_t, fin_t_in, end_t = fin(rows_in, cols_in, 2)
        scratch = dict(
            local=sems((64,)),
            cots=pieces,
            firsts=pieces,
            dfirsts=pieces,
            dmlp=act(width, F32),
            third=act(width, F32),
            mid=act(width, F32),
            cq=act(width),
            text=vm(text_proj.shape, BF),
            tproj=act(3 * width),
            cout=vm((width, width), BF),
            cwq=vm((width, width), BF),
            tout=vm((width, width), BF),
            tqkv=vm((width, 3 * width), BF),
            cin=act(width),
            cmix=act(width),
            words=vm(text_flat.shape, BF),
            st_out=stream_scratch(rows_out, cols_out, nb, 3),
            st_in=streams_in(),
            st_c=streams_in(),
            st_t=streams_in(),
            st_s=streams_in(),
            cur_out=vm(chip + (rows_out, cols_out), BF),
            cur_in=group,
            cur_c=group,
            cur_t=group,
            cur_s=group,
            send=vm((width, cols_in), BF),
            fin_out=fin_out,
            fin_in=fin_in,
            fin_c=fin_c,
            fin_t=fin_t,
            fin_s=fin_t,
            fin_out_in=fin_out_in,
            fin_in_in=fin_in_in,
            fin_c_in=fin_c_in,
            fin_t_in=fin_t_in,
            fin_s_in=fin_t_in,
            end_out=end_out,
            end_in=end_in,
            end_c=end_c,
            end_t=end_t,
            end_s=end_t,
            flat_out=flats["mlp_out"],
            flat_in=flats["mlp_in"],
            flat_c=flats["cross"],
            flat_t=flats["temporal"],
            flat_s=flats["spatial"],
            flat_ada=flats["ada"],
            core_sems=sems((2, 3, width // ROWS)),
            result_sems=sems((2, groups)),
            first_sems=sems((2, groups, chunks)),
            mod_sems=sems((2, bits)),
            text_acc=vm(text_proj.shape, F32),
            work=vm((ROWS, width), BF),
            dcb=act(width),
            dcq=act(width),
            dtext=vm(text_proj.shape, BF),
            dtb=act(width),
            dtp=act(3 * width),
            mod_sum=vm((8, width), F32),
            mod_in=vm((wide_bits, 8, width), F32),
            mod_all=vm((narrow, 8, width), F32),
        )
        back = pl.pallas_call(
            with_scratch(backward, scratch),
            grid_spec=pltpu.PrefetchScalarGridSpec(
                num_scalar_prefetch=2,
                grid=(1,),
                in_specs=[in_specs],
                out_specs=out_specs,
                scratch_shapes=jax.tree.leaves(scratch),
            ),
            out_shape=out_shape,
            compiler_params=params(collective_id=2, has_side_effects=True),
            cost_estimate=cost(74 * tokens * width * width, 70e6, tokens * ROWS * 30),
            name="backward",
        )(text_length, motion_free, ins)
        back = pl.pallas_call(
            copy_out,
            grid=(),
            in_specs=[jax.tree.map(lambda _: anywhere, out_shape)],
            out_specs=out_specs,
            out_shape=out_shape,
            scratch_shapes=[
                jax.tree.map(lambda leaf: vm(leaf.shape, leaf.dtype), out_shape),
                sems((len(jax.tree.leaves(out_shape)),)),
                sems((len(jax.tree.leaves(out_shape)),)),
            ],
            compiler_params=params(),
            cost_estimate=cost(0, 9e6),
            name="copy_out",
        )(back)
        grads = (
            [back["ada"]]
            + list(back["spatial"])
            + list(back["temporal"])
            + list(back["cross"])
            + list(back["mlp_in"])
            + list(back["mlp_out"])
        )
        return (
            back["result"].reshape(video.shape),
            back["video_grad"].reshape(video.shape),
        ) + tuple(g.reshape(-1) for g in grads)

    def flip(value, mask):
        return lax.ppermute(value, AXES, [(i, i ^ mask) for i in range(devices)])

    def bit_of(b):
        return jnp.bitwise_and(lax.shift_right_logical(index, b), 1)

    def gather_narrow(row):
        for b in range(wide_bits, bits):
            other = flip(row, 1 << b)
            mine = bit_of(b) == 0
            row = jnp.concatenate(
                [jnp.where(mine, row, other), jnp.where(mine, other, row)], 0
            )
        return row

    times = gather_narrow(timestep.astype(F32).reshape(1, 1))
    silu_all = silu_of(time_features(times[:, 0], width)).astype(BF).astype(F32)
    mine = width // devices
    silu_rows = lax.dynamic_slice_in_dim(silu_all, index * mine, mine, 1)

    results = [outs[4]] + [flip(outs[4 + j], j) for j in range(1, groups)]

    outs = pl.pallas_call(
        functools.partial(middle_backward, groups=groups, width=width, per_chunk=per_chunk),
        grid_spec=two_scalars(
            (chunks,),
            [chunk_piece() for _ in range(groups)]
            + [
                row_block(width),
                row_block(width),
                row_block(width),
                mod_spec,
                row_block(width),
                row_block(3 * width),
                row_block(width),
                fixed(text_proj.shape),
                fixed(cross_out_weight.shape),
                fixed(cross_query_weight.shape),
                fixed(temporal_out_weight.shape),
                fixed(temporal_qkv_weight.shape),
            ]
            + [chunk_piece() for _ in range(groups)],
            [
                row_block(width),
                row_block(width),
                fixed((text_pad, 2 * width)),
                row_block(width),
                row_block(3 * width),
                fixed((2, width)),
            ]
            + [chunk_piece() for _ in range(groups)],
            [pltpu.VMEM((text_pad, 2 * width), F32), pltpu.VMEM((ROWS, width), BF)],
        ),
        out_shape=[
            rows_of(width),
            rows_of(width),
            jax.ShapeDtypeStruct((text_pad, 2 * width), BF),
            rows_of(width),
            rows_of(3 * width),
            jax.ShapeDtypeStruct((2, width), F32),
        ]
        + [piece_shape] * groups,
        compiler_params=params(),
        cost_estimate=cost(20 * tokens * width * width, 25e6, tokens * ROWS * 18),
        name="middle_backward",
    )(
        text_length,
        motion_free,
        *cots,
        d_mlp_in,
        third,
        mid,
        mod,
        temporal_in,
        temporal_proj,
        cross_q,
        text_proj,
        cross_out_weight,
        cross_query_weight,
        temporal_out_weight,
        temporal_qkv_weight,
        *firsts,
    )
    d_cross_branch, d_cross_q, d_text, d_temporal_branch, d_temporal_proj, d_mod_two = outs[:6]
    d_firsts = [outs[6]] + [flip(outs[6 + j], j) for j in range(1, groups)]

    cross_send, cross_keep = weight_grads_call(
        core_arr,
        [(cross_in, d_cross_q), (text_flat, d_text), (cross_mix, d_cross_branch)],
    )
    temporal_send, temporal_keep = weight_grads_call(
        core_arr,
        [(temporal_in, d_temporal_proj), (temporal_mix, d_temporal_branch)],
    )

    d_spatial_branch, d_spatial_proj, d_gate_one = pl.pallas_call(
        functools.partial(spatial_backward, groups=groups, width=width),
        grid=(frames,),
        in_specs=[frame_piece() for _ in range(groups)]
        + [mod_spec, row_block(width), row_block(3 * width), fixed(spatial_out_weight.shape)],
        out_specs=[row_block(width), row_block(3 * width), fixed((1, width))],
        out_shape=[rows_of(width), rows_of(3 * width), jax.ShapeDtypeStruct((1, width), F32)],
        scratch_shapes=[pltpu.VMEM((ROWS, width), BF)],
        compiler_params=params(),
        cost_estimate=cost(8 * tokens * width * width, 10e6, tokens * patches * 12),
        name="spatial_backward",
    )(*d_firsts, mod, spatial_branch, spatial_proj, spatial_out_weight)

    spatial_send, spatial_keep = weight_grads_call(
        core_arr,
        [(spatial_in, d_spatial_proj), (spatial_mix, d_spatial_branch)],
    )

    out_block = pl.BlockSpec((1, groups, here, width), lambda f, *_: (f, 0, 0, 0))
    video_grad, result, d_mod_one = pl.pallas_call(
        functools.partial(video_backward, groups=groups, width=width),
        grid_spec=pltpu.PrefetchScalarGridSpec(
            num_scalar_prefetch=1,
            grid=(frames,),
            in_specs=[own_patches(j) for j in range(groups)]
            + [frame_piece() for _ in range(2 * groups)]
            + [mod_spec, row_block(3 * width), fixed(spatial_qkv_weight.shape)],
            out_specs=[out_block, out_block, fixed((2, width))],
        ),
        out_shape=[
            jax.ShapeDtypeStruct((frames, groups, here, width), F32),
            jax.ShapeDtypeStruct((frames, groups, here, width), BF),
            jax.ShapeDtypeStruct((2, width), F32),
        ],
        compiler_params=params(),
        cost_estimate=cost(6 * tokens * width * width, 12e6),
        name="video_backward",
    )(place, *[video_view] * groups, *d_firsts, *results, mod, d_spatial_proj, spatial_qkv_weight)
    video_grad = video_grad.reshape(video.shape)
    result = result.reshape(video.shape)

    d_mod = jnp.concatenate([d_mod_one, d_gate_one, d_mod_two, d_gate_two], 0)
    for b in range(wide_bits):
        d_mod = d_mod + flip(d_mod, 1 << b)
    d_mod_all = gather_narrow(d_mod[None])
    ada_rows = jnp.sum(silu_rows[:, :, None, None] * d_mod_all[:, None, :, :], 0)
    ada_grad = ada_rows.reshape(-1)

    chip_bits = list(range(1, bits))
    first_x = [wide_bits, 1]
    rest = [b for b in chip_bits if b not in first_x]
    order_a = first_x + rest
    order_b = first_x[::-1] + rest

    def join(send, keep):
        return keep.astype(F32) + flip(send, 1).astype(F32)

    def reduce_scatter(cur, order):
        cols = cur.shape[1]
        axes = sorted(chip_bits, reverse=True)
        for b in order:
            cur = cur.astype(BF)
            at = axes.index(b)
            view = cur.reshape(1 << at, 2, 1 << (len(axes) - at - 1), -1, cols)
            out = lax.dynamic_index_in_dim(view, 1 - bit_of(b), 1, keepdims=False)
            own = lax.dynamic_index_in_dim(view, bit_of(b), 1, keepdims=False)
            cur = own.astype(F32) + flip(out, 1 << b).astype(F32)
            axes.remove(b)
        cur = cur.reshape(2, -1, cols)
        own = lax.dynamic_index_in_dim(cur, core, 0, keepdims=False)
        other = flip(lax.dynamic_index_in_dim(cur, 1 - core, 0, keepdims=False), 1)
        low = jnp.where(core == 0, own, other)
        high = jnp.where(core == 0, other, own)
        return low, high

    def unpack(pair, widths):
        low, high = pair
        start, out = 0, []
        for w in widths:
            half = w // 2
            cols = slice(start, start + half)
            out.append(jnp.concatenate([low[:, cols], high[:, cols]], 1).reshape(-1))
            start += half
        return out

    mlp_out_grad = unpack(reduce_scatter(sum_out, order_a), [width])[0]
    mlp_in_grad = unpack(reduce_scatter(sum_in, order_b), [hidden])[0]
    cross_query_grad, cross_kv_grad, cross_out_grad = unpack(
        reduce_scatter(join(cross_send, cross_keep), order_a), [width, 2 * width, width]
    )
    temporal_qkv_grad, temporal_out_grad = unpack(
        reduce_scatter(join(temporal_send, temporal_keep), order_b), [3 * width, width]
    )
    spatial_qkv_grad, spatial_out_grad = unpack(
        reduce_scatter(join(spatial_send, spatial_keep), order_a), [3 * width, width]
    )
    return (
        result,
        video_grad,
        ada_grad,
        spatial_qkv_grad,
        spatial_out_grad,
        temporal_qkv_grad,
        temporal_out_grad,
        cross_query_grad,
        cross_kv_grad,
        cross_out_grad,
        mlp_in_grad,
        mlp_out_grad,
    )


def solution(mesh):
    tokens_spec = P("narrow", "wide", None, None)
    in_specs = (
        (tokens_spec, P("narrow", None, None), P("narrow"), P("narrow"), P("narrow"))
        + (P(),) * 10
        + (tokens_spec,)
    )
    out_specs = (tokens_spec, tokens_spec) + (P(AXES),) * 10
    return jax.shard_map(
        functools.partial(shards, mesh_shape=dict(mesh.shape)),
        mesh=mesh,
        in_specs=in_specs,
        out_specs=out_specs,
        check_vma=False,
    )
```

```python
import functools
import itertools
import math
import types

import jax
import jax.numpy as jnp
from jax import lax
from jax.experimental import pallas as pl
from jax.experimental.pallas import tpu as pltpu
from jax.sharding import PartitionSpec as P

HEAD_DIM = 64
SLAB = 2 * HEAD_DIM
SCALE = HEAD_DIM ** (-0.5)
EPSILON = 1e-06
NEG_LARGE = -1e30
BF = jnp.bfloat16
F32 = jnp.float32
AXES = ("narrow", "wide")
ROWS = 256
MESH = pl.DeviceIdType.MESH
VMEM_LIMIT = 60 * 1024 * 1024
Names = types.SimpleNamespace


def time_features(time_value, width):
    half = width // 2
    freqs = jnp.exp(-math.log(10000.0) * jnp.arange(half, dtype=F32) / half)
    angles = time_value[..., None] * freqs
    return jnp.concatenate([jnp.cos(angles), jnp.sin(angles)], axis=-1)


def silu_of(values):
    return values / (1.0 + jnp.exp(-values))


def normalize(values):
    mean = jnp.mean(values, -1, keepdims=True)
    centred = values - mean
    variance = jnp.mean(centred * centred, -1, keepdims=True)
    inv_std = lax.rsqrt(variance + EPSILON)
    return centred * inv_std, inv_std


def norm_back(grad_norm, normed, inv_std):
    return inv_std * (
        grad_norm
        - jnp.mean(grad_norm, -1, keepdims=True)
        - normed * jnp.mean(grad_norm * normed, -1, keepdims=True)
    )


def mm(left, right):
    return jnp.dot(left, right, preferred_element_type=F32)


def mm_nt(left, right):
    return lax.dot_general(left, right, (((1,), (1,)), ((), ())), preferred_element_type=F32)


def mm_tn(left, right):
    return lax.dot_general(left, right, (((0,), (0,)), ((), ())), preferred_element_type=F32)


def head_masks():
    lane = lax.broadcasted_iota(jnp.int32, (1, SLAB), 1)
    low = (lane < HEAD_DIM).astype(F32)
    return low.astype(BF), (1.0 - low).astype(BF)


def softmax_rows(scores):
    peak = jnp.max(scores, -1, keepdims=True)
    expd = jnp.exp(scores - peak)
    return expd * (1.0 / jnp.sum(expd, -1, keepdims=True))


def attend_slab(query, key, value, bias):
    mixed = None
    for mask in head_masks():
        scores = mm_nt(query * mask, key) * SCALE
        if bias is not None:
            scores = jnp.where(bias, scores, NEG_LARGE)
        probs = softmax_rows(scores).astype(BF)
        part = mm(probs, value * mask)
        mixed = part if mixed is None else mixed + part
    return mixed


def attend_slab_back(query, key, value, grad, bias):
    grad_query = grad_key = grad_value = 0.0
    for mask in head_masks():
        query_part = query * mask
        grad_part = grad * mask
        scores = mm_nt(query_part, key) * SCALE
        if bias is not None:
            scores = jnp.where(bias, scores, NEG_LARGE)
        probs = softmax_rows(scores)
        grad_probs = mm_nt(grad_part, value)
        inner = jnp.sum(grad_probs * probs, -1, keepdims=True)
        grad_scores = (probs * (grad_probs - inner)).astype(BF)
        grad_value = grad_value + mm_tn(probs.astype(BF), grad_part)
        grad_query = grad_query + mm(grad_scores, key * mask)
        grad_key = grad_key + mm_tn(grad_scores, query_part)
    return grad_query * SCALE, grad_key * SCALE, grad_value


def slab_at(index, offset=0):
    return pl.ds(pl.multiple_of(index * SLAB + offset, SLAB), SLAB)


def frame_mask(rows, per_chunk):
    row = lax.broadcasted_iota(jnp.int32, (rows, rows), 0)
    col = lax.broadcasted_iota(jnp.int32, (rows, rows), 1)
    return lax.rem(row, per_chunk) == lax.rem(col, per_chunk)


def part_of(mod, index, width):
    return mod[:, index * width : (index + 1) * width]


def cost(flops, bytes_accessed, transcendentals=0):
    return pl.CostEstimate(
        flops=int(flops), bytes_accessed=int(bytes_accessed), transcendentals=int(transcendentals)
    )


def params(**extra):
    return pltpu.CompilerParams(vmem_limit_bytes=VMEM_LIMIT, **extra)


def fixed(shape):
    rank = len(shape)
    return pl.BlockSpec(shape, lambda *_: (0,) * rank, pipeline_mode=pl.Buffered(1))


def partner(mask):
    wide = lax.axis_size("wide")
    me = lax.axis_index("narrow") * wide + lax.axis_index("wide")
    other = jnp.bitwise_xor(me, mask)
    return (lax.div(other, wide), lax.rem(other, wide))


def greet(masks):
    barrier = pltpu.get_barrier_semaphore()
    for mask in masks:
        pl.semaphore_signal(barrier, inc=1, device_id=partner(mask), device_id_type=MESH)
    pl.semaphore_wait(barrier, len(masks))


def send(src, dst, send_sem, recv_sem, mask):
    return pltpu.make_async_remote_copy(
        src_ref=src,
        dst_ref=dst,
        send_sem=send_sem,
        recv_sem=recv_sem,
        device_id=partner(mask),
        device_id_type=MESH,
    )


def spatial_forward(*refs, groups, width, frames):
    videos, refs = refs[:groups], refs[groups:]
    mod_ref, qkv_ref, out_ref, refs = refs[0], refs[1], refs[2], refs[3:]
    in_ref, proj_ref, mix_ref, branch_ref, refs = refs[0], refs[1], refs[2], refs[3], refs[4:]
    first_own, firsts, refs = refs[0], refs[1:groups], refs[groups:]
    out_buf, first_sems = refs
    frame = pl.program_id(0)
    others = range(1, groups)

    def first_copy(j, f):
        return send(
            out_buf.at[j - 1, f],
            firsts[j - 1].at[f],
            first_sems.at[0, j - 1, f],
            first_sems.at[1, j - 1, f],
            j,
        )

    @pl.when(frame == 0)
    def _():
        greet(list(others))

    mod = mod_ref[...]
    video = jnp.concatenate([v[...].reshape(-1, width) for v in videos], 0).astype(F32)
    normed, _ = normalize(video)
    entry = (normed * (1.0 + part_of(mod, 1, width)) + part_of(mod, 0, width)).astype(BF)
    in_ref[...] = entry
    proj_ref[...] = mm(entry, qkv_ref[...]).astype(BF)
    half = video.shape[0]
    share = video.shape[0] // groups
    for part in (0,):
        rows = slice(part * half, (part + 1) * half)

        def pair(index, carry):
            mixed = attend_slab(
                proj_ref[rows, slab_at(index)],
                proj_ref[:, slab_at(index, width)],
                proj_ref[:, slab_at(index, 2 * width)],
                None,
            )
            mix_ref[rows, slab_at(index)] = mixed.astype(BF)
            return carry

        lax.fori_loop(0, width // SLAB, pair, 0, unroll=6)
        branch = mm(mix_ref[rows, :], out_ref[...])
        first = (video[rows] + part_of(mod, 2, width) * branch).astype(BF)
        branch_ref[rows, :] = branch.astype(BF)
        for j in reversed(range(groups)):
            piece = first[j * share - part * half : (j + 1) * share - part * half]
            if j == 0:
                first_own[...] = piece.reshape(first_own.shape)
            else:
                out_buf[j - 1, frame] = piece
                first_copy(j, frame).start()

    @pl.when(frame == frames - 1)
    def _():
        for j in others:
            for f in range(frames):
                first_copy(j, f).wait()


def middle_forward(length_ref, keep_ref, *refs, groups, width, per_chunk, chunks):
    pieces, cot_all, refs = refs[:groups], refs[groups], refs[groups + 1 :]
    mod_ref, qkv_ref, tout_ref, cq_ref, text_ref, cout_ref = refs[:6]
    tin_ref, tproj_ref, tmix_ref, cin_ref, cq_out, cmix_ref, mlp_ref, mid_ref, third_ref = refs[6:15]
    cots, (cot_buf, load_sems, cot_sems) = refs[15 : 15 + groups], refs[15 + groups :]
    place = lax.axis_index("wide")

    def cot_load(j):
        source = cot_all.at[:, jnp.bitwise_xor(place, j)]
        return pltpu.make_async_copy(source, cot_buf.at[j], load_sems.at[j])

    def cot_copy(j):
        if j == 0:
            return pltpu.make_async_copy(cot_buf.at[0], cots[0], cot_sems.at[0, 0])
        return send(cot_buf.at[j], cots[j], cot_sems.at[0, j], cot_sems.at[1, j], j)

    @pl.when(pl.program_id(0) == 0)
    def _():
        for j in range(groups):
            cot_load(j).start()
        greet(list(range(1, groups)))
        for j in range(groups):
            cot_load(j).wait()
            cot_copy(j).start()

    mod = mod_ref[...]
    first = jnp.concatenate([p[...].reshape(-1, width) for p in pieces], 0).astype(F32)
    rows = first.shape[0]
    normed, _ = normalize(first)
    entry = normed.astype(BF)
    tin_ref[...] = entry
    tproj_ref[...] = mm(entry, qkv_ref[...]).astype(BF)
    same = frame_mask(rows, per_chunk)

    def pair(index, carry):
        mixed = attend_slab(
            tproj_ref[:, slab_at(index)],
            tproj_ref[:, slab_at(index, width)],
            tproj_ref[:, slab_at(index, 2 * width)],
            same,
        )
        tmix_ref[:, slab_at(index)] = mixed.astype(BF)
        return carry

    lax.fori_loop(0, width // SLAB, pair, 0, unroll=6)
    keep = (1 - keep_ref[0]).astype(F32)
    mid = first + keep * mm(tmix_ref[...], tout_ref[...])
    mid_ref[...] = mid
    normed, _ = normalize(mid)
    entry = normed.astype(BF)
    cin_ref[...] = entry
    cq_out[...] = mm(entry, cq_ref[...]).astype(BF)
    keys = text_ref.shape[0]
    valid = lax.broadcasted_iota(jnp.int32, (rows, keys), 1) < length_ref[0]

    def cross_pair(index, carry):
        mixed = attend_slab(
            cq_out[:, slab_at(index)],
            text_ref[:, slab_at(index)],
            text_ref[:, slab_at(index, width)],
            valid,
        )
        cmix_ref[:, slab_at(index)] = mixed.astype(BF)
        return carry

    lax.fori_loop(0, width // SLAB, cross_pair, 0, unroll=6)
    third = mid + mm(cmix_ref[...], cout_ref[...])
    third_ref[...] = third
    normed, _ = normalize(third)
    mlp_ref[...] = (normed * (1.0 + part_of(mod, 4, width)) + part_of(mod, 3, width)).astype(BF)

    @pl.when(pl.program_id(0) == chunks - 1)
    def _():
        for j in range(groups):
            cot_copy(j).wait()


def mlp_both(*refs, groups, width, steps):
    cots, refs = refs[:groups], refs[groups:]
    mlp_ref, third_ref, mod_ref, win_ref, wout_ref = refs[:5]
    sum_in, sum_out, dmlp_ref, dgate_ref = refs[5:9]
    results, scratch = refs[9 : 9 + groups], refs[9 + groups :]
    mlp_t, dbranch, branch, send_in, recv_in, send_out, keep_out, recv_out, in_sems, out_sems = scratch
    step = pl.program_id(0)
    half = steps // 2
    core = jnp.bitwise_and(lax.axis_index("wide"), 1)
    mod = mod_ref[...]
    gate = part_of(mod, 5, width)
    tokens = mlp_ref.shape[0]
    chunks = tokens // ROWS
    share = ROWS // groups

    def block_at(s):
        side = jnp.where(s < half, 1 - core, core)
        return side * half + lax.rem(s, half)

    def in_copy(s):
        return send(send_in.at[s], recv_in.at[s], in_sems.at[0, s], in_sems.at[1, s], 1)

    def out_copy(s):
        block = block_at(s)
        return send(
            send_out.at[block], recv_out.at[block], out_sems.at[0, block], out_sems.at[1, block], 1
        )

    @pl.when(step == 0)
    def _():
        greet([1])
        mlp_t[...] = mlp_ref[...].T
        for k in range(chunks):
            for j in range(groups):
                rows = pl.ds(k * ROWS + j * share, share)
                cot = cots[j][:, k].reshape(share, width).astype(F32)
                dbranch[rows, :] = (gate * cot).astype(BF)
        branch[...] = jnp.zeros_like(branch)
        dmlp_ref[...] = jnp.zeros_like(dmlp_ref)

    @pl.when(step >= 1)
    def _():
        out_copy(step - 1).start()

    @pl.when(jnp.logical_and(step >= 1, step <= half))
    def _():
        in_copy(step - 1).start()

    pre = mm(mlp_ref[...], win_ref[...])
    d_hidden = mm_nt(dbranch[...], wout_ref[...])
    square = pre * pre
    bend = jnp.tanh(0.7978845608 * pre * (1.0 + 0.044715 * square))
    ramp = 0.5 * (1.0 + bend)
    hidden = (pre * ramp).astype(BF)
    slope = ramp + 0.5 * pre * (1.0 - bend * bend) * (
        0.7978845608 * (1.0 + (3.0 * 0.044715) * square)
    )
    d_pre = (d_hidden * slope).astype(BF)
    hidden_t = hidden.T
    side = width // 2
    block = block_at(step)
    send_out[block] = mm(
        hidden_t, dbranch[:, pl.ds(pl.multiple_of((1 - core) * side, 128), side)]
    ).astype(BF)
    keep_out[block] = mm(
        hidden_t, dbranch[:, pl.ds(pl.multiple_of(core * side, 128), side)]
    ).astype(BF)
    grad_in = mm(mlp_t[...], d_pre)

    @pl.when(step < half)
    def _():
        send_in[step] = grad_in.astype(BF)

    @pl.when(step >= half)
    def _():
        in_copy(step - half).wait_recv()
        sum_in[...] = (grad_in + recv_in[step - half].astype(F32)).astype(BF)

    branch[...] += mm(hidden, wout_ref[...])
    dmlp_ref[...] += mm_nt(d_pre, win_ref[...])

    @pl.when(step == steps - 1)
    def _():
        out_copy(steps - 1).start()
        total = jnp.zeros((1, width), F32)
        for k in range(chunks):
            for j in range(groups):
                rows = pl.ds(k * ROWS + j * share, share)
                cot = cots[j][:, k].reshape(share, width).astype(F32)
                piece = branch[rows, :]
                total = total + jnp.sum(cot * piece, 0, keepdims=True)
                out = (third_ref[rows, :] + gate * piece).astype(BF)
                results[j][:, k] = out.reshape(results[j][:, k].shape)
        dgate_ref[...] = total
        for s in range(half):
            in_copy(s).wait_send()
        deep = send_out.shape[1]
        for s in range(steps):
            out_copy(s).wait_send()
            out_copy((s + half) % steps).wait_recv()
            block = block_at((s + half) % steps)
            rows = pl.ds(pl.multiple_of(block * deep, 16), deep)
            sum_out[rows, :] = (
                keep_out[block].astype(F32) + recv_out[block].astype(F32)
            ).astype(BF)


def middle_backward(length_ref, keep_ref, *refs, groups, width, per_chunk):
    cots, refs = refs[:groups], refs[groups:]
    dmlp_ref, third_ref, mid_ref, mod_ref = refs[:4]
    tin_ref, tproj_ref, cq_in, text_ref = refs[4:8]
    cout_ref, cq_ref, tout_ref, tqkv_ref = refs[8:12]
    first_refs, refs = refs[12 : 12 + groups], refs[12 + groups :]
    dcb_ref, dcq_ref, dtext_ref, dtb_ref, dtp_ref, dmod_ref = refs[:6]
    dfirsts = refs[6 : 6 + groups]
    text_acc, work = refs[6 + groups :]
    chunk = pl.program_id(0)
    mod = mod_ref[...]

    @pl.when(chunk == 0)
    def _():
        text_acc[...] = jnp.zeros_like(text_acc)
        dmod_ref[...] = jnp.zeros_like(dmod_ref)

    cot = jnp.concatenate([p[...].reshape(-1, width) for p in cots], 0).astype(F32)
    rows = cot.shape[0]
    d_mlp = dmlp_ref[...]
    normed, inv_std = normalize(third_ref[...])
    dmod_ref[0:1, :] += jnp.sum(d_mlp, 0, keepdims=True)
    dmod_ref[1:2, :] += jnp.sum(d_mlp * normed, 0, keepdims=True)
    d_third = cot + norm_back(d_mlp * (1.0 + part_of(mod, 4, width)), normed, inv_std)
    d_branch = d_third.astype(BF)
    dcb_ref[...] = d_branch
    work[...] = mm_nt(d_branch, cout_ref[...]).astype(BF)
    keys = text_ref.shape[0]
    valid = lax.broadcasted_iota(jnp.int32, (rows, keys), 1) < length_ref[0]

    def cross_pair(index, carry):
        at, after = slab_at(index), slab_at(index, width)
        grad_q, grad_k, grad_v = attend_slab_back(
            cq_in[:, at], text_ref[:, at], text_ref[:, after], work[:, at], valid
        )
        dcq_ref[:, at] = grad_q.astype(BF)
        text_acc[:, at] += grad_k
        text_acc[:, after] += grad_v
        return carry

    lax.fori_loop(0, width // SLAB, cross_pair, 0)
    dtext_ref[...] = text_acc[...].astype(BF)
    normed, inv_std = normalize(mid_ref[...])
    d_mid = d_third + norm_back(mm_nt(dcq_ref[...], cq_ref[...]), normed, inv_std)
    keep = (1 - keep_ref[0]).astype(F32)
    d_branch = (keep * d_mid).astype(BF)
    dtb_ref[...] = d_branch
    work[...] = mm_nt(d_branch, tout_ref[...]).astype(BF)
    same = frame_mask(rows, per_chunk)

    def pair(index, carry):
        at, after, last = slab_at(index), slab_at(index, width), slab_at(index, 2 * width)
        grad_q, grad_k, grad_v = attend_slab_back(
            tproj_ref[:, at], tproj_ref[:, after], tproj_ref[:, last], work[:, at], same
        )
        dtp_ref[:, at] = grad_q.astype(BF)
        dtp_ref[:, after] = grad_k.astype(BF)
        dtp_ref[:, last] = grad_v.astype(BF)
        return carry

    lax.fori_loop(0, width // SLAB, pair, 0)
    first = jnp.concatenate([p[...].reshape(-1, width) for p in first_refs], 0).astype(F32)
    normed, inv_std = normalize(first)
    d_first = d_mid + norm_back(mm_nt(dtp_ref[...], tqkv_ref[...]), normed, inv_std)
    d_first = d_first.astype(BF)
    share = rows // groups
    for j, ref in enumerate(dfirsts):
        ref[...] = d_first[j * share : (j + 1) * share].reshape(ref.shape)


def spatial_backward(*refs, groups, width):
    dfirsts, refs = refs[:groups], refs[groups:]
    mod_ref, branch_ref, proj_ref, out_ref = refs[:4]
    dsb_ref, dproj_ref, dgate_ref, work = refs[4:]
    frame = pl.program_id(0)
    mod = mod_ref[...]

    @pl.when(frame == 0)
    def _():
        dgate_ref[...] = jnp.zeros_like(dgate_ref)

    d_first = jnp.concatenate([p[...].reshape(-1, width) for p in dfirsts], 0).astype(F32)
    dgate_ref[...] += jnp.sum(d_first * branch_ref[...].astype(F32), 0, keepdims=True)
    d_branch = (part_of(mod, 2, width) * d_first).astype(BF)
    dsb_ref[...] = d_branch
    work[...] = mm_nt(d_branch, out_ref[...]).astype(BF)

    def pair(index, carry):
        at, after, last = slab_at(index), slab_at(index, width), slab_at(index, 2 * width)
        grad_q, grad_k, grad_v = attend_slab_back(
            proj_ref[:, at], proj_ref[:, after], proj_ref[:, last], work[:, at], None
        )
        dproj_ref[:, at] = grad_q.astype(BF)
        dproj_ref[:, after] = grad_k.astype(BF)
        dproj_ref[:, last] = grad_v.astype(BF)
        return carry

    lax.fori_loop(0, width // SLAB, pair, 0)


def video_backward(where_ref, *refs, groups, width):
    videos, refs = refs[:groups], refs[groups:]
    dfirsts, refs = refs[:groups], refs[groups:]
    results, refs = refs[:groups], refs[groups:]
    mod_ref, dproj_ref, qkv_ref, grad_ref, result_ref, dmod_ref = refs
    frame = pl.program_id(0)
    place = where_ref[0]
    mod = mod_ref[...]

    @pl.when(frame == 0)
    def _():
        dmod_ref[...] = jnp.zeros_like(dmod_ref)

    video = jnp.concatenate([v[...].reshape(-1, width) for v in videos], 0).astype(F32)
    d_first = jnp.concatenate([p[...].reshape(-1, width) for p in dfirsts], 0).astype(F32)
    normed, inv_std = normalize(video)
    d_in = mm_nt(dproj_ref[...], qkv_ref[...])
    dmod_ref[0:1, :] += jnp.sum(d_in, 0, keepdims=True)
    dmod_ref[1:2, :] += jnp.sum(d_in * normed, 0, keepdims=True)
    grad = d_first + norm_back(d_in * (1.0 + part_of(mod, 1, width)), normed, inv_std)
    share = grad.shape[0] // groups
    for j in range(groups):
        slot = jnp.bitwise_xor(place, j)
        grad_ref[0, slot] = grad[j * share : (j + 1) * share]
        result_ref[0, slot] = results[j][...].reshape(share, width)


class Stream:
    def __init__(self, cur, recv, sems, order, cols, fin, source=None):
        self.cur, self.recv, self.sems, self.fin = cur, recv, sems, fin
        self.order, self.cols, self.source = order, cols, source
        self.bits = sorted(order, reverse=True)
        wide = lax.axis_size("wide")
        me = lax.axis_index("narrow") * wide + lax.axis_index("wide")
        self.mine = {b: jnp.bitwise_and(lax.shift_right_logical(me, b), 1) for b in order}

    def where(self, stage):
        spots = []
        for b in self.bits:
            at = self.order.index(b)
            if at < stage:
                spots.append(self.mine[b])
            elif at == stage:
                spots.append(1 - self.mine[b])
            else:
                spots.append(slice(None))
        return tuple(spots) + (slice(None), self.cols)

    def copy(self, stage):
        base = self.cur if stage > 0 or self.source is None else self.source
        return send(
            base.at[self.where(stage)],
            self.recv[stage],
            self.sems.at[0, stage],
            self.sems.at[1, stage],
            1 << self.order[stage],
        )

    def add(self, stage):
        self.copy(stage).wait()
        left = [b for b in self.bits if self.order.index(b) > stage]
        count = len(left)

        def summed(place):
            spot = tuple(place.get(b, self.mine[b]) for b in self.bits) + (slice(None), self.cols)
            inner = tuple(place[b] for b in left)
            return spot, self.cur[spot].astype(F32) + self.recv[stage][inner].astype(F32)

        if not left:
            _, total = summed({})
            self.fin[:, :, self.cols] = total.reshape(self.fin.shape[0], -1, total.shape[1])
            return

        def body(i, carry):
            place = {
                b: jnp.bitwise_and(lax.shift_right_logical(i, count - 1 - k), 1)
                for k, b in enumerate(left)
            }
            spot, total = summed(place)
            self.cur[spot] = total.astype(BF)
            return carry

        lax.fori_loop(0, 1 << count, body, 0)

    def step(self, stage):
        self.add(stage)
        if stage + 1 < len(self.order):
            self.copy(stage + 1).start()


def stream_scratch(rows, cols, bits, parts):
    cols = cols // parts
    shapes = [pltpu.VMEM((2,) * k + (rows, cols), BF) for k in range(bits - 1, -1, -1)]
    return [shapes + [pltpu.SemaphoreType.DMA((2, bits))] for _ in range(parts)]


def stream_orders(wide_bits, bits):
    z_bits = [b for b in range(2, bits + 1) if b != wide_bits]
    return [
        [wide_bits, 1] + z_bits,
        [1, z_bits[0], wide_bits] + z_bits[1:],
        [z_bits[0], wide_bits, 1] + z_bits[1:],
    ]


def store_flat(out, value, first, pitch):
    for t in range(value.shape[1] // 128):
        out[pl.ds(first + t, value.shape[0], stride=pitch), :] = value[:, t * 128 : (t + 1) * 128]


class Finish:
    def __init__(self, fin, fin_in, sems, flats, outs):
        self.fin, self.fin_in, self.sems, self.flats, self.outs = fin, fin_in, sems, flats, outs
        self.core = jnp.bitwise_and(lax.axis_index("wide"), 1)

    def swap(self):
        return send(
            self.fin.at[1 - self.core], self.fin_in, self.sems.at[0], self.sems.at[1], 1
        )

    def writes(self):
        return [
            pltpu.make_async_copy(flat, out, self.sems.at[2 + k])
            for k, (flat, out) in enumerate(zip(self.flats, self.outs))
        ]

    def store(self):
        self.swap().wait()
        own, other = self.fin[self.core], self.fin_in[...]
        low = jnp.where(self.core == 0, own, other)
        high = jnp.where(self.core == 0, other, own)
        start = 0
        for flat in self.flats:
            pitch = flat.shape[0] // own.shape[0]
            half = pitch * 128 // 2
            store_flat(flat, low[:, start : start + half], 0, pitch)
            store_flat(flat, high[:, start : start + half], pitch // 2, pitch)
            start += half
        for write in self.writes():
            write.start()

    def wait(self):
        for write in self.writes():
            write.wait()


def grads_rows(pairs, side, part_at, dest, extra=None):
    rows = pl.ds(pl.multiple_of(part_at * ROWS, ROWS), ROWS)
    start = 0
    for left, right in pairs:
        part = right.shape[1] // 2
        cols = pl.ds(pl.multiple_of(side * part, 128), part)
        value = mm_tn(left[:, rows], right[:, cols])
        spot = (rows, slice(start, start + part))
        if extra is not None:
            value = value + extra[spot].astype(F32)
        dest[spot] = value.astype(BF)
        start += part


def flat_rows(ref):
    return ref.reshape(-1, ref.shape[-1])


def with_scratch(body, scratch):
    form = jax.tree.structure(scratch)
    count = form.num_leaves

    def kernel(*refs):
        body(*refs[:-count], jax.tree.unflatten(form, refs[-count:]))

    return kernel


def all_bits():
    total = lax.axis_size("wide") * lax.axis_size("narrow")
    return total.bit_length() - 1


def piece_rows(ref, chunk):
    groups = ref.shape[0]
    width = ref.shape[-1]
    return jnp.concatenate([ref[j, :, chunk].reshape(-1, width) for j in range(groups)], 0)


def frame_rows(ref, frame):
    width = ref.shape[-1]
    return jnp.concatenate([ref[j, frame].reshape(-1, width) for j in range(ref.shape[0])], 0)


def backward(length_ref, keep_ref, ins, outs, scratch):
    a, o, s = Names(**ins), Names(**outs), Names(**scratch)
    groups = len(a.cots)
    tokens, width = a.dmlp.shape
    chunks = tokens // ROWS
    frames = a.video.shape[0]
    share = ROWS // groups
    bits = all_bits() - 1
    wide_bits = lax.axis_size("wide").bit_length() - 1
    place, narrow_at = lax.axis_index("wide"), lax.axis_index("narrow")
    core = jnp.bitwise_and(place, 1)
    others = range(1, groups)
    counter = itertools.count()

    def load(src, dst):
        copy = pltpu.make_async_copy(src, dst, s.local.at[next(counter)])
        copy.start()
        return copy

    def wait_all(copies):
        for copy in copies:
            copy.wait()

    cross_loads = [load(a.cots[j], s.cots.at[j]) for j in range(groups)]
    cross_loads += [load(a.dmlp, s.dmlp), load(a.third, s.third), load(a.cout, s.cout)]
    cross_loads += [load(a.cq, s.cq), load(a.text, s.text)]
    cross_grad_loads = [load(a.cin, s.cin), load(a.words, s.words), load(a.cmix, s.cmix)]
    temporal_loads = [load(a.mid, s.mid), load(a.cwq, s.cwq), load(a.tout, s.tout)]
    temporal_loads += [load(a.tproj, s.tproj), load(a.tqkv, s.tqkv)]
    temporal_loads += [load(a.firsts[j], s.firsts.at[j]) for j in range(groups)]
    sum_loads = [load(a.sum_out, s.cur_out), load(a.sum_in, s.cur_in)]

    orders = stream_orders(wide_bits, bits)

    def split(cur, parts, fin, source=None):
        third = cur.shape[-1] // len(orders)
        return [
            Stream(cur, part[:-1], part[-1], order, slice(i * third, (i + 1) * third), fin, source)
            for i, (part, order) in enumerate(zip(parts, orders))
        ]

    r_out = split(s.cur_out, s.st_out, s.fin_out, a.sum_out)
    r_in = split(s.cur_in, s.st_in, s.fin_in, a.sum_in)
    r_c = split(s.cur_c, s.st_c, s.fin_c)
    r_t = split(s.cur_t, s.st_t, s.fin_t)
    r_s = split(s.cur_s, s.st_s, s.fin_s)
    e_out = Finish(s.fin_out, s.fin_out_in, s.end_out, s.flat_out, o.mlp_out)
    e_in = Finish(s.fin_in, s.fin_in_in, s.end_in, s.flat_in, o.mlp_in)
    e_c = Finish(s.fin_c, s.fin_c_in, s.end_c, s.flat_c, o.cross)
    e_t = Finish(s.fin_t, s.fin_t_in, s.end_t, s.flat_t, o.temporal)
    e_s = Finish(s.fin_s, s.fin_s_in, s.end_s, s.flat_s, o.spatial)
    greet(list(others) + [1 << b for b in range(wide_bits, bits + 1)])
    r_out[2].copy(0).start()
    r_in[1].copy(0).start()
    r_in[2].copy(0).start()
    r_out[1].copy(0).start()
    r_in[0].copy(0).start()

    def result_copy(j):
        target = o.result.at[:, place]
        held = s.dcq.reshape(groups, *a.results[0].shape).at[j]
        if j == 0:
            return pltpu.make_async_copy(held, target, s.result_sems.at[0, 0])
        return send(held, target, s.result_sems.at[0, j], s.result_sems.at[1, j], j)

    keys = s.text.shape[0]
    valid = lax.broadcasted_iota(jnp.int32, (ROWS, keys), 1) < length_ref[0]
    mod_scale = a.mod[:, 4 * width : 5 * width]
    work = s.work
    s.text_acc[...] = jnp.zeros_like(s.text_acc)
    s.mod_sum[...] = jnp.zeros_like(s.mod_sum)
    wait_all(cross_loads)

    def cross_chunk(k, carry):
        rows = pl.ds(pl.multiple_of(k * ROWS, ROWS), ROWS)
        cot = piece_rows(s.cots, k).astype(F32)
        d_mlp = s.dmlp[rows, :]
        normed, inv_std = normalize(s.third[rows, :])
        s.mod_sum[3:4, :] += jnp.sum(d_mlp, 0, keepdims=True)
        s.mod_sum[4:5, :] += jnp.sum(d_mlp * normed, 0, keepdims=True)
        d_third = cot + norm_back(d_mlp * (1.0 + mod_scale), normed, inv_std)
        s.dmlp[rows, :] = d_third
        d_branch = d_third.astype(BF)
        s.dcb[rows, :] = d_branch
        work[...] = mm_nt(d_branch, s.cout[...]).astype(BF)

        def pair(index, inner):
            at, after = slab_at(index), slab_at(index, width)
            grad_q, grad_k, grad_v = attend_slab_back(
                s.cq[rows, at], s.text[:, at], s.text[:, after], work[:, at], valid
            )
            s.dcq[rows, at] = grad_q.astype(BF)
            s.text_acc[:, at] += grad_k
            s.text_acc[:, after] += grad_v
            return inner

        lax.fori_loop(0, width // SLAB, pair, 0)
        return carry

    lax.fori_loop(0, chunks, cross_chunk, 0)
    s.dtext[...] = s.text_acc[...].astype(BF)
    wait_all(sum_loads)
    video_loads = [load(a.video.at[:, jnp.bitwise_xor(place, j)], s.cots.at[j]) for j in range(groups)]
    late_loads = [load(a.sout, s.cout), load(a.sbranch, s.cq)]

    wait_all(cross_grad_loads)
    pairs_c = [(s.cin, s.dcq), (s.words, s.dtext), (s.cmix, s.dcb)]

    def core_copy(cur, k, m):
        rows = pl.ds(pl.multiple_of(m * ROWS, ROWS), ROWS)
        return send(
            s.send.at[rows], flat_rows(cur).at[rows],
            s.core_sems.at[0, k, m], s.core_sems.at[1, k, m], 1,
        )

    def other_half(pairs, cur, k):
        def body(m, carry):
            grads_rows(pairs, 1 - core, m, s.send)
            core_copy(cur, k, m).start()
            return carry

        lax.fori_loop(0, width // ROWS, body, 0)

    def own_half(pairs, cur, k):
        def body(m, carry):
            core_copy(cur, k, m).wait()
            grads_rows(pairs, core, m, flat_rows(cur), flat_rows(cur))
            return carry

        lax.fori_loop(0, width // ROWS, body, 0)

    wait_all(temporal_loads)
    keep = (1 - keep_ref[0]).astype(F32)
    same = frame_mask(ROWS, a.firsts[0].shape[2])
    tproj, dtp = s.tproj, s.dtp

    def temporal_chunk(k):
        rows = slice(k * ROWS, (k + 1) * ROWS)
        normed, inv_std = normalize(s.mid[rows, :])
        d_mid = s.dmlp[rows, :] + norm_back(
            mm_nt(s.dcq[rows, :], s.cwq[...]), normed, inv_std
        )
        d_branch = (keep * d_mid).astype(BF)
        s.dtb[rows, :] = d_branch
        work[...] = mm_nt(d_branch, s.tout[...]).astype(BF)

        def pair(index, carry):
            at, after, last = slab_at(index), slab_at(index, width), slab_at(index, 2 * width)
            grad_q, grad_k, grad_v = attend_slab_back(
                tproj[rows, at], tproj[rows, after], tproj[rows, last], work[:, at], same
            )
            dtp[rows, at] = grad_q.astype(BF)
            dtp[rows, after] = grad_k.astype(BF)
            dtp[rows, last] = grad_v.astype(BF)
            return carry

        lax.fori_loop(0, width // SLAB, pair, 0)
        normed, inv_std = normalize(piece_rows(s.firsts, k).astype(F32))
        d_first = d_mid + norm_back(mm_nt(dtp[rows, :], s.tqkv[...]), normed, inv_std)
        d_first = d_first.astype(BF)
        for j in range(groups):
            buf = s.dfirsts if j == 0 else s.firsts
            buf[j, :, k] = d_first[j * share : (j + 1) * share].reshape(
                buf.shape[1:2] + buf.shape[3:]
            )

    def first_copy(j, k):
        return send(
            s.firsts.at[j, :, k], s.dfirsts.at[j, :, k],
            s.first_sems.at[0, j, k], s.first_sems.at[1, j, k], j,
        )

    gate = a.mod[:, 2 * width : 3 * width]
    scale = a.mod[:, width : 2 * width]

    def spatial_frame(f):
        rows = slice(f * ROWS, (f + 1) * ROWS)
        d_first = frame_rows(s.dfirsts, f).astype(F32)
        s.mod_sum[2:3, :] += jnp.sum(d_first * s.cq[rows, :].astype(F32), 0, keepdims=True)
        d_branch = (gate * d_first).astype(BF)
        s.dcb[rows, :] = d_branch
        work[...] = mm_nt(d_branch, s.cout[...]).astype(BF)

        def pair(index, carry):
            at, after, last = slab_at(index), slab_at(index, width), slab_at(index, 2 * width)
            grad_q, grad_k, grad_v = attend_slab_back(
                tproj[rows, at], tproj[rows, after], tproj[rows, last], work[:, at], None
            )
            dtp[rows, at] = grad_q.astype(BF)
            dtp[rows, after] = grad_k.astype(BF)
            dtp[rows, last] = grad_v.astype(BF)
            return carry

        lax.fori_loop(0, width // SLAB, pair, 0)

    def video_frame(f, carry):
        rows = pl.ds(pl.multiple_of(f * ROWS, ROWS), ROWS)
        video = frame_rows(s.cots, f).astype(F32)
        d_first = frame_rows(s.dfirsts, f).astype(F32)
        normed, inv_std = normalize(video)
        d_in = mm_nt(dtp[rows, :], s.tqkv[...])
        s.mod_sum[0:1, :] += jnp.sum(d_in, 0, keepdims=True)
        s.mod_sum[1:2, :] += jnp.sum(d_in * normed, 0, keepdims=True)
        grad = d_first + norm_back(d_in * (1.0 + scale), normed, inv_std)
        for j in range(groups):
            slot = jnp.bitwise_xor(place, j)
            at = pl.ds(pl.multiple_of(f * ROWS + slot * share, share), share)
            s.third[at, :] = grad[j * share : (j + 1) * share]
        return carry

    mod_all = s.mod_all

    def mod_copy(b):
        sems = s.mod_sems.at[0, b], s.mod_sems.at[1, b]
        if b < wide_bits:
            return send(s.mod_sum, s.mod_in.at[b], *sems, 1 << b)
        size = 1 << (b - wide_bits)
        span = mod_all.at[pl.ds(lax.div(narrow_at, size) * size, size)]
        return send(span, span, *sems, 1 << b)

    def mod_step(b):
        mod_copy(b).wait()
        if b < wide_bits:
            s.mod_sum[...] = s.mod_sum[...] + s.mod_in[b]
        if b == wide_bits - 1:
            mod_all[narrow_at] = s.mod_sum[...]
            mod_all[narrow_at, 6:7, :] = a.silu[...]
        if b < bits:
            mod_copy(b + 1).start()

    def ada_rows():
        mine = o.ada.shape[0] // (6 * width // 128)
        me = narrow_at * lax.axis_size("wide") + place
        row = lax.broadcasted_iota(jnp.int32, (mine, width), 0)
        col = lax.broadcasted_iota(jnp.int32, (mine, width), 1)
        picks = (col == me * mine + row).astype(F32).astype(BF)
        silu_mine = mm_nt(picks, mod_all[:, 6, :].astype(BF))
        pitch = 6 * width // 128
        for part in range(6):
            rows = 0.0
            for c in range(mod_all.shape[0]):
                rows = rows + silu_mine[:, c : c + 1] * mod_all[c, part : part + 1, :]
            store_flat(s.flat_ada, rows, part * width // 128, pitch)
        return load(s.flat_ada, o.ada)

    r_in[0].step(0)
    r_out[0].copy(0).start()
    r_in[1].step(0)
    other_half(pairs_c, s.cur_c, 0)
    temporal_chunk(0)
    for j in others:
        first_copy(j, 0).start()
    r_out[1].step(0)
    r_out[2].step(0)
    own_half(pairs_c, s.cur_c, 0)
    temporal_grad_loads = [load(a.tin, s.cin), load(a.tmix, s.cmix)]
    r_c[1].copy(0).start()
    r_c[2].copy(0).start()
    r_c[0].copy(0).start()
    r_in[0].step(1)
    temporal_chunk(1)
    late_loads += [load(a.sproj, s.tproj), load(a.sqkv, s.tqkv)]
    held = s.dcq.reshape(groups, *a.results[0].shape)
    result_loads = [load(a.results[j], held.at[j]) for j in range(groups)]
    for j in others:
        first_copy(j, 1).start()
    wait_all(temporal_grad_loads)
    pairs_t = [(s.cin, dtp), (s.cmix, s.dtb)]
    other_half(pairs_t, s.cur_t, 1)
    r_out[2].step(1)
    r_in[1].step(1)
    r_out[0].step(0)
    r_out[1].step(1)
    r_in[2].step(0)
    for j in others:
        first_copy(j, 0).wait()
    r_c[1].step(0)
    r_c[2].step(0)
    r_c[0].step(0)
    own_half(pairs_t, s.cur_t, 1)
    spatial_grad_loads = [load(a.sin, s.cin), load(a.smix, s.cmix)]
    r_t[2].copy(0).start()
    r_t[0].copy(0).start()
    for j in others:
        first_copy(j, 1).wait()
    wait_all(late_loads)
    spatial_frame(0)
    r_out[2].step(2)
    r_out[0].step(1)
    r_in[0].step(2)
    r_in[1].step(2)
    r_c[1].step(1)
    r_t[1].copy(0).start()
    r_out[1].step(2)
    r_in[2].step(1)
    spatial_frame(1)
    r_out[0].step(2)
    r_c[0].step(1)
    wait_all(spatial_grad_loads)
    pairs_s = [(s.cin, dtp), (s.cmix, s.dcb)]
    other_half(pairs_s, s.cur_s, 2)
    r_t[1].step(0)
    r_t[0].step(0)
    r_t[2].step(0)
    own_half(pairs_s, s.cur_s, 2)
    r_s[0].copy(0).start()
    r_s[1].copy(0).start()
    r_s[2].copy(0).start()
    r_c[2].step(1)
    r_c[1].step(2)
    r_t[1].step(1)
    r_c[0].step(2)
    r_out[1].step(3)
    r_t[0].step(1)
    r_t[2].step(1)
    r_c[1].step(3)
    wait_all(video_loads)
    lax.fori_loop(0, frames, video_frame, 0)
    grad_write = load(s.third, o.video_grad)
    s.mod_sum[5:6, :] = a.dgate_two[...]
    mod_copy(0).start()
    r_s[2].step(0)
    r_s[1].step(0)
    r_in[2].step(2)
    r_c[2].step(2)
    r_s[0].step(0)
    mod_step(0)
    r_t[1].step(2)
    r_in[2].step(3)
    r_in[1].step(3)
    r_t[2].step(2)
    r_s[2].step(1)
    mod_step(1)
    r_out[2].step(3)
    r_s[1].step(1)
    r_c[2].step(3)
    r_in[0].step(3)
    wait_all(result_loads)
    for j in range(groups):
        result_copy(j).start()
    r_s[0].step(1)
    mod_step(2)
    r_t[0].step(2)
    r_out[0].step(3)
    r_s[2].step(2)
    r_t[2].step(3)
    r_t[1].step(3)
    mod_step(3)
    r_s[1].step(2)
    e_in.swap().start()
    r_s[0].step(2)
    r_s[2].step(3)
    e_out.swap().start()
    e_in.store()
    r_c[0].step(3)
    r_s[1].step(3)
    mod_step(4)
    ada_write = ada_rows()
    r_t[0].step(3)
    e_out.store()
    e_t.swap().start()
    e_c.swap().start()
    r_s[0].step(3)
    e_t.store()
    e_s.swap().start()
    e_c.store()
    for j in range(groups):
        result_copy(j).wait()
    grad_write.wait()
    e_out.wait()
    e_in.wait()
    e_c.wait()
    e_t.wait()
    e_s.store()
    ada_write.wait()
    e_s.wait()


def copy_out(ins, outs, bufs, in_sems, out_sems):
    ins, outs, bufs = jax.tree.leaves(ins), jax.tree.leaves(outs), jax.tree.leaves(bufs)
    reads = [
        pltpu.make_async_copy(src, buf, in_sems.at[k])
        for k, (src, buf) in enumerate(zip(ins, bufs))
    ]
    writes = [
        pltpu.make_async_copy(buf, dst, out_sems.at[k])
        for k, (buf, dst) in enumerate(zip(bufs, outs))
    ]
    for read in reads:
        read.start()
    for read, write in zip(reads, writes):
        read.wait()
        write.start()
    for write in writes:
        write.wait()


def weight_grads(core_ref, *refs, count):
    pairs, outs = refs[: 2 * count], refs[2 * count :]
    core = core_ref[0]
    for sign, out in enumerate(outs):
        side = 1 - core if sign == 0 else core
        start = 0
        for k in range(count):
            left, right = pairs[2 * k], pairs[2 * k + 1]
            part = right.shape[1] // 2
            cols = pl.ds(pl.multiple_of(side * part, 128), part)
            out[:, start : start + part] = mm_tn(left[...], right[:, cols]).astype(BF)
            start += part


def weight_grads_call(core, pairs):
    depth = pairs[0][0].shape[1]
    total = sum(right.shape[1] for _, right in pairs)
    tile = 256
    specs = []
    for left, right in pairs:
        specs.append(pl.BlockSpec((left.shape[0], tile), lambda m, _: (0, m)))
        specs.append(fixed(right.shape))
    shape = jax.ShapeDtypeStruct((depth, total // 2), BF)
    flops = sum(2 * left.shape[0] * depth * right.shape[1] for left, right in pairs)
    return pl.pallas_call(
        functools.partial(weight_grads, count=len(pairs)),
        grid_spec=pltpu.PrefetchScalarGridSpec(
            num_scalar_prefetch=1,
            grid=(depth // tile,),
            in_specs=specs,
            out_specs=[pl.BlockSpec((tile, total // 2), lambda m, _: (m, 0))] * 2,
        ),
        out_shape=[shape, shape],
        compiler_params=params(),
        cost_estimate=cost(flops, 8e6),
        name="weight_grads",
    )(core, *[a for pair in pairs for a in pair])


def shards(
    video,
    text_states,
    text_length,
    timestep,
    motion_free,
    ada_weight,
    spatial_qkv_weight,
    spatial_out_weight,
    temporal_qkv_weight,
    temporal_out_weight,
    cross_query_weight,
    cross_kv_weight,
    cross_out_weight,
    mlp_in_weight,
    mlp_out_weight,
    cotangent,
    *,
    mesh_shape,
):
    clips, frames, patches, width = video.shape
    if clips != 1 or patches != ROWS:
        raise ValueError("unsupported shard")
    wide, narrow = mesh_shape["wide"], mesh_shape["narrow"]
    devices = wide * narrow
    groups = wide
    here = patches // groups
    tokens = frames * patches
    chunks = tokens // ROWS
    per_chunk = here // chunks
    hidden = mlp_in_weight.shape[1]
    text_rows = text_states.shape[1]
    text_pad = -(-text_rows // 128) * 128

    wide_at = lax.axis_index("wide")
    narrow_at = lax.axis_index("narrow")
    index = narrow_at * wide + wide_at
    core = jnp.bitwise_and(wide_at, 1)
    place = wide_at.reshape(1).astype(jnp.int32)
    core_arr = core.reshape(1).astype(jnp.int32)
    wide_bits = wide.bit_length() - 1
    bits = devices.bit_length() - 1

    cot_view = cotangent.reshape(frames, groups, here, width)

    silu_time = silu_of(time_features(timestep.astype(F32), width)).astype(BF)
    mod = mm(silu_time, ada_weight)
    text_flat = text_states.reshape(text_rows, width)
    text_flat = jnp.pad(text_flat, ((0, text_pad - text_rows), (0, 0)))
    text_proj = mm(text_flat, cross_kv_weight).astype(BF)

    video_view = video.reshape(frames, groups, here, width)

    def own_patches(j):
        return pl.BlockSpec(
            (1, 1, here, width),
            lambda f, *_: (f, jnp.bitwise_xor(lax.axis_index("wide"), j), 0, 0),
        )

    def frame_piece():
        return pl.BlockSpec((1, chunks, per_chunk, width), lambda f, *_: (f, 0, 0, 0))

    def chunk_piece():
        return pl.BlockSpec((frames, 1, per_chunk, width), lambda k, *_: (0, k, 0, 0))

    def row_block(cols):
        return pl.BlockSpec((ROWS, cols), lambda f, *_: (f, 0))

    piece_shape = jax.ShapeDtypeStruct((frames, chunks, per_chunk, width), BF)

    def rows_of(cols, dtype=BF):
        return jax.ShapeDtypeStruct((tokens, cols), dtype)

    mod_spec = fixed(mod.shape)
    anywhere = pl.BlockSpec(memory_space=pl.ANY)
    own_piece = jax.ShapeDtypeStruct((frames, here, width), BF)
    outs = pl.pallas_call(
        functools.partial(spatial_forward, groups=groups, width=width, frames=frames),
        grid_spec=pltpu.PrefetchScalarGridSpec(
            num_scalar_prefetch=0,
            grid=(frames,),
            in_specs=[own_patches(j) for j in range(groups)]
            + [mod_spec, fixed(spatial_qkv_weight.shape), fixed(spatial_out_weight.shape)],
            out_specs=[row_block(width), row_block(3 * width), row_block(width), row_block(width)]
            + [pl.BlockSpec((1, here, width), lambda f, *_: (f, 0, 0))]
            + [anywhere] * (groups - 1),
            scratch_shapes=[
                pltpu.VMEM((groups - 1, frames, here, width), BF),
                pltpu.SemaphoreType.DMA((2, groups - 1, frames)),
            ],
        ),
        out_shape=[rows_of(width), rows_of(3 * width), rows_of(width), rows_of(width)]
        + [own_piece] * groups,
        compiler_params=params(collective_id=0, has_side_effects=True),
        cost_estimate=cost(8 * tokens * width * width, 10e6, tokens * patches * 12),
        name="spatial_forward",
    )(*[video_view] * groups, mod, spatial_qkv_weight, spatial_out_weight)
    spatial_in, spatial_proj, spatial_mix, spatial_branch = outs[:4]
    firsts = [p.reshape(piece_shape.shape) for p in outs[4 : 4 + groups]]

    def two_scalars(grid, in_specs, out_specs, scratch=()):
        return pltpu.PrefetchScalarGridSpec(
            num_scalar_prefetch=2,
            grid=grid,
            in_specs=in_specs,
            out_specs=out_specs,
            scratch_shapes=scratch,
        )

    outs = pl.pallas_call(
        functools.partial(
            middle_forward, groups=groups, width=width, per_chunk=per_chunk, chunks=chunks
        ),
        grid_spec=two_scalars(
            (chunks,),
            [chunk_piece() for _ in range(groups)]
            + [
                anywhere,
                mod_spec,
                fixed(temporal_qkv_weight.shape),
                fixed(temporal_out_weight.shape),
                fixed(cross_query_weight.shape),
                fixed(text_proj.shape),
                fixed(cross_out_weight.shape),
            ],
            [
                row_block(width),
                row_block(3 * width),
                row_block(width),
                row_block(width),
                row_block(width),
                row_block(width),
                row_block(width),
                row_block(width),
                row_block(width),
            ]
            + [anywhere] * groups,
            [
                pltpu.VMEM((groups, frames, here, width), BF),
                pltpu.SemaphoreType.DMA((groups,)),
                pltpu.SemaphoreType.DMA((2, groups)),
            ],
        ),
        out_shape=[
            rows_of(width),
            rows_of(3 * width),
            rows_of(width),
            rows_of(width),
            rows_of(width),
            rows_of(width),
            rows_of(width),
            rows_of(width, F32),
            rows_of(width, F32),
        ]
        + [own_piece] * groups,
        compiler_params=params(collective_id=4, has_side_effects=True),
        cost_estimate=cost(12 * tokens * width * width, 20e6, tokens * ROWS * 18),
        name="middle_forward",
    )(
        text_length,
        motion_free,
        *firsts,
        cot_view,
        mod,
        temporal_qkv_weight,
        temporal_out_weight,
        cross_query_weight,
        text_proj,
        cross_out_weight,
    )
    temporal_in, temporal_proj, temporal_mix, cross_in, cross_q, cross_mix, mlp_in, mid, third = outs[:9]
    cots = [p.reshape(piece_shape.shape) for p in outs[9:]]

    steps = 4
    wide_h = hidden // steps

    def hidden_at(step):
        half = steps // 2
        side_bit = jnp.bitwise_and(lax.axis_index("wide"), 1)
        side = jnp.where(step < half, 1 - side_bit, side_bit)
        return side * half + lax.rem(step, half)

    whole_piece = fixed((frames, chunks, per_chunk, width))
    outs = pl.pallas_call(
        functools.partial(mlp_both, groups=groups, width=width, steps=steps),
        grid_spec=pltpu.PrefetchScalarGridSpec(
            num_scalar_prefetch=0,
            grid=(steps,),
            in_specs=[whole_piece] * groups
            + [
                fixed(mlp_in.shape),
                fixed(third.shape),
                mod_spec,
                pl.BlockSpec((width, wide_h), lambda s: (0, hidden_at(s))),
                pl.BlockSpec((wide_h, width), lambda s: (hidden_at(s), 0)),
            ],
            out_specs=[
                pl.BlockSpec((width, wide_h), lambda s: (0, jnp.maximum(s - steps // 2, 0))),
                fixed((hidden, width // 2)),
                fixed((tokens, width)),
                fixed((1, width)),
            ]
            + [whole_piece] * groups,
            scratch_shapes=[
                pltpu.VMEM((width, tokens), BF),
                pltpu.VMEM((tokens, width), BF),
                pltpu.VMEM((tokens, width), F32),
                pltpu.VMEM((steps // 2, width, wide_h), BF),
                pltpu.VMEM((steps // 2, width, wide_h), BF),
                pltpu.VMEM((steps, wide_h, width // 2), BF),
                pltpu.VMEM((steps, wide_h, width // 2), BF),
                pltpu.VMEM((steps, wide_h, width // 2), BF),
                pltpu.SemaphoreType.DMA((2, steps // 2)),
                pltpu.SemaphoreType.DMA((2, steps)),
            ],
        ),
        out_shape=[
            jax.ShapeDtypeStruct((width, hidden // 2), BF),
            jax.ShapeDtypeStruct((hidden, width // 2), BF),
            rows_of(width, F32),
            jax.ShapeDtypeStruct((1, width), F32),
        ]
        + [piece_shape] * groups,
        compiler_params=params(collective_id=1, has_side_effects=True),
        cost_estimate=cost(12 * tokens * width * hidden, 25e6, tokens * hidden),
        name="mlp_both",
    )(*cots, mlp_in, third, mod, mlp_in_weight, mlp_out_weight)
    sum_in, sum_out, d_mlp_in, d_gate_two = outs[:4]
    if bits == 5 and frames == 2 and width == 768 and hidden % 768 == 0:
        chip = (2,) * (bits - 1)
        nb = bits - 1
        rows_in, rows_out = 2 * width // devices, 2 * hidden // devices
        cols_in, cols_out = hidden // 2, width // 2
        vm, sems = pltpu.VMEM, pltpu.SemaphoreType.DMA
        act = lambda cols, dtype=BF: vm((tokens, cols), dtype)
        group = vm(chip + (rows_in, cols_in), BF)
        pieces = vm((groups, frames, chunks, per_chunk, width), BF)
        ins = dict(
            cots=tuple(cots),
            dmlp=d_mlp_in,
            third=third,
            mid=mid,
            mod=mod,
            silu=silu_time.astype(F32),
            dgate_two=d_gate_two,
            cq=cross_q,
            text=text_proj,
            tproj=temporal_proj,
            cout=cross_out_weight,
            cwq=cross_query_weight,
            tout=temporal_out_weight,
            tqkv=temporal_qkv_weight,
            firsts=tuple(firsts),
            cin=cross_in,
            cmix=cross_mix,
            words=text_flat,
            tin=temporal_in,
            tmix=temporal_mix,
            sum_out=sum_out.reshape(chip + (rows_out, cols_out)),
            sum_in=sum_in.reshape(chip + (rows_in, cols_in)),
            results=tuple(p.reshape(frames, here, width) for p in outs[4 : 4 + groups]),
            video=video.reshape(frames, groups, chunks, per_chunk, width),
            sbranch=spatial_branch,
            sout=spatial_out_weight,
            sproj=spatial_proj,
            sin=spatial_in,
            smix=spatial_mix,
            sqkv=spatial_qkv_weight,
        )
        in_specs = jax.tree.map(lambda _: anywhere, ins)
        for name in ("mod", "silu", "dgate_two"):
            in_specs[name] = fixed(ins[name].shape)

        def flat_shapes(elements):
            return tuple(jax.ShapeDtypeStruct((n // devices // 128, 128), F32) for n in elements)

        square = width * width
        out_shape = dict(
            result=jax.ShapeDtypeStruct((frames, groups, here, width), BF),
            video_grad=jax.ShapeDtypeStruct((tokens, width), F32),
            ada=flat_shapes([6 * square])[0],
            spatial=flat_shapes([3 * square, square]),
            temporal=flat_shapes([3 * square, square]),
            cross=flat_shapes([square, 2 * square, square]),
            mlp_in=flat_shapes([width * hidden]),
            mlp_out=flat_shapes([width * hidden]),
        )
        in_hbm = pl.BlockSpec(memory_space=pltpu.HBM)
        out_specs = jax.tree.map(lambda _: in_hbm, out_shape)
        flats = jax.tree.map(lambda leaf: vm(leaf.shape, F32), out_shape)

        def streams_in():
            return stream_scratch(rows_in, cols_in, nb, 3)

        def fin(rows, cols, count):
            return vm((2, rows // 2, cols), F32), vm((rows // 2, cols), F32), sems((2 + count,))

        fin_out, fin_out_in, end_out = fin(rows_out, cols_out, 1)
        fin_in, fin_in_in, end_in = fin(rows_in, cols_in, 1)
        fin_c, fin_c_in, end_c = fin(rows_in, cols_in, 3)
        fin_t, fin_t_in, end_t = fin(rows_in, cols_in, 2)
        scratch = dict(
            local=sems((64,)),
            cots=pieces,
            firsts=pieces,
            dfirsts=pieces,
            dmlp=act(width, F32),
            third=act(width, F32),
            mid=act(width, F32),
            cq=act(width),
            text=vm(text_proj.shape, BF),
            tproj=act(3 * width),
            cout=vm((width, width), BF),
            cwq=vm((width, width), BF),
            tout=vm((width, width), BF),
            tqkv=vm((width, 3 * width), BF),
            cin=act(width),
            cmix=act(width),
            words=vm(text_flat.shape, BF),
            st_out=stream_scratch(rows_out, cols_out, nb, 3),
            st_in=streams_in(),
            st_c=streams_in(),
            st_t=streams_in(),
            st_s=streams_in(),
            cur_out=vm(chip + (rows_out, cols_out), BF),
            cur_in=group,
            cur_c=group,
            cur_t=group,
            cur_s=group,
            send=vm((width, cols_in), BF),
            fin_out=fin_out,
            fin_in=fin_in,
            fin_c=fin_c,
            fin_t=fin_t,
            fin_s=fin_t,
            fin_out_in=fin_out_in,
            fin_in_in=fin_in_in,
            fin_c_in=fin_c_in,
            fin_t_in=fin_t_in,
            fin_s_in=fin_t_in,
            end_out=end_out,
            end_in=end_in,
            end_c=end_c,
            end_t=end_t,
            end_s=end_t,
            flat_out=flats["mlp_out"],
            flat_in=flats["mlp_in"],
            flat_c=flats["cross"],
            flat_t=flats["temporal"],
            flat_s=flats["spatial"],
            flat_ada=flats["ada"],
            core_sems=sems((2, 3, width // ROWS)),
            result_sems=sems((2, groups)),
            first_sems=sems((2, groups, chunks)),
            mod_sems=sems((2, bits)),
            text_acc=vm(text_proj.shape, F32),
            work=vm((ROWS, width), BF),
            dcb=act(width),
            dcq=act(width),
            dtext=vm(text_proj.shape, BF),
            dtb=act(width),
            dtp=act(3 * width),
            mod_sum=vm((8, width), F32),
            mod_in=vm((wide_bits, 8, width), F32),
            mod_all=vm((narrow, 8, width), F32),
        )
        back = pl.pallas_call(
            with_scratch(backward, scratch),
            grid_spec=pltpu.PrefetchScalarGridSpec(
                num_scalar_prefetch=2,
                grid=(1,),
                in_specs=[in_specs],
                out_specs=out_specs,
                scratch_shapes=jax.tree.leaves(scratch),
            ),
            out_shape=out_shape,
            compiler_params=params(collective_id=2, has_side_effects=True),
            cost_estimate=cost(74 * tokens * width * width, 70e6, tokens * ROWS * 30),
            name="backward",
        )(text_length, motion_free, ins)
        back = pl.pallas_call(
            copy_out,
            grid=(),
            in_specs=[jax.tree.map(lambda _: anywhere, out_shape)],
            out_specs=out_specs,
            out_shape=out_shape,
            scratch_shapes=[
                jax.tree.map(lambda leaf: vm(leaf.shape, leaf.dtype), out_shape),
                sems((len(jax.tree.leaves(out_shape)),)),
                sems((len(jax.tree.leaves(out_shape)),)),
            ],
            compiler_params=params(),
            cost_estimate=cost(0, 9e6),
            name="copy_out",
        )(back)
        grads = (
            [back["ada"]]
            + list(back["spatial"])
            + list(back["temporal"])
            + list(back["cross"])
            + list(back["mlp_in"])
            + list(back["mlp_out"])
        )
        return (
            back["result"].reshape(video.shape),
            back["video_grad"].reshape(video.shape),
        ) + tuple(g.reshape(-1) for g in grads)

    def flip(value, mask):
        return lax.ppermute(value, AXES, [(i, i ^ mask) for i in range(devices)])

    def bit_of(b):
        return jnp.bitwise_and(lax.shift_right_logical(index, b), 1)

    def gather_narrow(row):
        for b in range(wide_bits, bits):
            other = flip(row, 1 << b)
            mine = bit_of(b) == 0
            row = jnp.concatenate(
                [jnp.where(mine, row, other), jnp.where(mine, other, row)], 0
            )
        return row

    times = gather_narrow(timestep.astype(F32).reshape(1, 1))
    silu_all = silu_of(time_features(times[:, 0], width)).astype(BF).astype(F32)
    mine = width // devices
    silu_rows = lax.dynamic_slice_in_dim(silu_all, index * mine, mine, 1)

    results = [outs[4]] + [flip(outs[4 + j], j) for j in range(1, groups)]

    outs = pl.pallas_call(
        functools.partial(middle_backward, groups=groups, width=width, per_chunk=per_chunk),
        grid_spec=two_scalars(
            (chunks,),
            [chunk_piece() for _ in range(groups)]
            + [
                row_block(width),
                row_block(width),
                row_block(width),
                mod_spec,
                row_block(width),
                row_block(3 * width),
                row_block(width),
                fixed(text_proj.shape),
                fixed(cross_out_weight.shape),
                fixed(cross_query_weight.shape),
                fixed(temporal_out_weight.shape),
                fixed(temporal_qkv_weight.shape),
            ]
            + [chunk_piece() for _ in range(groups)],
            [
                row_block(width),
                row_block(width),
                fixed((text_pad, 2 * width)),
                row_block(width),
                row_block(3 * width),
                fixed((2, width)),
            ]
            + [chunk_piece() for _ in range(groups)],
            [pltpu.VMEM((text_pad, 2 * width), F32), pltpu.VMEM((ROWS, width), BF)],
        ),
        out_shape=[
            rows_of(width),
            rows_of(width),
            jax.ShapeDtypeStruct((text_pad, 2 * width), BF),
            rows_of(width),
            rows_of(3 * width),
            jax.ShapeDtypeStruct((2, width), F32),
        ]
        + [piece_shape] * groups,
        compiler_params=params(),
        cost_estimate=cost(20 * tokens * width * width, 25e6, tokens * ROWS * 18),
        name="middle_backward",
    )(
        text_length,
        motion_free,
        *cots,
        d_mlp_in,
        third,
        mid,
        mod,
        temporal_in,
        temporal_proj,
        cross_q,
        text_proj,
        cross_out_weight,
        cross_query_weight,
        temporal_out_weight,
        temporal_qkv_weight,
        *firsts,
    )
    d_cross_branch, d_cross_q, d_text, d_temporal_branch, d_temporal_proj, d_mod_two = outs[:6]
    d_firsts = [outs[6]] + [flip(outs[6 + j], j) for j in range(1, groups)]

    cross_send, cross_keep = weight_grads_call(
        core_arr,
        [(cross_in, d_cross_q), (text_flat, d_text), (cross_mix, d_cross_branch)],
    )
    temporal_send, temporal_keep = weight_grads_call(
        core_arr,
        [(temporal_in, d_temporal_proj), (temporal_mix, d_temporal_branch)],
    )

    d_spatial_branch, d_spatial_proj, d_gate_one = pl.pallas_call(
        functools.partial(spatial_backward, groups=groups, width=width),
        grid=(frames,),
        in_specs=[frame_piece() for _ in range(groups)]
        + [mod_spec, row_block(width), row_block(3 * width), fixed(spatial_out_weight.shape)],
        out_specs=[row_block(width), row_block(3 * width), fixed((1, width))],
        out_shape=[rows_of(width), rows_of(3 * width), jax.ShapeDtypeStruct((1, width), F32)],
        scratch_shapes=[pltpu.VMEM((ROWS, width), BF)],
        compiler_params=params(),
        cost_estimate=cost(8 * tokens * width * width, 10e6, tokens * patches * 12),
        name="spatial_backward",
    )(*d_firsts, mod, spatial_branch, spatial_proj, spatial_out_weight)

    spatial_send, spatial_keep = weight_grads_call(
        core_arr,
        [(spatial_in, d_spatial_proj), (spatial_mix, d_spatial_branch)],
    )

    out_block = pl.BlockSpec((1, groups, here, width), lambda f, *_: (f, 0, 0, 0))
    video_grad, result, d_mod_one = pl.pallas_call(
        functools.partial(video_backward, groups=groups, width=width),
        grid_spec=pltpu.PrefetchScalarGridSpec(
            num_scalar_prefetch=1,
            grid=(frames,),
            in_specs=[own_patches(j) for j in range(groups)]
            + [frame_piece() for _ in range(2 * groups)]
            + [mod_spec, row_block(3 * width), fixed(spatial_qkv_weight.shape)],
            out_specs=[out_block, out_block, fixed((2, width))],
        ),
        out_shape=[
            jax.ShapeDtypeStruct((frames, groups, here, width), F32),
            jax.ShapeDtypeStruct((frames, groups, here, width), BF),
            jax.ShapeDtypeStruct((2, width), F32),
        ],
        compiler_params=params(),
        cost_estimate=cost(6 * tokens * width * width, 12e6),
        name="video_backward",
    )(place, *[video_view] * groups, *d_firsts, *results, mod, d_spatial_proj, spatial_qkv_weight)
    video_grad = video_grad.reshape(video.shape)
    result = result.reshape(video.shape)

    d_mod = jnp.concatenate([d_mod_one, d_gate_one, d_mod_two, d_gate_two], 0)
    for b in range(wide_bits):
        d_mod = d_mod + flip(d_mod, 1 << b)
    d_mod_all = gather_narrow(d_mod[None])
    ada_rows = jnp.sum(silu_rows[:, :, None, None] * d_mod_all[:, None, :, :], 0)
    ada_grad = ada_rows.reshape(-1)

    chip_bits = list(range(1, bits))
    first_x = [wide_bits, 1]
    rest = [b for b in chip_bits if b not in first_x]
    order_a = first_x + rest
    order_b = first_x[::-1] + rest

    def join(send, keep):
        return keep.astype(F32) + flip(send, 1).astype(F32)

    def reduce_scatter(cur, order):
        cols = cur.shape[1]
        axes = sorted(chip_bits, reverse=True)
        for b in order:
            cur = cur.astype(BF)
            at = axes.index(b)
            view = cur.reshape(1 << at, 2, 1 << (len(axes) - at - 1), -1, cols)
            out = lax.dynamic_index_in_dim(view, 1 - bit_of(b), 1, keepdims=False)
            own = lax.dynamic_index_in_dim(view, bit_of(b), 1, keepdims=False)
            cur = own.astype(F32) + flip(out, 1 << b).astype(F32)
            axes.remove(b)
        cur = cur.reshape(2, -1, cols)
        own = lax.dynamic_index_in_dim(cur, core, 0, keepdims=False)
        other = flip(lax.dynamic_index_in_dim(cur, 1 - core, 0, keepdims=False), 1)
        low = jnp.where(core == 0, own, other)
        high = jnp.where(core == 0, other, own)
        return low, high

    def unpack(pair, widths):
        low, high = pair
        start, out = 0, []
        for w in widths:
            half = w // 2
            cols = slice(start, start + half)
            out.append(jnp.concatenate([low[:, cols], high[:, cols]], 1).reshape(-1))
            start += half
        return out

    mlp_out_grad = unpack(reduce_scatter(sum_out, order_a), [width])[0]
    mlp_in_grad = unpack(reduce_scatter(sum_in, order_b), [hidden])[0]
    cross_query_grad, cross_kv_grad, cross_out_grad = unpack(
        reduce_scatter(join(cross_send, cross_keep), order_a), [width, 2 * width, width]
    )
    temporal_qkv_grad, temporal_out_grad = unpack(
        reduce_scatter(join(temporal_send, temporal_keep), order_b), [3 * width, width]
    )
    spatial_qkv_grad, spatial_out_grad = unpack(
        reduce_scatter(join(spatial_send, spatial_keep), order_a), [3 * width, width]
    )
    return (
        result,
        video_grad,
        ada_grad,
        spatial_qkv_grad,
        spatial_out_grad,
        temporal_qkv_grad,
        temporal_out_grad,
        cross_query_grad,
        cross_kv_grad,
        cross_out_grad,
        mlp_in_grad,
        mlp_out_grad,
    )


def solution(mesh):
    tokens_spec = P("narrow", "wide", None, None)
    in_specs = (
        (tokens_spec, P("narrow", None, None), P("narrow"), P("narrow"), P("narrow"))
        + (P(),) * 10
        + (tokens_spec,)
    )
    out_specs = (tokens_spec, tokens_spec) + (P(AXES),) * 10
    return jax.shard_map(
        functools.partial(shards, mesh_shape=dict(mesh.shape)),
        mesh=mesh,
        in_specs=in_specs,
        out_specs=out_specs,
        check_vma=False,
    )
```

```python
import functools
import itertools
import math
import types

import jax
import jax.numpy as jnp
from jax import lax
from jax.experimental import pallas as pl
from jax.experimental.pallas import tpu as pltpu
from jax.sharding import PartitionSpec as P

HEAD_DIM = 64
SLAB = 2 * HEAD_DIM
SCALE = HEAD_DIM ** (-0.5)
EPSILON = 1e-06
NEG_LARGE = -1e30
BF = jnp.bfloat16
F32 = jnp.float32
AXES = ("narrow", "wide")
ROWS = 256
MESH = pl.DeviceIdType.MESH
VMEM_LIMIT = 60 * 1024 * 1024
Names = types.SimpleNamespace


def time_features(time_value, width):
    half = width // 2
    freqs = jnp.exp(-math.log(10000.0) * jnp.arange(half, dtype=F32) / half)
    angles = time_value[..., None] * freqs
    return jnp.concatenate([jnp.cos(angles), jnp.sin(angles)], axis=-1)


def silu_of(values):
    return values / (1.0 + jnp.exp(-values))


def normalize(values):
    mean = jnp.mean(values, -1, keepdims=True)
    centred = values - mean
    variance = jnp.mean(centred * centred, -1, keepdims=True)
    inv_std = lax.rsqrt(variance + EPSILON)
    return centred * inv_std, inv_std


def norm_back(grad_norm, normed, inv_std):
    return inv_std * (
        grad_norm
        - jnp.mean(grad_norm, -1, keepdims=True)
        - normed * jnp.mean(grad_norm * normed, -1, keepdims=True)
    )


def mm(left, right):
    return jnp.dot(left, right, preferred_element_type=F32)


def mm_nt(left, right):
    return lax.dot_general(left, right, (((1,), (1,)), ((), ())), preferred_element_type=F32)


def mm_tn(left, right):
    return lax.dot_general(left, right, (((0,), (0,)), ((), ())), preferred_element_type=F32)


def head_masks():
    lane = lax.broadcasted_iota(jnp.int32, (1, SLAB), 1)
    low = (lane < HEAD_DIM).astype(F32)
    return low.astype(BF), (1.0 - low).astype(BF)


def softmax_rows(scores):
    peak = jnp.max(scores, -1, keepdims=True)
    expd = jnp.exp(scores - peak)
    return expd * (1.0 / jnp.sum(expd, -1, keepdims=True))


def attend_slab(query, key, value, bias):
    mixed = None
    for mask in head_masks():
        scores = mm_nt(query * mask, key) * SCALE
        if bias is not None:
            scores = jnp.where(bias, scores, NEG_LARGE)
        probs = softmax_rows(scores).astype(BF)
        part = mm(probs, value * mask)
        mixed = part if mixed is None else mixed + part
    return mixed


def attend_slab_back(query, key, value, grad, bias):
    grad_query = grad_key = grad_value = 0.0
    for mask in head_masks():
        query_part = query * mask
        grad_part = grad * mask
        scores = mm_nt(query_part, key) * SCALE
        if bias is not None:
            scores = jnp.where(bias, scores, NEG_LARGE)
        probs = softmax_rows(scores)
        grad_probs = mm_nt(grad_part, value)
        inner = jnp.sum(grad_probs * probs, -1, keepdims=True)
        grad_scores = (probs * (grad_probs - inner)).astype(BF)
        grad_value = grad_value + mm_tn(probs.astype(BF), grad_part)
        grad_query = grad_query + mm(grad_scores, key * mask)
        grad_key = grad_key + mm_tn(grad_scores, query_part)
    return grad_query * SCALE, grad_key * SCALE, grad_value


def slab_at(index, offset=0):
    return pl.ds(pl.multiple_of(index * SLAB + offset, SLAB), SLAB)


def frame_mask(rows, per_chunk):
    row = lax.broadcasted_iota(jnp.int32, (rows, rows), 0)
    col = lax.broadcasted_iota(jnp.int32, (rows, rows), 1)
    return lax.rem(row, per_chunk) == lax.rem(col, per_chunk)


def part_of(mod, index, width):
    return mod[:, index * width : (index + 1) * width]


def cost(flops, bytes_accessed, transcendentals=0):
    return pl.CostEstimate(
        flops=int(flops), bytes_accessed=int(bytes_accessed), transcendentals=int(transcendentals)
    )


def params(**extra):
    return pltpu.CompilerParams(vmem_limit_bytes=VMEM_LIMIT, **extra)


def fixed(shape):
    rank = len(shape)
    return pl.BlockSpec(shape, lambda *_: (0,) * rank, pipeline_mode=pl.Buffered(1))


def partner(mask):
    wide = lax.axis_size("wide")
    me = lax.axis_index("narrow") * wide + lax.axis_index("wide")
    other = jnp.bitwise_xor(me, mask)
    return (lax.div(other, wide), lax.rem(other, wide))


def greet(masks):
    barrier = pltpu.get_barrier_semaphore()
    for mask in masks:
        pl.semaphore_signal(barrier, inc=1, device_id=partner(mask), device_id_type=MESH)
    pl.semaphore_wait(barrier, len(masks))


def send(src, dst, send_sem, recv_sem, mask):
    return pltpu.make_async_remote_copy(
        src_ref=src,
        dst_ref=dst,
        send_sem=send_sem,
        recv_sem=recv_sem,
        device_id=partner(mask),
        device_id_type=MESH,
    )


def spatial_forward(*refs, groups, width, frames):
    videos, refs = refs[:groups], refs[groups:]
    mod_ref, qkv_ref, out_ref, refs = refs[0], refs[1], refs[2], refs[3:]
    in_ref, proj_ref, mix_ref, branch_ref, refs = refs[0], refs[1], refs[2], refs[3], refs[4:]
    first_own, firsts, refs = refs[0], refs[1:groups], refs[groups:]
    out_buf, first_sems = refs
    frame = pl.program_id(0)
    others = range(1, groups)

    def first_copy(j, f):
        return send(
            out_buf.at[j - 1, f],
            firsts[j - 1].at[f],
            first_sems.at[0, j - 1, f],
            first_sems.at[1, j - 1, f],
            j,
        )

    @pl.when(frame == 0)
    def _():
        greet(list(others))

    mod = mod_ref[...]
    video = jnp.concatenate([v[...].reshape(-1, width) for v in videos], 0).astype(F32)
    normed, _ = normalize(video)
    entry = (normed * (1.0 + part_of(mod, 1, width)) + part_of(mod, 0, width)).astype(BF)
    in_ref[...] = entry
    proj_ref[...] = mm(entry, qkv_ref[...]).astype(BF)
    half = video.shape[0]
    share = video.shape[0] // groups
    for part in (0,):
        rows = slice(part * half, (part + 1) * half)

        def pair(index, carry):
            mixed = attend_slab(
                proj_ref[rows, slab_at(index)],
                proj_ref[:, slab_at(index, width)],
                proj_ref[:, slab_at(index, 2 * width)],
                None,
            )
            mix_ref[rows, slab_at(index)] = mixed.astype(BF)
            return carry

        lax.fori_loop(0, width // SLAB, pair, 0, unroll=6)
        branch = mm(mix_ref[rows, :], out_ref[...])
        first = (video[rows] + part_of(mod, 2, width) * branch).astype(BF)
        branch_ref[rows, :] = branch.astype(BF)
        for j in reversed(range(groups)):
            piece = first[j * share - part * half : (j + 1) * share - part * half]
            if j == 0:
                first_own[...] = piece.reshape(first_own.shape)
            else:
                out_buf[j - 1, frame] = piece
                first_copy(j, frame).start()

    @pl.when(frame == frames - 1)
    def _():
        for j in others:
            for f in range(frames):
                first_copy(j, f).wait()


def middle_forward(length_ref, keep_ref, *refs, groups, width, per_chunk, chunks):
    pieces, cot_all, refs = refs[:groups], refs[groups], refs[groups + 1 :]
    mod_ref, qkv_ref, tout_ref, cq_ref, text_ref, cout_ref = refs[:6]
    tin_ref, tproj_ref, tmix_ref, cin_ref, cq_out, cmix_ref, mlp_ref, mid_ref, third_ref = refs[6:15]
    cots, (cot_buf, load_sems, cot_sems) = refs[15 : 15 + groups], refs[15 + groups :]
    place = lax.axis_index("wide")

    def cot_load(j):
        source = cot_all.at[:, jnp.bitwise_xor(place, j)]
        return pltpu.make_async_copy(source, cot_buf.at[j], load_sems.at[j])

    def cot_copy(j):
        if j == 0:
            return pltpu.make_async_copy(cot_buf.at[0], cots[0], cot_sems.at[0, 0])
        return send(cot_buf.at[j], cots[j], cot_sems.at[0, j], cot_sems.at[1, j], j)

    @pl.when(pl.program_id(0) == 0)
    def _():
        for j in range(groups):
            cot_load(j).start()
        greet(list(range(1, groups)))
        for j in range(groups):
            cot_load(j).wait()
            cot_copy(j).start()

    mod = mod_ref[...]
    first = jnp.concatenate([p[...].reshape(-1, width) for p in pieces], 0).astype(F32)
    rows = first.shape[0]
    normed, _ = normalize(first)
    entry = normed.astype(BF)
    tin_ref[...] = entry
    tproj_ref[...] = mm(entry, qkv_ref[...]).astype(BF)
    same = frame_mask(rows, per_chunk)

    def pair(index, carry):
        mixed = attend_slab(
            tproj_ref[:, slab_at(index)],
            tproj_ref[:, slab_at(index, width)],
            tproj_ref[:, slab_at(index, 2 * width)],
            same,
        )
        tmix_ref[:, slab_at(index)] = mixed.astype(BF)
        return carry

    lax.fori_loop(0, width // SLAB, pair, 0, unroll=6)
    keep = (1 - keep_ref[0]).astype(F32)
    mid = first + keep * mm(tmix_ref[...], tout_ref[...])
    mid_ref[...] = mid
    normed, _ = normalize(mid)
    entry = normed.astype(BF)
    cin_ref[...] = entry
    cq_out[...] = mm(entry, cq_ref[...]).astype(BF)
    keys = text_ref.shape[0]
    valid = lax.broadcasted_iota(jnp.int32, (rows, keys), 1) < length_ref[0]

    def cross_pair(index, carry):
        mixed = attend_slab(
            cq_out[:, slab_at(index)],
            text_ref[:, slab_at(index)],
            text_ref[:, slab_at(index, width)],
            valid,
        )
        cmix_ref[:, slab_at(index)] = mixed.astype(BF)
        return carry

    lax.fori_loop(0, width // SLAB, cross_pair, 0, unroll=6)
    third = mid + mm(cmix_ref[...], cout_ref[...])
    third_ref[...] = third
    normed, _ = normalize(third)
    mlp_ref[...] = (normed * (1.0 + part_of(mod, 4, width)) + part_of(mod, 3, width)).astype(BF)

    @pl.when(pl.program_id(0) == chunks - 1)
    def _():
        for j in range(groups):
            cot_copy(j).wait()


def mlp_both(*refs, groups, width, steps):
    cots, refs = refs[:groups], refs[groups:]
    mlp_ref, third_ref, mod_ref, win_ref, wout_ref = refs[:5]
    sum_in, sum_out, dmlp_ref, dgate_ref = refs[5:9]
    results, scratch = refs[9 : 9 + groups], refs[9 + groups :]
    mlp_t, dbranch, branch, send_in, recv_in, send_out, keep_out, recv_out, in_sems, out_sems = scratch
    step = pl.program_id(0)
    half = steps // 2
    core = jnp.bitwise_and(lax.axis_index("wide"), 1)
    mod = mod_ref[...]
    gate = part_of(mod, 5, width)
    tokens = mlp_ref.shape[0]
    chunks = tokens // ROWS
    share = ROWS // groups

    def block_at(s):
        side = jnp.where(s < half, 1 - core, core)
        return side * half + lax.rem(s, half)

    def in_copy(s):
        return send(send_in.at[s], recv_in.at[s], in_sems.at[0, s], in_sems.at[1, s], 1)

    def out_copy(s):
        block = block_at(s)
        return send(
            send_out.at[block], recv_out.at[block], out_sems.at[0, block], out_sems.at[1, block], 1
        )

    @pl.when(step == 0)
    def _():
        greet([1])
        mlp_t[...] = mlp_ref[...].T
        for k in range(chunks):
            for j in range(groups):
                rows = pl.ds(k * ROWS + j * share, share)
                cot = cots[j][:, k].reshape(share, width).astype(F32)
                dbranch[rows, :] = (gate * cot).astype(BF)
        branch[...] = jnp.zeros_like(branch)
        dmlp_ref[...] = jnp.zeros_like(dmlp_ref)

    @pl.when(step >= 1)
    def _():
        out_copy(step - 1).start()

    @pl.when(jnp.logical_and(step >= 1, step <= half))
    def _():
        in_copy(step - 1).start()

    pre = mm(mlp_ref[...], win_ref[...])
    d_hidden = mm_nt(dbranch[...], wout_ref[...])
    square = pre * pre
    bend = jnp.tanh(0.7978845608 * pre * (1.0 + 0.044715 * square))
    ramp = 0.5 * (1.0 + bend)
    hidden = (pre * ramp).astype(BF)
    slope = ramp + 0.5 * pre * (1.0 - bend * bend) * (
        0.7978845608 * (1.0 + (3.0 * 0.044715) * square)
    )
    d_pre = (d_hidden * slope).astype(BF)
    hidden_t = hidden.T
    side = width // 2
    block = block_at(step)
    send_out[block] = mm(
        hidden_t, dbranch[:, pl.ds(pl.multiple_of((1 - core) * side, 128), side)]
    ).astype(BF)
    keep_out[block] = mm(
        hidden_t, dbranch[:, pl.ds(pl.multiple_of(core * side, 128), side)]
    ).astype(BF)
    grad_in = mm(mlp_t[...], d_pre)

    @pl.when(step < half)
    def _():
        send_in[step] = grad_in.astype(BF)

    @pl.when(step >= half)
    def _():
        in_copy(step - half).wait_recv()
        sum_in[...] = (grad_in + recv_in[step - half].astype(F32)).astype(BF)

    branch[...] += mm(hidden, wout_ref[...])
    dmlp_ref[...] += mm_nt(d_pre, win_ref[...])

    @pl.when(step == steps - 1)
    def _():
        out_copy(steps - 1).start()
        total = jnp.zeros((1, width), F32)
        for k in range(chunks):
            for j in range(groups):
                rows = pl.ds(k * ROWS + j * share, share)
                cot = cots[j][:, k].reshape(share, width).astype(F32)
                piece = branch[rows, :]
                total = total + jnp.sum(cot * piece, 0, keepdims=True)
                out = (third_ref[rows, :] + gate * piece).astype(BF)
                results[j][:, k] = out.reshape(results[j][:, k].shape)
        dgate_ref[...] = total
        for s in range(half):
            in_copy(s).wait_send()
        deep = send_out.shape[1]
        for s in range(steps):
            out_copy(s).wait_send()
            out_copy((s + half) % steps).wait_recv()
            block = block_at((s + half) % steps)
            rows = pl.ds(pl.multiple_of(block * deep, 16), deep)
            sum_out[rows, :] = (
                keep_out[block].astype(F32) + recv_out[block].astype(F32)
            ).astype(BF)


def middle_backward(length_ref, keep_ref, *refs, groups, width, per_chunk):
    cots, refs = refs[:groups], refs[groups:]
    dmlp_ref, third_ref, mid_ref, mod_ref = refs[:4]
    tin_ref, tproj_ref, cq_in, text_ref = refs[4:8]
    cout_ref, cq_ref, tout_ref, tqkv_ref = refs[8:12]
    first_refs, refs = refs[12 : 12 + groups], refs[12 + groups :]
    dcb_ref, dcq_ref, dtext_ref, dtb_ref, dtp_ref, dmod_ref = refs[:6]
    dfirsts = refs[6 : 6 + groups]
    text_acc, work = refs[6 + groups :]
    chunk = pl.program_id(0)
    mod = mod_ref[...]

    @pl.when(chunk == 0)
    def _():
        text_acc[...] = jnp.zeros_like(text_acc)
        dmod_ref[...] = jnp.zeros_like(dmod_ref)

    cot = jnp.concatenate([p[...].reshape(-1, width) for p in cots], 0).astype(F32)
    rows = cot.shape[0]
    d_mlp = dmlp_ref[...]
    normed, inv_std = normalize(third_ref[...])
    dmod_ref[0:1, :] += jnp.sum(d_mlp, 0, keepdims=True)
    dmod_ref[1:2, :] += jnp.sum(d_mlp * normed, 0, keepdims=True)
    d_third = cot + norm_back(d_mlp * (1.0 + part_of(mod, 4, width)), normed, inv_std)
    d_branch = d_third.astype(BF)
    dcb_ref[...] = d_branch
    work[...] = mm_nt(d_branch, cout_ref[...]).astype(BF)
    keys = text_ref.shape[0]
    valid = lax.broadcasted_iota(jnp.int32, (rows, keys), 1) < length_ref[0]

    def cross_pair(index, carry):
        at, after = slab_at(index), slab_at(index, width)
        grad_q, grad_k, grad_v = attend_slab_back(
            cq_in[:, at], text_ref[:, at], text_ref[:, after], work[:, at], valid
        )
        dcq_ref[:, at] = grad_q.astype(BF)
        text_acc[:, at] += grad_k
        text_acc[:, after] += grad_v
        return carry

    lax.fori_loop(0, width // SLAB, cross_pair, 0)
    dtext_ref[...] = text_acc[...].astype(BF)
    normed, inv_std = normalize(mid_ref[...])
    d_mid = d_third + norm_back(mm_nt(dcq_ref[...], cq_ref[...]), normed, inv_std)
    keep = (1 - keep_ref[0]).astype(F32)
    d_branch = (keep * d_mid).astype(BF)
    dtb_ref[...] = d_branch
    work[...] = mm_nt(d_branch, tout_ref[...]).astype(BF)
    same = frame_mask(rows, per_chunk)

    def pair(index, carry):
        at, after, last = slab_at(index), slab_at(index, width), slab_at(index, 2 * width)
        grad_q, grad_k, grad_v = attend_slab_back(
            tproj_ref[:, at], tproj_ref[:, after], tproj_ref[:, last], work[:, at], same
        )
        dtp_ref[:, at] = grad_q.astype(BF)
        dtp_ref[:, after] = grad_k.astype(BF)
        dtp_ref[:, last] = grad_v.astype(BF)
        return carry

    lax.fori_loop(0, width // SLAB, pair, 0)
    first = jnp.concatenate([p[...].reshape(-1, width) for p in first_refs], 0).astype(F32)
    normed, inv_std = normalize(first)
    d_first = d_mid + norm_back(mm_nt(dtp_ref[...], tqkv_ref[...]), normed, inv_std)
    d_first = d_first.astype(BF)
    share = rows // groups
    for j, ref in enumerate(dfirsts):
        ref[...] = d_first[j * share : (j + 1) * share].reshape(ref.shape)


def spatial_backward(*refs, groups, width):
    dfirsts, refs = refs[:groups], refs[groups:]
    mod_ref, branch_ref, proj_ref, out_ref = refs[:4]
    dsb_ref, dproj_ref, dgate_ref, work = refs[4:]
    frame = pl.program_id(0)
    mod = mod_ref[...]

    @pl.when(frame == 0)
    def _():
        dgate_ref[...] = jnp.zeros_like(dgate_ref)

    d_first = jnp.concatenate([p[...].reshape(-1, width) for p in dfirsts], 0).astype(F32)
    dgate_ref[...] += jnp.sum(d_first * branch_ref[...].astype(F32), 0, keepdims=True)
    d_branch = (part_of(mod, 2, width) * d_first).astype(BF)
    dsb_ref[...] = d_branch
    work[...] = mm_nt(d_branch, out_ref[...]).astype(BF)

    def pair(index, carry):
        at, after, last = slab_at(index), slab_at(index, width), slab_at(index, 2 * width)
        grad_q, grad_k, grad_v = attend_slab_back(
            proj_ref[:, at], proj_ref[:, after], proj_ref[:, last], work[:, at], None
        )
        dproj_ref[:, at] = grad_q.astype(BF)
        dproj_ref[:, after] = grad_k.astype(BF)
        dproj_ref[:, last] = grad_v.astype(BF)
        return carry

    lax.fori_loop(0, width // SLAB, pair, 0)


def video_backward(where_ref, *refs, groups, width):
    videos, refs = refs[:groups], refs[groups:]
    dfirsts, refs = refs[:groups], refs[groups:]
    results, refs = refs[:groups], refs[groups:]
    mod_ref, dproj_ref, qkv_ref, grad_ref, result_ref, dmod_ref = refs
    frame = pl.program_id(0)
    place = where_ref[0]
    mod = mod_ref[...]

    @pl.when(frame == 0)
    def _():
        dmod_ref[...] = jnp.zeros_like(dmod_ref)

    video = jnp.concatenate([v[...].reshape(-1, width) for v in videos], 0).astype(F32)
    d_first = jnp.concatenate([p[...].reshape(-1, width) for p in dfirsts], 0).astype(F32)
    normed, inv_std = normalize(video)
    d_in = mm_nt(dproj_ref[...], qkv_ref[...])
    dmod_ref[0:1, :] += jnp.sum(d_in, 0, keepdims=True)
    dmod_ref[1:2, :] += jnp.sum(d_in * normed, 0, keepdims=True)
    grad = d_first + norm_back(d_in * (1.0 + part_of(mod, 1, width)), normed, inv_std)
    share = grad.shape[0] // groups
    for j in range(groups):
        slot = jnp.bitwise_xor(place, j)
        grad_ref[0, slot] = grad[j * share : (j + 1) * share]
        result_ref[0, slot] = results[j][...].reshape(share, width)


class Stream:
    def __init__(self, cur, recv, sems, order, cols, fin, source=None):
        self.cur, self.recv, self.sems, self.fin = cur, recv, sems, fin
        self.order, self.cols, self.source = order, cols, source
        self.bits = sorted(order, reverse=True)
        wide = lax.axis_size("wide")
        me = lax.axis_index("narrow") * wide + lax.axis_index("wide")
        self.mine = {b: jnp.bitwise_and(lax.shift_right_logical(me, b), 1) for b in order}

    def where(self, stage):
        spots = []
        for b in self.bits:
            at = self.order.index(b)
            if at < stage:
                spots.append(self.mine[b])
            elif at == stage:
                spots.append(1 - self.mine[b])
            else:
                spots.append(slice(None))
        return tuple(spots) + (slice(None), self.cols)

    def copy(self, stage):
        base = self.cur if stage > 0 or self.source is None else self.source
        return send(
            base.at[self.where(stage)],
            self.recv[stage],
            self.sems.at[0, stage],
            self.sems.at[1, stage],
            1 << self.order[stage],
        )

    def add(self, stage):
        self.copy(stage).wait()
        left = [b for b in self.bits if self.order.index(b) > stage]
        count = len(left)

        def summed(place):
            spot = tuple(place.get(b, self.mine[b]) for b in self.bits) + (slice(None), self.cols)
            inner = tuple(place[b] for b in left)
            return spot, self.cur[spot].astype(F32) + self.recv[stage][inner].astype(F32)

        if not left:
            _, total = summed({})
            self.fin[:, :, self.cols] = total.reshape(self.fin.shape[0], -1, total.shape[1])
            return

        def body(i, carry):
            place = {
                b: jnp.bitwise_and(lax.shift_right_logical(i, count - 1 - k), 1)
                for k, b in enumerate(left)
            }
            spot, total = summed(place)
            self.cur[spot] = total.astype(BF)
            return carry

        lax.fori_loop(0, 1 << count, body, 0)

    def step(self, stage):
        self.add(stage)
        if stage + 1 < len(self.order):
            self.copy(stage + 1).start()


def stream_scratch(rows, cols, bits, parts):
    cols = cols // parts
    shapes = [pltpu.VMEM((2,) * k + (rows, cols), BF) for k in range(bits - 1, -1, -1)]
    return [shapes + [pltpu.SemaphoreType.DMA((2, bits))] for _ in range(parts)]


def stream_orders(wide_bits, bits):
    z_bits = [b for b in range(2, bits + 1) if b != wide_bits]
    return [
        [wide_bits, 1] + z_bits,
        [1, z_bits[0], wide_bits] + z_bits[1:],
        [z_bits[0], wide_bits, 1] + z_bits[1:],
    ]


def store_flat(out, value, first, pitch):
    for t in range(value.shape[1] // 128):
        out[pl.ds(first + t, value.shape[0], stride=pitch), :] = value[:, t * 128 : (t + 1) * 128]


class Finish:
    def __init__(self, fin, fin_in, sems, flats, outs):
        self.fin, self.fin_in, self.sems, self.flats, self.outs = fin, fin_in, sems, flats, outs
        self.core = jnp.bitwise_and(lax.axis_index("wide"), 1)

    def swap(self):
        return send(
            self.fin.at[1 - self.core], self.fin_in, self.sems.at[0], self.sems.at[1], 1
        )

    def writes(self):
        return [
            pltpu.make_async_copy(flat, out, self.sems.at[2 + k])
            for k, (flat, out) in enumerate(zip(self.flats, self.outs))
        ]

    def store(self):
        self.swap().wait()
        own, other = self.fin[self.core], self.fin_in[...]
        low = jnp.where(self.core == 0, own, other)
        high = jnp.where(self.core == 0, other, own)
        start = 0
        for flat in self.flats:
            pitch = flat.shape[0] // own.shape[0]
            half = pitch * 128 // 2
            store_flat(flat, low[:, start : start + half], 0, pitch)
            store_flat(flat, high[:, start : start + half], pitch // 2, pitch)
            start += half
        for write in self.writes():
            write.start()

    def wait(self):
        for write in self.writes():
            write.wait()


def grads_rows(pairs, side, part_at, dest, extra=None):
    rows = pl.ds(pl.multiple_of(part_at * ROWS, ROWS), ROWS)
    start = 0
    for left, right in pairs:
        part = right.shape[1] // 2
        cols = pl.ds(pl.multiple_of(side * part, 128), part)
        value = mm_tn(left[:, rows], right[:, cols])
        spot = (rows, slice(start, start + part))
        if extra is not None:
            value = value + extra[spot].astype(F32)
        dest[spot] = value.astype(BF)
        start += part


def flat_rows(ref):
    return ref.reshape(-1, ref.shape[-1])


def with_scratch(body, scratch):
    form = jax.tree.structure(scratch)
    count = form.num_leaves

    def kernel(*refs):
        body(*refs[:-count], jax.tree.unflatten(form, refs[-count:]))

    return kernel


def all_bits():
    total = lax.axis_size("wide") * lax.axis_size("narrow")
    return total.bit_length() - 1


def piece_rows(ref, chunk):
    groups = ref.shape[0]
    width = ref.shape[-1]
    return jnp.concatenate([ref[j, :, chunk].reshape(-1, width) for j in range(groups)], 0)


def frame_rows(ref, frame):
    width = ref.shape[-1]
    return jnp.concatenate([ref[j, frame].reshape(-1, width) for j in range(ref.shape[0])], 0)


def backward(length_ref, keep_ref, ins, outs, scratch):
    a, o, s = Names(**ins), Names(**outs), Names(**scratch)
    groups = len(a.cots)
    tokens, width = a.dmlp.shape
    chunks = tokens // ROWS
    frames = a.video.shape[0]
    share = ROWS // groups
    bits = all_bits() - 1
    wide_bits = lax.axis_size("wide").bit_length() - 1
    place, narrow_at = lax.axis_index("wide"), lax.axis_index("narrow")
    core = jnp.bitwise_and(place, 1)
    others = range(1, groups)
    counter = itertools.count()

    def load(src, dst):
        copy = pltpu.make_async_copy(src, dst, s.local.at[next(counter)])
        copy.start()
        return copy

    def wait_all(copies):
        for copy in copies:
            copy.wait()

    cross_loads = [load(a.cots[j], s.cots.at[j]) for j in range(groups)]
    cross_loads += [load(a.dmlp, s.dmlp), load(a.third, s.third), load(a.cout, s.cout)]
    cross_loads += [load(a.cq, s.cq), load(a.text, s.text)]
    cross_grad_loads = [load(a.cin, s.cin), load(a.words, s.words), load(a.cmix, s.cmix)]
    temporal_loads = [load(a.mid, s.mid), load(a.cwq, s.cwq), load(a.tout, s.tout)]
    temporal_loads += [load(a.tproj, s.tproj), load(a.tqkv, s.tqkv)]
    temporal_loads += [load(a.firsts[j], s.firsts.at[j]) for j in range(groups)]
    sum_loads = [load(a.sum_out, s.cur_out), load(a.sum_in, s.cur_in)]

    orders = stream_orders(wide_bits, bits)

    def split(cur, parts, fin, source=None):
        third = cur.shape[-1] // len(orders)
        return [
            Stream(cur, part[:-1], part[-1], order, slice(i * third, (i + 1) * third), fin, source)
            for i, (part, order) in enumerate(zip(parts, orders))
        ]

    r_out = split(s.cur_out, s.st_out, s.fin_out, a.sum_out)
    r_in = split(s.cur_in, s.st_in, s.fin_in, a.sum_in)
    r_c = split(s.cur_c, s.st_c, s.fin_c)
    r_t = split(s.cur_t, s.st_t, s.fin_t)
    r_s = split(s.cur_s, s.st_s, s.fin_s)
    e_out = Finish(s.fin_out, s.fin_out_in, s.end_out, s.flat_out, o.mlp_out)
    e_in = Finish(s.fin_in, s.fin_in_in, s.end_in, s.flat_in, o.mlp_in)
    e_c = Finish(s.fin_c, s.fin_c_in, s.end_c, s.flat_c, o.cross)
    e_t = Finish(s.fin_t, s.fin_t_in, s.end_t, s.flat_t, o.temporal)
    e_s = Finish(s.fin_s, s.fin_s_in, s.end_s, s.flat_s, o.spatial)
    greet(list(others) + [1 << b for b in range(wide_bits, bits + 1)])
    r_out[2].copy(0).start()
    r_in[1].copy(0).start()
    r_in[2].copy(0).start()
    r_out[1].copy(0).start()
    r_in[0].copy(0).start()

    def result_copy(j):
        target = o.result.at[:, place]
        held = s.dcq.reshape(groups, *a.results[0].shape).at[j]
        if j == 0:
            return pltpu.make_async_copy(held, target, s.result_sems.at[0, 0])
        return send(held, target, s.result_sems.at[0, j], s.result_sems.at[1, j], j)

    keys = s.text.shape[0]
    valid = lax.broadcasted_iota(jnp.int32, (ROWS, keys), 1) < length_ref[0]
    mod_scale = a.mod[:, 4 * width : 5 * width]
    work = s.work
    s.text_acc[...] = jnp.zeros_like(s.text_acc)
    s.mod_sum[...] = jnp.zeros_like(s.mod_sum)
    wait_all(cross_loads)

    def cross_chunk(k, carry):
        rows = pl.ds(pl.multiple_of(k * ROWS, ROWS), ROWS)
        cot = piece_rows(s.cots, k).astype(F32)
        d_mlp = s.dmlp[rows, :]
        normed, inv_std = normalize(s.third[rows, :])
        s.mod_sum[3:4, :] += jnp.sum(d_mlp, 0, keepdims=True)
        s.mod_sum[4:5, :] += jnp.sum(d_mlp * normed, 0, keepdims=True)
        d_third = cot + norm_back(d_mlp * (1.0 + mod_scale), normed, inv_std)
        s.dmlp[rows, :] = d_third
        d_branch = d_third.astype(BF)
        s.dcb[rows, :] = d_branch
        work[...] = mm_nt(d_branch, s.cout[...]).astype(BF)

        def pair(index, inner):
            at, after = slab_at(index), slab_at(index, width)
            grad_q, grad_k, grad_v = attend_slab_back(
                s.cq[rows, at], s.text[:, at], s.text[:, after], work[:, at], valid
            )
            s.dcq[rows, at] = grad_q.astype(BF)
            s.text_acc[:, at] += grad_k
            s.text_acc[:, after] += grad_v
            return inner

        lax.fori_loop(0, width // SLAB, pair, 0, unroll=2)
        return carry

    lax.fori_loop(0, chunks, cross_chunk, 0)
    s.dtext[...] = s.text_acc[...].astype(BF)
    wait_all(sum_loads)
    video_loads = [load(a.video.at[:, jnp.bitwise_xor(place, j)], s.cots.at[j]) for j in range(groups)]
    late_loads = [load(a.sout, s.cout), load(a.sbranch, s.cq)]

    wait_all(cross_grad_loads)
    pairs_c = [(s.cin, s.dcq), (s.words, s.dtext), (s.cmix, s.dcb)]

    def core_copy(cur, k, m):
        rows = pl.ds(pl.multiple_of(m * ROWS, ROWS), ROWS)
        return send(
            s.send.at[rows], flat_rows(cur).at[rows],
            s.core_sems.at[0, k, m], s.core_sems.at[1, k, m], 1,
        )

    def other_half(pairs, cur, k):
        def body(m, carry):
            grads_rows(pairs, 1 - core, m, s.send)
            core_copy(cur, k, m).start()
            return carry

        lax.fori_loop(0, width // ROWS, body, 0)

    def own_half(pairs, cur, k):
        def body(m, carry):
            core_copy(cur, k, m).wait()
            grads_rows(pairs, core, m, flat_rows(cur), flat_rows(cur))
            return carry

        lax.fori_loop(0, width // ROWS, body, 0)

    wait_all(temporal_loads)
    keep = (1 - keep_ref[0]).astype(F32)
    same = frame_mask(ROWS, a.firsts[0].shape[2])
    tproj, dtp = s.tproj, s.dtp

    def temporal_chunk(k):
        rows = slice(k * ROWS, (k + 1) * ROWS)
        normed, inv_std = normalize(s.mid[rows, :])
        d_mid = s.dmlp[rows, :] + norm_back(
            mm_nt(s.dcq[rows, :], s.cwq[...]), normed, inv_std
        )
        d_branch = (keep * d_mid).astype(BF)
        s.dtb[rows, :] = d_branch
        work[...] = mm_nt(d_branch, s.tout[...]).astype(BF)

        def pair(index, carry):
            at, after, last = slab_at(index), slab_at(index, width), slab_at(index, 2 * width)
            grad_q, grad_k, grad_v = attend_slab_back(
                tproj[rows, at], tproj[rows, after], tproj[rows, last], work[:, at], same
            )
            dtp[rows, at] = grad_q.astype(BF)
            dtp[rows, after] = grad_k.astype(BF)
            dtp[rows, last] = grad_v.astype(BF)
            return carry

        lax.fori_loop(0, width // SLAB, pair, 0, unroll=2)
        normed, inv_std = normalize(piece_rows(s.firsts, k).astype(F32))
        d_first = d_mid + norm_back(mm_nt(dtp[rows, :], s.tqkv[...]), normed, inv_std)
        d_first = d_first.astype(BF)
        for j in range(groups):
            buf = s.dfirsts if j == 0 else s.firsts
            buf[j, :, k] = d_first[j * share : (j + 1) * share].reshape(
                buf.shape[1:2] + buf.shape[3:]
            )

    def first_copy(j, k):
        return send(
            s.firsts.at[j, :, k], s.dfirsts.at[j, :, k],
            s.first_sems.at[0, j, k], s.first_sems.at[1, j, k], j,
        )

    gate = a.mod[:, 2 * width : 3 * width]
    scale = a.mod[:, width : 2 * width]

    def spatial_frame(f):
        rows = slice(f * ROWS, (f + 1) * ROWS)
        d_first = frame_rows(s.dfirsts, f).astype(F32)
        s.mod_sum[2:3, :] += jnp.sum(d_first * s.cq[rows, :].astype(F32), 0, keepdims=True)
        d_branch = (gate * d_first).astype(BF)
        s.dcb[rows, :] = d_branch
        work[...] = mm_nt(d_branch, s.cout[...]).astype(BF)

        def pair(index, carry):
            at, after, last = slab_at(index), slab_at(index, width), slab_at(index, 2 * width)
            grad_q, grad_k, grad_v = attend_slab_back(
                tproj[rows, at], tproj[rows, after], tproj[rows, last], work[:, at], None
            )
            dtp[rows, at] = grad_q.astype(BF)
            dtp[rows, after] = grad_k.astype(BF)
            dtp[rows, last] = grad_v.astype(BF)
            return carry

        lax.fori_loop(0, width // SLAB, pair, 0)

    def video_frame(f, carry):
        rows = pl.ds(pl.multiple_of(f * ROWS, ROWS), ROWS)
        video = frame_rows(s.cots, f).astype(F32)
        d_first = frame_rows(s.dfirsts, f).astype(F32)
        normed, inv_std = normalize(video)
        d_in = mm_nt(dtp[rows, :], s.tqkv[...])
        s.mod_sum[0:1, :] += jnp.sum(d_in, 0, keepdims=True)
        s.mod_sum[1:2, :] += jnp.sum(d_in * normed, 0, keepdims=True)
        grad = d_first + norm_back(d_in * (1.0 + scale), normed, inv_std)
        for j in range(groups):
            slot = jnp.bitwise_xor(place, j)
            at = pl.ds(pl.multiple_of(f * ROWS + slot * share, share), share)
            s.third[at, :] = grad[j * share : (j + 1) * share]
        return carry

    mod_all = s.mod_all

    def mod_copy(b):
        sems = s.mod_sems.at[0, b], s.mod_sems.at[1, b]
        if b < wide_bits:
            return send(s.mod_sum, s.mod_in.at[b], *sems, 1 << b)
        size = 1 << (b - wide_bits)
        span = mod_all.at[pl.ds(lax.div(narrow_at, size) * size, size)]
        return send(span, span, *sems, 1 << b)

    def mod_step(b):
        mod_copy(b).wait()
        if b < wide_bits:
            s.mod_sum[...] = s.mod_sum[...] + s.mod_in[b]
        if b == wide_bits - 1:
            mod_all[narrow_at] = s.mod_sum[...]
            mod_all[narrow_at, 6:7, :] = a.silu[...]
        if b < bits:
            mod_copy(b + 1).start()

    def ada_rows():
        mine = o.ada.shape[0] // (6 * width // 128)
        me = narrow_at * lax.axis_size("wide") + place
        row = lax.broadcasted_iota(jnp.int32, (mine, width), 0)
        col = lax.broadcasted_iota(jnp.int32, (mine, width), 1)
        picks = (col == me * mine + row).astype(F32).astype(BF)
        silu_mine = mm_nt(picks, mod_all[:, 6, :].astype(BF))
        pitch = 6 * width // 128
        for part in range(6):
            rows = 0.0
            for c in range(mod_all.shape[0]):
                rows = rows + silu_mine[:, c : c + 1] * mod_all[c, part : part + 1, :]
            store_flat(s.flat_ada, rows, part * width // 128, pitch)
        return load(s.flat_ada, o.ada)

    r_in[0].step(0)
    r_out[0].copy(0).start()
    r_in[1].step(0)
    other_half(pairs_c, s.cur_c, 0)
    temporal_chunk(0)
    for j in others:
        first_copy(j, 0).start()
    r_out[1].step(0)
    r_out[2].step(0)
    own_half(pairs_c, s.cur_c, 0)
    temporal_grad_loads = [load(a.tin, s.cin), load(a.tmix, s.cmix)]
    r_c[1].copy(0).start()
    r_c[2].copy(0).start()
    r_c[0].copy(0).start()
    r_in[0].step(1)
    temporal_chunk(1)
    late_loads += [load(a.sproj, s.tproj), load(a.sqkv, s.tqkv)]
    held = s.dcq.reshape(groups, *a.results[0].shape)
    result_loads = [load(a.results[j], held.at[j]) for j in range(groups)]
    for j in others:
        first_copy(j, 1).start()
    wait_all(temporal_grad_loads)
    pairs_t = [(s.cin, dtp), (s.cmix, s.dtb)]
    other_half(pairs_t, s.cur_t, 1)
    r_out[2].step(1)
    r_in[1].step(1)
    r_out[0].step(0)
    r_out[1].step(1)
    r_in[2].step(0)
    for j in others:
        first_copy(j, 0).wait()
    r_c[1].step(0)
    r_c[2].step(0)
    r_c[0].step(0)
    own_half(pairs_t, s.cur_t, 1)
    spatial_grad_loads = [load(a.sin, s.cin), load(a.smix, s.cmix)]
    r_t[2].copy(0).start()
    r_t[0].copy(0).start()
    for j in others:
        first_copy(j, 1).wait()
    wait_all(late_loads)
    spatial_frame(0)
    r_out[2].step(2)
    r_out[0].step(1)
    r_in[0].step(2)
    r_in[1].step(2)
    r_c[1].step(1)
    r_t[1].copy(0).start()
    r_out[1].step(2)
    r_in[2].step(1)
    spatial_frame(1)
    r_out[0].step(2)
    r_c[0].step(1)
    wait_all(spatial_grad_loads)
    pairs_s = [(s.cin, dtp), (s.cmix, s.dcb)]
    other_half(pairs_s, s.cur_s, 2)
    r_t[1].step(0)
    r_t[0].step(0)
    r_t[2].step(0)
    own_half(pairs_s, s.cur_s, 2)
    r_s[0].copy(0).start()
    r_s[1].copy(0).start()
    r_s[2].copy(0).start()
    r_c[2].step(1)
    r_c[1].step(2)
    r_t[1].step(1)
    r_c[0].step(2)
    r_out[1].step(3)
    r_t[0].step(1)
    r_t[2].step(1)
    r_c[1].step(3)
    wait_all(video_loads)
    lax.fori_loop(0, frames, video_frame, 0)
    grad_write = load(s.third, o.video_grad)
    s.mod_sum[5:6, :] = a.dgate_two[...]
    mod_copy(0).start()
    r_s[2].step(0)
    r_s[1].step(0)
    r_in[2].step(2)
    r_c[2].step(2)
    r_s[0].step(0)
    mod_step(0)
    r_t[1].step(2)
    r_in[2].step(3)
    r_in[1].step(3)
    r_t[2].step(2)
    r_s[2].step(1)
    mod_step(1)
    r_out[2].step(3)
    r_s[1].step(1)
    r_c[2].step(3)
    r_in[0].step(3)
    wait_all(result_loads)
    for j in range(groups):
        result_copy(j).start()
    r_s[0].step(1)
    mod_step(2)
    r_t[0].step(2)
    r_out[0].step(3)
    r_s[2].step(2)
    r_t[2].step(3)
    r_t[1].step(3)
    mod_step(3)
    r_s[1].step(2)
    e_in.swap().start()
    r_s[0].step(2)
    r_s[2].step(3)
    e_out.swap().start()
    e_in.store()
    r_c[0].step(3)
    r_s[1].step(3)
    mod_step(4)
    ada_write = ada_rows()
    r_t[0].step(3)
    e_out.store()
    e_t.swap().start()
    e_c.swap().start()
    r_s[0].step(3)
    e_t.store()
    e_s.swap().start()
    e_c.store()
    for j in range(groups):
        result_copy(j).wait()
    grad_write.wait()
    e_out.wait()
    e_in.wait()
    e_c.wait()
    e_t.wait()
    e_s.store()
    ada_write.wait()
    e_s.wait()


def copy_out(ins, outs, bufs, in_sems, out_sems):
    ins, outs, bufs = jax.tree.leaves(ins), jax.tree.leaves(outs), jax.tree.leaves(bufs)
    reads = [
        pltpu.make_async_copy(src, buf, in_sems.at[k])
        for k, (src, buf) in enumerate(zip(ins, bufs))
    ]
    writes = [
        pltpu.make_async_copy(buf, dst, out_sems.at[k])
        for k, (buf, dst) in enumerate(zip(bufs, outs))
    ]
    for read in reads:
        read.start()
    for read, write in zip(reads, writes):
        read.wait()
        write.start()
    for write in writes:
        write.wait()


def weight_grads(core_ref, *refs, count):
    pairs, outs = refs[: 2 * count], refs[2 * count :]
    core = core_ref[0]
    for sign, out in enumerate(outs):
        side = 1 - core if sign == 0 else core
        start = 0
        for k in range(count):
            left, right = pairs[2 * k], pairs[2 * k + 1]
            part = right.shape[1] // 2
            cols = pl.ds(pl.multiple_of(side * part, 128), part)
            out[:, start : start + part] = mm_tn(left[...], right[:, cols]).astype(BF)
            start += part


def weight_grads_call(core, pairs):
    depth = pairs[0][0].shape[1]
    total = sum(right.shape[1] for _, right in pairs)
    tile = 256
    specs = []
    for left, right in pairs:
        specs.append(pl.BlockSpec((left.shape[0], tile), lambda m, _: (0, m)))
        specs.append(fixed(right.shape))
    shape = jax.ShapeDtypeStruct((depth, total // 2), BF)
    flops = sum(2 * left.shape[0] * depth * right.shape[1] for left, right in pairs)
    return pl.pallas_call(
        functools.partial(weight_grads, count=len(pairs)),
        grid_spec=pltpu.PrefetchScalarGridSpec(
            num_scalar_prefetch=1,
            grid=(depth // tile,),
            in_specs=specs,
            out_specs=[pl.BlockSpec((tile, total // 2), lambda m, _: (m, 0))] * 2,
        ),
        out_shape=[shape, shape],
        compiler_params=params(),
        cost_estimate=cost(flops, 8e6),
        name="weight_grads",
    )(core, *[a for pair in pairs for a in pair])


def shards(
    video,
    text_states,
    text_length,
    timestep,
    motion_free,
    ada_weight,
    spatial_qkv_weight,
    spatial_out_weight,
    temporal_qkv_weight,
    temporal_out_weight,
    cross_query_weight,
    cross_kv_weight,
    cross_out_weight,
    mlp_in_weight,
    mlp_out_weight,
    cotangent,
    *,
    mesh_shape,
):
    clips, frames, patches, width = video.shape
    if clips != 1 or patches != ROWS:
        raise ValueError("unsupported shard")
    wide, narrow = mesh_shape["wide"], mesh_shape["narrow"]
    devices = wide * narrow
    groups = wide
    here = patches // groups
    tokens = frames * patches
    chunks = tokens // ROWS
    per_chunk = here // chunks
    hidden = mlp_in_weight.shape[1]
    text_rows = text_states.shape[1]
    text_pad = -(-text_rows // 128) * 128

    wide_at = lax.axis_index("wide")
    narrow_at = lax.axis_index("narrow")
    index = narrow_at * wide + wide_at
    core = jnp.bitwise_and(wide_at, 1)
    place = wide_at.reshape(1).astype(jnp.int32)
    core_arr = core.reshape(1).astype(jnp.int32)
    wide_bits = wide.bit_length() - 1
    bits = devices.bit_length() - 1

    cot_view = cotangent.reshape(frames, groups, here, width)

    silu_time = silu_of(time_features(timestep.astype(F32), width)).astype(BF)
    mod = mm(silu_time, ada_weight)
    text_flat = text_states.reshape(text_rows, width)
    text_flat = jnp.pad(text_flat, ((0, text_pad - text_rows), (0, 0)))
    text_proj = mm(text_flat, cross_kv_weight).astype(BF)

    video_view = video.reshape(frames, groups, here, width)

    def own_patches(j):
        return pl.BlockSpec(
            (1, 1, here, width),
            lambda f, *_: (f, jnp.bitwise_xor(lax.axis_index("wide"), j), 0, 0),
        )

    def frame_piece():
        return pl.BlockSpec((1, chunks, per_chunk, width), lambda f, *_: (f, 0, 0, 0))

    def chunk_piece():
        return pl.BlockSpec((frames, 1, per_chunk, width), lambda k, *_: (0, k, 0, 0))

    def row_block(cols):
        return pl.BlockSpec((ROWS, cols), lambda f, *_: (f, 0))

    piece_shape = jax.ShapeDtypeStruct((frames, chunks, per_chunk, width), BF)

    def rows_of(cols, dtype=BF):
        return jax.ShapeDtypeStruct((tokens, cols), dtype)

    mod_spec = fixed(mod.shape)
    anywhere = pl.BlockSpec(memory_space=pl.ANY)
    own_piece = jax.ShapeDtypeStruct((frames, here, width), BF)
    outs = pl.pallas_call(
        functools.partial(spatial_forward, groups=groups, width=width, frames=frames),
        grid_spec=pltpu.PrefetchScalarGridSpec(
            num_scalar_prefetch=0,
            grid=(frames,),
            in_specs=[own_patches(j) for j in range(groups)]
            + [mod_spec, fixed(spatial_qkv_weight.shape), fixed(spatial_out_weight.shape)],
            out_specs=[row_block(width), row_block(3 * width), row_block(width), row_block(width)]
            + [pl.BlockSpec((1, here, width), lambda f, *_: (f, 0, 0))]
            + [anywhere] * (groups - 1),
            scratch_shapes=[
                pltpu.VMEM((groups - 1, frames, here, width), BF),
                pltpu.SemaphoreType.DMA((2, groups - 1, frames)),
            ],
        ),
        out_shape=[rows_of(width), rows_of(3 * width), rows_of(width), rows_of(width)]
        + [own_piece] * groups,
        compiler_params=params(collective_id=0, has_side_effects=True),
        cost_estimate=cost(8 * tokens * width * width, 10e6, tokens * patches * 12),
        name="spatial_forward",
    )(*[video_view] * groups, mod, spatial_qkv_weight, spatial_out_weight)
    spatial_in, spatial_proj, spatial_mix, spatial_branch = outs[:4]
    firsts = [p.reshape(piece_shape.shape) for p in outs[4 : 4 + groups]]

    def two_scalars(grid, in_specs, out_specs, scratch=()):
        return pltpu.PrefetchScalarGridSpec(
            num_scalar_prefetch=2,
            grid=grid,
            in_specs=in_specs,
            out_specs=out_specs,
            scratch_shapes=scratch,
        )

    outs = pl.pallas_call(
        functools.partial(
            middle_forward, groups=groups, width=width, per_chunk=per_chunk, chunks=chunks
        ),
        grid_spec=two_scalars(
            (chunks,),
            [chunk_piece() for _ in range(groups)]
            + [
                anywhere,
                mod_spec,
                fixed(temporal_qkv_weight.shape),
                fixed(temporal_out_weight.shape),
                fixed(cross_query_weight.shape),
                fixed(text_proj.shape),
                fixed(cross_out_weight.shape),
            ],
            [
                row_block(width),
                row_block(3 * width),
                row_block(width),
                row_block(width),
                row_block(width),
                row_block(width),
                row_block(width),
                row_block(width),
                row_block(width),
            ]
            + [anywhere] * groups,
            [
                pltpu.VMEM((groups, frames, here, width), BF),
                pltpu.SemaphoreType.DMA((groups,)),
                pltpu.SemaphoreType.DMA((2, groups)),
            ],
        ),
        out_shape=[
            rows_of(width),
            rows_of(3 * width),
            rows_of(width),
            rows_of(width),
            rows_of(width),
            rows_of(width),
            rows_of(width),
            rows_of(width, F32),
            rows_of(width, F32),
        ]
        + [own_piece] * groups,
        compiler_params=params(collective_id=4, has_side_effects=True),
        cost_estimate=cost(12 * tokens * width * width, 20e6, tokens * ROWS * 18),
        name="middle_forward",
    )(
        text_length,
        motion_free,
        *firsts,
        cot_view,
        mod,
        temporal_qkv_weight,
        temporal_out_weight,
        cross_query_weight,
        text_proj,
        cross_out_weight,
    )
    temporal_in, temporal_proj, temporal_mix, cross_in, cross_q, cross_mix, mlp_in, mid, third = outs[:9]
    cots = [p.reshape(piece_shape.shape) for p in outs[9:]]

    steps = 4
    wide_h = hidden // steps

    def hidden_at(step):
        half = steps // 2
        side_bit = jnp.bitwise_and(lax.axis_index("wide"), 1)
        side = jnp.where(step < half, 1 - side_bit, side_bit)
        return side * half + lax.rem(step, half)

    whole_piece = fixed((frames, chunks, per_chunk, width))
    outs = pl.pallas_call(
        functools.partial(mlp_both, groups=groups, width=width, steps=steps),
        grid_spec=pltpu.PrefetchScalarGridSpec(
            num_scalar_prefetch=0,
            grid=(steps,),
            in_specs=[whole_piece] * groups
            + [
                fixed(mlp_in.shape),
                fixed(third.shape),
                mod_spec,
                pl.BlockSpec((width, wide_h), lambda s: (0, hidden_at(s))),
                pl.BlockSpec((wide_h, width), lambda s: (hidden_at(s), 0)),
            ],
            out_specs=[
                pl.BlockSpec((width, wide_h), lambda s: (0, jnp.maximum(s - steps // 2, 0))),
                fixed((hidden, width // 2)),
                fixed((tokens, width)),
                fixed((1, width)),
            ]
            + [whole_piece] * groups,
            scratch_shapes=[
                pltpu.VMEM((width, tokens), BF),
                pltpu.VMEM((tokens, width), BF),
                pltpu.VMEM((tokens, width), F32),
                pltpu.VMEM((steps // 2, width, wide_h), BF),
                pltpu.VMEM((steps // 2, width, wide_h), BF),
                pltpu.VMEM((steps, wide_h, width // 2), BF),
                pltpu.VMEM((steps, wide_h, width // 2), BF),
                pltpu.VMEM((steps, wide_h, width // 2), BF),
                pltpu.SemaphoreType.DMA((2, steps // 2)),
                pltpu.SemaphoreType.DMA((2, steps)),
            ],
        ),
        out_shape=[
            jax.ShapeDtypeStruct((width, hidden // 2), BF),
            jax.ShapeDtypeStruct((hidden, width // 2), BF),
            rows_of(width, F32),
            jax.ShapeDtypeStruct((1, width), F32),
        ]
        + [piece_shape] * groups,
        compiler_params=params(collective_id=1, has_side_effects=True),
        cost_estimate=cost(12 * tokens * width * hidden, 25e6, tokens * hidden),
        name="mlp_both",
    )(*cots, mlp_in, third, mod, mlp_in_weight, mlp_out_weight)
    sum_in, sum_out, d_mlp_in, d_gate_two = outs[:4]
    if bits == 5 and frames == 2 and width == 768 and hidden % 768 == 0:
        chip = (2,) * (bits - 1)
        nb = bits - 1
        rows_in, rows_out = 2 * width // devices, 2 * hidden // devices
        cols_in, cols_out = hidden // 2, width // 2
        vm, sems = pltpu.VMEM, pltpu.SemaphoreType.DMA
        act = lambda cols, dtype=BF: vm((tokens, cols), dtype)
        group = vm(chip + (rows_in, cols_in), BF)
        pieces = vm((groups, frames, chunks, per_chunk, width), BF)
        ins = dict(
            cots=tuple(cots),
            dmlp=d_mlp_in,
            third=third,
            mid=mid,
            mod=mod,
            silu=silu_time.astype(F32),
            dgate_two=d_gate_two,
            cq=cross_q,
            text=text_proj,
            tproj=temporal_proj,
            cout=cross_out_weight,
            cwq=cross_query_weight,
            tout=temporal_out_weight,
            tqkv=temporal_qkv_weight,
            firsts=tuple(firsts),
            cin=cross_in,
            cmix=cross_mix,
            words=text_flat,
            tin=temporal_in,
            tmix=temporal_mix,
            sum_out=sum_out.reshape(chip + (rows_out, cols_out)),
            sum_in=sum_in.reshape(chip + (rows_in, cols_in)),
            results=tuple(p.reshape(frames, here, width) for p in outs[4 : 4 + groups]),
            video=video.reshape(frames, groups, chunks, per_chunk, width),
            sbranch=spatial_branch,
            sout=spatial_out_weight,
            sproj=spatial_proj,
            sin=spatial_in,
            smix=spatial_mix,
            sqkv=spatial_qkv_weight,
        )
        in_specs = jax.tree.map(lambda _: anywhere, ins)
        for name in ("mod", "silu", "dgate_two"):
            in_specs[name] = fixed(ins[name].shape)

        def flat_shapes(elements):
            return tuple(jax.ShapeDtypeStruct((n // devices // 128, 128), F32) for n in elements)

        square = width * width
        out_shape = dict(
            result=jax.ShapeDtypeStruct((frames, groups, here, width), BF),
            video_grad=jax.ShapeDtypeStruct((tokens, width), F32),
            ada=flat_shapes([6 * square])[0],
            spatial=flat_shapes([3 * square, square]),
            temporal=flat_shapes([3 * square, square]),
            cross=flat_shapes([square, 2 * square, square]),
            mlp_in=flat_shapes([width * hidden]),
            mlp_out=flat_shapes([width * hidden]),
        )
        in_hbm = pl.BlockSpec(memory_space=pltpu.HBM)
        out_specs = jax.tree.map(lambda _: in_hbm, out_shape)
        flats = jax.tree.map(lambda leaf: vm(leaf.shape, F32), out_shape)

        def streams_in():
            return stream_scratch(rows_in, cols_in, nb, 3)

        def fin(rows, cols, count):
            return vm((2, rows // 2, cols), F32), vm((rows // 2, cols), F32), sems((2 + count,))

        fin_out, fin_out_in, end_out = fin(rows_out, cols_out, 1)
        fin_in, fin_in_in, end_in = fin(rows_in, cols_in, 1)
        fin_c, fin_c_in, end_c = fin(rows_in, cols_in, 3)
        fin_t, fin_t_in, end_t = fin(rows_in, cols_in, 2)
        scratch = dict(
            local=sems((64,)),
            cots=pieces,
            firsts=pieces,
            dfirsts=pieces,
            dmlp=act(width, F32),
            third=act(width, F32),
            mid=act(width, F32),
            cq=act(width),
            text=vm(text_proj.shape, BF),
            tproj=act(3 * width),
            cout=vm((width, width), BF),
            cwq=vm((width, width), BF),
            tout=vm((width, width), BF),
            tqkv=vm((width, 3 * width), BF),
            cin=act(width),
            cmix=act(width),
            words=vm(text_flat.shape, BF),
            st_out=stream_scratch(rows_out, cols_out, nb, 3),
            st_in=streams_in(),
            st_c=streams_in(),
            st_t=streams_in(),
            st_s=streams_in(),
            cur_out=vm(chip + (rows_out, cols_out), BF),
            cur_in=group,
            cur_c=group,
            cur_t=group,
            cur_s=group,
            send=vm((width, cols_in), BF),
            fin_out=fin_out,
            fin_in=fin_in,
            fin_c=fin_c,
            fin_t=fin_t,
            fin_s=fin_t,
            fin_out_in=fin_out_in,
            fin_in_in=fin_in_in,
            fin_c_in=fin_c_in,
            fin_t_in=fin_t_in,
            fin_s_in=fin_t_in,
            end_out=end_out,
            end_in=end_in,
            end_c=end_c,
            end_t=end_t,
            end_s=end_t,
            flat_out=flats["mlp_out"],
            flat_in=flats["mlp_in"],
            flat_c=flats["cross"],
            flat_t=flats["temporal"],
            flat_s=flats["spatial"],
            flat_ada=flats["ada"],
            core_sems=sems((2, 3, width // ROWS)),
            result_sems=sems((2, groups)),
            first_sems=sems((2, groups, chunks)),
            mod_sems=sems((2, bits)),
            text_acc=vm(text_proj.shape, F32),
            work=vm((ROWS, width), BF),
            dcb=act(width),
            dcq=act(width),
            dtext=vm(text_proj.shape, BF),
            dtb=act(width),
            dtp=act(3 * width),
            mod_sum=vm((8, width), F32),
            mod_in=vm((wide_bits, 8, width), F32),
            mod_all=vm((narrow, 8, width), F32),
        )
        back = pl.pallas_call(
            with_scratch(backward, scratch),
            grid_spec=pltpu.PrefetchScalarGridSpec(
                num_scalar_prefetch=2,
                grid=(1,),
                in_specs=[in_specs],
                out_specs=out_specs,
                scratch_shapes=jax.tree.leaves(scratch),
            ),
            out_shape=out_shape,
            compiler_params=params(collective_id=2, has_side_effects=True),
            cost_estimate=cost(74 * tokens * width * width, 70e6, tokens * ROWS * 30),
            name="backward",
        )(text_length, motion_free, ins)
        back = pl.pallas_call(
            copy_out,
            grid=(),
            in_specs=[jax.tree.map(lambda _: anywhere, out_shape)],
            out_specs=out_specs,
            out_shape=out_shape,
            scratch_shapes=[
                jax.tree.map(lambda leaf: vm(leaf.shape, leaf.dtype), out_shape),
                sems((len(jax.tree.leaves(out_shape)),)),
                sems((len(jax.tree.leaves(out_shape)),)),
            ],
            compiler_params=params(),
            cost_estimate=cost(0, 9e6),
            name="copy_out",
        )(back)
        grads = (
            [back["ada"]]
            + list(back["spatial"])
            + list(back["temporal"])
            + list(back["cross"])
            + list(back["mlp_in"])
            + list(back["mlp_out"])
        )
        return (
            back["result"].reshape(video.shape),
            back["video_grad"].reshape(video.shape),
        ) + tuple(g.reshape(-1) for g in grads)

    def flip(value, mask):
        return lax.ppermute(value, AXES, [(i, i ^ mask) for i in range(devices)])

    def bit_of(b):
        return jnp.bitwise_and(lax.shift_right_logical(index, b), 1)

    def gather_narrow(row):
        for b in range(wide_bits, bits):
            other = flip(row, 1 << b)
            mine = bit_of(b) == 0
            row = jnp.concatenate(
                [jnp.where(mine, row, other), jnp.where(mine, other, row)], 0
            )
        return row

    times = gather_narrow(timestep.astype(F32).reshape(1, 1))
    silu_all = silu_of(time_features(times[:, 0], width)).astype(BF).astype(F32)
    mine = width // devices
    silu_rows = lax.dynamic_slice_in_dim(silu_all, index * mine, mine, 1)

    results = [outs[4]] + [flip(outs[4 + j], j) for j in range(1, groups)]

    outs = pl.pallas_call(
        functools.partial(middle_backward, groups=groups, width=width, per_chunk=per_chunk),
        grid_spec=two_scalars(
            (chunks,),
            [chunk_piece() for _ in range(groups)]
            + [
                row_block(width),
                row_block(width),
                row_block(width),
                mod_spec,
                row_block(width),
                row_block(3 * width),
                row_block(width),
                fixed(text_proj.shape),
                fixed(cross_out_weight.shape),
                fixed(cross_query_weight.shape),
                fixed(temporal_out_weight.shape),
                fixed(temporal_qkv_weight.shape),
            ]
            + [chunk_piece() for _ in range(groups)],
            [
                row_block(width),
                row_block(width),
                fixed((text_pad, 2 * width)),
                row_block(width),
                row_block(3 * width),
                fixed((2, width)),
            ]
            + [chunk_piece() for _ in range(groups)],
            [pltpu.VMEM((text_pad, 2 * width), F32), pltpu.VMEM((ROWS, width), BF)],
        ),
        out_shape=[
            rows_of(width),
            rows_of(width),
            jax.ShapeDtypeStruct((text_pad, 2 * width), BF),
            rows_of(width),
            rows_of(3 * width),
            jax.ShapeDtypeStruct((2, width), F32),
        ]
        + [piece_shape] * groups,
        compiler_params=params(),
        cost_estimate=cost(20 * tokens * width * width, 25e6, tokens * ROWS * 18),
        name="middle_backward",
    )(
        text_length,
        motion_free,
        *cots,
        d_mlp_in,
        third,
        mid,
        mod,
        temporal_in,
        temporal_proj,
        cross_q,
        text_proj,
        cross_out_weight,
        cross_query_weight,
        temporal_out_weight,
        temporal_qkv_weight,
        *firsts,
    )
    d_cross_branch, d_cross_q, d_text, d_temporal_branch, d_temporal_proj, d_mod_two = outs[:6]
    d_firsts = [outs[6]] + [flip(outs[6 + j], j) for j in range(1, groups)]

    cross_send, cross_keep = weight_grads_call(
        core_arr,
        [(cross_in, d_cross_q), (text_flat, d_text), (cross_mix, d_cross_branch)],
    )
    temporal_send, temporal_keep = weight_grads_call(
        core_arr,
        [(temporal_in, d_temporal_proj), (temporal_mix, d_temporal_branch)],
    )

    d_spatial_branch, d_spatial_proj, d_gate_one = pl.pallas_call(
        functools.partial(spatial_backward, groups=groups, width=width),
        grid=(frames,),
        in_specs=[frame_piece() for _ in range(groups)]
        + [mod_spec, row_block(width), row_block(3 * width), fixed(spatial_out_weight.shape)],
        out_specs=[row_block(width), row_block(3 * width), fixed((1, width))],
        out_shape=[rows_of(width), rows_of(3 * width), jax.ShapeDtypeStruct((1, width), F32)],
        scratch_shapes=[pltpu.VMEM((ROWS, width), BF)],
        compiler_params=params(),
        cost_estimate=cost(8 * tokens * width * width, 10e6, tokens * patches * 12),
        name="spatial_backward",
    )(*d_firsts, mod, spatial_branch, spatial_proj, spatial_out_weight)

    spatial_send, spatial_keep = weight_grads_call(
        core_arr,
        [(spatial_in, d_spatial_proj), (spatial_mix, d_spatial_branch)],
    )

    out_block = pl.BlockSpec((1, groups, here, width), lambda f, *_: (f, 0, 0, 0))
    video_grad, result, d_mod_one = pl.pallas_call(
        functools.partial(video_backward, groups=groups, width=width),
        grid_spec=pltpu.PrefetchScalarGridSpec(
            num_scalar_prefetch=1,
            grid=(frames,),
            in_specs=[own_patches(j) for j in range(groups)]
            + [frame_piece() for _ in range(2 * groups)]
            + [mod_spec, row_block(3 * width), fixed(spatial_qkv_weight.shape)],
            out_specs=[out_block, out_block, fixed((2, width))],
        ),
        out_shape=[
            jax.ShapeDtypeStruct((frames, groups, here, width), F32),
            jax.ShapeDtypeStruct((frames, groups, here, width), BF),
            jax.ShapeDtypeStruct((2, width), F32),
        ],
        compiler_params=params(),
        cost_estimate=cost(6 * tokens * width * width, 12e6),
        name="video_backward",
    )(place, *[video_view] * groups, *d_firsts, *results, mod, d_spatial_proj, spatial_qkv_weight)
    video_grad = video_grad.reshape(video.shape)
    result = result.reshape(video.shape)

    d_mod = jnp.concatenate([d_mod_one, d_gate_one, d_mod_two, d_gate_two], 0)
    for b in range(wide_bits):
        d_mod = d_mod + flip(d_mod, 1 << b)
    d_mod_all = gather_narrow(d_mod[None])
    ada_rows = jnp.sum(silu_rows[:, :, None, None] * d_mod_all[:, None, :, :], 0)
    ada_grad = ada_rows.reshape(-1)

    chip_bits = list(range(1, bits))
    first_x = [wide_bits, 1]
    rest = [b for b in chip_bits if b not in first_x]
    order_a = first_x + rest
    order_b = first_x[::-1] + rest

    def join(send, keep):
        return keep.astype(F32) + flip(send, 1).astype(F32)

    def reduce_scatter(cur, order):
        cols = cur.shape[1]
        axes = sorted(chip_bits, reverse=True)
        for b in order:
            cur = cur.astype(BF)
            at = axes.index(b)
            view = cur.reshape(1 << at, 2, 1 << (len(axes) - at - 1), -1, cols)
            out = lax.dynamic_index_in_dim(view, 1 - bit_of(b), 1, keepdims=False)
            own = lax.dynamic_index_in_dim(view, bit_of(b), 1, keepdims=False)
            cur = own.astype(F32) + flip(out, 1 << b).astype(F32)
            axes.remove(b)
        cur = cur.reshape(2, -1, cols)
        own = lax.dynamic_index_in_dim(cur, core, 0, keepdims=False)
        other = flip(lax.dynamic_index_in_dim(cur, 1 - core, 0, keepdims=False), 1)
        low = jnp.where(core == 0, own, other)
        high = jnp.where(core == 0, other, own)
        return low, high

    def unpack(pair, widths):
        low, high = pair
        start, out = 0, []
        for w in widths:
            half = w // 2
            cols = slice(start, start + half)
            out.append(jnp.concatenate([low[:, cols], high[:, cols]], 1).reshape(-1))
            start += half
        return out

    mlp_out_grad = unpack(reduce_scatter(sum_out, order_a), [width])[0]
    mlp_in_grad = unpack(reduce_scatter(sum_in, order_b), [hidden])[0]
    cross_query_grad, cross_kv_grad, cross_out_grad = unpack(
        reduce_scatter(join(cross_send, cross_keep), order_a), [width, 2 * width, width]
    )
    temporal_qkv_grad, temporal_out_grad = unpack(
        reduce_scatter(join(temporal_send, temporal_keep), order_b), [3 * width, width]
    )
    spatial_qkv_grad, spatial_out_grad = unpack(
        reduce_scatter(join(spatial_send, spatial_keep), order_a), [3 * width, width]
    )
    return (
        result,
        video_grad,
        ada_grad,
        spatial_qkv_grad,
        spatial_out_grad,
        temporal_qkv_grad,
        temporal_out_grad,
        cross_query_grad,
        cross_kv_grad,
        cross_out_grad,
        mlp_in_grad,
        mlp_out_grad,
    )


def solution(mesh):
    tokens_spec = P("narrow", "wide", None, None)
    in_specs = (
        (tokens_spec, P("narrow", None, None), P("narrow"), P("narrow"), P("narrow"))
        + (P(),) * 10
        + (tokens_spec,)
    )
    out_specs = (tokens_spec, tokens_spec) + (P(AXES),) * 10
    return jax.shard_map(
        functools.partial(shards, mesh_shape=dict(mesh.shape)),
        mesh=mesh,
        in_specs=in_specs,
        out_specs=out_specs,
        check_vma=False,
    )
```
